32 devices in a mesh: dp: 8 (over z, y), tensor: 4 (over x, core).
Axes of the slice: x: 2, y: 2, z: 4, core: 2. Of those that a mesh axis runs over, the one named last changes fastest.
Arguments:
- image_tokens: bfloat16 [16, 1024, 1536], P('dp', 'tensor'), may hold values from -6 to 6
- text_tokens: bfloat16 [16, 160, 1536], P('dp', 'tensor'), may hold values from -6 to 6
- conditioning: bfloat16 [16, 1536], P('dp'), may hold values from -6 to 6
- group_seqs: int32 [8], P('dp'), may hold values from 0 to 2, as said below
- ada_weight: bfloat16 [2, 6, 1536, 1536], P(None, None, 'dp', 'tensor'), may hold values from -0.15625 to 0.15625
- ada_bias: bfloat16 [2, 6, 1536], replicated, may hold values from -3 to 3
- qkv_weight: bfloat16 [2, 3, 1536, 1536], P(None, None, 'dp', 'tensor'), may hold values from -0.15625 to 0.15625
- qv_bias: bfloat16 [2, 2, 1536], replicated, may hold values from -3 to 3
- proj_weight: bfloat16 [2, 1536, 1536], P(None, 'tensor', 'dp'), may hold values from -2.5 to 2.5
- proj_bias: bfloat16 [2, 1536], replicated, may hold values from -3 to 3
- fc1_weight: bfloat16 [2, 1536, 6144], P(None, 'dp', 'tensor'), may hold values from -0.15625 to 0.15625
- fc1_bias: bfloat16 [2, 6144], replicated, may hold values from -3 to 3
- fc2_weight: bfloat16 [2, 6144, 1536], P(None, 'tensor', 'dp'), may hold values from -0.078125 to 0.078125
- fc2_bias: bfloat16 [2, 1536], replicated, may hold values from -3 to 3
- image_cot: bfloat16 [16, 1024, 1536], P('dp', 'tensor'), may hold values from -6 to 6
- text_cot: bfloat16 [16, 160, 1536], P('dp', 'tensor'), may hold values from -6 to 6
Outputs:
- image_out: bfloat16 [16, 1024, 1536], P('dp', 'tensor')
- text_out: bfloat16 [16, 160, 1536], P('dp', 'tensor')
- image_grad: float32 [16, 1024, 1536], P('dp', 'tensor')
- text_grad: float32 [16, 160, 1536], P('dp', 'tensor')
- cond_grad: float32 [16, 1536], P('dp', 'tensor')
- ada_weight_grad: float32 [2, 6, 1536, 1536], P(None, None, 'dp', 'tensor')
- ada_bias_grad: float32 [2, 6, 1536], replicated
- qkv_weight_grad: float32 [2, 3, 1536, 1536], P(None, None, 'dp', 'tensor')
- qv_bias_grad: float32 [2, 2, 1536], replicated
- proj_weight_grad: float32 [2, 1536, 1536], P(None, 'tensor', 'dp')
- proj_bias_grad: float32 [2, 1536], replicated
- fc1_weight_grad: float32 [2, 1536, 6144], P(None, 'dp', 'tensor')
- fc1_bias_grad: float32 [2, 6144], replicated
- fc2_weight_grad: float32 [2, 6144, 1536], P(None, 'tensor', 'dp')
- fc2_bias_grad: float32 [2, 1536], replicated
The draws below stay inside these ranges and needn't reach their ends.
Inputs may be any that keep to these rules, and one draw needn't show every extreme that they name: A data group's sequences fill its first group_seqs[g] slots; its other slots of 2 are empty. The counts sum to 8; in every draw some group holds 2 sequences and some none.
All inputs are finite; a program needn't handle non-finite values.
Results may differ from the reference program's by a relative error of at most 0.02.
Values may be sent and summed in bfloat16 or wider, within the bound.
No kernel may reach another device: no remote copies, remote signals or barrier semaphores. Data moves between devices by JAX's collectives and lax.ppermute only.
A program may use at most 512 MiB of HBM per device.

```python
import math
import jax
import jax.numpy as jnp
from jax import lax

D = 1536
HEADS = 24
HEAD_DIM = 64
FF = 6144
IMG = 1024
TXT = 160
CAP = 2
SEQS = 8
SLOTS = 16


def draw_group_seqs(key, part):
    order = jax.random.permutation(key, SEQS)
    quarter = SEQS // 4
    return jnp.where(order < quarter, CAP, jnp.where(order < 2 * quarter, 0, 1)).astype(jnp.int32)


def block_levels(rng, shape, cuts, smallest, high):
    def one(position, blocks):
        steps = jax.random.uniform(jax.random.fold_in(jax.random.fold_in(rng, 6), position), (blocks,), jnp.float32, smallest / len(cuts), high / len(cuts))
        return jnp.repeat(jnp.exp(steps), shape[position] // blocks).reshape((-1,) + (1,) * (len(shape) - position - 1))

    level = one(*cuts[0])
    for cut in cuts[1:]:
        level = level * one(*cut)
    return level


def noise(stream_key, dims, scale, bound, split=(), kind=jnp.bfloat16):
    factor_of = block_levels(stream_key, dims, split, -0.22, 0.18) if split else 1.0
    entries = jax.random.normal(stream_key, dims, jnp.float32) * scale * factor_of
    return jnp.minimum(jnp.maximum(entries, -bound), bound).astype(kind)


def setup_inputs(seed: int = 0) -> dict:
    seeds = jax.random.split(jax.random.key(seed), 17)
    return {
        "image_tokens": noise(seeds[0], (SLOTS, IMG, D), 1.0, 6.0, ((0, 8), (1, 4))),
        "text_tokens": noise(seeds[1], (SLOTS, TXT, D), 1.0, 6.0, ((0, 8), (1, 4))),
        "conditioning": noise(seeds[2], (SLOTS, D), 1.0, 6.0, ((0, 8),)),
        "group_seqs": draw_group_seqs(jax.random.fold_in(seeds[16], 71), 0),
        "ada_weight": noise(seeds[4], (2, 6, D, D), D ** -0.5, 0.15625, ((2, 8), (3, 4))),
        "ada_bias": noise(seeds[5], (2, 6, D), 0.5, 3.0),
        "qkv_weight": noise(seeds[6], (2, 3, D, D), D ** -0.5, 0.15625, ((2, 8), (3, 4))),
        "qv_bias": noise(seeds[7], (2, 2, D), 0.5, 3.0),
        "proj_weight": noise(seeds[8], (2, D, D), (max(D // 256, 4)) ** -0.5, 2.5, ((1, 4), (2, 8))),
        "proj_bias": noise(seeds[9], (2, D), 0.5, 3.0),
        "fc1_weight": noise(seeds[10], (2, D, FF), D ** -0.5, 0.15625, ((1, 8), (2, 4))),
        "fc1_bias": noise(seeds[11], (2, FF), 0.5, 3.0),
        "fc2_weight": noise(seeds[12], (2, FF, D), FF ** -0.5, 0.078125, ((1, 4), (2, 8))),
        "fc2_bias": noise(seeds[13], (2, D), 0.5, 3.0),
        "image_cot": noise(seeds[14], (SLOTS, IMG, D), 1.0, 6.0, ((0, 8), (1, 4))),
        "text_cot": noise(seeds[15], (SLOTS, TXT, D), 1.0, 6.0, ((0, 8), (1, 4))),
    }


@jax.custom_vjp
def low(v):
    return lax.optimization_barrier(v.astype(jnp.bfloat16)).astype(jnp.float32)

@jax.custom_vjp
def low_back(v):
    return v

def low_keep(v):
    return (low(v), None)

def low_pass(kept, grad):
    return (grad,)

def back_keep(v):
    return (v, None)

def back_low(kept, grad):
    return (low(grad),)
low.defvjp(low_keep, low_pass)
low_back.defvjp(back_keep, back_low)
epsilon = 1e-06
highest = lax.Precision.HIGHEST

def modulate_norm(values, shift_vec, scale_vec):
    average = lax.optimization_barrier(jnp.mean(values, -1, keepdims=True))
    centred = values - average
    spread = lax.optimization_barrier(jnp.mean(centred * centred, -1, keepdims=True))
    return centred * lax.rsqrt(spread + epsilon) * (1.0 + scale_vec) + shift_vec

def block_seq(params, image_seq, text_seq, cond_seq):
    ada_weight, ada_bias, qkv_weight, qv_bias, proj_weight, proj_bias, fc1_weight, fc1_bias, fc2_weight, fc2_bias = params
    cond_act = low(jax.nn.silu(cond_seq))
    modulation = low_back(jnp.einsum('d,sjdn->sjn', cond_act, ada_weight, precision=highest) + ada_bias)
    streams = (image_seq, text_seq)
    queries, keys_list, values_list = ([], [], [])
    for stream in range(2):
        first_low = low(modulate_norm(streams[stream], modulation[stream, 0], modulation[stream, 1]))
        projected = jnp.einsum('ld,jdn->jln', first_low, qkv_weight[stream], precision=highest)
        queries.append(projected[0] + qv_bias[stream, 0])
        keys_list.append(projected[1])
        values_list.append(projected[2] + qv_bias[stream, 1])
    query_all = low(low_back(jnp.concatenate(queries, 0)))
    key_all = low(low_back(jnp.concatenate(keys_list, 0)))
    value_all = low(low_back(jnp.concatenate(values_list, 0)))
    length = query_all.shape[0]
    query_heads = query_all.reshape(length, HEADS, HEAD_DIM)
    key_heads = key_all.reshape(length, HEADS, HEAD_DIM)
    value_heads = value_all.reshape(length, HEADS, HEAD_DIM)
    scores = low_back(jnp.einsum('qhe,khe->hqk', query_heads, key_heads, precision=highest) * (1.0 / math.sqrt(HEAD_DIM)))
    attn_probs = low(jax.nn.softmax(scores, axis=-1))
    attended = jnp.einsum('hqk,khe->qhe', attn_probs, value_heads, precision=highest).reshape(length, HEADS * HEAD_DIM)
    attended = low(low_back(attended))
    split_at = image_seq.shape[0]
    pieces = (attended[:split_at], attended[split_at:])
    results = []
    for stream in range(2):
        branch = low_back(jnp.dot(pieces[stream], proj_weight[stream], precision=highest) + proj_bias[stream])
        after_attn = streams[stream] + modulation[stream, 2] * branch
        second = low(modulate_norm(after_attn, modulation[stream, 3], modulation[stream, 4]))
        pre_act = low_back(jnp.dot(second, fc1_weight[stream], precision=highest) + fc1_bias[stream])
        activated = low(jax.nn.gelu(pre_act, approximate=True))
        mlp_out = low_back(jnp.dot(activated, fc2_weight[stream], precision=highest) + fc2_bias[stream])
        results.append(after_attn + modulation[stream, 5] * mlp_out)
    return (results[0], results[1])

def reference(image_tokens, text_tokens, conditioning, group_seqs, ada_weight, ada_bias, qkv_weight, qv_bias, proj_weight, proj_bias, fc1_weight, fc1_bias, fc2_weight, fc2_bias, image_cot, text_cot):
    slot_count = image_tokens.shape[0]
    slot_ids = jnp.arange(slot_count, dtype=jnp.int32)
    live_mask = slot_ids % CAP < group_seqs[slot_ids // CAP]
    live_ids = jnp.nonzero(live_mask, size=SEQS)[0].astype(jnp.int32)
    params = tuple((array.astype(jnp.float32) for array in (ada_weight, ada_bias, qkv_weight, qv_bias, proj_weight, proj_bias, fc1_weight, fc1_bias, fc2_weight, fc2_bias)))

    def whole(params, image_all, text_all, cond_all):

        def step(carry, item):
            image_seq, text_seq, cond_seq = item
            return (carry, block_seq(params, image_seq, text_seq, cond_seq))
        _, outputs = lax.scan(jax.checkpoint(step), jnp.zeros((), jnp.float32), (image_all[live_ids], text_all[live_ids], cond_all[live_ids]))
        image_rows, text_rows = outputs
        return (jnp.zeros_like(image_all).at[live_ids].set(image_rows), jnp.zeros_like(text_all).at[live_ids].set(text_rows))
    outputs, backward = jax.vjp(whole, params, image_tokens.astype(jnp.float32), text_tokens.astype(jnp.float32), conditioning.astype(jnp.float32))
    param_grads, image_grad, text_grad, cond_grad = backward((image_cot.astype(jnp.float32), text_cot.astype(jnp.float32)))
    return (outputs[0].astype(jnp.bfloat16), outputs[1].astype(jnp.bfloat16), image_grad, text_grad, cond_grad, param_grads[0], param_grads[1], param_grads[2], param_grads[3], param_grads[4], param_grads[5], param_grads[6], param_grads[7], param_grads[8], param_grads[9])
```

```python
import math

import jax
import jax.numpy as jnp
from jax import lax
from jax.sharding import PartitionSpec as P

HEAD_DIM = 64
EPSILON = 1e-06
F32 = jnp.float32
BF16 = jnp.bfloat16


def hop(value, axis, mask, size):
    return lax.ppermute(value, axis, [(i, i ^ mask) for i in range(size)])


def spread_rows(rows, axis, size):
    mask = 1
    while mask < size:
        rows = jnp.concatenate([rows, hop(rows, axis, mask, size)], 0)
        mask *= 2
    return rows


def collect_rows(parts, axis, size):
    mask = size // 2
    while mask >= 1:
        half = parts.shape[0] // 2
        parts = parts[:half] + hop(parts[half:], axis, mask, size)
        mask //= 2
    return parts


def add_all(value, axis, size):
    mask = 1
    while mask < size:
        value = value + hop(value, axis, mask, size)
        mask *= 2
    return value


class Ring:
    def __init__(self, size):
        self.size = size
        self.order = list(range(0, size, 2)) + list(range(size - 1, 0, -2))
        self.ahead = [(self.order[i], self.order[(i + 1) % size]) for i in range(size)]
        self.back = [(b, a) for a, b in self.ahead]
        place = [0] * size
        for position, device in enumerate(self.order):
            place[device] = position
        self.mine = jnp.asarray(place, jnp.int32)[lax.axis_index("dp")]
        self.table = jnp.asarray(self.order, jnp.int32)

    def device(self, distance):
        return self.table[(self.mine + distance) % self.size]

    def forward(self, value):
        return lax.ppermute(value, "dp", self.ahead)

    def backward(self, value):
        return lax.ppermute(value, "dp", self.back)

    def gather(self, shard):
        half = self.size // 2
        pieces = [(self.device(0), 0, shard)]
        ahead = back = shard
        for step in range(1, half):
            ahead, back = self.forward(ahead), self.backward(back)
            pieces.append((self.device(-step), 0, ahead))
            pieces.append((self.device(step), 0, back))
        pieces.append((self.device(half), 0, self.forward(ahead[:1])))
        pieces.append((self.device(half), 1, self.backward(back[1:])))
        return pieces

    def scatter(self, chunk):
        half = self.size // 2
        far = chunk(self.device(half))
        ahead, back = self.forward(far[:1]), self.backward(far[1:])
        for step in range(half - 1, 0, -1):
            mine_a, mine_b = chunk(self.device(step)), chunk(self.device(-step))
            if step == half - 1:
                sum_a = jnp.concatenate(
                    [mine_a[:1].astype(F32) + ahead.astype(F32), mine_a[1:].astype(F32)], 0
                )
                sum_b = jnp.concatenate(
                    [mine_b[:1].astype(F32), mine_b[1:].astype(F32) + back.astype(F32)], 0
                )
            else:
                sum_a = mine_a.astype(F32) + ahead.astype(F32)
                sum_b = mine_b.astype(F32) + back.astype(F32)
            ahead, back = self.forward(sum_a.astype(BF16)), self.backward(sum_b.astype(BF16))
        return chunk(self.device(0)).astype(F32) + ahead.astype(F32) + back.astype(F32)


def assemble(pieces, axis, size):
    shape = list(pieces[0][2].shape)
    shape.insert(axis, size)
    full = jnp.zeros(shape, pieces[0][2].dtype)
    for device, stream, piece in pieces:
        starts = [jnp.int32(0)] * len(shape)
        starts[0] = jnp.int32(stream)
        starts[axis] = device
        full = lax.dynamic_update_slice(full, jnp.expand_dims(piece, axis), starts)
    return full


def gather_tokens(part):
    across = hop(part, "tensor", 2, 4)
    beside = hop(part, "tensor", 1, 4)
    corner = hop(across, "tensor", 1, 4)
    full = jnp.stack([part, beside, across, corner], 1)
    return full.reshape(part.shape[0], -1, part.shape[2])


def scatter_tokens(partial):
    blocks = partial.reshape(partial.shape[0], 4, -1, partial.shape[2])
    corner = hop(blocks[:, 3], "tensor", 1, 4)
    beside = hop(blocks[:, 1], "tensor", 1, 4)
    send = (blocks[:, 2].astype(F32) + corner.astype(F32)).astype(BF16)
    across = hop(send, "tensor", 2, 4)
    return blocks[:, 0].astype(F32) + beside.astype(F32) + across.astype(F32)


def normalize(values):
    average = jnp.mean(values, -1, keepdims=True)
    centred = values - average
    spread = jnp.mean(centred * centred, -1, keepdims=True)
    inverse = lax.rsqrt(spread + EPSILON)
    return centred * inverse, inverse


def norm_back(grad, normed, inverse, scale_vec):
    scaled = grad * (1.0 + scale_vec[:, None, :])
    input_grad = inverse * (
        scaled
        - jnp.mean(scaled, -1, keepdims=True)
        - normed * jnp.mean(scaled * normed, -1, keepdims=True)
    )
    return input_grad, jnp.sum(grad, 1), jnp.sum(grad * normed, 1)


def gelu_tanh(values):
    return jax.nn.gelu(values, approximate=True)


def split_heads(matrix):
    return matrix.reshape(matrix.shape[0], matrix.shape[1] // HEAD_DIM, HEAD_DIM)


def dot(spec, a, b):
    return jnp.einsum(spec, a, b, preferred_element_type=F32)


def attend(query_block, key_block, value_block):
    factor = 1.0 / math.sqrt(HEAD_DIM)
    query_heads = split_heads(query_block)
    key_heads = split_heads(key_block)
    value_heads = split_heads(value_block)
    scores = dot("qhe,khe->hqk", query_heads, key_heads) * factor
    row_top = jnp.max(scores, -1, keepdims=True)
    total_log = row_top + jnp.log(jnp.sum(jnp.exp(scores - row_top), -1, keepdims=True))
    attn_probs = jnp.exp(scores - total_log).astype(BF16)
    output = dot("hqk,khe->qhe", attn_probs, value_heads)
    return (output.reshape(query_block.shape).astype(BF16), total_log)


def attend_back(query_block, key_block, value_block, total_log, out_grad):
    factor = 1.0 / math.sqrt(HEAD_DIM)
    query_heads = split_heads(query_block)
    key_heads = split_heads(key_block)
    value_heads = split_heads(value_block)
    grad_heads = split_heads(out_grad)
    scores = dot("qhe,khe->hqk", query_heads, key_heads) * factor
    attn_probs = jnp.exp(scores - total_log)
    prob_grad = dot("qhe,khe->hqk", grad_heads, value_heads)
    row_inner = jnp.sum(attn_probs * prob_grad, -1, keepdims=True)
    score_grad = (attn_probs * (prob_grad - row_inner)).astype(BF16)
    query_grad = dot("hqk,khe->qhe", score_grad, key_heads) * factor
    key_grad = dot("hqk,qhe->khe", score_grad, query_heads) * factor
    value_grad = dot("hqk,qhe->khe", attn_probs.astype(BF16), grad_heads)
    flat_shape = query_block.shape
    return jnp.stack(
        [
            query_grad.reshape(flat_shape),
            key_grad.reshape(flat_shape),
            value_grad.reshape(flat_shape),
        ]
    ).astype(BF16)


def on_device(
    groups,
    image_tokens,
    text_tokens,
    conditioning,
    group_seqs,
    ada_weight,
    ada_bias,
    qkv_weight,
    qv_bias,
    proj_weight,
    proj_bias,
    fc1_weight,
    fc1_bias,
    fc2_weight,
    fc2_bias,
    image_cot,
    text_cot,
):
    column = lax.axis_index("tensor")
    group = lax.axis_index("dp")
    ring = Ring(groups)
    slots = image_tokens.shape[0]
    width = image_tokens.shape[2]
    rows = qkv_weight.shape[2]
    col_width = qkv_weight.shape[-1]
    hidden = fc1_weight.shape[-1]

    qkv_pieces = ring.gather(qkv_weight)
    proj_turned = jnp.swapaxes(proj_weight, 1, 2)
    fc2_turned = jnp.swapaxes(fc2_weight, 1, 2)
    _, _, proj_turned, fc1_shard = lax.optimization_barrier(
        (qkv_pieces[-1][2], qkv_pieces[-2][2], proj_turned, fc1_weight)
    )
    proj_pieces = ring.gather(proj_turned)
    fc1_pieces = ring.gather(fc1_shard)
    _, _, fc2_turned = lax.optimization_barrier(
        (fc1_pieces[-4][2], fc1_pieces[-3][2], fc2_turned)
    )
    fc2_pieces = ring.gather(fc2_turned)
    qkv_full = assemble(qkv_pieces, 2, groups).reshape(2, 3, width, col_width)
    proj_full = assemble(proj_pieces, 1, groups).reshape(2, width, col_width)
    fc1_full = assemble(fc1_pieces, 1, groups).reshape(2, width, hidden)
    fc2_full = assemble(fc2_pieces, 1, groups).reshape(2, width, hidden)

    ada_part = lax.dynamic_slice_in_dim(ada_bias.astype(F32), column * col_width, col_width, 2)
    qv_part = lax.dynamic_slice_in_dim(qv_bias.astype(F32), column * col_width, col_width, 2)
    fc1_part = lax.dynamic_slice_in_dim(fc1_bias.astype(F32), column * hidden, hidden, 1)
    proj_add = proj_bias.astype(F32)
    fc2_add = fc2_bias.astype(F32)
    live_mask = (jnp.arange(slots, dtype=jnp.int32) < group_seqs[0]).astype(F32)[:, None, None]

    cond_act, silu_back = jax.vjp(jax.nn.silu, conditioning.astype(F32))
    cond_all = spread_rows(cond_act.astype(BF16), "dp", groups)
    cond_rows = lax.dynamic_index_in_dim(
        cond_all.reshape(-1, groups, rows), group, 1, keepdims=False
    )
    modul_parts = dot("cd,sjdn->csjn", cond_rows, ada_weight)
    modul_local = collect_rows(modul_parts, "dp", groups) + ada_part[None]
    modulation = lax.all_gather(modul_local, "tensor", axis=3, tiled=True)

    streams = (image_tokens.astype(F32), text_tokens.astype(F32))
    out_grad = [image_cot.astype(F32) * live_mask, text_cot.astype(F32) * live_mask]
    first_normed = [normalize(streams[s]) for s in range(2)]
    first_full = [
        gather_tokens(
            (
                first_normed[s][0] * (1.0 + modulation[:, s, 1][:, None, :])
                + modulation[:, s, 0][:, None, :]
            ).astype(BF16)
        )
        for s in range(2)
    ]
    mlp_round = [
        (out_grad[s] * modulation[:, s, 5][:, None, :]).astype(BF16) for s in range(2)
    ]
    mlp_full = [gather_tokens(mlp_round[s]) for s in range(2)]
    joined_list = []
    for s in range(2):
        projected = dot("cld,jdn->jcln", first_full[s], qkv_full[s])
        offsets = jnp.stack([qv_part[s, 0], jnp.zeros_like(qv_part[s, 0]), qv_part[s, 1]])
        joined_list.append((projected + offsets[:, None, None, :]).astype(BF16))
    joined = jnp.concatenate(joined_list, 2)
    attended_rows, totals = [], []
    for slot in range(slots):
        attended_slot, total_log = attend(joined[0, slot], joined[1, slot], joined[2, slot])
        attended_rows.append(attended_slot)
        totals.append(total_log)
    attended = jnp.stack(attended_rows)
    split_at = first_full[0].shape[1]
    pieces = (attended[:, :split_at], attended[:, split_at:])
    branches = [
        scatter_tokens(dot("cln,dn->cld", pieces[s], proj_full[s]).astype(BF16)) + proj_add[s]
        for s in range(2)
    ]
    after_attn = [
        streams[s] + modulation[:, s, 2][:, None, :] * branches[s] for s in range(2)
    ]
    second_normed = [normalize(after_attn[s]) for s in range(2)]
    second_full = [
        gather_tokens(
            (
                second_normed[s][0] * (1.0 + modulation[:, s, 4][:, None, :])
                + modulation[:, s, 3][:, None, :]
            ).astype(BF16)
        )
        for s in range(2)
    ]
    activated, pre_round, fc1_grad, fc2_grad = [], [], [], []
    for s in range(2):
        pre_act = dot("cld,df->clf", second_full[s], fc1_full[s]) + fc1_part[s]
        act, gelu_back = jax.vjp(gelu_tanh, pre_act)
        activated.append(act.astype(BF16))
        act_grad = dot("cld,df->clf", mlp_full[s], fc2_full[s])
        pre_round.append(gelu_back(act_grad)[0].astype(BF16))
    fc2_grad = jnp.stack(
        [dot("cld,clf->df", mlp_full[s], activated[s]).astype(BF16) for s in range(2)]
    ).reshape(2, groups, rows, hidden)
    fc2_sum = ring.scatter(lambda d: lax.dynamic_index_in_dim(fc2_grad, d, 1, keepdims=False))
    fc1_grad = jnp.stack(
        [dot("cld,clf->df", second_full[s], pre_round[s]).astype(BF16) for s in range(2)]
    ).reshape(2, groups, rows, hidden)
    fc1_sum = ring.scatter(lambda d: lax.dynamic_index_in_dim(fc1_grad, d, 1, keepdims=False))
    second_grad = [
        scatter_tokens(dot("clf,df->cld", pre_round[s], fc1_full[s]).astype(BF16))
        for s in range(2)
    ]
    mlp_out = [
        scatter_tokens(dot("clf,df->cld", activated[s], fc2_full[s]).astype(BF16)) + fc2_add[s]
        for s in range(2)
    ]
    outs = [
        (
            (after_attn[s] + modulation[:, s, 5][:, None, :] * mlp_out[s]) * live_mask
        ).astype(BF16)
        for s in range(2)
    ]
    gate_two = [jnp.sum(out_grad[s] * mlp_out[s], 1) for s in range(2)]
    fc2_bias_local = jnp.stack([jnp.sum(mlp_round[s].astype(F32), (0, 1)) for s in range(2)])
    fc1_bias_local = jnp.stack([jnp.sum(pre_round[s].astype(F32), (0, 1)) for s in range(2)])

    residual_grads, shift_two, scale_two, gate_one, branch_round = [], [], [], [], []
    for s in range(2):
        input_part, shift_part, scale_part = norm_back(
            second_grad[s], second_normed[s][0], second_normed[s][1], modulation[:, s, 4]
        )
        residual = out_grad[s] + input_part
        residual_grads.append(residual)
        shift_two.append(shift_part)
        scale_two.append(scale_part)
        gate_one.append(jnp.sum(residual * branches[s], 1))
        branch_round.append((residual * modulation[:, s, 2][:, None, :]).astype(BF16))
    branch_full = [gather_tokens(branch_round[s]) for s in range(2)]
    proj_bias_local = jnp.stack([jnp.sum(branch_round[s].astype(F32), (0, 1)) for s in range(2)])
    attended_grad = jnp.concatenate(
        [dot("cld,dn->cln", branch_full[s], proj_full[s]) for s in range(2)], 1
    ).astype(BF16)
    proj_grad = jnp.stack(
        [dot("cld,cln->dn", branch_full[s], pieces[s]).astype(BF16) for s in range(2)]
    ).reshape(2, groups, rows, col_width)
    proj_sum = ring.scatter(lambda d: lax.dynamic_index_in_dim(proj_grad, d, 1, keepdims=False))
    qkv_rows = [
        attend_back(
            joined[0, slot], joined[1, slot], joined[2, slot], totals[slot], attended_grad[slot]
        )
        for slot in range(slots)
    ]
    qkv_round = jnp.stack(qkv_rows, 1)
    qkv_parts = (qkv_round[:, :, :split_at], qkv_round[:, :, split_at:])
    first_grad = [
        scatter_tokens(dot("jcln,jdn->cld", qkv_parts[s], qkv_full[s]).astype(BF16))
        for s in range(2)
    ]
    qkv_grad = jnp.stack(
        [dot("cld,jcln->jdn", first_full[s], qkv_parts[s]).astype(BF16) for s in range(2)]
    ).reshape(2, 3, groups, rows, col_width)
    qkv_sum = ring.scatter(lambda d: lax.dynamic_index_in_dim(qkv_grad, d, 2, keepdims=False))
    qv_bias_local = jnp.stack(
        [jnp.sum(qkv_parts[s][0::2].astype(F32), (1, 2)) for s in range(2)]
    )
    input_grads, modul_grads = [], []
    for s in range(2):
        input_part, shift_part, scale_part = norm_back(
            first_grad[s], first_normed[s][0], first_normed[s][1], modulation[:, s, 1]
        )
        input_grads.append(residual_grads[s] + input_part)
        modul_grads.append(
            jnp.stack(
                [
                    shift_part,
                    scale_part,
                    gate_one[s],
                    shift_two[s],
                    scale_two[s],
                    gate_two[s],
                ],
                1,
            )
        )
    modul_grad = jnp.stack(modul_grads, 1).reshape(slots, 2, 6, 4, col_width)
    modul_blocks = jnp.stack(
        [
            lax.dynamic_index_in_dim(modul_grad, column ^ mask, 3, keepdims=False)
            for mask in range(4)
        ]
    )
    modul_round = collect_rows(modul_blocks, "tensor", 4)[0].astype(BF16)
    modul_all = spread_rows(modul_round, "dp", groups)
    ada_grad = dot("cd,csjn->sjdn", cond_rows, modul_all)
    ada_bias_part = jnp.sum(modul_all.astype(F32), 0)
    cond_part = add_all(dot("csjn,sjdn->cd", modul_all, ada_weight), "tensor", 4)
    cond_blocks = cond_part.reshape(groups, slots, rows)
    cond_terms = spread_rows(cond_blocks[None], "dp", groups)
    masks = jnp.arange(groups, dtype=jnp.int32)
    cond_term = jnp.stack(
        [
            lax.dynamic_index_in_dim(
                lax.dynamic_index_in_dim(cond_terms, group ^ d, 0, keepdims=False),
                group ^ d,
                0,
                keepdims=False,
            )
            for d in range(groups)
        ],
        1,
    ).reshape(slots, width)
    del masks
    cond_grad = lax.dynamic_slice_in_dim(
        silu_back(cond_term)[0], column * col_width, col_width, 1
    )

    split_sums = jnp.concatenate([qv_bias_local.reshape(-1), fc1_bias_local.reshape(-1)])
    token_sums = jnp.concatenate([proj_bias_local.reshape(-1), fc2_bias_local.reshape(-1)])
    bias_local = add_all(jnp.concatenate([split_sums, token_sums]), "dp", groups)
    bias_local = jnp.concatenate([bias_local, ada_bias_part.reshape(-1)])
    bias_all = lax.all_gather(bias_local, "tensor")
    cut_a = qv_bias_local.size
    cut_b = cut_a + fc1_bias_local.size
    cut_c = cut_b + proj_bias_local.size
    cut_d = cut_c + fc2_bias_local.size

    def by_column(block, shape):
        return jnp.moveaxis(block.reshape((4,) + shape), 0, -2).reshape(
            shape[:-1] + (4 * shape[-1],)
        )

    qv_bias_grad = by_column(bias_all[:, :cut_a], qv_bias_local.shape)
    fc1_bias_grad = by_column(bias_all[:, cut_a:cut_b], fc1_bias_local.shape)
    proj_bias_grad = jnp.sum(bias_all[:, cut_b:cut_c], 0).reshape(proj_bias_local.shape)
    fc2_bias_grad = jnp.sum(bias_all[:, cut_c:cut_d], 0).reshape(fc2_bias_local.shape)
    ada_bias_grad = by_column(bias_all[:, cut_d:], ada_bias_part.shape)
    return (
        outs[0],
        outs[1],
        input_grads[0],
        input_grads[1],
        cond_grad,
        ada_grad,
        ada_bias_grad,
        qkv_sum,
        qv_bias_grad,
        jnp.swapaxes(proj_sum, 1, 2),
        proj_bias_grad,
        fc1_sum,
        fc1_bias_grad,
        jnp.swapaxes(fc2_sum, 1, 2),
        fc2_bias_grad,
    )


def solution(mesh):
    groups = mesh.shape["dp"]
    in_specs = (
        P("dp", "tensor", None),
        P("dp", "tensor", None),
        P("dp", None),
        P("dp"),
        P(None, None, "dp", "tensor"),
        P(),
        P(None, None, "dp", "tensor"),
        P(),
        P(None, "tensor", "dp"),
        P(),
        P(None, "dp", "tensor"),
        P(),
        P(None, "tensor", "dp"),
        P(),
        P("dp", "tensor", None),
        P("dp", "tensor", None),
    )
    out_specs = (
        P("dp", "tensor", None),
        P("dp", "tensor", None),
        P("dp", "tensor", None),
        P("dp", "tensor", None),
        P("dp", "tensor"),
        P(None, None, "dp", "tensor"),
        P(),
        P(None, None, "dp", "tensor"),
        P(),
        P(None, "tensor", "dp"),
        P(),
        P(None, "dp", "tensor"),
        P(),
        P(None, "tensor", "dp"),
        P(),
    )

    def step(*args):
        return on_device(groups, *args)

    return jax.shard_map(
        step, mesh=mesh, in_specs=in_specs, out_specs=out_specs, check_vma=False
    )
```

```python
import math

import jax
import jax.numpy as jnp
from jax import lax
from jax.experimental import pallas as pl
from jax.experimental.pallas import tpu as pltpu
from jax.sharding import PartitionSpec as P

HEAD_DIM = 64
PAIR = 2 * HEAD_DIM
FACTOR = 1.0 / math.sqrt(HEAD_DIM)
BLOCK = 512
EPSILON = 1e-06
F32 = jnp.float32
BF16 = jnp.bfloat16


def hop(value, axis, mask, size):
    return lax.ppermute(value, axis, [(i, i ^ mask) for i in range(size)])


def spread_rows(rows, axis, size):
    mask = 1
    while mask < size:
        rows = jnp.concatenate([rows, hop(rows, axis, mask, size)], 0)
        mask *= 2
    return rows


def collect_rows(parts, axis, size):
    mask = size // 2
    while mask >= 1:
        half = parts.shape[0] // 2
        parts = parts[:half] + hop(parts[half:], axis, mask, size)
        mask //= 2
    return parts


def add_all(value, axis, size):
    mask = 1
    while mask < size:
        value = value + hop(value, axis, mask, size)
        mask *= 2
    return value


class Ring:
    def __init__(self, size):
        self.size = size
        self.order = list(range(0, size, 2)) + list(range(size - 1, 0, -2))
        self.ahead = [(self.order[i], self.order[(i + 1) % size]) for i in range(size)]
        self.back = [(b, a) for a, b in self.ahead]
        place = [0] * size
        for position, device in enumerate(self.order):
            place[device] = position
        self.mine = jnp.asarray(place, jnp.int32)[lax.axis_index("dp")]
        self.table = jnp.asarray(self.order, jnp.int32)

    def device(self, distance):
        return self.table[(self.mine + distance) % self.size]

    def forward(self, value):
        return lax.ppermute(value, "dp", self.ahead)

    def backward(self, value):
        return lax.ppermute(value, "dp", self.back)

    def gather(self, shard):
        half = self.size // 2
        pieces = [(self.device(0), 0, shard)]
        ahead = back = shard
        for step in range(1, half):
            ahead, back = self.forward(ahead), self.backward(back)
            pieces.append((self.device(-step), 0, ahead))
            pieces.append((self.device(step), 0, back))
        pieces.append((self.device(half), 0, self.forward(ahead[:1])))
        pieces.append((self.device(half), 1, self.backward(back[1:])))
        return pieces

    def scatter(self, chunk):
        half = self.size // 2
        far = chunk(self.device(half))
        ahead, back = self.forward(far[:1]), self.backward(far[1:])
        for step in range(half - 1, 0, -1):
            mine_a, mine_b = chunk(self.device(step)), chunk(self.device(-step))
            if step == half - 1:
                sum_a = jnp.concatenate(
                    [mine_a[:1].astype(F32) + ahead.astype(F32), mine_a[1:].astype(F32)], 0
                )
                sum_b = jnp.concatenate(
                    [mine_b[:1].astype(F32), mine_b[1:].astype(F32) + back.astype(F32)], 0
                )
            else:
                sum_a = mine_a.astype(F32) + ahead.astype(F32)
                sum_b = mine_b.astype(F32) + back.astype(F32)
            ahead, back = self.forward(sum_a.astype(BF16)), self.backward(sum_b.astype(BF16))
        return chunk(self.device(0)).astype(F32) + ahead.astype(F32) + back.astype(F32)


def assemble(pieces, axis, size):
    shape = list(pieces[0][2].shape)
    shape.insert(axis, size)
    full = jnp.zeros(shape, pieces[0][2].dtype)
    for device, stream, piece in pieces:
        starts = [jnp.int32(0)] * len(shape)
        starts[0] = jnp.int32(stream)
        starts[axis] = device
        full = lax.dynamic_update_slice(full, jnp.expand_dims(piece, axis), starts)
    return full


def gather_tokens(part):
    across = hop(part, "tensor", 2, 4)
    beside = hop(part, "tensor", 1, 4)
    corner = hop(across, "tensor", 1, 4)
    full = jnp.stack([part, beside, across, corner], 1)
    return full.reshape(part.shape[0], -1, part.shape[2])


def scatter_tokens(partial):
    blocks = partial.reshape(partial.shape[0], 4, -1, partial.shape[2])
    corner = hop(blocks[:, 3], "tensor", 1, 4)
    beside = hop(blocks[:, 1], "tensor", 1, 4)
    send = (blocks[:, 2].astype(F32) + corner.astype(F32)).astype(BF16)
    across = hop(send, "tensor", 2, 4)
    return blocks[:, 0].astype(F32) + beside.astype(F32) + across.astype(F32)


def normalize(values):
    average = jnp.mean(values, -1, keepdims=True)
    centred = values - average
    spread = jnp.mean(centred * centred, -1, keepdims=True)
    inverse = lax.rsqrt(spread + EPSILON)
    return centred * inverse, inverse


def norm_back(grad, normed, inverse, scale_vec):
    scaled = grad * (1.0 + scale_vec[:, None, :])
    input_grad = inverse * (
        scaled
        - jnp.mean(scaled, -1, keepdims=True)
        - normed * jnp.mean(scaled * normed, -1, keepdims=True)
    )
    return input_grad, jnp.sum(grad, 1), jnp.sum(grad * normed, 1)


def gelu_tanh(values):
    return jax.nn.gelu(values, approximate=True)


def dot(spec, a, b):
    return jnp.einsum(spec, a, b, preferred_element_type=F32)


def lane_masks(dtype):
    lane = lax.broadcasted_iota(jnp.int32, (1, PAIR), 1)
    low = (lane < HEAD_DIM).astype(F32)
    return [low.astype(dtype), (1.0 - low).astype(dtype)]

def dot_nt(a,b): return lax.dot_general(a,b,(((1,),(1,)),((),())),preferred_element_type=F32)
def dot_nn(a,b): return lax.dot_general(a,b,(((1,),(0,)),((),())),preferred_element_type=F32)
def dot_tn(a,b): return lax.dot_general(a,b,(((0,),(0,)),((),())),preferred_element_type=F32)

def row_blocks(image_rows, text_rows, block):
    blocks=[(0,i,min(block,image_rows-i),i) for i in range(0,image_rows,block)]
    blocks.append((1,0,text_rows,image_rows))
    return blocks

def attend_kernel(img, txt, out_img, out_txt, lse):
    refs, outs = (img, txt), (out_img, out_txt)
    keys=[r[0,:,PAIR:2*PAIR] for r in refs]
    values=[r[0,:,2*PAIR:3*PAIR] for r in refs]
    masks=lane_masks(F32)
    low=[m.astype(BF16) for m in masks]
    for part,start,size,place in row_blocks(img.shape[1],txt.shape[1],BLOCK):
        query=refs[part][0,pl.ds(start,size),0:PAIR]*jnp.asarray(FACTOR,BF16)
        total=None; logs=None
        for head in range(2):
            masked=query*low[head]
            scores=[dot_nt(masked,k) for k in keys]
            top=jnp.maximum(jnp.max(scores[0],-1,keepdims=True),jnp.max(scores[1],-1,keepdims=True))
            probs=[jnp.exp(s-top) for s in scores]
            denom=jnp.sum(probs[0],-1,keepdims=True)+jnp.sum(probs[1],-1,keepdims=True)
            mixed=dot_nn(probs[0].astype(BF16),values[0])+dot_nn(probs[1].astype(BF16),values[1])
            mixed=mixed*(masks[head]/denom)
            log=(top+jnp.log(denom))*masks[head]
            total=mixed if total is None else total+mixed
            logs=log if logs is None else logs+log
        outs[part][0,pl.ds(start,size),:]=total.astype(BF16)
        turned=jnp.transpose(logs)
        lse[0,0,0:1,pl.ds(place,size)]=turned[0:1]
        lse[0,0,1:2,pl.ds(place,size)]=turned[HEAD_DIM:HEAD_DIM+1]

def attend(img, txt, slots, pairs):
    ni,nt=img.shape[1],txt.shape[1]
    spec=lambda n,w: pl.BlockSpec((1,n,w),lambda c,p:(c,0,p))
    flops=slots*pairs*2*2*2*(ni+nt)**2*PAIR
    return pl.pallas_call(
        attend_kernel, grid=(slots,pairs),
        in_specs=[spec(ni,3*PAIR),spec(nt,3*PAIR)],
        out_specs=[spec(ni,PAIR),spec(nt,PAIR),pl.BlockSpec((1,1,2,ni+nt),lambda c,p:(c,p,0,0))],
        out_shape=[jax.ShapeDtypeStruct((slots,ni,pairs*PAIR),BF16),jax.ShapeDtypeStruct((slots,nt,pairs*PAIR),BF16),
                   jax.ShapeDtypeStruct((slots,pairs,2,ni+nt),F32)],
        compiler_params=pltpu.CompilerParams(vmem_limit_bytes=48<<20),
        cost_estimate=pl.CostEstimate(flops=flops,bytes_accessed=slots*pairs*(ni+nt)*PAIR*8,transcendentals=slots*pairs*2*(ni+nt)**2),
        name="attend")(img,txt)

def attend_back_kernel(img, txt, o_img, o_txt, g_img, g_txt, lse, d_img, d_txt, dk_img, dk_txt, dv_img, dv_txt):
    refs,o_refs,g_refs,d_refs=(img,txt),(o_img,o_txt),(g_img,g_txt),(d_img,d_txt)
    dk,dv=(dk_img,dk_txt),(dv_img,dv_txt)
    keys=[r[0,:,PAIR:2*PAIR] for r in refs]
    values=[r[0,:,2*PAIR:3*PAIR] for r in refs]
    low=lane_masks(BF16)
    first=True
    for part,start,size,place in row_blocks(img.shape[1],txt.shape[1],BLOCK):
        rows=pl.ds(start,size)
        query=refs[part][0,rows,0:PAIR]*jnp.asarray(FACTOR,BF16)
        grad=g_refs[part][0,rows,:]
        inner=jnp.transpose(grad.astype(F32)*o_refs[part][0,rows,:].astype(F32))
        query_grad=None
        for head in range(2):
            q=query*low[head]; g=grad*low[head]
            delta=jnp.sum(inner[head*HEAD_DIM:(head+1)*HEAD_DIM],0,keepdims=True)
            log=lse[0,0,head:head+1,pl.ds(place,size)]
            for kp in range(2):
                probs=jnp.exp(dot_nt(keys[kp],q)-log)
                prob_grad=dot_nt(values[kp],g)
                score_grad=(probs*(prob_grad-delta)).astype(BF16)
                v_part=dot_nn(probs.astype(BF16),g)
                k_part=dot_nn(score_grad,q)
                q_part=dot_tn(score_grad,keys[kp]*low[head])
                query_grad=q_part if query_grad is None else query_grad+q_part
                if first:
                    dv[kp][...]=v_part; dk[kp][...]=k_part
                else:
                    dv[kp][...]+=v_part; dk[kp][...]+=k_part
            first=False
        d_refs[part][0,rows,0:PAIR]=(query_grad*FACTOR).astype(BF16)
    for kp in range(2):
        d_refs[kp][0,:,PAIR:2*PAIR]=dk[kp][...].astype(BF16)
        d_refs[kp][0,:,2*PAIR:3*PAIR]=dv[kp][...].astype(BF16)

def attend_back(img, txt, o_img, o_txt, g_img, g_txt, lse):
    slots,ni=img.shape[:2]; nt=txt.shape[1]; pairs=lse.shape[1]
    spec=lambda n,w: pl.BlockSpec((1,n,w),lambda c,p:(c,0,p))
    flops=slots*pairs*2*5*2*(ni+nt)**2*PAIR
    return pl.pallas_call(
        attend_back_kernel, grid=(slots,pairs),
        in_specs=[spec(ni,3*PAIR),spec(nt,3*PAIR),spec(ni,PAIR),spec(nt,PAIR),spec(ni,PAIR),spec(nt,PAIR),
                  pl.BlockSpec((1,1,2,ni+nt),lambda c,p:(c,p,0,0))],
        out_specs=[spec(ni,3*PAIR),spec(nt,3*PAIR)],
        out_shape=[jax.ShapeDtypeStruct(img.shape,BF16),jax.ShapeDtypeStruct(txt.shape,BF16)],
        scratch_shapes=[pltpu.VMEM((ni,PAIR),F32),pltpu.VMEM((nt,PAIR),F32)]*2,
        compiler_params=pltpu.CompilerParams(vmem_limit_bytes=48<<20),
        cost_estimate=pl.CostEstimate(flops=flops,bytes_accessed=slots*pairs*(ni+nt)*PAIR*16,transcendentals=slots*pairs*2*(ni+nt)**2),
        name="attend_back")(img,txt,o_img,o_txt,g_img,g_txt,lse)


def on_device(
    groups,
    image_tokens,
    text_tokens,
    conditioning,
    group_seqs,
    ada_weight,
    ada_bias,
    qkv_weight,
    qv_bias,
    proj_weight,
    proj_bias,
    fc1_weight,
    fc1_bias,
    fc2_weight,
    fc2_bias,
    image_cot,
    text_cot,
):
    column = lax.axis_index("tensor")
    group = lax.axis_index("dp")
    ring = Ring(groups)
    slots = image_tokens.shape[0]
    width = image_tokens.shape[2]
    rows = qkv_weight.shape[2]
    col_width = qkv_weight.shape[-1]
    hidden = fc1_weight.shape[-1]

    pairs = col_width // PAIR
    qkv_turned = jnp.transpose(
        qkv_weight.reshape(2, 3, rows, pairs, PAIR), (0, 2, 3, 1, 4)
    ).reshape(2, rows, 3 * col_width)
    qkv_pieces = ring.gather(qkv_turned)
    proj_turned = jnp.swapaxes(proj_weight, 1, 2)
    fc2_turned = jnp.swapaxes(fc2_weight, 1, 2)
    _, _, proj_turned, fc1_shard = lax.optimization_barrier(
        (qkv_pieces[-1][2], qkv_pieces[-2][2], proj_turned, fc1_weight)
    )
    proj_pieces = ring.gather(proj_turned)
    fc1_pieces = ring.gather(fc1_shard)
    _, _, fc2_turned = lax.optimization_barrier(
        (fc1_pieces[-4][2], fc1_pieces[-3][2], fc2_turned)
    )
    fc2_pieces = ring.gather(fc2_turned)
    qkv_full = assemble(qkv_pieces, 1, groups).reshape(2, width, 3 * col_width)
    proj_full = assemble(proj_pieces, 1, groups).reshape(2, width, col_width)
    fc1_full = assemble(fc1_pieces, 1, groups).reshape(2, width, hidden)
    fc2_full = assemble(fc2_pieces, 1, groups).reshape(2, width, hidden)

    ada_part = lax.dynamic_slice_in_dim(ada_bias.astype(F32), column * col_width, col_width, 2)
    qv_part = lax.dynamic_slice_in_dim(qv_bias.astype(F32), column * col_width, col_width, 2)
    fc1_part = lax.dynamic_slice_in_dim(fc1_bias.astype(F32), column * hidden, hidden, 1)
    proj_add = proj_bias.astype(F32)
    fc2_add = fc2_bias.astype(F32)
    live_mask = (jnp.arange(slots, dtype=jnp.int32) < group_seqs[0]).astype(F32)[:, None, None]

    cond_act, silu_back = jax.vjp(jax.nn.silu, conditioning.astype(F32))
    cond_all = spread_rows(cond_act.astype(BF16), "dp", groups)
    cond_rows = lax.dynamic_index_in_dim(
        cond_all.reshape(-1, groups, rows), group, 1, keepdims=False
    )
    modul_parts = dot("cd,sjdn->csjn", cond_rows, ada_weight)
    modul_local = collect_rows(modul_parts, "dp", groups) + ada_part[None]
    modulation = lax.all_gather(modul_local, "tensor", axis=3, tiled=True)

    streams = (image_tokens.astype(F32), text_tokens.astype(F32))
    out_grad = [image_cot.astype(F32) * live_mask, text_cot.astype(F32) * live_mask]
    first_normed = [normalize(streams[s]) for s in range(2)]
    first_full = [
        gather_tokens(
            (
                first_normed[s][0] * (1.0 + modulation[:, s, 1][:, None, :])
                + modulation[:, s, 0][:, None, :]
            ).astype(BF16)
        )
        for s in range(2)
    ]
    mlp_round = [
        (out_grad[s] * modulation[:, s, 5][:, None, :]).astype(BF16) for s in range(2)
    ]
    mlp_full = [gather_tokens(mlp_round[s]) for s in range(2)]
    offsets = jnp.stack([qv_part[:, 0], jnp.zeros_like(qv_part[:, 0]), qv_part[:, 1]], 1)
    offsets = jnp.swapaxes(offsets.reshape(2, 3, pairs, PAIR), 1, 2).reshape(2, 3 * col_width)
    qkv = [
        (dot("cld,dn->cln", first_full[s], qkv_full[s]) + offsets[s]).astype(BF16)
        for s in range(2)
    ]
    *pieces, total_log = attend(qkv[0], qkv[1], slots, pairs)
    branches = [
        scatter_tokens(dot("cln,dn->cld", pieces[s], proj_full[s]).astype(BF16)) + proj_add[s]
        for s in range(2)
    ]
    after_attn = [
        streams[s] + modulation[:, s, 2][:, None, :] * branches[s] for s in range(2)
    ]
    second_normed = [normalize(after_attn[s]) for s in range(2)]
    second_full = [
        gather_tokens(
            (
                second_normed[s][0] * (1.0 + modulation[:, s, 4][:, None, :])
                + modulation[:, s, 3][:, None, :]
            ).astype(BF16)
        )
        for s in range(2)
    ]
    activated, pre_round, fc1_grad, fc2_grad = [], [], [], []
    for s in range(2):
        pre_act = dot("cld,df->clf", second_full[s], fc1_full[s]) + fc1_part[s]
        act, gelu_back = jax.vjp(gelu_tanh, pre_act)
        activated.append(act.astype(BF16))
        act_grad = dot("cld,df->clf", mlp_full[s], fc2_full[s])
        pre_round.append(gelu_back(act_grad)[0].astype(BF16))
    fc2_grad = jnp.stack(
        [dot("cld,clf->df", mlp_full[s], activated[s]).astype(BF16) for s in range(2)]
    ).reshape(2, groups, rows, hidden)
    fc2_sum = ring.scatter(lambda d: lax.dynamic_index_in_dim(fc2_grad, d, 1, keepdims=False))
    fc1_grad = jnp.stack(
        [dot("cld,clf->df", second_full[s], pre_round[s]).astype(BF16) for s in range(2)]
    ).reshape(2, groups, rows, hidden)
    fc1_sum = ring.scatter(lambda d: lax.dynamic_index_in_dim(fc1_grad, d, 1, keepdims=False))
    second_grad = [
        scatter_tokens(dot("clf,df->cld", pre_round[s], fc1_full[s]).astype(BF16))
        for s in range(2)
    ]
    mlp_out = [
        scatter_tokens(dot("clf,df->cld", activated[s], fc2_full[s]).astype(BF16)) + fc2_add[s]
        for s in range(2)
    ]
    outs = [
        (
            (after_attn[s] + modulation[:, s, 5][:, None, :] * mlp_out[s]) * live_mask
        ).astype(BF16)
        for s in range(2)
    ]
    gate_two = [jnp.sum(out_grad[s] * mlp_out[s], 1) for s in range(2)]
    fc2_bias_local = jnp.stack([jnp.sum(mlp_round[s].astype(F32), (0, 1)) for s in range(2)])
    fc1_bias_local = jnp.stack([jnp.sum(pre_round[s].astype(F32), (0, 1)) for s in range(2)])

    residual_grads, shift_two, scale_two, gate_one, branch_round = [], [], [], [], []
    for s in range(2):
        input_part, shift_part, scale_part = norm_back(
            second_grad[s], second_normed[s][0], second_normed[s][1], modulation[:, s, 4]
        )
        residual = out_grad[s] + input_part
        residual_grads.append(residual)
        shift_two.append(shift_part)
        scale_two.append(scale_part)
        gate_one.append(jnp.sum(residual * branches[s], 1))
        branch_round.append((residual * modulation[:, s, 2][:, None, :]).astype(BF16))
    branch_full = [gather_tokens(branch_round[s]) for s in range(2)]
    proj_bias_local = jnp.stack([jnp.sum(branch_round[s].astype(F32), (0, 1)) for s in range(2)])
    attended_grad = [
        dot("cld,dn->cln", branch_full[s], proj_full[s]).astype(BF16) for s in range(2)
    ]
    proj_grad = jnp.stack(
        [dot("cld,cln->dn", branch_full[s], pieces[s]).astype(BF16) for s in range(2)]
    ).reshape(2, groups, rows, col_width)
    proj_sum = ring.scatter(lambda d: lax.dynamic_index_in_dim(proj_grad, d, 1, keepdims=False))
    qkv_parts = attend_back(qkv[0], qkv[1], *pieces, *attended_grad, total_log)
    first_grad = [
        scatter_tokens(dot("cln,dn->cld", qkv_parts[s], qkv_full[s]).astype(BF16))
        for s in range(2)
    ]
    qkv_grad = jnp.stack(
        [dot("cld,cln->dn", first_full[s], qkv_parts[s]).astype(BF16) for s in range(2)]
    ).reshape(2, groups, rows, 3 * col_width)
    qkv_sum = ring.scatter(lambda d: lax.dynamic_index_in_dim(qkv_grad, d, 1, keepdims=False))
    qkv_sum = jnp.transpose(
        qkv_sum.reshape(2, rows, pairs, 3, PAIR), (0, 3, 1, 2, 4)
    ).reshape(qkv_weight.shape)
    qv_bias_local = jnp.stack([jnp.sum(qkv_parts[s].astype(F32), (0, 1)) for s in range(2)])
    qv_bias_local = jnp.swapaxes(
        qv_bias_local.reshape(2, pairs, 3, PAIR)[:, :, 0::2], 1, 2
    ).reshape(2, 2, col_width)
    input_grads, modul_grads = [], []
    for s in range(2):
        input_part, shift_part, scale_part = norm_back(
            first_grad[s], first_normed[s][0], first_normed[s][1], modulation[:, s, 1]
        )
        input_grads.append(residual_grads[s] + input_part)
        modul_grads.append(
            jnp.stack(
                [
                    shift_part,
                    scale_part,
                    gate_one[s],
                    shift_two[s],
                    scale_two[s],
                    gate_two[s],
                ],
                1,
            )
        )
    modul_grad = jnp.stack(modul_grads, 1).reshape(slots, 2, 6, 4, col_width)
    modul_blocks = jnp.stack(
        [
            lax.dynamic_index_in_dim(modul_grad, column ^ mask, 3, keepdims=False)
            for mask in range(4)
        ]
    )
    modul_round = collect_rows(modul_blocks, "tensor", 4)[0].astype(BF16)
    modul_all = spread_rows(modul_round, "dp", groups)
    ada_grad = dot("cd,csjn->sjdn", cond_rows, modul_all)
    ada_bias_part = jnp.sum(modul_all.astype(F32), 0)
    cond_part = add_all(dot("csjn,sjdn->cd", modul_all, ada_weight), "tensor", 4)
    cond_blocks = cond_part.reshape(groups, slots, rows)
    cond_terms = spread_rows(cond_blocks[None], "dp", groups)
    masks = jnp.arange(groups, dtype=jnp.int32)
    cond_term = jnp.stack(
        [
            lax.dynamic_index_in_dim(
                lax.dynamic_index_in_dim(cond_terms, group ^ d, 0, keepdims=False),
                group ^ d,
                0,
                keepdims=False,
            )
            for d in range(groups)
        ],
        1,
    ).reshape(slots, width)
    del masks
    cond_grad = lax.dynamic_slice_in_dim(
        silu_back(cond_term)[0], column * col_width, col_width, 1
    )

    split_sums = jnp.concatenate([qv_bias_local.reshape(-1), fc1_bias_local.reshape(-1)])
    token_sums = jnp.concatenate([proj_bias_local.reshape(-1), fc2_bias_local.reshape(-1)])
    bias_local = add_all(jnp.concatenate([split_sums, token_sums]), "dp", groups)
    bias_local = jnp.concatenate([bias_local, ada_bias_part.reshape(-1)])
    bias_all = lax.all_gather(bias_local, "tensor")
    cut_a = qv_bias_local.size
    cut_b = cut_a + fc1_bias_local.size
    cut_c = cut_b + proj_bias_local.size
    cut_d = cut_c + fc2_bias_local.size

    def by_column(block, shape):
        return jnp.moveaxis(block.reshape((4,) + shape), 0, -2).reshape(
            shape[:-1] + (4 * shape[-1],)
        )

    qv_bias_grad = by_column(bias_all[:, :cut_a], qv_bias_local.shape)
    fc1_bias_grad = by_column(bias_all[:, cut_a:cut_b], fc1_bias_local.shape)
    proj_bias_grad = jnp.sum(bias_all[:, cut_b:cut_c], 0).reshape(proj_bias_local.shape)
    fc2_bias_grad = jnp.sum(bias_all[:, cut_c:cut_d], 0).reshape(fc2_bias_local.shape)
    ada_bias_grad = by_column(bias_all[:, cut_d:], ada_bias_part.shape)
    return (
        outs[0],
        outs[1],
        input_grads[0],
        input_grads[1],
        cond_grad,
        ada_grad,
        ada_bias_grad,
        qkv_sum,
        qv_bias_grad,
        jnp.swapaxes(proj_sum, 1, 2),
        proj_bias_grad,
        fc1_sum,
        fc1_bias_grad,
        jnp.swapaxes(fc2_sum, 1, 2),
        fc2_bias_grad,
    )


def solution(mesh):
    groups = mesh.shape["dp"]
    in_specs = (
        P("dp", "tensor", None),
        P("dp", "tensor", None),
        P("dp", None),
        P("dp"),
        P(None, None, "dp", "tensor"),
        P(),
        P(None, None, "dp", "tensor"),
        P(),
        P(None, "tensor", "dp"),
        P(),
        P(None, "dp", "tensor"),
        P(),
        P(None, "tensor", "dp"),
        P(),
        P("dp", "tensor", None),
        P("dp", "tensor", None),
    )
    out_specs = (
        P("dp", "tensor", None),
        P("dp", "tensor", None),
        P("dp", "tensor", None),
        P("dp", "tensor", None),
        P("dp", "tensor"),
        P(None, None, "dp", "tensor"),
        P(),
        P(None, None, "dp", "tensor"),
        P(),
        P(None, "tensor", "dp"),
        P(),
        P(None, "dp", "tensor"),
        P(),
        P(None, "tensor", "dp"),
        P(),
    )

    def step(*args):
        return on_device(groups, *args)

    return jax.shard_map(
        step, mesh=mesh, in_specs=in_specs, out_specs=out_specs, check_vma=False
    )
```

```python
import math

import jax
import jax.numpy as jnp
from jax import lax
from jax.experimental import pallas as pl
from jax.experimental.pallas import tpu as pltpu
from jax.sharding import PartitionSpec as P

HEAD_DIM = 64
PAIR = 2 * HEAD_DIM
FACTOR = 1.0 / math.sqrt(HEAD_DIM)
VMEM = 60 << 20
FLOPS_PER_US = 460000000
EPSILON = 1e-06
F32 = jnp.float32
BF16 = jnp.bfloat16


def hop(value, axis, mask, size):
    return lax.ppermute(value, axis, [(i, i ^ mask) for i in range(size)])


def halves(size):
    low = 1
    while low * low < size:
        low *= 2
    return low, size // low


def spread(value, axis, size):
    low, high = halves(size)
    held = jnp.stack(
        [value] + [hop(value, axis, low * step, size) for step in range(1, high)]
    )
    full = [held] + [hop(held, axis, mask, size) for mask in range(1, low)]
    return jnp.stack(full, 1).reshape((size,) + value.shape)


def exchange(blocks, axis, size):
    low, high = halves(size)
    blocks = blocks.reshape((high, low) + blocks.shape[1:])
    held = jnp.stack(
        [blocks[0]] + [hop(blocks[step], axis, low * step, size) for step in range(1, high)]
    )
    full = [held[:, 0]] + [hop(held[:, mask], axis, mask, size) for mask in range(1, low)]
    return jnp.stack(full, 1).reshape((size,) + blocks.shape[2:])


def collect(blocks, axis, size):
    low, high = halves(size)
    blocks = blocks.reshape((high, low) + blocks.shape[1:])
    held = blocks[0] + sum(
        hop(blocks[step], axis, low * step, size) for step in range(1, high)
    )
    return held[0] + sum(hop(held[mask], axis, mask, size) for mask in range(1, low))


def add_all(value, axis, size):
    mask = 1
    while mask < size:
        value = value + hop(value, axis, mask, size)
        mask *= 2
    return value


class Order:
    def __init__(self, seed):
        self.token = seed

    def __call__(self, *values):
        self.token, *values = lax.optimization_barrier((self.token, *values))
        return values[0] if len(values) == 1 else values

    def run(self, function, *values):
        results = function(*self(*values)) if len(values) > 1 else function(self(*values))
        return self(*results) if isinstance(results, (tuple, list)) else self(results)


class Ring:
    def __init__(self, size):
        self.size = size
        self.order = list(range(0, size, 2)) + list(range(size - 1, 0, -2))
        self.ahead = [(self.order[i], self.order[(i + 1) % size]) for i in range(size)]
        self.back = [(b, a) for a, b in self.ahead]
        place = [0] * size
        for position, device in enumerate(self.order):
            place[device] = position
        self.mine = jnp.asarray(place, jnp.int32)[lax.axis_index("dp")]
        self.table = jnp.asarray(self.order, jnp.int32)

    def devices(self, distances):
        return self.table[(self.mine + jnp.asarray(distances, jnp.int32)) % self.size]

    def forward(self, value):
        return lax.ppermute(value, "dp", self.ahead)

    def backward(self, value):
        return lax.ppermute(value, "dp", self.back)


class Gather:
    def __init__(self, ring, shard):
        self.ring, self.step = ring, 0
        self.pieces, self.distances, self.streams = [shard], [0], [0]
        self.send(shard, shard)

    def send(self, ahead, back):
        self.step += 1
        if self.step == self.ring.size // 2:
            ahead, back = ahead[:1], back[1:]
        self.moving = (self.ring.forward(ahead), self.ring.backward(back))

    def arrive(self, order):
        ahead, back = order(*self.moving)
        last = self.step == self.ring.size // 2
        self.pieces += [ahead, back]
        self.distances += [-self.step, self.step]
        self.streams += [0, 1 if last else 0]
        if not last:
            self.send(ahead, back)
        return last

    def finish(self, order):
        while len(self.pieces) < self.ring.size + 1:
            self.arrive(order)
        return assemble(
            self.pieces, self.streams, self.ring.devices(self.distances), self.ring.size
        )


class Scatter:
    def __init__(self, ring, image, text, form="plain"):
        self.ring, self.image, self.text, self.form = ring, image, text, form
        self.left = ring.size // 2
        far = ring.devices([self.left])[0]
        chunk = [lax.dynamic_index_in_dim(g, far, 0) for g in (image, text)]
        self.moving = (ring.forward(chunk[0]), ring.backward(chunk[1]))

    def arrive(self, order):
        ahead, back = order(*self.moving)
        self.left -= 1
        places = self.ring.devices([self.left, -self.left])
        if self.left == 0:
            self.total = ring_total(self.image, self.text, ahead, back, places, self.form)
            return True
        ahead, back = order(*ring_add(self.image, self.text, ahead, back, places))
        self.moving = (self.ring.forward(ahead), self.ring.backward(back))
        return False

    def finish(self, order):
        while self.left:
            self.arrive(order)
        return self.total


def kernel_call(kernel, name, cost_us, grid, in_specs, out_specs, out_shape, scalars=0, **more):
    return pl.pallas_call(
        kernel,
        grid_spec=pltpu.PrefetchScalarGridSpec(
            num_scalar_prefetch=scalars,
            grid=grid,
            in_specs=in_specs,
            out_specs=out_specs,
            scratch_shapes=more.pop("scratch", ()),
        ),
        out_shape=out_shape,
        compiler_params=pltpu.CompilerParams(vmem_limit_bytes=VMEM),
        cost_estimate=pl.CostEstimate(
            flops=int(cost_us * FLOPS_PER_US), bytes_accessed=1, transcendentals=0
        ),
        name=name,
        **more,
    )


def assemble(pieces, streams, places, size):
    count = len(pieces)
    parts, rows, width = pieces[0].shape[1:]
    moves = [
        (i, streams[i] + s, s, part)
        for i in range(count)
        for s in range(pieces[i].shape[0])
        for part in range(parts)
    ]

    def kernel(place, *refs):
        shards, full = refs[:count], refs[count : count + 2]
        held, sems_in, sems_out = refs[count + 2 : -2], refs[-2], refs[-1]
        ins = [pltpu.make_async_copy(shards[i], held[i], sems_in.at[i]) for i in range(count)]
        for copy in ins:
            copy.start()
        outs, last = [], -1
        for m, (i, stream, s, part) in enumerate(moves):
            if i != last:
                ins[i].wait()
                last = i
            spot = full[stream].at[place[i], :, pl.ds(part * width, width)]
            outs.append(pltpu.make_async_copy(held[i].at[s, part], spot, sems_out.at[m]))
            outs[-1].start()
        for copy in outs:
            copy.wait()

    whole = pl.BlockSpec(memory_space=pltpu.HBM)
    out = jax.ShapeDtypeStruct((size, rows, parts * width), BF16)
    full = kernel_call(
        kernel,
        "assemble",
        5e-7 * math.prod(out.shape) * 2.5 + 1,
        (1,),
        [whole] * count,
        [whole] * 2,
        [out] * 2,
        scalars=1,
        scratch=[pltpu.VMEM(p.shape, p.dtype) for p in pieces]
        + [pltpu.SemaphoreType.DMA((count,)), pltpu.SemaphoreType.DMA((len(moves),))],
    )(places, *pieces)
    return [f.reshape(size * rows, parts * width) for f in full]


def ring_specs(image, ahead, back, block):
    width = image.shape[2]

    def local(which):
        return pl.BlockSpec((1, block, width), lambda i, place: (place[which], i, 0))

    def moved(value):
        return pl.BlockSpec((value.shape[0], block, width), lambda i, place: (0, i, 0))

    return [local(0), local(0), local(1), local(1), moved(ahead), moved(back)]


def ring_add(image, text, ahead, back, places):
    size, rows, width = image.shape
    block = rows // 4 if rows % 64 == 0 else rows
    whole = ahead.shape[0] == 2

    def kernel(place, image_a, text_a, image_b, text_b, ahead, back, send_a, send_b):
        send_a[0] = (image_a[0].astype(F32) + ahead[0].astype(F32)).astype(BF16)
        send_b[1] = (text_b[0].astype(F32) + back[back.shape[0] - 1].astype(F32)).astype(BF16)
        if whole:
            send_a[1] = (text_a[0].astype(F32) + ahead[1].astype(F32)).astype(BF16)
            send_b[0] = (image_b[0].astype(F32) + back[0].astype(F32)).astype(BF16)
        else:
            send_a[1] = text_a[0]
            send_b[0] = image_b[0]

    out = pl.BlockSpec((2, block, width), lambda i, place: (0, i, 0))
    return kernel_call(
        kernel,
        "ring_add",
        1 + 7e-6 * image.shape[1] * image.shape[2] * 2,
        (rows // block,),
        ring_specs(image, ahead, back, block),
        [out] * 2,
        [jax.ShapeDtypeStruct((2, rows, width), BF16)] * 2,
        scalars=1,
    )(places, image, text, image, text, ahead, back)


def ring_total(image, text, ahead, back, places, form):
    size, rows, width = image.shape
    turned = form == "turned"
    block = rows if turned or rows % 64 else rows // 4
    part = width // 3

    def kernel(place, image_a, text_a, image_b, text_b, ahead, back, total):
        for s, mine in enumerate((image_a, text_a)):
            value = mine[0].astype(F32) + ahead[s].astype(F32) + back[s].astype(F32)
            if form == "parts":
                for j in range(3):
                    total[s, j] = value[:, j * part : (j + 1) * part]
            else:
                total[s] = jnp.transpose(value) if turned else value

    if form == "parts":
        out = pl.BlockSpec((2, 3, block, part), lambda i, place: (0, 0, i, 0))
        shape = (2, 3, rows, part)
    elif turned:
        out = pl.BlockSpec((2, width, rows), lambda i, place: (0, 0, 0))
        shape = (2, width, rows)
    else:
        out = pl.BlockSpec((2, block, width), lambda i, place: (0, i, 0))
        shape = (2, rows, width)
    return kernel_call(
        kernel,
        "ring_total",
        1 + 7e-6 * image.shape[1] * image.shape[2] * 2,
        (rows // block,),
        ring_specs(image, ahead, back, block),
        out,
        jax.ShapeDtypeStruct(shape, F32),
        scalars=1,
    )(places, image, text, image, text, ahead, back)


class Spread:
    def __init__(self, part):
        self.part = part
        self.across = hop(part, "tensor", 2, 4)
        self.beside = hop(part, "tensor", 1, 4)

    def arrive(self, order):
        self.across = order(self.across)
        self.corner = hop(self.across, "tensor", 1, 4)

    def finish(self, order):
        beside, corner = order(self.beside, self.corner)
        return [self.part, beside, self.across, corner]


class Collect:
    def __init__(self, own, beside, across, corner):
        self.own, self.kept = own, across
        self.corner = hop(corner, "tensor", 1, 4)
        self.beside = hop(beside, "tensor", 1, 4)

    def arrive(self, order):
        corner = order(self.corner)
        send = (self.kept.astype(F32) + corner.astype(F32)).astype(BF16)
        self.across = hop(order(send), "tensor", 2, 4)

    def finish(self, order):
        return [self.own, *order(self.beside, self.across)]


def piece_specs(pieces, block=None):
    if isinstance(pieces, (list, tuple)):
        shape = pieces[0].shape
        spec = pl.BlockSpec(shape, lambda j: (0, 0, 0), pipeline_mode=pl.Buffered(1))
        return [spec] * 4, list(pieces), shape
    shape = pieces.shape[1:]
    specs = [
        pl.BlockSpec(
            (None,) + shape, lambda j, k=k: (k, 0, 0, 0), pipeline_mode=pl.Buffered(1)
        )
        for k in range(4)
    ]
    return specs, [pieces] * 4, shape


def column_block(width):
    for block in (512, 384, 256, 128):
        if width % block == 0:
            return block
    return width


def rows_times(
    pieces, weights, image, turned, outputs, finish=None, extras=(), extra_specs=(), columns=None
):
    specs, arrays, (slots, tokens, depth) = piece_specs(pieces)
    start, count = columns or (0, weights[0].shape[1])
    width = weights[0].shape[0] if turned else count
    block = column_block(math.gcd(start, width))
    text = tokens - image
    spots = [(k, c) for k in range(4) for c in range(slots)]
    dims = DOT_NT if turned else DOT_NN
    split = outputs == "split"
    count = 4 if split else outputs

    def kernel(*refs):
        rows, (image_w, text_w) = refs[:4], refs[4:6]
        more, outs = refs[6 : 6 + len(extras)], refs[6 + len(extras) :]

        def store(stream, spot, sums):
            k, c = spot
            cut = slice(0, image) if stream == 0 else slice(image, tokens)
            values = [sums] if finish is None else finish(stream, spot, cut, sums, *more)
            for which, value in enumerate(values):
                if split:
                    outs[k][c, cut] = value.astype(BF16)
                else:
                    outs[which][k, c, cut] = value.astype(BF16)

        for spot in spots:
            store(0, spot, mul(rows[spot[0]][spot[1], :image], image_w[...], dims))
        joined = jnp.concatenate([rows[k][c, image:] for k, c in spots], 0)
        sums = mul(joined, text_w[...], dims)
        for i, spot in enumerate(spots):
            store(1, spot, sums[i * text : (i + 1) * text])

    if turned:
        weight = pl.BlockSpec((block, depth), lambda j: (j, start // depth))
    else:
        weight = pl.BlockSpec((depth, block), lambda j: (0, start // block + j))
    if split:
        out = pl.BlockSpec((slots, tokens, block), lambda j: (0, 0, j))
        shape = jax.ShapeDtypeStruct((slots, tokens, width), BF16)
    else:
        out = pl.BlockSpec((4, slots, tokens, block), lambda j: (0, 0, 0, j))
        shape = jax.ShapeDtypeStruct((4, slots, tokens, width), BF16)
    return kernel_call(
        kernel,
        "rows_times",
        1 + 3e-9 * 4 * slots * tokens * depth * width,
        (width // block,),
        specs + [weight, weight] + [make(block) for make in extra_specs],
        [out] * count,
        [shape] * count,
    )(*arrays, *weights, *extras)


def weight_grad(pieces, grads, image, size):
    specs, arrays, (slots, tokens, depth) = piece_specs(pieces)
    width = grads.shape[3]
    block = column_block(width)
    text = tokens - image
    spots = [(k, c) for k in range(4) for c in range(slots)]

    def kernel(a, b, c, d, grad, image_out, text_out, sums, image_turned, text_turned):
        rows = (a, b, c, d)

        @pl.when(pl.program_id(0) == 0)
        def _():
            for i, (k, s) in enumerate(spots):
                image_turned[:, pl.ds(i * image, image)] = jnp.transpose(rows[k][s, :image])
            text_turned[...] = jnp.transpose(
                jnp.concatenate([rows[k][s, image:] for k, s in spots], 0)
            )

        image_grads = jnp.concatenate([grad[k, s, :image] for k, s in spots], 0)
        text_grads = jnp.concatenate([grad[k, s, image:] for k, s in spots], 0)
        image_out[...] = (
            mul(image_turned[...], image_grads, DOT_NN).astype(BF16).reshape(image_out.shape)
        )
        text_out[...] = (
            mul(text_turned[...], text_grads, DOT_NN).astype(BF16).reshape(text_out.shape)
        )
        sums[0:1] = jnp.sum(image_grads.astype(F32), 0, keepdims=True)
        sums[1:2] = jnp.sum(text_grads.astype(F32), 0, keepdims=True)

    out = pl.BlockSpec((size, depth // size, block), lambda j: (0, 0, j))
    shape = jax.ShapeDtypeStruct((size, depth // size, width), BF16)
    return kernel_call(
        kernel,
        "weight_grad",
        1 + 3.4e-9 * 4 * slots * tokens * depth * width,
        (width // block,),
        specs + [pl.BlockSpec((4, slots, tokens, block), lambda j: (0, 0, 0, j))],
        [out, out, pl.BlockSpec((2, block), lambda j: (0, j))],
        [shape, shape, jax.ShapeDtypeStruct((2, width), F32)],
        scratch=[
            pltpu.VMEM((depth, len(spots) * image), BF16),
            pltpu.VMEM((depth, len(spots) * text), BF16),
        ],
    )(*arrays, grads)


def mul(a, b, dims):
    return lax.dot_general(a, b, dims, preferred_element_type=F32)


DOT_NN = (((1,), (0,)), ((), ()))
DOT_NT = (((1,), (1,)), ((), ()))
DOT_TN = (((0,), (0,)), ((), ()))


def lane_masks(dtype):
    lane = lax.broadcasted_iota(jnp.int32, (1, PAIR), 1)
    low = (lane < HEAD_DIM).astype(F32)
    return [low.astype(dtype), (1.0 - low).astype(dtype)]


def stream_rows(ref, image, stream):
    cut = slice(0, image) if stream == 0 else slice(image, ref.shape[2])
    return jnp.concatenate([ref[k, 0, cut] for k in range(4)], 0)


def query_blocks(image, text):
    return [(0, (0, 1), 0), (0, (2, 3), 2 * image), (1, (0, 1, 2, 3), 4 * image)]


def attend(qkv, image, slot, earlier):
    _, slots, tokens, width = qkv.shape
    text, pairs = tokens - image, width // (3 * PAIR)

    def kernel(q, k, v, *refs):
        out, logs_out = refs[-2:]
        keys = [stream_rows(k, image, s) for s in range(2)]
        values = [stream_rows(v, image, s) for s in range(2)]
        masks = lane_masks(F32)
        low = [m.astype(BF16) for m in masks]
        for stream, members, place in query_blocks(image, text):
            cut = slice(0, image) if stream == 0 else slice(image, tokens)
            size = image if stream == 0 else text
            query = jnp.concatenate([q[m, 0, cut] for m in members], 0)
            query = query * jnp.asarray(FACTOR, BF16)
            total = logs = None
            for head in range(2):
                scores = [mul(query * low[head], key, DOT_NT) for key in keys]
                top = jnp.maximum(
                    jnp.max(scores[0], -1, keepdims=True), jnp.max(scores[1], -1, keepdims=True)
                )
                probs = [jnp.exp(s - top) for s in scores]
                denom = jnp.sum(probs[0], -1, keepdims=True) + jnp.sum(
                    probs[1], -1, keepdims=True
                )
                mixed = mul(probs[0].astype(BF16), values[0], DOT_NN) + mul(
                    probs[1].astype(BF16), values[1], DOT_NN
                )
                mixed = mixed * (masks[head] / denom)
                log = (top + jnp.log(denom)) * masks[head]
                total = mixed if total is None else total + mixed
                logs = log if logs is None else logs + log
            for i, m in enumerate(members):
                out[m, 0, cut] = total[i * size : (i + 1) * size].astype(BF16)
            turned = jnp.transpose(logs)
            span = pl.ds(place, size * len(members))
            logs_out[0, 0, 0:1, span] = turned[0:1]
            logs_out[0, 0, 1:2, span] = turned[HEAD_DIM : HEAD_DIM + 1]

    def spec(which):
        return pl.BlockSpec((4, 1, tokens, PAIR), lambda p: (0, slot, 0, which * pairs + p))

    total = 4 * tokens
    return kernel_call(
        kernel,
        "attend",
        15,
        (pairs,),
        [spec(0), spec(1), spec(2)] + [pl.BlockSpec(memory_space=pl.ANY)] * len(earlier),
        [spec(0), pl.BlockSpec((1, 1, 2, total), lambda p: (slot, p, 0, 0))],
        [
            jax.ShapeDtypeStruct((4, slots, tokens, pairs * PAIR), BF16),
            jax.ShapeDtypeStruct((slots, pairs, 2, total), F32),
        ],
        input_output_aliases={3: 0, 4: 1} if earlier else {},
    )(qkv, qkv, qkv, *earlier)


def attend_back(qkv, mixed, grads, logs, image, slot, earlier):
    _, slots, tokens, width = qkv.shape
    text, pairs = tokens - image, width // (3 * PAIR)

    def kernel(q, k, v, mixed, grads, logs, *refs):
        out, key_image, key_text, value_image, value_text = refs[-5:]
        key_sums, value_sums = (key_image, key_text), (value_image, value_text)
        keys = [stream_rows(k, image, s) for s in range(2)]
        values = [stream_rows(v, image, s) for s in range(2)]
        low = lane_masks(BF16)
        pair = pl.program_id(0)

        def lanes(which):
            return pl.ds(pl.multiple_of((which * pairs + pair) * PAIR, PAIR), PAIR)

        first = True
        for stream, members, place in query_blocks(image, text):
            cut = slice(0, image) if stream == 0 else slice(image, tokens)
            size = image if stream == 0 else text
            query = jnp.concatenate([q[m, 0, cut] for m in members], 0)
            query = query * jnp.asarray(FACTOR, BF16)
            grad = jnp.concatenate([grads[m, 0, cut] for m in members], 0)
            output = jnp.concatenate([mixed[m, 0, cut] for m in members], 0)
            inner = jnp.transpose(grad.astype(F32) * output.astype(F32))
            query_grad = None
            for head in range(2):
                head_q, head_g = query * low[head], grad * low[head]
                half = slice(head * HEAD_DIM, (head + 1) * HEAD_DIM)
                delta = jnp.sum(inner[half], 0, keepdims=True)
                log = logs[0, 0, head : head + 1, pl.ds(place, size * len(members))]
                for part in range(2):
                    probs = jnp.exp(mul(keys[part], head_q, DOT_NT) - log)
                    prob_grad = mul(values[part], head_g, DOT_NT)
                    score_grad = (probs * (prob_grad - delta)).astype(BF16)
                    value_part = mul(probs.astype(BF16), head_g, DOT_NN)
                    key_part = mul(score_grad, head_q, DOT_NN)
                    query_part = mul(score_grad, keys[part] * low[head], DOT_TN)
                    query_grad = query_part if query_grad is None else query_grad + query_part
                    if first:
                        value_sums[part][...] = value_part
                        key_sums[part][...] = key_part
                    else:
                        value_sums[part][...] += value_part
                        key_sums[part][...] += key_part
                first = False
            query_grad = query_grad * FACTOR
            for i, m in enumerate(members):
                out[m, 0, cut, lanes(0)] = query_grad[i * size : (i + 1) * size].astype(BF16)
        for which, sums in ((1, key_sums), (2, value_sums)):
            for m in range(4):
                out[m, 0, :image, lanes(which)] = sums[0][
                    m * image : (m + 1) * image
                ].astype(BF16)
                out[m, 0, image:, lanes(which)] = sums[1][m * text : (m + 1) * text].astype(BF16)

    def spec(which):
        return pl.BlockSpec((4, 1, tokens, PAIR), lambda p: (0, slot, 0, which * pairs + p))

    before = [] if earlier is None else [earlier]
    return kernel_call(
        kernel,
        "attend_back",
        29,
        (pairs,),
        [
            spec(0),
            spec(1),
            spec(2),
            spec(0),
            spec(0),
            pl.BlockSpec((1, 1, 2, 4 * tokens), lambda p: (slot, p, 0, 0)),
        ]
        + [pl.BlockSpec(memory_space=pl.ANY)] * len(before),
        pl.BlockSpec((4, 1, tokens, width), lambda p: (0, slot, 0, 0)),
        jax.ShapeDtypeStruct(qkv.shape, BF16),
        scratch=[pltpu.VMEM((4 * image, PAIR), F32), pltpu.VMEM((4 * text, PAIR), F32)] * 2,
        input_output_aliases={6: 0} if before else {},
    )(qkv, qkv, qkv, mixed, grads, logs, *before)


def normalize(values):
    average = jnp.mean(values, -1, keepdims=True)
    centred = values - average
    spread = jnp.mean(centred * centred, -1, keepdims=True)
    inverse = lax.rsqrt(spread + EPSILON)
    return centred * inverse, inverse


def norm_back(grad, normed, inverse, scale):
    scaled = grad * (1.0 + scale)
    return inverse * (
        scaled
        - jnp.mean(scaled, -1, keepdims=True)
        - normed * jnp.mean(scaled * normed, -1, keepdims=True)
    )


def add_up(values):
    return jnp.sum(values, 0, keepdims=True)


def per_slot(function, name, seqs, ins, outs):
    slots = ins[0].shape[0]

    def spec(shape, whole):
        rest = (0,) * (len(shape) - 1)
        if whole:
            return pl.BlockSpec(shape, lambda c, seqs: (0,) + rest)
        return pl.BlockSpec((1,) + tuple(shape[1:]), lambda c, seqs: (c,) + rest)

    def kernel(seqs, *refs):
        function((pl.program_id(0) < seqs[0]).astype(F32), *refs)

    return kernel_call(
        kernel,
        name,
        6,
        (slots,),
        [spec(value.shape, value.ndim == 2) for value in ins],
        [spec(shape, False) for shape, _ in outs],
        [jax.ShapeDtypeStruct(shape, dtype) for shape, dtype in outs],
        scalars=1,
    )(seqs, *ins)


def enter(live, image, text, image_cot, text_cot, vecs, first, mlp_round, sums):
    cut = image.shape[1]
    for s, (tokens, cot, rows) in enumerate(
        ((image, image_cot, slice(0, cut)), (text, text_cot, slice(cut, None)))
    ):
        normed, _ = normalize(tokens[0].astype(F32))
        first[0, rows] = (normed * (1.0 + vecs[0, s, 1:2]) + vecs[0, s, 0:1]).astype(BF16)
        rounded = (cot[0].astype(F32) * live * vecs[0, s, 5:6]).astype(BF16)
        mlp_round[0, rows] = rounded
        sums[0, s : s + 1] = add_up(rounded.astype(F32))


def middle(live, image, text, own, beside, across, vecs, bias, after, branch, second):
    cut = image.shape[1]
    for s, (tokens, rows) in enumerate(((image, slice(0, cut)), (text, slice(cut, None)))):
        value = own[0, rows].astype(F32) + beside[0, rows].astype(F32)
        value = value + across[0, rows].astype(F32) + bias[s : s + 1]
        result = tokens[0].astype(F32) + vecs[0, s, 2:3] * value
        normed, _ = normalize(result)
        branch[0, rows] = value
        after[0, rows] = result
        second[0, rows] = (normed * (1.0 + vecs[0, s, 4:5]) + vecs[0, s, 3:4]).astype(BF16)


def middle_back(
    live, image_cot, text_cot, own, beside, across, vecs, after, branch, residual, rounded, sums
):
    cut = image_cot.shape[1]
    for s, (cot, rows) in enumerate(((image_cot, slice(0, cut)), (text_cot, slice(cut, None)))):
        grad = own[0, rows].astype(F32) + beside[0, rows].astype(F32)
        grad = grad + across[0, rows].astype(F32)
        normed, inverse = normalize(after[0, rows])
        value = cot[0].astype(F32) * live + norm_back(grad, normed, inverse, vecs[0, s, 4:5])
        residual[0, rows] = value
        low = (value * vecs[0, s, 2:3]).astype(BF16)
        rounded[0, rows] = low
        sums[0, s, 0:1] = add_up(value * branch[0, rows])
        sums[0, s, 1:2] = add_up(grad)
        sums[0, s, 2:3] = add_up(grad * normed)
        sums[0, s, 3:4] = add_up(low.astype(F32))


def leave(
    live, image_cot, text_cot, own, beside, across, vecs, after, bias, image_out, text_out, sums
):
    cut = image_cot.shape[1]
    for s, (cot, rows, out) in enumerate(
        ((image_cot, slice(0, cut), image_out), (text_cot, slice(cut, None), text_out))
    ):
        value = own[0, rows].astype(F32) + beside[0, rows].astype(F32)
        value = value + across[0, rows].astype(F32) + bias[s : s + 1]
        out[0] = ((after[0, rows] + vecs[0, s, 5:6] * value) * live).astype(BF16)
        sums[0, s : s + 1] = add_up(cot[0].astype(F32) * live * value)


def enter_back(
    live, image, text, own, beside, across, vecs, residual, image_grad, text_grad, sums
):
    cut = image.shape[1]
    for s, (tokens, rows, out) in enumerate(
        ((image, slice(0, cut), image_grad), (text, slice(cut, None), text_grad))
    ):
        grad = own[0, rows].astype(F32) + beside[0, rows].astype(F32)
        grad = grad + across[0, rows].astype(F32)
        normed, inverse = normalize(tokens[0].astype(F32))
        out[0] = residual[0, rows] + norm_back(grad, normed, inverse, vecs[0, s, 1:2])
        sums[0, s, 0:1] = add_up(grad)
        sums[0, s, 1:2] = add_up(grad * normed)


def bias_spec(block):
    return pl.BlockSpec((2, block), lambda j: (0, j))


def add_bias(stream, spot, cut, sums, bias):
    return [sums + bias[stream : stream + 1]]


def gelu_both(stream, spot, cut, sums, bias):
    value = sums + bias[stream : stream + 1]
    factor = math.sqrt(2.0 / math.pi)
    square = value * value
    bend = jnp.tanh(factor * (value + 0.044715 * value * square))
    half = 0.5 * (1.0 + bend)
    slope = half + 0.5 * value * (1.0 - bend * bend) * factor * (1.0 + 0.134145 * square)
    return [value * half, slope]


def times_slope(stream, spot, cut, sums, slope):
    return [sums * slope[spot[0], spot[1], cut].astype(F32)]


def dot(spec, a, b):
    return jnp.einsum(spec, a, b, preferred_element_type=F32)


def on_device(
    groups,
    image_tokens,
    text_tokens,
    conditioning,
    group_seqs,
    ada_weight,
    ada_bias,
    qkv_weight,
    qv_bias,
    proj_weight,
    proj_bias,
    fc1_weight,
    fc1_bias,
    fc2_weight,
    fc2_bias,
    image_cot,
    text_cot,
):
    column = lax.axis_index("tensor")
    group = lax.axis_index("dp")
    ring = Ring(groups)
    order = Order(group_seqs)
    slots, image, width = image_tokens.shape
    text = text_tokens.shape[1]
    tokens = image + text
    rows = qkv_weight.shape[2]
    col_width = qkv_weight.shape[-1]
    hidden = fc1_weight.shape[-1]
    both = range(2)

    proj_turned = jnp.swapaxes(proj_weight, 1, 2)[:, None]
    fc1_shard = fc1_weight[:, None]
    fc2_turned = jnp.swapaxes(fc2_weight, 1, 2)[:, None]

    ada_part = lax.dynamic_slice_in_dim(ada_bias.astype(F32), column * col_width, col_width, 2)
    qv_part = lax.dynamic_slice_in_dim(qv_bias.astype(F32), column * col_width, col_width, 2)
    fc1_part = lax.dynamic_slice_in_dim(fc1_bias.astype(F32), column * hidden, hidden, 1)
    offsets = jnp.stack([qv_part[:, 0], jnp.zeros_like(qv_part[:, 0]), qv_part[:, 1]], 1)
    offsets = offsets.reshape(2, 3 * col_width)
    proj_add = proj_bias.astype(F32)
    fc2_add = fc2_bias.astype(F32)

    cond_act, silu_back = jax.vjp(jax.nn.silu, conditioning.astype(F32))
    cond_low = cond_act.astype(BF16).reshape(slots, groups, rows)
    cond_sends = jnp.stack(
        [
            lax.dynamic_index_in_dim(cond_low, group ^ mask, 1, keepdims=False)
            for mask in range(groups)
        ]
    )
    cond_rows = order(exchange(cond_sends, "dp", groups)).reshape(groups * slots, rows)
    modul_parts = order(dot("cd,sjdn->csjn", cond_rows, ada_weight))
    modul_parts = modul_parts.reshape((groups, slots) + modul_parts.shape[1:])
    modul_local = order(collect(modul_parts, "dp", groups) + ada_part[None])
    qkv_ring = Gather(ring, order(jnp.concatenate([qkv_weight, proj_turned], 1)))
    qkv_part = (0, 3 * col_width)
    proj_part = (3 * col_width, col_width)
    vecs = order(lax.all_gather(modul_local, "tensor", axis=3, tiled=True))

    first, mlp_round, fc2_bias_local = order.run(
        lambda *a: per_slot(
            enter,
            "enter",
            group_seqs,
            a,
            [
                ((slots, tokens, width), BF16),
                ((slots, tokens, width), BF16),
                ((slots, 2, width), F32),
            ],
        ),
        image_tokens,
        text_tokens,
        image_cot,
        text_cot,
        vecs,
    )
    qkv_ring.arrive(order)
    first_move = Spread(order(first))
    qkv_ring.arrive(order)
    qkv_ring.arrive(order)
    first_move.arrive(order)
    first_full = first_move.finish(order)
    qkv_ring.arrive(order)
    fc1_ring = Gather(ring, order(fc1_shard))
    mlp_move = Spread(order(mlp_round))
    qkv_full = order(*qkv_ring.finish(order))

    qkv = order.run(
        lambda *a: rows_times(
            a[:4], a[4:], image, False, 1, add_bias, (offsets,), (bias_spec,), qkv_part
        ),
        *first_full,
        *qkv_full,
    )
    fc1_ring.arrive(order)
    mixed = ()
    for slot in range(slots):
        mixed = order.run(
            lambda *a, slot=slot: attend(a[0], image, slot, a[1:]), *((qkv,) + tuple(mixed))
        )
    mixed, logs = mixed
    fc1_ring.arrive(order)
    mlp_move.arrive(order)
    branch_parts = order.run(
        lambda *a: rows_times(a[0], a[1:], image, True, "split", columns=proj_part),
        mixed,
        *qkv_full,
    )
    branch_move = Collect(*order(*branch_parts))
    mlp_full = mlp_move.finish(order)
    branch_move.arrive(order)
    fc1_ring.arrive(order)
    fc1_ring.arrive(order)
    fc2_ring = Gather(ring, order(fc2_turned))
    branch_terms = branch_move.finish(order)
    after, branch, second = order.run(
        lambda *a: per_slot(
            middle,
            "middle",
            group_seqs,
            a,
            [
                ((slots, tokens, width), F32),
                ((slots, tokens, width), F32),
                ((slots, tokens, width), BF16),
            ],
        ),
        image_tokens,
        text_tokens,
        *branch_terms,
        vecs,
        proj_add,
    )
    second_move = Spread(second)
    fc1_full = order(*fc1_ring.finish(order))
    fc2_ring.arrive(order)
    fc2_ring.arrive(order)
    second_move.arrive(order)
    second_full = second_move.finish(order)
    activated, slope = order.run(
        lambda *a: rows_times(
            a[:4], a[4:], image, False, 2, gelu_both, (fc1_part,), (bias_spec,)
        ),
        *second_full,
        *fc1_full,
    )
    fc2_ring.arrive(order)
    *fc2_grad, _ = order.run(
        lambda *a: weight_grad(a[:4], a[4], image, groups), *mlp_full, activated
    )
    fc2_ring.arrive(order)
    fc2_sums = Scatter(ring, *order(*fc2_grad), "turned")
    fc2_full = order(*fc2_ring.finish(order))
    pre_round = order.run(
        lambda *a: rows_times(
            a[:4],
            a[4:],
            image,
            False,
            1,
            times_slope,
            (slope,),
            (
                lambda block: pl.BlockSpec(
                    (4, slots, tokens, block), lambda j: (0, 0, 0, j)
                ),
            ),
        ),
        *mlp_full,
        *fc2_full,
    )
    fc2_sums.arrive(order)
    second_parts = order.run(
        lambda *a: rows_times(a[0], a[1:], image, True, "split"), pre_round, *fc1_full
    )
    second_back = Collect(*second_parts)
    second_back.arrive(order)
    *fc1_grad, fc1_bias_local = order.run(
        lambda *a: weight_grad(a[:4], a[4], image, groups), *second_full, pre_round
    )
    fc1_sums = Scatter(ring, *order(*fc1_grad))
    mlp_parts = order.run(
        lambda *a: rows_times(a[0], a[1:], image, True, "split"), activated, *fc2_full
    )
    fc2_sums.arrive(order)
    second_terms = second_back.finish(order)
    residual, branch_round, middle_vecs = order.run(
        lambda *a: per_slot(
            middle_back,
            "middle_back",
            group_seqs,
            a,
            [
                ((slots, tokens, width), F32),
                ((slots, tokens, width), BF16),
                ((slots, 2, 4, width), F32),
            ],
        ),
        image_cot,
        text_cot,
        *second_terms,
        vecs,
        after,
        branch,
    )
    branch_back = Spread(branch_round)
    fc2_sums.arrive(order)
    fc1_sums.arrive(order)
    branch_back.arrive(order)
    branch_full = branch_back.finish(order)
    mixed_grad = order.run(
        lambda *a: rows_times(a[:4], a[4:], image, False, 1, columns=proj_part),
        *branch_full,
        *qkv_full,
    )
    mlp_back = Collect(*order(*mlp_parts))
    mlp_back.arrive(order)
    *proj_grad, _ = order.run(
        lambda *a: weight_grad(a[:4], a[4], image, groups), *branch_full, mixed
    )
    fc2_sums.arrive(order)
    proj_sum = lax.psum_scatter(
        jnp.stack(order(*proj_grad), 1), "dp", scatter_dimension=0, tiled=False
    )
    qkv_grads = None
    for slot in range(slots):
        given = (qkv, mixed, mixed_grad, logs) + (() if slot == 0 else (qkv_grads,))
        qkv_grads = order.run(
            lambda *a, slot=slot: attend_back(
                *a[:4], image, slot, a[4] if len(a) > 4 else None
            ),
            *given,
        )
        if slot == 0:
            fc1_sums.arrive(order)
    mlp_terms = mlp_back.finish(order)
    fc1_sums.arrive(order)
    *qkv_grad, qv_sums = order.run(
        lambda *a: weight_grad(a[:4], a[4], image, groups), *first_full, qkv_grads
    )
    qkv_sums = Scatter(ring, *order(*qkv_grad), "parts")
    first_parts = order.run(
        lambda *a: rows_times(a[0], a[1:], image, True, "split", columns=qkv_part),
        qkv_grads,
        *qkv_full,
    )
    fc1_sums.arrive(order)
    first_back = Collect(*first_parts)
    first_back.arrive(order)
    qkv_sums.arrive(order)
    qv_bias_local = qv_sums.reshape(2, 3, col_width)[:, 0::2]
    proj_bias_local = jnp.sum(middle_vecs[:, :, 3], 0)
    fc2_bias_local = jnp.sum(fc2_bias_local, 0)
    split_sums = jnp.concatenate([qv_bias_local.reshape(-1), fc1_bias_local.reshape(-1)])
    token_sums = jnp.concatenate([proj_bias_local.reshape(-1), fc2_bias_local.reshape(-1)])
    bias_local = add_all(jnp.concatenate([split_sums, token_sums]), "dp", groups)
    bias_all = order(lax.all_gather(order(bias_local), "tensor"))
    cut_a = qv_bias_local.size
    cut_b = cut_a + fc1_bias_local.size
    cut_c = cut_b + proj_bias_local.size
    cut_d = cut_c + fc2_bias_local.size

    def by_column(block, shape):
        return jnp.moveaxis(block.reshape((4,) + shape), 0, -2).reshape(
            shape[:-1] + (4 * shape[-1],)
        )

    qv_bias_grad = by_column(bias_all[:, :cut_a], qv_bias_local.shape)
    fc1_bias_grad = by_column(bias_all[:, cut_a:cut_b], fc1_bias_local.shape)
    proj_bias_grad = jnp.sum(bias_all[:, cut_b:cut_c], 0).reshape(proj_bias_local.shape)
    fc2_bias_grad = jnp.sum(bias_all[:, cut_c:cut_d], 0).reshape(fc2_bias_local.shape)
    image_out, text_out, gate_two = order.run(
        lambda *a: per_slot(
            leave,
            "leave",
            group_seqs,
            a,
            [
                (image_tokens.shape, BF16),
                (text_tokens.shape, BF16),
                ((slots, 2, width), F32),
            ],
        ),
        image_cot,
        text_cot,
        *mlp_terms,
        vecs,
        after,
        fc2_add,
    )
    qkv_sums.arrive(order)
    first_terms = first_back.finish(order)
    image_grad, text_grad, enter_vecs = order.run(
        lambda *a: per_slot(
            enter_back,
            "enter_back",
            group_seqs,
            a,
            [
                (image_tokens.shape, F32),
                (text_tokens.shape, F32),
                ((slots, 2, 2, width), F32),
            ],
        ),
        image_tokens,
        text_tokens,
        *first_terms,
        vecs,
        residual,
    )
    qkv_sums.arrive(order)
    modul_grad = jnp.concatenate(
        [
            enter_vecs,
            middle_vecs[:, :, 0:3],
            gate_two[:, :, None],
        ],
        2,
    ).reshape(slots, 2, 6, 4, col_width)
    modul_blocks = jnp.stack(
        [
            lax.dynamic_index_in_dim(modul_grad, column ^ mask, 3, keepdims=False)
            for mask in range(4)
        ]
    )
    modul_round = order(collect(modul_blocks, "tensor", 4).astype(BF16))
    modul_all = order(spread(modul_round, "dp", groups))
    modul_all = modul_all.reshape((groups * slots,) + modul_round.shape[1:])
    cond_part = dot("csjn,sjdn->cd", modul_all, ada_weight)
    ada_bias_part = jnp.sum(modul_all.astype(F32), 0)
    last = jnp.concatenate([cond_part.reshape(-1), ada_bias_part.reshape(-1)])
    last = order(spread(order(last), "tensor", 4))
    cond_part = jnp.sum(last[:, : cond_part.size], 0).reshape(groups, slots, rows)
    cond_terms = order(exchange(cond_part, "dp", groups))
    cond_term = jnp.stack(
        [
            lax.dynamic_index_in_dim(cond_terms, group ^ place, 0, keepdims=False)
            for place in range(groups)
        ],
        1,
    ).reshape(slots, width)
    cond_grad = lax.dynamic_slice_in_dim(
        silu_back(cond_term)[0], column * col_width, col_width, 1
    )
    ada_bias_grad = jnp.stack(
        [
            lax.dynamic_index_in_dim(
                last[:, cond_part.size :], column ^ place, 0, keepdims=False
            ).reshape(ada_bias_part.shape)
            for place in range(4)
        ],
        2,
    ).reshape(ada_bias.shape)
    ada_grad = dot("cd,csjn->sjdn", cond_rows, modul_all)
    fc2_sum, fc1_sum = fc2_sums.finish(order), fc1_sums.finish(order)
    proj_sum = jnp.swapaxes(order(proj_sum).astype(F32), 1, 2)
    qkv_sum = qkv_sums.finish(order)
    cond_grad = order(cond_grad)
    live = jnp.arange(slots, dtype=jnp.int32) < order.token[0]
    cond_grad = jnp.where(live[:, None], cond_grad, 0.0)
    return (
        image_out,
        text_out,
        image_grad,
        text_grad,
        cond_grad,
        ada_grad,
        ada_bias_grad,
        qkv_sum,
        qv_bias_grad,
        proj_sum,
        proj_bias_grad,
        fc1_sum,
        fc1_bias_grad,
        fc2_sum,
        fc2_bias_grad,
    )


def solution(mesh):
    groups = mesh.shape["dp"]
    in_specs = (
        P("dp", "tensor", None),
        P("dp", "tensor", None),
        P("dp", None),
        P("dp"),
        P(None, None, "dp", "tensor"),
        P(),
        P(None, None, "dp", "tensor"),
        P(),
        P(None, "tensor", "dp"),
        P(),
        P(None, "dp", "tensor"),
        P(),
        P(None, "tensor", "dp"),
        P(),
        P("dp", "tensor", None),
        P("dp", "tensor", None),
    )
    out_specs = (
        P("dp", "tensor", None),
        P("dp", "tensor", None),
        P("dp", "tensor", None),
        P("dp", "tensor", None),
        P("dp", "tensor"),
        P(None, None, "dp", "tensor"),
        P(),
        P(None, None, "dp", "tensor"),
        P(),
        P(None, "tensor", "dp"),
        P(),
        P(None, "dp", "tensor"),
        P(),
        P(None, "tensor", "dp"),
        P(),
    )

    def step(*args):
        return on_device(groups, *args)

    return jax.shard_map(
        step, mesh=mesh, in_specs=in_specs, out_specs=out_specs, check_vma=False
    )
```

```python
import math

import jax
import jax.numpy as jnp
from jax import lax
from jax.experimental import pallas as pl
from jax.experimental.pallas import tpu as pltpu
from jax.sharding import PartitionSpec as P

HEAD_DIM = 64
PAIR = 2 * HEAD_DIM
FACTOR = 1.0 / math.sqrt(HEAD_DIM)
VMEM = 60 << 20
FLOPS_PER_US = 460000000
EPSILON = 1e-06
F32 = jnp.float32
BF16 = jnp.bfloat16


def hop(value, axis, mask, size):
    return lax.ppermute(value, axis, [(i, i ^ mask) for i in range(size)])


def halves(size):
    low = 1
    while low * low < size:
        low *= 2
    return low, size // low


def spread(value, axis, size):
    low, high = halves(size)
    held = jnp.stack(
        [value] + [hop(value, axis, low * step, size) for step in range(1, high)]
    )
    full = [held] + [hop(held, axis, mask, size) for mask in range(1, low)]
    return jnp.stack(full, 1).reshape((size,) + value.shape)


def exchange(blocks, axis, size):
    low, high = halves(size)
    blocks = blocks.reshape((high, low) + blocks.shape[1:])
    held = jnp.stack(
        [blocks[0]] + [hop(blocks[step], axis, low * step, size) for step in range(1, high)]
    )
    full = [held[:, 0]] + [hop(held[:, mask], axis, mask, size) for mask in range(1, low)]
    return jnp.stack(full, 1).reshape((size,) + blocks.shape[2:])


def collect(blocks, axis, size):
    low, high = halves(size)
    blocks = blocks.reshape((high, low) + blocks.shape[1:])
    held = blocks[0] + sum(
        hop(blocks[step], axis, low * step, size) for step in range(1, high)
    )
    return held[0] + sum(hop(held[mask], axis, mask, size) for mask in range(1, low))


def by_column(block, shape):
    return jnp.moveaxis(block.reshape((4,) + shape), 0, -2).reshape(
        shape[:-1] + (4 * shape[-1],)
    )


class Order:
    def __init__(self, seed):
        self.token = seed

    def __call__(self, *values):
        self.token, *values = lax.optimization_barrier((self.token, *values))
        return values[0] if len(values) == 1 else values

    def run(self, function, *values):
        results = function(*self(*values)) if len(values) > 1 else function(self(*values))
        return self(*results) if isinstance(results, (tuple, list)) else self(results)


class Ring:
    def __init__(self, size):
        self.size = size
        self.order = list(range(0, size, 2)) + list(range(size - 1, 0, -2))
        self.ahead = [(self.order[i], self.order[(i + 1) % size]) for i in range(size)]
        self.back = [(b, a) for a, b in self.ahead]
        place = [0] * size
        for position, device in enumerate(self.order):
            place[device] = position
        self.mine = jnp.asarray(place, jnp.int32)[lax.axis_index("dp")]
        self.table = jnp.asarray(self.order, jnp.int32)

    def devices(self, distances):
        return self.table[(self.mine + jnp.asarray(distances, jnp.int32)) % self.size]

    def forward(self, value):
        return lax.ppermute(value, "dp", self.ahead)

    def backward(self, value):
        return lax.ppermute(value, "dp", self.back)


class Gather:
    def __init__(self, ring, shard):
        self.ring, self.step = ring, 0
        self.pieces, self.distances, self.streams = [shard], [0], [0]
        self.send(shard, shard)

    def send(self, ahead, back):
        self.step += 1
        if self.step == self.ring.size // 2:
            ahead, back = ahead[:1], back[1:]
        self.moving = (self.ring.forward(ahead), self.ring.backward(back))

    def arrive(self, order):
        ahead, back = order(*self.moving)
        last = self.step == self.ring.size // 2
        self.pieces += [ahead, back]
        self.distances += [-self.step, self.step]
        self.streams += [0, 1 if last else 0]
        if not last:
            self.send(ahead, back)
        return last

    def finish(self, order):
        while len(self.pieces) < self.ring.size + 1:
            self.arrive(order)
        return assemble(
            self.pieces, self.streams, self.ring.devices(self.distances), self.ring.size
        )


class Scatter:
    def __init__(self, ring, image, text, form="plain"):
        self.ring, self.image, self.text, self.form = ring, image, text, form
        self.left = ring.size // 2
        far = ring.devices([self.left])[0]
        chunk = [lax.dynamic_index_in_dim(g, far, 0) for g in (image, text)]
        self.moving = (ring.forward(chunk[0]), ring.backward(chunk[1]))

    def arrive(self, order):
        ahead, back = order(*self.moving)
        self.left -= 1
        places = self.ring.devices([self.left, -self.left])
        if self.left == 0:
            self.total = ring_total(self.image, self.text, ahead, back, places, self.form)
            return True
        ahead, back = order(*ring_add(self.image, self.text, ahead, back, places))
        self.moving = (self.ring.forward(ahead), self.ring.backward(back))
        return False

    def finish(self, order):
        while self.left:
            self.arrive(order)
        return self.total


def kernel_call(kernel, name, cost_us, grid, in_specs, out_specs, out_shape, scalars=0, **more):
    return pl.pallas_call(
        kernel,
        grid_spec=pltpu.PrefetchScalarGridSpec(
            num_scalar_prefetch=scalars,
            grid=grid,
            in_specs=in_specs,
            out_specs=out_specs,
            scratch_shapes=more.pop("scratch", ()),
        ),
        out_shape=out_shape,
        compiler_params=pltpu.CompilerParams(vmem_limit_bytes=VMEM),
        cost_estimate=pl.CostEstimate(
            flops=int(cost_us * FLOPS_PER_US), bytes_accessed=1, transcendentals=0
        ),
        name=name,
        **more,
    )


def assemble(pieces, streams, places, size):
    count = len(pieces)
    parts, rows, width = pieces[0].shape[1:]
    moves = [
        (i, streams[i] + s, s, part)
        for i in range(count)
        for s in range(pieces[i].shape[0])
        for part in range(parts)
    ]

    def kernel(place, *refs):
        shards, full = refs[:count], refs[count : count + 2]
        held, sems_in, sems_out = refs[count + 2 : -2], refs[-2], refs[-1]
        ins = [pltpu.make_async_copy(shards[i], held[i], sems_in.at[i]) for i in range(count)]
        for copy in ins:
            copy.start()
        outs, last = [], -1
        for m, (i, stream, s, part) in enumerate(moves):
            if i != last:
                ins[i].wait()
                last = i
            spot = full[stream].at[place[i], :, pl.ds(part * width, width)]
            outs.append(pltpu.make_async_copy(held[i].at[s, part], spot, sems_out.at[m]))
            outs[-1].start()
        for copy in outs:
            copy.wait()

    whole = pl.BlockSpec(memory_space=pltpu.HBM)
    out = jax.ShapeDtypeStruct((size, rows, parts * width), BF16)
    full = kernel_call(
        kernel,
        "assemble",
        5e-7 * math.prod(out.shape) * 2.5 + 1,
        (1,),
        [whole] * count,
        [whole] * 2,
        [out] * 2,
        scalars=1,
        scratch=[pltpu.VMEM(p.shape, p.dtype) for p in pieces]
        + [pltpu.SemaphoreType.DMA((count,)), pltpu.SemaphoreType.DMA((len(moves),))],
    )(places, *pieces)
    return [f.reshape(size * rows, parts * width) for f in full]


def ring_specs(image, ahead, back, block):
    width = image.shape[2]

    def local(which):
        return pl.BlockSpec((1, block, width), lambda i, place: (place[which], i, 0))

    def moved(value):
        return pl.BlockSpec((value.shape[0], block, width), lambda i, place: (0, i, 0))

    return [local(0), local(0), local(1), local(1), moved(ahead), moved(back)]


def ring_add(image, text, ahead, back, places):
    size, rows, width = image.shape
    block = rows // 4 if rows % 64 == 0 else rows
    whole = ahead.shape[0] == 2

    def kernel(place, image_a, text_a, image_b, text_b, ahead, back, send_a, send_b):
        send_a[0] = (image_a[0].astype(F32) + ahead[0].astype(F32)).astype(BF16)
        send_b[1] = (text_b[0].astype(F32) + back[back.shape[0] - 1].astype(F32)).astype(BF16)
        if whole:
            send_a[1] = (text_a[0].astype(F32) + ahead[1].astype(F32)).astype(BF16)
            send_b[0] = (image_b[0].astype(F32) + back[0].astype(F32)).astype(BF16)
        else:
            send_a[1] = text_a[0]
            send_b[0] = image_b[0]

    out = pl.BlockSpec((2, block, width), lambda i, place: (0, i, 0))
    return kernel_call(
        kernel,
        "ring_add",
        1 + 7e-6 * image.shape[1] * image.shape[2] * 2,
        (rows // block,),
        ring_specs(image, ahead, back, block),
        [out] * 2,
        [jax.ShapeDtypeStruct((2, rows, width), BF16)] * 2,
        scalars=1,
    )(places, image, text, image, text, ahead, back)


def ring_total(image, text, ahead, back, places, form):
    size, rows, width = image.shape
    block = rows // 4 if form == "plain" and rows % 64 == 0 else rows
    part = width // 4

    def kernel(place, image_a, text_a, image_b, text_b, ahead, back, total, *more):
        for s, mine in enumerate((image_a, text_a)):
            value = mine[0].astype(F32) + ahead[s].astype(F32) + back[s].astype(F32)
            if form == "parts":
                for j in range(3):
                    total[s, j] = value[:, j * part : (j + 1) * part]
                more[0][s] = jnp.transpose(value[:, 3 * part :])
            else:
                total[s] = jnp.transpose(value) if form == "turned" else value

    shapes = {
        "plain": [(2, rows, width)],
        "turned": [(2, width, rows)],
        "parts": [(2, 3, rows, part), (2, part, rows)],
    }[form]
    if form == "plain":
        outs = [pl.BlockSpec((2, block, width), lambda i, place: (0, i, 0))]
    else:
        outs = [
            pl.BlockSpec(shape, lambda i, place, n=len(shape): (0,) * n) for shape in shapes
        ]
    total = kernel_call(
        kernel,
        "ring_total",
        1 + 7e-6 * image.shape[1] * image.shape[2] * 2,
        (rows // block,),
        ring_specs(image, ahead, back, block),
        outs,
        [jax.ShapeDtypeStruct(shape, F32) for shape in shapes],
        scalars=1,
    )(places, image, text, image, text, ahead, back)
    return total if form == "parts" else total[0]


class Spread:
    def __init__(self, part):
        self.part = part
        self.across = hop(part, "tensor", 2, 4)
        self.beside = hop(part, "tensor", 1, 4)

    def arrive(self, order):
        self.across, self.beside = order(self.across, self.beside)
        self.corner = hop(self.across, "tensor", 1, 4)

    def finish(self, order):
        return [self.part, self.beside, self.across, order(self.corner)]


class Collect:
    def __init__(self, own, beside, across, corner):
        self.own, self.kept = own, across
        self.corner = hop(corner, "tensor", 1, 4)
        self.beside = hop(beside, "tensor", 1, 4)

    def arrive(self, order):
        corner = order(self.corner)
        send = (self.kept.astype(F32) + corner.astype(F32)).astype(BF16)
        self.across = hop(order(send), "tensor", 2, 4)
        self.beside = order(self.beside)

    def finish(self, order):
        return [self.own, self.beside, order(self.across)]


def piece_specs(pieces, block=None):
    if isinstance(pieces, (list, tuple)):
        shape = pieces[0].shape
        spec = pl.BlockSpec(shape, lambda j: (0, 0, 0), pipeline_mode=pl.Buffered(1))
        return [spec] * 4, list(pieces), shape
    shape = pieces.shape[1:]
    specs = [
        pl.BlockSpec(
            (None,) + shape, lambda j, k=k: (k, 0, 0, 0), pipeline_mode=pl.Buffered(1)
        )
        for k in range(4)
    ]
    return specs, [pieces] * 4, shape


def column_block(width):
    for block in (512, 384, 256, 128):
        if width % block == 0:
            return block
    return width


def rows_times(
    pieces, weights, image, turned, outputs, finish=None, extras=(), extra_specs=(), columns=None
):
    specs, arrays, (slots, tokens, depth) = piece_specs(pieces)
    start, count = columns or (0, weights[0].shape[1])
    width = weights[0].shape[0] if turned else count
    block = column_block(math.gcd(start, width))
    text = tokens - image
    spots = [(k, c) for k in range(4) for c in range(slots)]
    dims = DOT_NT if turned else DOT_NN
    split = outputs == "split"
    count = 4 if split else outputs

    def kernel(*refs):
        rows, (image_w, text_w) = refs[:4], refs[4:6]
        more, outs = refs[6 : 6 + len(extras)], refs[6 + len(extras) :]

        def store(stream, spot, sums):
            k, c = spot
            cut = slice(0, image) if stream == 0 else slice(image, tokens)
            values = [sums] if finish is None else finish(stream, spot, cut, sums, *more)
            for which, value in enumerate(values):
                if split:
                    outs[k][c, cut] = value.astype(BF16)
                else:
                    outs[which][k, c, cut] = value.astype(BF16)

        for spot in spots:
            store(0, spot, mul(rows[spot[0]][spot[1], :image], image_w[...], dims))
        joined = jnp.concatenate([rows[k][c, image:] for k, c in spots], 0)
        sums = mul(joined, text_w[...], dims)
        for i, spot in enumerate(spots):
            store(1, spot, sums[i * text : (i + 1) * text])

    if turned:
        weight = pl.BlockSpec((block, depth), lambda j: (j, start // depth))
    else:
        weight = pl.BlockSpec((depth, block), lambda j: (0, start // block + j))
    if split:
        out = pl.BlockSpec((slots, tokens, block), lambda j: (0, 0, j))
        shape = jax.ShapeDtypeStruct((slots, tokens, width), BF16)
    else:
        out = pl.BlockSpec((4, slots, tokens, block), lambda j: (0, 0, 0, j))
        shape = jax.ShapeDtypeStruct((4, slots, tokens, width), BF16)
    return kernel_call(
        kernel,
        "rows_times",
        1 + 3e-9 * 4 * slots * tokens * depth * width,
        (width // block,),
        specs + [weight, weight] + [make(block) for make in extra_specs],
        [out] * count,
        [shape] * count,
    )(*arrays, *weights, *extras)


def weight_grad(pieces, grads, image, size, first=0, total=None, earlier=()):
    specs, arrays, (slots, tokens, depth) = piece_specs(pieces)
    width = grads.shape[3]
    block = column_block(math.gcd(first, width))
    text = tokens - image
    spots = [(k, c) for k in range(4) for c in range(slots)]

    def kernel(a, b, c, d, grad, *refs):
        rows = (a, b, c, d)
        image_out, text_out, sums, image_turned, text_turned = refs[-5:]

        @pl.when(pl.program_id(0) == 0)
        def _():
            for i, (k, s) in enumerate(spots):
                image_turned[:, pl.ds(i * image, image)] = jnp.transpose(rows[k][s, :image])
            text_turned[...] = jnp.transpose(
                jnp.concatenate([rows[k][s, image:] for k, s in spots], 0)
            )

        image_grads = jnp.concatenate([grad[k, s, :image] for k, s in spots], 0)
        text_grads = jnp.concatenate([grad[k, s, image:] for k, s in spots], 0)
        image_out[...] = (
            mul(image_turned[...], image_grads, DOT_NN).astype(BF16).reshape(image_out.shape)
        )
        text_out[...] = (
            mul(text_turned[...], text_grads, DOT_NN).astype(BF16).reshape(text_out.shape)
        )
        sums[0:1] = jnp.sum(image_grads.astype(F32), 0, keepdims=True)
        sums[1:2] = jnp.sum(text_grads.astype(F32), 0, keepdims=True)

    out = pl.BlockSpec((size, depth // size, block), lambda j: (0, 0, first // block + j))
    shape = jax.ShapeDtypeStruct((size, depth // size, total or width), BF16)
    return kernel_call(
        kernel,
        "weight_grad",
        1 + 3.4e-9 * 4 * slots * tokens * depth * width,
        (width // block,),
        specs
        + [pl.BlockSpec((4, slots, tokens, block), lambda j: (0, 0, 0, j))]
        + [pl.BlockSpec(memory_space=pl.ANY)] * len(earlier),
        [out, out, pl.BlockSpec((2, block), lambda j: (0, j))],
        [shape, shape, jax.ShapeDtypeStruct((2, width), F32)],
        scratch=[
            pltpu.VMEM((depth, len(spots) * image), BF16),
            pltpu.VMEM((depth, len(spots) * text), BF16),
        ],
        input_output_aliases={5: 0, 6: 1} if earlier else {},
    )(*arrays, grads, *earlier)


def mul(a, b, dims):
    return lax.dot_general(a, b, dims, preferred_element_type=F32)


DOT_NN = (((1,), (0,)), ((), ()))
DOT_NT = (((1,), (1,)), ((), ()))
DOT_TN = (((0,), (0,)), ((), ()))


def lane_masks(dtype):
    lane = lax.broadcasted_iota(jnp.int32, (1, PAIR), 1)
    low = (lane < HEAD_DIM).astype(F32)
    return [low.astype(dtype), (1.0 - low).astype(dtype)]


def stream_rows(ref, image, stream):
    cut = slice(0, image) if stream == 0 else slice(image, ref.shape[2])
    return jnp.concatenate([ref[k, 0, cut] for k in range(4)], 0)


def query_blocks(image, text):
    return [(0, (0, 1), 0), (0, (2, 3), 2 * image), (1, (0, 1, 2, 3), 4 * image)]


def attend(qkv, image, slot, earlier):
    _, slots, tokens, width = qkv.shape
    text, pairs = tokens - image, width // (3 * PAIR)

    def kernel(q, k, v, *refs):
        out, logs_out = refs[-2:]
        keys = [stream_rows(k, image, s) for s in range(2)]
        values = [stream_rows(v, image, s) for s in range(2)]
        masks = lane_masks(F32)
        low = [m.astype(BF16) for m in masks]
        for stream, members, place in query_blocks(image, text):
            cut = slice(0, image) if stream == 0 else slice(image, tokens)
            size = image if stream == 0 else text
            query = jnp.concatenate([q[m, 0, cut] for m in members], 0)
            query = query * jnp.asarray(FACTOR, BF16)
            total = logs = None
            for head in range(2):
                scores = [mul(query * low[head], key, DOT_NT) for key in keys]
                top = jnp.maximum(
                    jnp.max(scores[0], -1, keepdims=True), jnp.max(scores[1], -1, keepdims=True)
                )
                probs = [jnp.exp(s - top) for s in scores]
                denom = jnp.sum(probs[0], -1, keepdims=True) + jnp.sum(
                    probs[1], -1, keepdims=True
                )
                mixed = mul(probs[0].astype(BF16), values[0], DOT_NN) + mul(
                    probs[1].astype(BF16), values[1], DOT_NN
                )
                mixed = mixed * (masks[head] / denom)
                log = (top + jnp.log(denom)) * masks[head]
                total = mixed if total is None else total + mixed
                logs = log if logs is None else logs + log
            for i, m in enumerate(members):
                out[m, 0, cut] = total[i * size : (i + 1) * size].astype(BF16)
            turned = jnp.transpose(logs)
            span = pl.ds(place, size * len(members))
            logs_out[0, 0, 0:1, span] = turned[0:1]
            logs_out[0, 0, 1:2, span] = turned[HEAD_DIM : HEAD_DIM + 1]

    def spec(which):
        return pl.BlockSpec((4, 1, tokens, PAIR), lambda p: (0, slot, 0, which * pairs + p))

    total = 4 * tokens
    return kernel_call(
        kernel,
        "attend",
        15,
        (pairs,),
        [spec(0), spec(1), spec(2)] + [pl.BlockSpec(memory_space=pl.ANY)] * len(earlier),
        [spec(0), pl.BlockSpec((1, 1, 2, total), lambda p: (slot, p, 0, 0))],
        [
            jax.ShapeDtypeStruct((4, slots, tokens, pairs * PAIR), BF16),
            jax.ShapeDtypeStruct((slots, pairs, 2, total), F32),
        ],
        input_output_aliases={3: 0, 4: 1} if earlier else {},
    )(qkv, qkv, qkv, *earlier)


def attend_back(qkv, mixed, grads, logs, image, slot, earlier):
    _, slots, tokens, width = qkv.shape
    text, pairs = tokens - image, width // (3 * PAIR)

    def kernel(q, k, v, mixed, grads, logs, *refs):
        out, key_image, key_text, value_image, value_text = refs[-5:]
        key_sums, value_sums = (key_image, key_text), (value_image, value_text)
        keys = [stream_rows(k, image, s) for s in range(2)]
        values = [stream_rows(v, image, s) for s in range(2)]
        low = lane_masks(BF16)
        pair = pl.program_id(0)

        def lanes(which):
            return pl.ds(pl.multiple_of((which * pairs + pair) * PAIR, PAIR), PAIR)

        first = True
        for stream, members, place in query_blocks(image, text):
            cut = slice(0, image) if stream == 0 else slice(image, tokens)
            size = image if stream == 0 else text
            query = jnp.concatenate([q[m, 0, cut] for m in members], 0)
            query = query * jnp.asarray(FACTOR, BF16)
            grad = jnp.concatenate([grads[m, 0, cut] for m in members], 0)
            output = jnp.concatenate([mixed[m, 0, cut] for m in members], 0)
            inner = jnp.transpose(grad.astype(F32) * output.astype(F32))
            query_grad = None
            for head in range(2):
                head_q, head_g = query * low[head], grad * low[head]
                half = slice(head * HEAD_DIM, (head + 1) * HEAD_DIM)
                delta = jnp.sum(inner[half], 0, keepdims=True)
                log = logs[0, 0, head : head + 1, pl.ds(place, size * len(members))]
                for part in range(2):
                    probs = jnp.exp(mul(keys[part], head_q, DOT_NT) - log)
                    prob_grad = mul(values[part], head_g, DOT_NT)
                    score_grad = (probs * (prob_grad - delta)).astype(BF16)
                    value_part = mul(probs.astype(BF16), head_g, DOT_NN)
                    key_part = mul(score_grad, head_q, DOT_NN)
                    query_part = mul(score_grad, keys[part] * low[head], DOT_TN)
                    query_grad = query_part if query_grad is None else query_grad + query_part
                    if first:
                        value_sums[part][...] = value_part
                        key_sums[part][...] = key_part
                    else:
                        value_sums[part][...] += value_part
                        key_sums[part][...] += key_part
                first = False
            query_grad = query_grad * FACTOR
            for i, m in enumerate(members):
                out[m, 0, cut, lanes(0)] = query_grad[i * size : (i + 1) * size].astype(BF16)
        for which, sums in ((1, key_sums), (2, value_sums)):
            for m in range(4):
                out[m, 0, :image, lanes(which)] = sums[0][
                    m * image : (m + 1) * image
                ].astype(BF16)
                out[m, 0, image:, lanes(which)] = sums[1][m * text : (m + 1) * text].astype(BF16)

    def spec(which):
        return pl.BlockSpec((4, 1, tokens, PAIR), lambda p: (0, slot, 0, which * pairs + p))

    before = [] if earlier is None else [earlier]
    return kernel_call(
        kernel,
        "attend_back",
        29,
        (pairs,),
        [
            spec(0),
            spec(1),
            spec(2),
            spec(0),
            spec(0),
            pl.BlockSpec((1, 1, 2, 4 * tokens), lambda p: (slot, p, 0, 0)),
        ]
        + [pl.BlockSpec(memory_space=pl.ANY)] * len(before),
        pl.BlockSpec((4, 1, tokens, width), lambda p: (0, slot, 0, 0)),
        jax.ShapeDtypeStruct(qkv.shape, BF16),
        scratch=[pltpu.VMEM((4 * image, PAIR), F32), pltpu.VMEM((4 * text, PAIR), F32)] * 2,
        input_output_aliases={6: 0} if before else {},
    )(qkv, qkv, qkv, mixed, grads, logs, *before)


def normalize(values):
    average = jnp.mean(values, -1, keepdims=True)
    centred = values - average
    spread = jnp.mean(centred * centred, -1, keepdims=True)
    inverse = lax.rsqrt(spread + EPSILON)
    return centred * inverse, inverse


def norm_back(grad, normed, inverse, scale):
    scaled = grad * (1.0 + scale)
    return inverse * (
        scaled
        - jnp.mean(scaled, -1, keepdims=True)
        - normed * jnp.mean(scaled * normed, -1, keepdims=True)
    )


def add_up(values):
    return jnp.sum(values, 0, keepdims=True)


def per_slot(function, name, seqs, ins, outs):
    slots = ins[0].shape[0]

    def spec(shape, whole):
        rest = (0,) * (len(shape) - 1)
        if whole:
            return pl.BlockSpec(shape, lambda c, seqs: (0,) + rest)
        return pl.BlockSpec((1,) + tuple(shape[1:]), lambda c, seqs: (c,) + rest)

    def kernel(seqs, *refs):
        function((pl.program_id(0) < seqs[0]).astype(F32), *refs)

    return kernel_call(
        kernel,
        name,
        6,
        (slots,),
        [spec(value.shape, value.ndim == 2) for value in ins],
        [spec(shape, False) for shape, _ in outs],
        [jax.ShapeDtypeStruct(shape, dtype) for shape, dtype in outs],
        scalars=1,
    )(seqs, *ins)


def enter(live, image, text, image_cot, text_cot, vecs, first, mlp_round, sums):
    cut = image.shape[1]
    for s, (tokens, cot, rows) in enumerate(
        ((image, image_cot, slice(0, cut)), (text, text_cot, slice(cut, None)))
    ):
        normed, _ = normalize(tokens[0].astype(F32))
        first[0, rows] = (normed * (1.0 + vecs[0, s, 1:2]) + vecs[0, s, 0:1]).astype(BF16)
        rounded = (cot[0].astype(F32) * live * vecs[0, s, 5:6]).astype(BF16)
        mlp_round[0, rows] = rounded
        sums[0, s : s + 1] = add_up(rounded.astype(F32))


def middle(live, image, text, own, beside, across, vecs, bias, after, branch, second):
    cut = image.shape[1]
    for s, (tokens, rows) in enumerate(((image, slice(0, cut)), (text, slice(cut, None)))):
        value = own[0, rows].astype(F32) + beside[0, rows].astype(F32)
        value = value + across[0, rows].astype(F32) + bias[s : s + 1]
        result = tokens[0].astype(F32) + vecs[0, s, 2:3] * value
        normed, _ = normalize(result)
        branch[0, rows] = value
        after[0, rows] = result
        second[0, rows] = (normed * (1.0 + vecs[0, s, 4:5]) + vecs[0, s, 3:4]).astype(BF16)


def middle_back(
    live, image_cot, text_cot, own, beside, across, vecs, after, branch, residual, rounded, sums
):
    cut = image_cot.shape[1]
    for s, (cot, rows) in enumerate(((image_cot, slice(0, cut)), (text_cot, slice(cut, None)))):
        grad = own[0, rows].astype(F32) + beside[0, rows].astype(F32)
        grad = grad + across[0, rows].astype(F32)
        normed, inverse = normalize(after[0, rows])
        value = cot[0].astype(F32) * live + norm_back(grad, normed, inverse, vecs[0, s, 4:5])
        residual[0, rows] = value
        low = (value * vecs[0, s, 2:3]).astype(BF16)
        rounded[0, rows] = low
        sums[0, s, 0:1] = add_up(value * branch[0, rows])
        sums[0, s, 1:2] = add_up(grad)
        sums[0, s, 2:3] = add_up(grad * normed)
        sums[0, s, 3:4] = add_up(low.astype(F32))


def leave(
    live, image_cot, text_cot, own, beside, across, vecs, after, bias, image_out, text_out, sums
):
    cut = image_cot.shape[1]
    for s, (cot, rows, out) in enumerate(
        ((image_cot, slice(0, cut), image_out), (text_cot, slice(cut, None), text_out))
    ):
        value = own[0, rows].astype(F32) + beside[0, rows].astype(F32)
        value = value + across[0, rows].astype(F32) + bias[s : s + 1]
        out[0] = ((after[0, rows] + vecs[0, s, 5:6] * value) * live).astype(BF16)
        sums[0, s : s + 1] = add_up(cot[0].astype(F32) * live * value)


def enter_back(
    live, image, text, own, beside, across, vecs, residual, image_grad, text_grad, sums
):
    cut = image.shape[1]
    for s, (tokens, rows, out) in enumerate(
        ((image, slice(0, cut), image_grad), (text, slice(cut, None), text_grad))
    ):
        grad = own[0, rows].astype(F32) + beside[0, rows].astype(F32)
        grad = grad + across[0, rows].astype(F32)
        normed, inverse = normalize(tokens[0].astype(F32))
        out[0] = residual[0, rows] + norm_back(grad, normed, inverse, vecs[0, s, 1:2])
        sums[0, s, 0:1] = add_up(grad)
        sums[0, s, 1:2] = add_up(grad * normed)


def bias_spec(block):
    return pl.BlockSpec((2, block), lambda j: (0, j))


def add_bias(stream, spot, cut, sums, bias):
    return [sums + bias[stream : stream + 1]]


def gelu_both(stream, spot, cut, sums, bias):
    value = sums + bias[stream : stream + 1]
    factor = math.sqrt(2.0 / math.pi)
    square = value * value
    bend = jnp.tanh(factor * (value + 0.044715 * value * square))
    half = 0.5 * (1.0 + bend)
    slope = half + 0.5 * value * (1.0 - bend * bend) * factor * (1.0 + 0.134145 * square)
    return [value * half, slope]


def times_slope(stream, spot, cut, sums, slope):
    return [sums * slope[spot[0], spot[1], cut].astype(F32)]


def dot(spec, a, b):
    return jnp.einsum(spec, a, b, preferred_element_type=F32)


def on_device(
    groups,
    image_tokens,
    text_tokens,
    conditioning,
    group_seqs,
    ada_weight,
    ada_bias,
    qkv_weight,
    qv_bias,
    proj_weight,
    proj_bias,
    fc1_weight,
    fc1_bias,
    fc2_weight,
    fc2_bias,
    image_cot,
    text_cot,
):
    column = lax.axis_index("tensor")
    group = lax.axis_index("dp")
    ring = Ring(groups)
    order = Order(group_seqs)
    slots, image, width = image_tokens.shape
    text = text_tokens.shape[1]
    tokens = image + text
    rows = qkv_weight.shape[2]
    col_width = qkv_weight.shape[-1]
    hidden = fc1_weight.shape[-1]
    both = range(2)

    proj_turned = jnp.swapaxes(proj_weight, 1, 2)[:, None]
    fc1_shard = fc1_weight[:, None]
    fc2_turned = jnp.swapaxes(fc2_weight, 1, 2)[:, None]

    ada_part = lax.dynamic_slice_in_dim(ada_bias.astype(F32), column * col_width, col_width, 2)
    qv_part = lax.dynamic_slice_in_dim(qv_bias.astype(F32), column * col_width, col_width, 2)
    fc1_part = lax.dynamic_slice_in_dim(fc1_bias.astype(F32), column * hidden, hidden, 1)
    offsets = jnp.stack([qv_part[:, 0], jnp.zeros_like(qv_part[:, 0]), qv_part[:, 1]], 1)
    offsets = offsets.reshape(2, 3 * col_width)
    proj_add = proj_bias.astype(F32)
    fc2_add = fc2_bias.astype(F32)

    cond_act, silu_back = jax.vjp(jax.nn.silu, conditioning.astype(F32))
    cond_low = cond_act.astype(BF16).reshape(slots, groups, rows)
    cond_sends = jnp.stack(
        [
            lax.dynamic_index_in_dim(cond_low, group ^ mask, 1, keepdims=False)
            for mask in range(groups)
        ]
    )
    cond_rows = order(exchange(cond_sends, "dp", groups)).reshape(groups * slots, rows)
    modul_parts = order(dot("cd,sjdn->csjn", cond_rows, ada_weight))
    modul_parts = modul_parts.reshape((groups, slots) + modul_parts.shape[1:])
    modul_local = order(collect(modul_parts, "dp", groups) + ada_part[None])
    qkv_ring = Gather(ring, order(jnp.concatenate([qkv_weight, proj_turned], 1)))
    qkv_part = (0, 3 * col_width)
    proj_part = (3 * col_width, col_width)
    vecs = order(lax.all_gather(modul_local, "tensor", axis=3, tiled=True))

    first, mlp_round, fc2_bias_local = order.run(
        lambda *a: per_slot(
            enter,
            "enter",
            group_seqs,
            a,
            [
                ((slots, tokens, width), BF16),
                ((slots, tokens, width), BF16),
                ((slots, 2, width), F32),
            ],
        ),
        image_tokens,
        text_tokens,
        image_cot,
        text_cot,
        vecs,
    )
    qkv_ring.arrive(order)
    first_move = Spread(order(first))
    qkv_ring.arrive(order)
    qkv_ring.arrive(order)
    first_move.arrive(order)
    first_full = first_move.finish(order)
    qkv_ring.arrive(order)
    fc1_ring = Gather(ring, order(fc1_shard))
    mlp_move = Spread(order(mlp_round))
    qkv_full = order(*qkv_ring.finish(order))

    qkv = order.run(
        lambda *a: rows_times(
            a[:4], a[4:], image, False, 1, add_bias, (offsets,), (bias_spec,), qkv_part
        ),
        *first_full,
        *qkv_full,
    )
    fc1_ring.arrive(order)
    mixed = ()
    for slot in range(slots):
        mixed = order.run(
            lambda *a, slot=slot: attend(a[0], image, slot, a[1:]), *((qkv,) + tuple(mixed))
        )
    mixed, logs = mixed
    fc1_ring.arrive(order)
    mlp_move.arrive(order)
    branch_parts = order.run(
        lambda *a: rows_times(a[0], a[1:], image, True, "split", columns=proj_part),
        mixed,
        *qkv_full,
    )
    branch_move = Collect(*order(*branch_parts))
    mlp_full = mlp_move.finish(order)
    branch_move.arrive(order)
    fc1_ring.arrive(order)
    fc1_ring.arrive(order)
    fc2_ring = Gather(ring, order(fc2_turned))
    branch_terms = branch_move.finish(order)
    after, branch, second = order.run(
        lambda *a: per_slot(
            middle,
            "middle",
            group_seqs,
            a,
            [
                ((slots, tokens, width), F32),
                ((slots, tokens, width), F32),
                ((slots, tokens, width), BF16),
            ],
        ),
        image_tokens,
        text_tokens,
        *branch_terms,
        vecs,
        proj_add,
    )
    second_move = Spread(second)
    fc1_full = order(*fc1_ring.finish(order))
    fc2_ring.arrive(order)
    fc2_ring.arrive(order)
    second_move.arrive(order)
    second_full = second_move.finish(order)
    activated, slope = order.run(
        lambda *a: rows_times(
            a[:4], a[4:], image, False, 2, gelu_both, (fc1_part,), (bias_spec,)
        ),
        *second_full,
        *fc1_full,
    )
    fc2_ring.arrive(order)
    *fc2_grad, _ = order.run(
        lambda *a: weight_grad(a[:4], a[4], image, groups), *mlp_full, activated
    )
    fc2_ring.arrive(order)
    fc2_sums = Scatter(ring, *order(*fc2_grad), "turned")
    fc2_full = order(*fc2_ring.finish(order))
    pre_round = order.run(
        lambda *a: rows_times(
            a[:4],
            a[4:],
            image,
            False,
            1,
            times_slope,
            (slope,),
            (
                lambda block: pl.BlockSpec(
                    (4, slots, tokens, block), lambda j: (0, 0, 0, j)
                ),
            ),
        ),
        *mlp_full,
        *fc2_full,
    )
    fc2_sums.arrive(order)
    second_parts = order.run(
        lambda *a: rows_times(a[0], a[1:], image, True, "split"), pre_round, *fc1_full
    )
    second_back = Collect(*second_parts)
    second_back.arrive(order)
    *fc1_grad, fc1_bias_local = order.run(
        lambda *a: weight_grad(a[:4], a[4], image, groups), *second_full, pre_round
    )
    fc1_sums = Scatter(ring, *order(*fc1_grad))
    mlp_parts = order.run(
        lambda *a: rows_times(a[0], a[1:], image, True, "split"), activated, *fc2_full
    )
    fc2_sums.arrive(order)
    second_terms = second_back.finish(order)
    residual, branch_round, middle_vecs = order.run(
        lambda *a: per_slot(
            middle_back,
            "middle_back",
            group_seqs,
            a,
            [
                ((slots, tokens, width), F32),
                ((slots, tokens, width), BF16),
                ((slots, 2, 4, width), F32),
            ],
        ),
        image_cot,
        text_cot,
        *second_terms,
        vecs,
        after,
        branch,
    )
    branch_back = Spread(branch_round)
    fc2_sums.arrive(order)
    fc1_sums.arrive(order)
    branch_back.arrive(order)
    branch_full = branch_back.finish(order)
    mixed_grad = order.run(
        lambda *a: rows_times(a[:4], a[4:], image, False, 1, columns=proj_part),
        *branch_full,
        *qkv_full,
    )
    mlp_back = Collect(*order(*mlp_parts))
    mlp_back.arrive(order)
    *proj_grad, _ = order.run(
        lambda *a: weight_grad(a[:4], a[4], image, groups, 3 * col_width, 4 * col_width),
        *branch_full,
        mixed,
    )
    qkv_grads = None
    for slot in range(slots):
        given = (qkv, mixed, mixed_grad, logs) + (() if slot == 0 else (qkv_grads,))
        qkv_grads = order.run(
            lambda *a, slot=slot: attend_back(
                *a[:4], image, slot, a[4] if len(a) > 4 else None
            ),
            *given,
        )
        if slot == 0:
            fc2_sums.arrive(order)
            fc1_sums.arrive(order)
    mlp_terms = mlp_back.finish(order)
    fc1_sums.arrive(order)
    *qkv_grad, qv_sums = order.run(
        lambda *a: weight_grad(
            a[:4], a[4], image, groups, 0, 4 * col_width, a[5:]
        ),
        *first_full,
        qkv_grads,
        *proj_grad,
    )
    fc1_sums.arrive(order)
    qkv_sums = Scatter(ring, *order(*qkv_grad), "parts")
    first_parts = order.run(
        lambda *a: rows_times(a[0], a[1:], image, True, "split", columns=qkv_part),
        qkv_grads,
        *qkv_full,
    )
    qkv_sums.arrive(order)
    first_back = Collect(*order(*first_parts))
    first_back.arrive(order)
    qv_bias_local = qv_sums.reshape(2, 3, col_width)[:, 0::2]
    proj_bias_local = jnp.sum(middle_vecs[:, :, 3], 0)
    fc2_bias_local = jnp.sum(fc2_bias_local, 0)
    split_sums = jnp.concatenate([qv_bias_local.reshape(-1), fc1_bias_local.reshape(-1)])
    token_sums = jnp.concatenate([proj_bias_local.reshape(-1), fc2_bias_local.reshape(-1)])
    bias_local = jnp.concatenate([split_sums, token_sums])
    image_out, text_out, gate_two = order.run(
        lambda *a: per_slot(
            leave,
            "leave",
            group_seqs,
            a,
            [
                (image_tokens.shape, BF16),
                (text_tokens.shape, BF16),
                ((slots, 2, width), F32),
            ],
        ),
        image_cot,
        text_cot,
        *mlp_terms,
        vecs,
        after,
        fc2_add,
    )
    qkv_sums.arrive(order)
    first_terms = first_back.finish(order)
    image_grad, text_grad, enter_vecs = order.run(
        lambda *a: per_slot(
            enter_back,
            "enter_back",
            group_seqs,
            a,
            [
                (image_tokens.shape, F32),
                (text_tokens.shape, F32),
                ((slots, 2, 2, width), F32),
            ],
        ),
        image_tokens,
        text_tokens,
        *first_terms,
        vecs,
        residual,
    )
    modul_grad = jnp.concatenate(
        [
            enter_vecs,
            middle_vecs[:, :, 0:3],
            gate_two[:, :, None],
        ],
        2,
    ).reshape(slots, 2, 6, 4, col_width)
    modul_blocks = jnp.stack(
        [
            lax.dynamic_index_in_dim(modul_grad, column ^ mask, 3, keepdims=False)
            for mask in range(4)
        ]
    )
    modul_round = order(collect(modul_blocks, "tensor", 4).astype(BF16))
    qkv_sums.arrive(order)
    shared = jnp.concatenate([modul_round.astype(F32).reshape(-1), bias_local])
    shared = order(spread(order(shared), "dp", groups))
    modul_all = shared[:, : modul_round.size].astype(BF16)
    modul_all = modul_all.reshape((groups * slots,) + modul_round.shape[1:])
    bias_local = jnp.sum(shared[:, modul_round.size :], 0)
    cond_part = dot("csjn,sjdn->cd", modul_all, ada_weight)
    ada_bias_part = jnp.sum(modul_all.astype(F32), 0)
    last = jnp.concatenate([cond_part.reshape(-1), ada_bias_part.reshape(-1), bias_local])
    last = order(spread(order(last), "tensor", 4))
    cond_part = jnp.sum(last[:, : cond_part.size], 0).reshape(groups, slots, rows)
    cond_terms = order(exchange(cond_part, "dp", groups))
    cond_term = jnp.stack(
        [
            lax.dynamic_index_in_dim(cond_terms, group ^ place, 0, keepdims=False)
            for place in range(groups)
        ],
        1,
    ).reshape(slots, width)
    cond_grad = lax.dynamic_slice_in_dim(
        silu_back(cond_term)[0], column * col_width, col_width, 1
    )
    last = jnp.stack(
        [
            lax.dynamic_index_in_dim(last[:, cond_part.size :], column ^ place, 0, keepdims=False)
            for place in range(4)
        ]
    )
    ada_bias_grad = by_column(last[:, : ada_bias_part.size], ada_bias_part.shape)
    bias_all = last[:, ada_bias_part.size :]
    cut_a = qv_bias_local.size
    cut_b = cut_a + fc1_bias_local.size
    cut_c = cut_b + proj_bias_local.size
    cut_d = cut_c + fc2_bias_local.size

    qv_bias_grad = by_column(bias_all[:, :cut_a], qv_bias_local.shape)
    fc1_bias_grad = by_column(bias_all[:, cut_a:cut_b], fc1_bias_local.shape)
    proj_bias_grad = jnp.sum(bias_all[:, cut_b:cut_c], 0).reshape(proj_bias_local.shape)
    fc2_bias_grad = jnp.sum(bias_all[:, cut_c:cut_d], 0).reshape(fc2_bias_local.shape)
    ada_grad = dot("cd,csjn->sjdn", cond_rows, modul_all)
    fc2_sum, fc1_sum = fc2_sums.finish(order), fc1_sums.finish(order)
    qkv_sum, proj_sum = qkv_sums.finish(order)
    cond_grad = order(cond_grad)
    live = jnp.arange(slots, dtype=jnp.int32) < order.token[0]
    cond_grad = jnp.where(live[:, None], cond_grad, 0.0)
    return (
        image_out,
        text_out,
        image_grad,
        text_grad,
        cond_grad,
        ada_grad,
        ada_bias_grad,
        qkv_sum,
        qv_bias_grad,
        proj_sum,
        proj_bias_grad,
        fc1_sum,
        fc1_bias_grad,
        fc2_sum,
        fc2_bias_grad,
    )


def solution(mesh):
    groups = mesh.shape["dp"]
    in_specs = (
        P("dp", "tensor", None),
        P("dp", "tensor", None),
        P("dp", None),
        P("dp"),
        P(None, None, "dp", "tensor"),
        P(),
        P(None, None, "dp", "tensor"),
        P(),
        P(None, "tensor", "dp"),
        P(),
        P(None, "dp", "tensor"),
        P(),
        P(None, "tensor", "dp"),
        P(),
        P("dp", "tensor", None),
        P("dp", "tensor", None),
    )
    out_specs = (
        P("dp", "tensor", None),
        P("dp", "tensor", None),
        P("dp", "tensor", None),
        P("dp", "tensor", None),
        P("dp", "tensor"),
        P(None, None, "dp", "tensor"),
        P(),
        P(None, None, "dp", "tensor"),
        P(),
        P(None, "tensor", "dp"),
        P(),
        P(None, "dp", "tensor"),
        P(),
        P(None, "tensor", "dp"),
        P(),
    )

    def step(*args):
        return on_device(groups, *args)

    return jax.shard_map(
        step, mesh=mesh, in_specs=in_specs, out_specs=out_specs, check_vma=False
    )
```

```python
import math

import jax
import jax.numpy as jnp
from jax import lax
from jax.experimental import pallas as pl
from jax.experimental.pallas import tpu as pltpu
from jax.sharding import PartitionSpec as P

HEAD_DIM = 64
PAIR = 2 * HEAD_DIM
FACTOR = 1.0 / math.sqrt(HEAD_DIM)
VMEM = 60 << 20
FLOPS_PER_US = 460000000
EPSILON = 1e-06
F32 = jnp.float32
BF16 = jnp.bfloat16


def hop(value, axis, mask, size):
    return lax.ppermute(value, axis, [(i, i ^ mask) for i in range(size)])


def halves(size):
    low = 1
    while low * low < size:
        low *= 2
    return low, size // low


def spread(value, axis, size):
    low, high = halves(size)
    held = jnp.stack(
        [value] + [hop(value, axis, low * step, size) for step in range(1, high)]
    )
    full = [held] + [hop(held, axis, mask, size) for mask in range(1, low)]
    return jnp.stack(full, 1).reshape((size,) + value.shape)


def exchange(blocks, axis, size):
    low, high = halves(size)
    blocks = blocks.reshape((high, low) + blocks.shape[1:])
    held = jnp.stack(
        [blocks[0]] + [hop(blocks[step], axis, low * step, size) for step in range(1, high)]
    )
    full = [held[:, 0]] + [hop(held[:, mask], axis, mask, size) for mask in range(1, low)]
    return jnp.stack(full, 1).reshape((size,) + blocks.shape[2:])


def collect(blocks, axis, size):
    low, high = halves(size)
    blocks = blocks.reshape((high, low) + blocks.shape[1:])
    held = blocks[0] + sum(
        hop(blocks[step], axis, low * step, size) for step in range(1, high)
    )
    return held[0] + sum(hop(held[mask], axis, mask, size) for mask in range(1, low))


def by_column(block, shape):
    return jnp.moveaxis(block.reshape((4,) + shape), 0, -2).reshape(
        shape[:-1] + (4 * shape[-1],)
    )


class Order:
    def __init__(self, seed):
        self.token = seed

    def __call__(self, *values):
        self.token, *values = lax.optimization_barrier((self.token, *values))
        return values[0] if len(values) == 1 else values

    def run(self, function, *values):
        results = function(*self(*values)) if len(values) > 1 else function(self(*values))
        return self(*results) if isinstance(results, (tuple, list)) else self(results)


class Ring:
    def __init__(self, size):
        self.size = size
        self.order = list(range(0, size, 2)) + list(range(size - 1, 0, -2))
        self.ahead = [(self.order[i], self.order[(i + 1) % size]) for i in range(size)]
        self.back = [(b, a) for a, b in self.ahead]
        place = [0] * size
        for position, device in enumerate(self.order):
            place[device] = position
        self.mine = jnp.asarray(place, jnp.int32)[lax.axis_index("dp")]
        self.table = jnp.asarray(self.order, jnp.int32)

    def devices(self, distances):
        return self.table[(self.mine + jnp.asarray(distances, jnp.int32)) % self.size]

    def forward(self, value):
        return lax.ppermute(value, "dp", self.ahead)

    def backward(self, value):
        return lax.ppermute(value, "dp", self.back)


class Gather:
    def __init__(self, ring, shard):
        self.ring, self.step = ring, 0
        self.pieces, self.distances, self.streams = [shard], [0], [0]
        self.placed, self.full = 0, ()
        self.send(shard, shard)

    def send(self, ahead, back):
        self.step += 1
        if self.step == self.ring.size // 2:
            ahead, back = ahead[:1], back[1:]
        self.moving = (self.ring.forward(ahead), self.ring.backward(back))

    def arrive(self, order):
        ahead, back = order(*self.moving)
        last = self.step == self.ring.size // 2
        self.pieces += [ahead, back]
        self.distances += [-self.step, self.step]
        self.streams += [0, 1 if last else 0]
        if not last:
            self.send(ahead, back)
        return last

    def finish(self, order):
        while len(self.pieces) < self.ring.size + 1:
            self.arrive(order)
        self.place(order)
        return [f.reshape(-1, f.shape[2]) for f in self.full]

    def place(self, order):
        new = slice(self.placed, None)
        places = self.ring.devices(self.distances[new])
        self.full = order(
            *assemble(self.pieces[new], self.streams[new], places, self.ring.size, self.full)
        )
        self.placed = len(self.pieces)


class Scatter:
    def __init__(self, ring, image, text, form="plain"):
        self.ring, self.image, self.text, self.form = ring, image, text, form
        self.left = ring.size // 2
        far = ring.devices([self.left])[0]
        chunk = [lax.dynamic_index_in_dim(g, far, 0) for g in (image, text)]
        self.moving = (ring.forward(chunk[0]), ring.backward(chunk[1]))

    def arrive(self, order):
        ahead, back = order(*self.moving)
        self.left -= 1
        places = self.ring.devices([self.left, -self.left])
        if self.left == 0:
            self.total = ring_total(self.image, self.text, ahead, back, places, self.form)
            return True
        ahead, back = order(*ring_add(self.image, self.text, ahead, back, places))
        self.moving = (self.ring.forward(ahead), self.ring.backward(back))
        return False

    def finish(self, order):
        while self.left:
            self.arrive(order)
        return self.total


def kernel_call(kernel, name, cost_us, grid, in_specs, out_specs, out_shape, scalars=0, **more):
    return pl.pallas_call(
        kernel,
        grid_spec=pltpu.PrefetchScalarGridSpec(
            num_scalar_prefetch=scalars,
            grid=grid,
            in_specs=in_specs,
            out_specs=out_specs,
            scratch_shapes=more.pop("scratch", ()),
        ),
        out_shape=out_shape,
        compiler_params=pltpu.CompilerParams(vmem_limit_bytes=VMEM),
        cost_estimate=pl.CostEstimate(
            flops=int(cost_us * FLOPS_PER_US), bytes_accessed=1, transcendentals=0
        ),
        name=name,
        **more,
    )


def assemble(pieces, streams, places, size, earlier):
    count = len(pieces)
    parts, rows, width = pieces[0].shape[1:]
    moves = [
        (i, streams[i] + s, s, part)
        for i in range(count)
        for s in range(pieces[i].shape[0])
        for part in range(parts)
    ]

    def kernel(place, *refs):
        shards, refs = refs[:count], refs[count + len(earlier) :]
        full, held, sems_in, sems_out = refs[:2], refs[2:-2], refs[-2], refs[-1]
        ins = [pltpu.make_async_copy(shards[i], held[i], sems_in.at[i]) for i in range(count)]
        for copy in ins:
            copy.start()
        outs, last = [], -1
        for m, (i, stream, s, part) in enumerate(moves):
            if i != last:
                ins[i].wait()
                last = i
            spot = full[stream].at[place[i], :, pl.ds(part * width, width)]
            outs.append(pltpu.make_async_copy(held[i].at[s, part], spot, sems_out.at[m]))
            outs[-1].start()
        for copy in outs:
            copy.wait()

    whole = pl.BlockSpec(memory_space=pltpu.HBM)
    out = jax.ShapeDtypeStruct((size, rows, parts * width), BF16)
    return kernel_call(
        kernel,
        "assemble",
        1 + 3e-7 * sum(math.prod(p.shape) for p in pieces),
        (1,),
        [whole] * (count + len(earlier)),
        [whole] * 2,
        [out] * 2,
        scalars=1,
        scratch=[pltpu.VMEM(p.shape, p.dtype) for p in pieces]
        + [pltpu.SemaphoreType.DMA((count,)), pltpu.SemaphoreType.DMA((len(moves),))],
        input_output_aliases={count + 1: 0, count + 2: 1} if earlier else {},
    )(places, *pieces, *earlier)


def ring_specs(image, ahead, back, block):
    width = image.shape[2]

    def local(which):
        return pl.BlockSpec((1, block, width), lambda i, place: (place[which], i, 0))

    def moved(value):
        return pl.BlockSpec((value.shape[0], block, width), lambda i, place: (0, i, 0))

    return [local(0), local(0), local(1), local(1), moved(ahead), moved(back)]


def ring_add(image, text, ahead, back, places):
    size, rows, width = image.shape
    block = rows // 4 if rows % 64 == 0 else rows
    whole = ahead.shape[0] == 2

    def kernel(place, image_a, text_a, image_b, text_b, ahead, back, send_a, send_b):
        send_a[0] = (image_a[0].astype(F32) + ahead[0].astype(F32)).astype(BF16)
        send_b[1] = (text_b[0].astype(F32) + back[back.shape[0] - 1].astype(F32)).astype(BF16)
        if whole:
            send_a[1] = (text_a[0].astype(F32) + ahead[1].astype(F32)).astype(BF16)
            send_b[0] = (image_b[0].astype(F32) + back[0].astype(F32)).astype(BF16)
        else:
            send_a[1] = text_a[0]
            send_b[0] = image_b[0]

    out = pl.BlockSpec((2, block, width), lambda i, place: (0, i, 0))
    return kernel_call(
        kernel,
        "ring_add",
        1 + 7e-6 * image.shape[1] * image.shape[2] * 2,
        (rows // block,),
        ring_specs(image, ahead, back, block),
        [out] * 2,
        [jax.ShapeDtypeStruct((2, rows, width), BF16)] * 2,
        scalars=1,
    )(places, image, text, image, text, ahead, back)


def ring_total(image, text, ahead, back, places, form):
    size, rows, width = image.shape
    block = rows // 4 if rows % 64 == 0 else rows
    part = width // 4

    def kernel(place, image_a, text_a, image_b, text_b, ahead, back, total, *more):
        for s, mine in enumerate((image_a, text_a)):
            value = mine[0].astype(F32) + ahead[s].astype(F32) + back[s].astype(F32)
            if form == "parts":
                for j in range(3):
                    total[s, j] = value[:, j * part : (j + 1) * part]
                more[0][s] = value[:, 3 * part :]
            else:
                total[s] = value

    shapes = {
        "plain": [(2, rows, width)],
        "parts": [(2, 3, rows, part), (2, rows, part)],
    }[form]
    outs = [
        pl.BlockSpec(
            shape[:-2] + (block, shape[-1]),
            lambda i, place, lead=len(shape) - 2: (0,) * lead + (i, 0),
        )
        for shape in shapes
    ]
    total = kernel_call(
        kernel,
        "ring_total",
        1 + 7e-6 * image.shape[1] * image.shape[2] * 2,
        (rows // block,),
        ring_specs(image, ahead, back, block),
        outs,
        [jax.ShapeDtypeStruct(shape, F32) for shape in shapes],
        scalars=1,
    )(places, image, text, image, text, ahead, back)
    return total if form == "parts" else total[0]


class Spread:
    def __init__(self, part):
        self.part = part
        self.across = hop(part, "tensor", 2, 4)
        self.beside = hop(part, "tensor", 1, 4)

    def arrive(self, order):
        self.across, self.beside = order(self.across, self.beside)
        self.corner = hop(self.across, "tensor", 1, 4)

    def finish(self, order):
        return [self.part, self.beside, self.across, order(self.corner)]


class Collect:
    def __init__(self, own, beside, across, corner):
        self.own, self.kept = own, across
        self.corner = hop(corner, "tensor", 1, 4)
        self.beside = hop(beside, "tensor", 1, 4)

    def arrive(self, order):
        corner = order(self.corner)
        send = (self.kept.astype(F32) + corner.astype(F32)).astype(BF16)
        self.across = hop(order(send), "tensor", 2, 4)
        self.beside = order(self.beside)

    def finish(self, order):
        return [self.own, self.beside, order(self.across)]


def piece_specs(pieces, block=None):
    if isinstance(pieces, (list, tuple)):
        shape = pieces[0].shape
        spec = pl.BlockSpec(shape, lambda j: (0, 0, 0), pipeline_mode=pl.Buffered(1))
        return [spec] * 4, list(pieces), shape
    shape = pieces.shape[1:]
    specs = [
        pl.BlockSpec(
            (None,) + shape, lambda j, k=k: (k, 0, 0, 0), pipeline_mode=pl.Buffered(1)
        )
        for k in range(4)
    ]
    return specs, [pieces] * 4, shape


def column_block(width):
    for block in (512, 384, 256, 128):
        if width % block == 0:
            return block
    return width


def rows_times(
    pieces, weights, image, turned, outputs, finish=None, extras=(), extra_specs=(), columns=None
):
    specs, arrays, (slots, tokens, depth) = piece_specs(pieces)
    start, count = columns or (0, weights[0].shape[1])
    width = weights[0].shape[0] if turned else count
    block = column_block(math.gcd(start, width))
    text = tokens - image
    spots = [(k, c) for k in range(4) for c in range(slots)]
    dims = DOT_NT if turned else DOT_NN
    split = outputs == "split"
    count = 4 if split else outputs

    def kernel(*refs):
        rows, (image_w, text_w) = refs[:4], refs[4:6]
        more, outs = refs[6 : 6 + len(extras)], refs[6 + len(extras) :]

        def store(stream, spot, sums):
            k, c = spot
            cut = slice(0, image) if stream == 0 else slice(image, tokens)
            values = [sums] if finish is None else finish(stream, spot, cut, sums, *more)
            for which, value in enumerate(values):
                if split:
                    outs[k][c, cut] = value.astype(BF16)
                else:
                    outs[which][k, c, cut] = value.astype(BF16)

        for spot in spots:
            store(0, spot, mul(rows[spot[0]][spot[1], :image], image_w[...], dims))
        joined = jnp.concatenate([rows[k][c, image:] for k, c in spots], 0)
        sums = mul(joined, text_w[...], dims)
        for i, spot in enumerate(spots):
            store(1, spot, sums[i * text : (i + 1) * text])

    if turned:
        weight = pl.BlockSpec((block, depth), lambda j: (j, start // depth))
    else:
        weight = pl.BlockSpec((depth, block), lambda j: (0, start // block + j))
    if split:
        out = pl.BlockSpec((slots, tokens, block), lambda j: (0, 0, j))
        shape = jax.ShapeDtypeStruct((slots, tokens, width), BF16)
    else:
        out = pl.BlockSpec((4, slots, tokens, block), lambda j: (0, 0, 0, j))
        shape = jax.ShapeDtypeStruct((4, slots, tokens, width), BF16)
    return kernel_call(
        kernel,
        "rows_times",
        1 + 3e-9 * 4 * slots * tokens * depth * width,
        (width // block,),
        specs + [weight, weight] + [make(block) for make in extra_specs],
        [out] * count,
        [shape] * count,
    )(*arrays, *weights, *extras)


def weight_grad(pieces, grads, image, size, first=0, total=None, earlier=()):
    specs, arrays, (slots, tokens, depth) = piece_specs(pieces)
    width = grads.shape[3]
    block = column_block(math.gcd(first, width))
    text = tokens - image
    spots = [(k, c) for k in range(4) for c in range(slots)]

    def kernel(a, b, c, d, grad, *refs):
        rows = (a, b, c, d)
        image_out, text_out, sums, image_turned, text_turned = refs[-5:]

        @pl.when(pl.program_id(0) == 0)
        def _():
            for i, (k, s) in enumerate(spots):
                image_turned[:, pl.ds(i * image, image)] = jnp.transpose(rows[k][s, :image])
            text_turned[...] = jnp.transpose(
                jnp.concatenate([rows[k][s, image:] for k, s in spots], 0)
            )

        image_grads = jnp.concatenate([grad[k, s, :image] for k, s in spots], 0)
        text_grads = jnp.concatenate([grad[k, s, image:] for k, s in spots], 0)
        image_out[...] = (
            mul(image_turned[...], image_grads, DOT_NN).astype(BF16).reshape(image_out.shape)
        )
        text_out[...] = (
            mul(text_turned[...], text_grads, DOT_NN).astype(BF16).reshape(text_out.shape)
        )
        sums[0:1] = jnp.sum(image_grads.astype(F32), 0, keepdims=True)
        sums[1:2] = jnp.sum(text_grads.astype(F32), 0, keepdims=True)

    out = pl.BlockSpec((size, depth // size, block), lambda j: (0, 0, first // block + j))
    shape = jax.ShapeDtypeStruct((size, depth // size, total or width), BF16)
    return kernel_call(
        kernel,
        "weight_grad",
        1 + 3.4e-9 * 4 * slots * tokens * depth * width,
        (width // block,),
        specs
        + [pl.BlockSpec((4, slots, tokens, block), lambda j: (0, 0, 0, j))]
        + [pl.BlockSpec(memory_space=pl.ANY)] * len(earlier),
        [out, out, pl.BlockSpec((2, block), lambda j: (0, j))],
        [shape, shape, jax.ShapeDtypeStruct((2, width), F32)],
        scratch=[
            pltpu.VMEM((depth, len(spots) * image), BF16),
            pltpu.VMEM((depth, len(spots) * text), BF16),
        ],
        input_output_aliases={5: 0, 6: 1} if earlier else {},
    )(*arrays, grads, *earlier)


def mul(a, b, dims):
    return lax.dot_general(a, b, dims, preferred_element_type=F32)


DOT_NN = (((1,), (0,)), ((), ()))
DOT_NT = (((1,), (1,)), ((), ()))
DOT_TN = (((0,), (0,)), ((), ()))


def lane_masks(dtype):
    lane = lax.broadcasted_iota(jnp.int32, (1, PAIR), 1)
    low = (lane < HEAD_DIM).astype(F32)
    return [low.astype(dtype), (1.0 - low).astype(dtype)]


def stream_rows(ref, image, stream):
    cut = slice(0, image) if stream == 0 else slice(image, ref.shape[2])
    return jnp.concatenate([ref[k, 0, cut] for k in range(4)], 0)


def query_blocks(image, text):
    return [(0, (0, 1), 0), (0, (2, 3), 2 * image), (1, (0, 1, 2, 3), 4 * image)]


def attend(qkv, image, slot, earlier):
    _, slots, tokens, width = qkv.shape
    text, pairs = tokens - image, width // (3 * PAIR)

    def kernel(q, k, v, *refs):
        out, logs_out = refs[-2:]
        keys = [stream_rows(k, image, s) for s in range(2)]
        values = [stream_rows(v, image, s) for s in range(2)]
        masks = lane_masks(F32)
        low = [m.astype(BF16) for m in masks]
        for stream, members, place in query_blocks(image, text):
            cut = slice(0, image) if stream == 0 else slice(image, tokens)
            size = image if stream == 0 else text
            query = jnp.concatenate([q[m, 0, cut] for m in members], 0)
            query = query * jnp.asarray(FACTOR, BF16)
            total = logs = None
            for head in range(2):
                scores = [mul(query * low[head], key, DOT_NT) for key in keys]
                top = jnp.maximum(
                    jnp.max(scores[0], -1, keepdims=True), jnp.max(scores[1], -1, keepdims=True)
                )
                probs = [jnp.exp(s - top) for s in scores]
                denom = jnp.sum(probs[0], -1, keepdims=True) + jnp.sum(
                    probs[1], -1, keepdims=True
                )
                mixed = mul(probs[0].astype(BF16), values[0], DOT_NN) + mul(
                    probs[1].astype(BF16), values[1], DOT_NN
                )
                mixed = mixed * (masks[head] / denom)
                log = (top + jnp.log(denom)) * masks[head]
                total = mixed if total is None else total + mixed
                logs = log if logs is None else logs + log
            for i, m in enumerate(members):
                out[m, 0, cut] = total[i * size : (i + 1) * size].astype(BF16)
            turned = jnp.transpose(logs)
            span = pl.ds(place, size * len(members))
            logs_out[0, 0, 0:1, span] = turned[0:1]
            logs_out[0, 0, 1:2, span] = turned[HEAD_DIM : HEAD_DIM + 1]

    def spec(which):
        return pl.BlockSpec((4, 1, tokens, PAIR), lambda p: (0, slot, 0, which * pairs + p))

    total = 4 * tokens
    return kernel_call(
        kernel,
        "attend",
        15,
        (pairs,),
        [spec(0), spec(1), spec(2)] + [pl.BlockSpec(memory_space=pl.ANY)] * len(earlier),
        [spec(0), pl.BlockSpec((1, 1, 2, total), lambda p: (slot, p, 0, 0))],
        [
            jax.ShapeDtypeStruct((4, slots, tokens, pairs * PAIR), BF16),
            jax.ShapeDtypeStruct((slots, pairs, 2, total), F32),
        ],
        input_output_aliases={3: 0, 4: 1} if earlier else {},
    )(qkv, qkv, qkv, *earlier)


def attend_back(qkv, mixed, grads, logs, image, slot, earlier):
    _, slots, tokens, width = qkv.shape
    text, pairs = tokens - image, width // (3 * PAIR)

    def kernel(q, k, v, mixed, grads, logs, *refs):
        out, key_image, key_text, value_image, value_text = refs[-5:]
        key_sums, value_sums = (key_image, key_text), (value_image, value_text)
        keys = [stream_rows(k, image, s) for s in range(2)]
        values = [stream_rows(v, image, s) for s in range(2)]
        low = lane_masks(BF16)
        pair = pl.program_id(0)

        def lanes(which):
            return pl.ds(pl.multiple_of((which * pairs + pair) * PAIR, PAIR), PAIR)

        first = True
        for stream, members, place in query_blocks(image, text):
            cut = slice(0, image) if stream == 0 else slice(image, tokens)
            size = image if stream == 0 else text
            query = jnp.concatenate([q[m, 0, cut] for m in members], 0)
            query = query * jnp.asarray(FACTOR, BF16)
            grad = jnp.concatenate([grads[m, 0, cut] for m in members], 0)
            output = jnp.concatenate([mixed[m, 0, cut] for m in members], 0)
            inner = jnp.transpose(grad.astype(F32) * output.astype(F32))
            query_grad = None
            for head in range(2):
                head_q, head_g = query * low[head], grad * low[head]
                half = slice(head * HEAD_DIM, (head + 1) * HEAD_DIM)
                delta = jnp.sum(inner[half], 0, keepdims=True)
                log = logs[0, 0, head : head + 1, pl.ds(place, size * len(members))]
                for part in range(2):
                    probs = jnp.exp(mul(keys[part], head_q, DOT_NT) - log)
                    prob_grad = mul(values[part], head_g, DOT_NT)
                    score_grad = (probs * (prob_grad - delta)).astype(BF16)
                    value_part = mul(probs.astype(BF16), head_g, DOT_NN)
                    key_part = mul(score_grad, head_q, DOT_NN)
                    query_part = mul(score_grad, keys[part] * low[head], DOT_TN)
                    query_grad = query_part if query_grad is None else query_grad + query_part
                    if first:
                        value_sums[part][...] = value_part
                        key_sums[part][...] = key_part
                    else:
                        value_sums[part][...] += value_part
                        key_sums[part][...] += key_part
                first = False
            query_grad = query_grad * FACTOR
            for i, m in enumerate(members):
                out[m, 0, cut, lanes(0)] = query_grad[i * size : (i + 1) * size].astype(BF16)
        for which, sums in ((1, key_sums), (2, value_sums)):
            for m in range(4):
                out[m, 0, :image, lanes(which)] = sums[0][
                    m * image : (m + 1) * image
                ].astype(BF16)
                out[m, 0, image:, lanes(which)] = sums[1][m * text : (m + 1) * text].astype(BF16)

    def spec(which):
        return pl.BlockSpec((4, 1, tokens, PAIR), lambda p: (0, slot, 0, which * pairs + p))

    before = [] if earlier is None else [earlier]
    return kernel_call(
        kernel,
        "attend_back",
        29,
        (pairs,),
        [
            spec(0),
            spec(1),
            spec(2),
            spec(0),
            spec(0),
            pl.BlockSpec((1, 1, 2, 4 * tokens), lambda p: (slot, p, 0, 0)),
        ]
        + [pl.BlockSpec(memory_space=pl.ANY)] * len(before),
        pl.BlockSpec((4, 1, tokens, width), lambda p: (0, slot, 0, 0)),
        jax.ShapeDtypeStruct(qkv.shape, BF16),
        scratch=[pltpu.VMEM((4 * image, PAIR), F32), pltpu.VMEM((4 * text, PAIR), F32)] * 2,
        input_output_aliases={6: 0} if before else {},
    )(qkv, qkv, qkv, mixed, grads, logs, *before)


def normalize(values):
    average = jnp.mean(values, -1, keepdims=True)
    centred = values - average
    spread = jnp.mean(centred * centred, -1, keepdims=True)
    inverse = lax.rsqrt(spread + EPSILON)
    return centred * inverse, inverse


def norm_back(grad, normed, inverse, scale):
    scaled = grad * (1.0 + scale)
    return inverse * (
        scaled
        - jnp.mean(scaled, -1, keepdims=True)
        - normed * jnp.mean(scaled * normed, -1, keepdims=True)
    )


def add_up(values):
    return jnp.sum(values, 0, keepdims=True)


def per_slot(function, name, seqs, ins, outs):
    slots = ins[0].shape[0]

    def spec(shape, whole):
        rest = (0,) * (len(shape) - 1)
        if whole:
            return pl.BlockSpec(shape, lambda c, seqs: (0,) + rest)
        return pl.BlockSpec((1,) + tuple(shape[1:]), lambda c, seqs: (c,) + rest)

    def kernel(seqs, *refs):
        function((pl.program_id(0) < seqs[0]).astype(F32), *refs)

    return kernel_call(
        kernel,
        name,
        6,
        (slots,),
        [spec(value.shape, value.ndim == 2) for value in ins],
        [spec(shape, False) for shape, _ in outs],
        [jax.ShapeDtypeStruct(shape, dtype) for shape, dtype in outs],
        scalars=1,
    )(seqs, *ins)


def enter(live, image, text, image_cot, text_cot, vecs, first, mlp_round, sums):
    cut = image.shape[1]
    for s, (tokens, cot, rows) in enumerate(
        ((image, image_cot, slice(0, cut)), (text, text_cot, slice(cut, None)))
    ):
        normed, _ = normalize(tokens[0].astype(F32))
        first[0, rows] = (normed * (1.0 + vecs[0, s, 1:2]) + vecs[0, s, 0:1]).astype(BF16)
        rounded = (cot[0].astype(F32) * live * vecs[0, s, 5:6]).astype(BF16)
        mlp_round[0, rows] = rounded
        sums[0, s : s + 1] = add_up(rounded.astype(F32))


def middle(live, image, text, own, beside, across, vecs, bias, after, branch, second):
    cut = image.shape[1]
    for s, (tokens, rows) in enumerate(((image, slice(0, cut)), (text, slice(cut, None)))):
        value = own[0, rows].astype(F32) + beside[0, rows].astype(F32)
        value = value + across[0, rows].astype(F32) + bias[s : s + 1]
        result = tokens[0].astype(F32) + vecs[0, s, 2:3] * value
        normed, _ = normalize(result)
        branch[0, rows] = value
        after[0, rows] = result
        second[0, rows] = (normed * (1.0 + vecs[0, s, 4:5]) + vecs[0, s, 3:4]).astype(BF16)


def middle_back(
    live, image_cot, text_cot, own, beside, across, vecs, after, branch, residual, rounded, sums
):
    cut = image_cot.shape[1]
    for s, (cot, rows) in enumerate(((image_cot, slice(0, cut)), (text_cot, slice(cut, None)))):
        grad = own[0, rows].astype(F32) + beside[0, rows].astype(F32)
        grad = grad + across[0, rows].astype(F32)
        normed, inverse = normalize(after[0, rows])
        value = cot[0].astype(F32) * live + norm_back(grad, normed, inverse, vecs[0, s, 4:5])
        residual[0, rows] = value
        low = (value * vecs[0, s, 2:3]).astype(BF16)
        rounded[0, rows] = low
        sums[0, s, 0:1] = add_up(value * branch[0, rows])
        sums[0, s, 1:2] = add_up(grad)
        sums[0, s, 2:3] = add_up(grad * normed)
        sums[0, s, 3:4] = add_up(low.astype(F32))


def leave(
    live, image_cot, text_cot, own, beside, across, vecs, after, bias, image_out, text_out, sums
):
    cut = image_cot.shape[1]
    for s, (cot, rows, out) in enumerate(
        ((image_cot, slice(0, cut), image_out), (text_cot, slice(cut, None), text_out))
    ):
        value = own[0, rows].astype(F32) + beside[0, rows].astype(F32)
        value = value + across[0, rows].astype(F32) + bias[s : s + 1]
        out[0] = ((after[0, rows] + vecs[0, s, 5:6] * value) * live).astype(BF16)
        sums[0, s : s + 1] = add_up(cot[0].astype(F32) * live * value)


def enter_back(
    live, image, text, own, beside, across, vecs, residual, image_grad, text_grad, sums
):
    cut = image.shape[1]
    for s, (tokens, rows, out) in enumerate(
        ((image, slice(0, cut), image_grad), (text, slice(cut, None), text_grad))
    ):
        grad = own[0, rows].astype(F32) + beside[0, rows].astype(F32)
        grad = grad + across[0, rows].astype(F32)
        normed, inverse = normalize(tokens[0].astype(F32))
        out[0] = residual[0, rows] + norm_back(grad, normed, inverse, vecs[0, s, 1:2])
        sums[0, s, 0:1] = add_up(grad)
        sums[0, s, 1:2] = add_up(grad * normed)


def bias_spec(block):
    return pl.BlockSpec((2, block), lambda j: (0, j))


def add_bias(stream, spot, cut, sums, bias):
    return [sums + bias[stream : stream + 1]]


def gelu_both(stream, spot, cut, sums, bias):
    value = sums + bias[stream : stream + 1]
    factor = math.sqrt(2.0 / math.pi)
    square = value * value
    bend = jnp.tanh(factor * (value + 0.044715 * value * square))
    half = 0.5 * (1.0 + bend)
    slope = half + 0.5 * value * (1.0 - bend * bend) * factor * (1.0 + 0.134145 * square)
    return [value * half, slope]


def times_slope(stream, spot, cut, sums, slope):
    return [sums * slope[spot[0], spot[1], cut].astype(F32)]


def dot(spec, a, b):
    return jnp.einsum(spec, a, b, preferred_element_type=F32)


def on_device(
    groups,
    image_tokens,
    text_tokens,
    conditioning,
    group_seqs,
    ada_weight,
    ada_bias,
    qkv_weight,
    qv_bias,
    proj_weight,
    proj_bias,
    fc1_weight,
    fc1_bias,
    fc2_weight,
    fc2_bias,
    image_cot,
    text_cot,
):
    column = lax.axis_index("tensor")
    group = lax.axis_index("dp")
    ring = Ring(groups)
    order = Order(group_seqs)
    slots, image, width = image_tokens.shape
    text = text_tokens.shape[1]
    tokens = image + text
    rows = qkv_weight.shape[2]
    col_width = qkv_weight.shape[-1]
    hidden = fc1_weight.shape[-1]
    both = range(2)

    proj_turned = jnp.swapaxes(proj_weight, 1, 2)[:, None]
    fc1_shard = fc1_weight[:, None]
    fc2_turned = jnp.swapaxes(fc2_weight, 1, 2)[:, None]

    ada_part = lax.dynamic_slice_in_dim(ada_bias.astype(F32), column * col_width, col_width, 2)
    qv_part = lax.dynamic_slice_in_dim(qv_bias.astype(F32), column * col_width, col_width, 2)
    fc1_part = lax.dynamic_slice_in_dim(fc1_bias.astype(F32), column * hidden, hidden, 1)
    offsets = jnp.stack([qv_part[:, 0], jnp.zeros_like(qv_part[:, 0]), qv_part[:, 1]], 1)
    offsets = offsets.reshape(2, 3 * col_width)
    proj_add = proj_bias.astype(F32)
    fc2_add = fc2_bias.astype(F32)

    cond_act, silu_back = jax.vjp(jax.nn.silu, conditioning.astype(F32))
    cond_low = cond_act.astype(BF16).reshape(slots, groups, rows)
    cond_sends = jnp.stack(
        [
            lax.dynamic_index_in_dim(cond_low, group ^ mask, 1, keepdims=False)
            for mask in range(groups)
        ]
    )
    cond_rows = order(exchange(cond_sends, "dp", groups)).reshape(groups * slots, rows)
    modul_parts = order(dot("cd,sjdn->csjn", cond_rows, ada_weight))
    modul_parts = modul_parts.reshape((groups, slots) + modul_parts.shape[1:])
    modul_local = order(collect(modul_parts, "dp", groups) + ada_part[None])
    qkv_ring = Gather(ring, order(jnp.concatenate([qkv_weight, proj_turned], 1)))
    qkv_part = (0, 3 * col_width)
    proj_part = (3 * col_width, col_width)
    vecs = order(lax.all_gather(modul_local, "tensor", axis=3, tiled=True))

    first, mlp_round, fc2_bias_local = order.run(
        lambda *a: per_slot(
            enter,
            "enter",
            group_seqs,
            a,
            [
                ((slots, tokens, width), BF16),
                ((slots, tokens, width), BF16),
                ((slots, 2, width), F32),
            ],
        ),
        image_tokens,
        text_tokens,
        image_cot,
        text_cot,
        vecs,
    )
    qkv_ring.arrive(order)
    first_move = Spread(order(first))
    qkv_ring.arrive(order)
    qkv_ring.arrive(order)
    first_move.arrive(order)
    first_full = first_move.finish(order)
    qkv_ring.place(order)
    qkv_ring.arrive(order)
    fc1_ring = Gather(ring, order(fc1_shard))
    mlp_move = Spread(order(mlp_round))
    qkv_full = qkv_ring.finish(order)

    qkv = order.run(
        lambda *a: rows_times(
            a[:4], a[4:], image, False, 1, add_bias, (offsets,), (bias_spec,), qkv_part
        ),
        *first_full,
        *qkv_full,
    )
    fc1_ring.arrive(order)
    mixed = ()
    for slot in range(slots):
        mixed = order.run(
            lambda *a, slot=slot: attend(a[0], image, slot, a[1:]), *((qkv,) + tuple(mixed))
        )
    mixed, logs = mixed
    fc1_ring.arrive(order)
    mlp_move.arrive(order)
    branch_parts = order.run(
        lambda *a: rows_times(a[0], a[1:], image, True, "split", columns=proj_part),
        mixed,
        *qkv_full,
    )
    branch_move = Collect(*order(*branch_parts))
    mlp_full = mlp_move.finish(order)
    branch_move.arrive(order)
    fc1_ring.arrive(order)
    fc1_ring.arrive(order)
    fc2_ring = Gather(ring, order(fc2_turned))
    branch_terms = branch_move.finish(order)
    after, branch, second = order.run(
        lambda *a: per_slot(
            middle,
            "middle",
            group_seqs,
            a,
            [
                ((slots, tokens, width), F32),
                ((slots, tokens, width), F32),
                ((slots, tokens, width), BF16),
            ],
        ),
        image_tokens,
        text_tokens,
        *branch_terms,
        vecs,
        proj_add,
    )
    second_move = Spread(second)
    fc1_full = fc1_ring.finish(order)
    fc2_ring.arrive(order)
    fc2_ring.arrive(order)
    second_move.arrive(order)
    second_full = second_move.finish(order)
    activated, slope = order.run(
        lambda *a: rows_times(
            a[:4], a[4:], image, False, 2, gelu_both, (fc1_part,), (bias_spec,)
        ),
        *second_full,
        *fc1_full,
    )
    fc2_ring.arrive(order)
    *fc2_grad, _ = order.run(
        lambda *a: weight_grad(a[:4], a[4], image, groups), *mlp_full, activated
    )
    fc2_ring.arrive(order)
    fc2_sums = Scatter(ring, *order(*fc2_grad))
    fc2_full = fc2_ring.finish(order)
    pre_round = order.run(
        lambda *a: rows_times(
            a[:4],
            a[4:],
            image,
            False,
            1,
            times_slope,
            (slope,),
            (
                lambda block: pl.BlockSpec(
                    (4, slots, tokens, block), lambda j: (0, 0, 0, j)
                ),
            ),
        ),
        *mlp_full,
        *fc2_full,
    )
    fc2_sums.arrive(order)
    second_parts = order.run(
        lambda *a: rows_times(a[0], a[1:], image, True, "split"), pre_round, *fc1_full
    )
    second_back = Collect(*second_parts)
    second_back.arrive(order)
    *fc1_grad, fc1_bias_local = order.run(
        lambda *a: weight_grad(a[:4], a[4], image, groups), *second_full, pre_round
    )
    fc1_sums = Scatter(ring, *order(*fc1_grad))
    mlp_parts = order.run(
        lambda *a: rows_times(a[0], a[1:], image, True, "split"), activated, *fc2_full
    )
    fc2_sums.arrive(order)
    second_terms = second_back.finish(order)
    residual, branch_round, middle_vecs = order.run(
        lambda *a: per_slot(
            middle_back,
            "middle_back",
            group_seqs,
            a,
            [
                ((slots, tokens, width), F32),
                ((slots, tokens, width), BF16),
                ((slots, 2, 4, width), F32),
            ],
        ),
        image_cot,
        text_cot,
        *second_terms,
        vecs,
        after,
        branch,
    )
    branch_back = Spread(branch_round)
    fc2_sums.arrive(order)
    fc1_sums.arrive(order)
    branch_back.arrive(order)
    branch_full = branch_back.finish(order)
    mixed_grad = order.run(
        lambda *a: rows_times(a[:4], a[4:], image, False, 1, columns=proj_part),
        *branch_full,
        *qkv_full,
    )
    mlp_back = Collect(*order(*mlp_parts))
    mlp_back.arrive(order)
    *proj_grad, _ = order.run(
        lambda *a: weight_grad(a[:4], a[4], image, groups, 3 * col_width, 4 * col_width),
        *branch_full,
        mixed,
    )
    qkv_grads = None
    for slot in range(slots):
        given = (qkv, mixed, mixed_grad, logs) + (() if slot == 0 else (qkv_grads,))
        qkv_grads = order.run(
            lambda *a, slot=slot: attend_back(
                *a[:4], image, slot, a[4] if len(a) > 4 else None
            ),
            *given,
        )
        if slot == 0:
            fc2_sums.arrive(order)
            fc1_sums.arrive(order)
    mlp_terms = mlp_back.finish(order)
    fc1_sums.arrive(order)
    first_parts = order.run(
        lambda *a: rows_times(a[0], a[1:], image, True, "split", columns=qkv_part),
        qkv_grads,
        *qkv_full,
    )
    first_back = Collect(*first_parts)
    first_back.arrive(order)
    *qkv_grad, qv_sums = order.run(
        lambda *a: weight_grad(
            a[:4], a[4], image, groups, 0, 4 * col_width, a[5:]
        ),
        *first_full,
        qkv_grads,
        *proj_grad,
    )
    fc1_sums.arrive(order)
    qkv_sums = Scatter(ring, *order(*qkv_grad), "parts")
    qv_bias_local = qv_sums.reshape(2, 3, col_width)[:, 0::2]
    proj_bias_local = jnp.sum(middle_vecs[:, :, 3], 0)
    fc2_bias_local = jnp.sum(fc2_bias_local, 0)
    split_sums = jnp.concatenate([qv_bias_local.reshape(-1), fc1_bias_local.reshape(-1)])
    token_sums = jnp.concatenate([proj_bias_local.reshape(-1), fc2_bias_local.reshape(-1)])
    bias_local = jnp.concatenate([split_sums, token_sums])
    image_out, text_out, gate_two = order.run(
        lambda *a: per_slot(
            leave,
            "leave",
            group_seqs,
            a,
            [
                (image_tokens.shape, BF16),
                (text_tokens.shape, BF16),
                ((slots, 2, width), F32),
            ],
        ),
        image_cot,
        text_cot,
        *mlp_terms,
        vecs,
        after,
        fc2_add,
    )
    fc2_sum = order(fc2_sums.finish(order))
    fc1_sum = order(fc1_sums.finish(order))
    qkv_sums.arrive(order)
    first_terms = first_back.finish(order)
    image_grad, text_grad, enter_vecs = order.run(
        lambda *a: per_slot(
            enter_back,
            "enter_back",
            group_seqs,
            a,
            [
                (image_tokens.shape, F32),
                (text_tokens.shape, F32),
                ((slots, 2, 2, width), F32),
            ],
        ),
        image_tokens,
        text_tokens,
        *first_terms,
        vecs,
        residual,
    )
    modul_grad = jnp.concatenate(
        [
            enter_vecs,
            middle_vecs[:, :, 0:3],
            gate_two[:, :, None],
        ],
        2,
    ).reshape(slots, 2, 6, 4, col_width)
    modul_blocks = jnp.stack(
        [
            lax.dynamic_index_in_dim(modul_grad, column ^ mask, 3, keepdims=False)
            for mask in range(4)
        ]
    )
    modul_round = order(collect(modul_blocks, "tensor", 4).astype(BF16))
    qkv_sums.arrive(order)
    shared = jnp.concatenate([modul_round.astype(F32).reshape(-1), bias_local])
    shared = order(spread(order(shared), "dp", groups))
    qkv_sums.arrive(order)
    shared = order(shared)
    modul_all = shared[:, : modul_round.size].astype(BF16)
    modul_all = modul_all.reshape((groups * slots,) + modul_round.shape[1:])
    bias_local = jnp.sum(shared[:, modul_round.size :], 0)
    cond_part = dot("csjn,sjdn->cd", modul_all, ada_weight)
    ada_bias_part = jnp.sum(modul_all.astype(F32), 0)
    last = jnp.concatenate([cond_part.reshape(-1), ada_bias_part.reshape(-1), bias_local])
    last = order(spread(order(last), "tensor", 4))
    cond_part = jnp.sum(last[:, : cond_part.size], 0).reshape(groups, slots, rows)
    cond_terms = order(exchange(cond_part, "dp", groups))
    cond_term = jnp.stack(
        [
            lax.dynamic_index_in_dim(cond_terms, group ^ place, 0, keepdims=False)
            for place in range(groups)
        ],
        1,
    ).reshape(slots, width)
    cond_grad = lax.dynamic_slice_in_dim(
        silu_back(cond_term)[0], column * col_width, col_width, 1
    )
    last = jnp.stack(
        [
            lax.dynamic_index_in_dim(last[:, cond_part.size :], column ^ place, 0, keepdims=False)
            for place in range(4)
        ]
    )
    ada_bias_grad = by_column(last[:, : ada_bias_part.size], ada_bias_part.shape)
    bias_all = last[:, ada_bias_part.size :]
    cut_a = qv_bias_local.size
    cut_b = cut_a + fc1_bias_local.size
    cut_c = cut_b + proj_bias_local.size
    cut_d = cut_c + fc2_bias_local.size

    qv_bias_grad = by_column(bias_all[:, :cut_a], qv_bias_local.shape)
    fc1_bias_grad = by_column(bias_all[:, cut_a:cut_b], fc1_bias_local.shape)
    proj_bias_grad = jnp.sum(bias_all[:, cut_b:cut_c], 0).reshape(proj_bias_local.shape)
    fc2_bias_grad = jnp.sum(bias_all[:, cut_c:cut_d], 0).reshape(fc2_bias_local.shape)
    ada_grad = dot("cd,csjn->sjdn", cond_rows, modul_all)
    qkv_sum, proj_sum = qkv_sums.finish(order)
    cond_grad = order(cond_grad)
    live = jnp.arange(slots, dtype=jnp.int32) < order.token[0]
    cond_grad = jnp.where(live[:, None], cond_grad, 0.0)
    return (
        image_out,
        text_out,
        image_grad,
        text_grad,
        cond_grad,
        ada_grad,
        ada_bias_grad,
        qkv_sum,
        qv_bias_grad,
        jnp.swapaxes(proj_sum, 1, 2),
        proj_bias_grad,
        fc1_sum,
        fc1_bias_grad,
        jnp.swapaxes(fc2_sum, 1, 2),
        fc2_bias_grad,
    )


def solution(mesh):
    groups = mesh.shape["dp"]
    in_specs = (
        P("dp", "tensor", None),
        P("dp", "tensor", None),
        P("dp", None),
        P("dp"),
        P(None, None, "dp", "tensor"),
        P(),
        P(None, None, "dp", "tensor"),
        P(),
        P(None, "tensor", "dp"),
        P(),
        P(None, "dp", "tensor"),
        P(),
        P(None, "tensor", "dp"),
        P(),
        P("dp", "tensor", None),
        P("dp", "tensor", None),
    )
    out_specs = (
        P("dp", "tensor", None),
        P("dp", "tensor", None),
        P("dp", "tensor", None),
        P("dp", "tensor", None),
        P("dp", "tensor"),
        P(None, None, "dp", "tensor"),
        P(),
        P(None, None, "dp", "tensor"),
        P(),
        P(None, "tensor", "dp"),
        P(),
        P(None, "dp", "tensor"),
        P(),
        P(None, "tensor", "dp"),
        P(),
    )

    def step(*args):
        return on_device(groups, *args)

    return jax.shard_map(
        step, mesh=mesh, in_specs=in_specs, out_specs=out_specs, check_vma=False
    )
```

```python
import math

import jax
import jax.numpy as jnp
from jax import lax
from jax.experimental import pallas as pl
from jax.experimental.pallas import tpu as pltpu
from jax.sharding import PartitionSpec as P

HEAD_DIM = 64
PAIR = 2 * HEAD_DIM
FACTOR = 1.0 / math.sqrt(HEAD_DIM)
VMEM = 60 << 20
FLOPS_PER_US = 460000000
EPSILON = 1e-06
F32 = jnp.float32
BF16 = jnp.bfloat16


def hop(value, axis, mask, size):
    return lax.ppermute(value, axis, [(i, i ^ mask) for i in range(size)])


def halves(size):
    low = 1
    while low * low < size:
        low *= 2
    return low, size // low


def spread(value, axis, size):
    low, high = halves(size)
    held = jnp.stack(
        [value] + [hop(value, axis, low * step, size) for step in range(1, high)]
    )
    full = [held] + [hop(held, axis, mask, size) for mask in range(1, low)]
    return jnp.stack(full, 1).reshape((size,) + value.shape)


def exchange(blocks, axis, size):
    low, high = halves(size)
    blocks = blocks.reshape((high, low) + blocks.shape[1:])
    held = jnp.stack(
        [blocks[0]] + [hop(blocks[step], axis, low * step, size) for step in range(1, high)]
    )
    full = [held[:, 0]] + [hop(held[:, mask], axis, mask, size) for mask in range(1, low)]
    return jnp.stack(full, 1).reshape((size,) + blocks.shape[2:])


def collect(blocks, axis, size):
    low, high = halves(size)
    blocks = blocks.reshape((high, low) + blocks.shape[1:])
    held = blocks[0] + sum(
        hop(blocks[step], axis, low * step, size) for step in range(1, high)
    )
    return held[0] + sum(hop(held[mask], axis, mask, size) for mask in range(1, low))


def by_column(block, shape):
    return jnp.moveaxis(block.reshape((4,) + shape), 0, -2).reshape(
        shape[:-1] + (4 * shape[-1],)
    )


class Order:
    def __init__(self, seed):
        self.token = seed

    def __call__(self, *values):
        self.token, *values = lax.optimization_barrier((self.token, *values))
        return values[0] if len(values) == 1 else values

    def run(self, function, *values):
        results = function(*self(*values)) if len(values) > 1 else function(self(*values))
        return self(*results) if isinstance(results, (tuple, list)) else self(results)


class Ring:
    def __init__(self, size):
        self.size = size
        self.order = list(range(0, size, 2)) + list(range(size - 1, 0, -2))
        self.ahead = [(self.order[i], self.order[(i + 1) % size]) for i in range(size)]
        self.back = [(b, a) for a, b in self.ahead]
        place = [0] * size
        for position, device in enumerate(self.order):
            place[device] = position
        self.mine = jnp.asarray(place, jnp.int32)[lax.axis_index("dp")]
        self.table = jnp.asarray(self.order, jnp.int32)

    def devices(self, distances):
        return self.table[(self.mine + jnp.asarray(distances, jnp.int32)) % self.size]

    def forward(self, value):
        return lax.ppermute(value, "dp", self.ahead)

    def backward(self, value):
        return lax.ppermute(value, "dp", self.back)


class Gather:
    def __init__(self, ring, shard):
        self.ring, self.step = ring, 0
        self.pieces, self.distances, self.streams = [shard], [0], [0]
        self.placed, self.full = 0, ()
        self.send(shard, shard)

    def send(self, ahead, back):
        self.step += 1
        if self.step == self.ring.size // 2:
            ahead, back = ahead[:1], back[1:]
        self.moving = (self.ring.forward(ahead), self.ring.backward(back))

    def arrive(self, order):
        ahead, back = order(*self.moving)
        last = self.step == self.ring.size // 2
        self.pieces += [ahead, back]
        self.distances += [-self.step, self.step]
        self.streams += [0, 1 if last else 0]
        if not last:
            self.send(ahead, back)
        return last

    def finish(self, order):
        while len(self.pieces) < self.ring.size + 1:
            self.arrive(order)
        self.place(order)
        return [f.reshape(-1, f.shape[2]) for f in self.full]

    def place(self, order):
        new = slice(self.placed, None)
        places = self.ring.devices(self.distances[new])
        self.full = order(
            *assemble(self.pieces[new], self.streams[new], places, self.ring.size, self.full)
        )
        self.placed = len(self.pieces)


class Scatter:
    def __init__(self, ring, image, text, far_image, far_text, form="plain"):
        self.ring, self.image, self.text, self.form = ring, image, text, form
        self.left = ring.size // 2
        self.moving = (ring.forward(far_image), ring.backward(far_text))

    def arrive(self, order):
        ahead, back = order(*self.moving)
        self.left -= 1
        places = self.ring.devices([self.left, -self.left])
        if self.left == 0:
            self.total = ring_total(self.image, self.text, ahead, back, places, self.form)
            return True
        ahead, back = order(*ring_add(self.image, self.text, ahead, back, places))
        self.moving = (self.ring.forward(ahead), self.ring.backward(back))
        return False

    def finish(self, order):
        while self.left:
            self.arrive(order)
        return self.total


def kernel_call(kernel, name, cost_us, grid, in_specs, out_specs, out_shape, scalars=0, **more):
    return pl.pallas_call(
        kernel,
        grid_spec=pltpu.PrefetchScalarGridSpec(
            num_scalar_prefetch=scalars,
            grid=grid,
            in_specs=in_specs,
            out_specs=out_specs,
            scratch_shapes=more.pop("scratch", ()),
        ),
        out_shape=out_shape,
        compiler_params=pltpu.CompilerParams(vmem_limit_bytes=VMEM),
        cost_estimate=pl.CostEstimate(
            flops=int(cost_us * FLOPS_PER_US), bytes_accessed=1, transcendentals=0
        ),
        name=name,
        **more,
    )


def assemble(pieces, streams, places, size, earlier):
    count = len(pieces)
    parts, rows, width = pieces[0].shape[1:]
    moves = [
        (i, streams[i] + s, s, part)
        for i in range(count)
        for s in range(pieces[i].shape[0])
        for part in range(parts)
    ]

    def kernel(place, *refs):
        shards, refs = refs[:count], refs[count + len(earlier) :]
        full, held, sems_in, sems_out = refs[:2], refs[2:-2], refs[-2], refs[-1]
        ins = [pltpu.make_async_copy(shards[i], held[i], sems_in.at[i]) for i in range(count)]
        for copy in ins:
            copy.start()
        outs, last = [], -1
        for m, (i, stream, s, part) in enumerate(moves):
            if i != last:
                ins[i].wait()
                last = i
            spot = full[stream].at[place[i], :, pl.ds(part * width, width)]
            outs.append(pltpu.make_async_copy(held[i].at[s, part], spot, sems_out.at[m]))
            outs[-1].start()
        for copy in outs:
            copy.wait()

    whole = pl.BlockSpec(memory_space=pltpu.HBM)
    out = jax.ShapeDtypeStruct((size, rows, parts * width), BF16)
    return kernel_call(
        kernel,
        "assemble",
        1 + 3e-7 * sum(math.prod(p.shape) for p in pieces),
        (1,),
        [whole] * (count + len(earlier)),
        [whole] * 2,
        [out] * 2,
        scalars=1,
        scratch=[pltpu.VMEM(p.shape, p.dtype) for p in pieces]
        + [pltpu.SemaphoreType.DMA((count,)), pltpu.SemaphoreType.DMA((len(moves),))],
        input_output_aliases={count + 1: 0, count + 2: 1} if earlier else {},
    )(places, *pieces, *earlier)


def ring_specs(image, ahead, back, block):
    width = image.shape[2]

    def local(which):
        return pl.BlockSpec((1, block, width), lambda i, place: (place[which], i, 0))

    def moved(value):
        return pl.BlockSpec((value.shape[0], block, width), lambda i, place: (0, i, 0))

    return [local(0), local(0), local(1), local(1), moved(ahead), moved(back)]


def ring_add(image, text, ahead, back, places):
    size, rows, width = image.shape
    block = rows // 4 if rows % 64 == 0 else rows
    whole = ahead.shape[0] == 2

    def kernel(place, image_a, text_a, image_b, text_b, ahead, back, send_a, send_b):
        send_a[0] = (image_a[0].astype(F32) + ahead[0].astype(F32)).astype(BF16)
        send_b[1] = (text_b[0].astype(F32) + back[back.shape[0] - 1].astype(F32)).astype(BF16)
        if whole:
            send_a[1] = (text_a[0].astype(F32) + ahead[1].astype(F32)).astype(BF16)
            send_b[0] = (image_b[0].astype(F32) + back[0].astype(F32)).astype(BF16)
        else:
            send_a[1] = text_a[0]
            send_b[0] = image_b[0]

    out = pl.BlockSpec((2, block, width), lambda i, place: (0, i, 0))
    return kernel_call(
        kernel,
        "ring_add",
        1 + 7e-6 * image.shape[1] * image.shape[2] * 2,
        (rows // block,),
        ring_specs(image, ahead, back, block),
        [out] * 2,
        [jax.ShapeDtypeStruct((2, rows, width), BF16)] * 2,
        scalars=1,
    )(places, image, text, image, text, ahead, back)


def ring_total(image, text, ahead, back, places, form):
    size, rows, width = image.shape
    block = rows // 4 if rows % 64 == 0 else rows
    part = width // 4

    def kernel(place, image_a, text_a, image_b, text_b, ahead, back, total, *more):
        for s, mine in enumerate((image_a, text_a)):
            value = mine[0].astype(F32) + ahead[s].astype(F32) + back[s].astype(F32)
            if form == "parts":
                for j in range(3):
                    total[s, j] = value[:, j * part : (j + 1) * part]
                more[0][s] = value[:, 3 * part :]
            else:
                total[s] = value

    shapes = {
        "plain": [(2, rows, width)],
        "parts": [(2, 3, rows, part), (2, rows, part)],
    }[form]
    outs = [
        pl.BlockSpec(
            shape[:-2] + (block, shape[-1]),
            lambda i, place, lead=len(shape) - 2: (0,) * lead + (i, 0),
        )
        for shape in shapes
    ]
    total = kernel_call(
        kernel,
        "ring_total",
        1 + 7e-6 * image.shape[1] * image.shape[2] * 2,
        (rows // block,),
        ring_specs(image, ahead, back, block),
        outs,
        [jax.ShapeDtypeStruct(shape, F32) for shape in shapes],
        scalars=1,
    )(places, image, text, image, text, ahead, back)
    return total if form == "parts" else total[0]


class Spread:
    def __init__(self, part):
        self.part = part
        self.across = hop(part, "tensor", 2, 4)
        self.beside = hop(part, "tensor", 1, 4)

    def arrive(self, order):
        self.across, self.beside = order(self.across, self.beside)
        self.corner = hop(self.across, "tensor", 1, 4)

    def finish(self, order):
        return [self.part, self.beside, self.across, order(self.corner)]


class Collect:
    def __init__(self, own, beside, across, corner):
        self.own, self.kept = own, across
        self.corner = hop(corner, "tensor", 1, 4)
        self.beside = hop(beside, "tensor", 1, 4)

    def arrive(self, order):
        corner = order(self.corner)
        send = (self.kept.astype(F32) + corner.astype(F32)).astype(BF16)
        self.across = hop(order(send), "tensor", 2, 4)
        self.beside = order(self.beside)

    def finish(self, order):
        return [self.own, self.beside, order(self.across)]


def piece_specs(pieces, block=None):
    if isinstance(pieces, (list, tuple)):
        shape = pieces[0].shape
        spec = pl.BlockSpec(shape, lambda j, *_: (0, 0, 0), pipeline_mode=pl.Buffered(1))
        return [spec] * 4, list(pieces), shape
    shape = pieces.shape[1:]
    specs = [
        pl.BlockSpec(
            (None,) + shape, lambda j, *_, k=k: (k, 0, 0, 0), pipeline_mode=pl.Buffered(1)
        )
        for k in range(4)
    ]
    return specs, [pieces] * 4, shape


def column_block(width):
    for block in (512, 384, 256, 128):
        if width % block == 0:
            return block
    return width


def rows_times(
    pieces, weights, image, turned, outputs, finish=None, extras=(), extra_specs=(), columns=None
):
    specs, arrays, (slots, tokens, depth) = piece_specs(pieces)
    start, count = columns or (0, weights[0].shape[1])
    width = weights[0].shape[0] if turned else count
    block = column_block(math.gcd(start, width))
    text = tokens - image
    spots = [(k, c) for k in range(4) for c in range(slots)]
    dims = DOT_NT if turned else DOT_NN
    split = outputs == "split"
    count = 4 if split else outputs

    def kernel(*refs):
        rows, (image_w, text_w) = refs[:4], refs[4:6]
        more, outs = refs[6 : 6 + len(extras)], refs[6 + len(extras) :]

        def store(stream, spot, sums):
            k, c = spot
            cut = slice(0, image) if stream == 0 else slice(image, tokens)
            values = [sums] if finish is None else finish(stream, spot, cut, sums, *more)
            for which, value in enumerate(values):
                if split:
                    outs[k][c, cut] = value.astype(BF16)
                else:
                    outs[which][k, c, cut] = value.astype(BF16)

        for spot in spots:
            store(0, spot, mul(rows[spot[0]][spot[1], :image], image_w[...], dims))
        joined = jnp.concatenate([rows[k][c, image:] for k, c in spots], 0)
        sums = mul(joined, text_w[...], dims)
        for i, spot in enumerate(spots):
            store(1, spot, sums[i * text : (i + 1) * text])

    if turned:
        weight = pl.BlockSpec((block, depth), lambda j: (j, start // depth))
    else:
        weight = pl.BlockSpec((depth, block), lambda j: (0, start // block + j))
    if split:
        out = pl.BlockSpec((slots, tokens, block), lambda j: (0, 0, j))
        shape = jax.ShapeDtypeStruct((slots, tokens, width), BF16)
    else:
        out = pl.BlockSpec((4, slots, tokens, block), lambda j: (0, 0, 0, j))
        shape = jax.ShapeDtypeStruct((4, slots, tokens, width), BF16)
    return kernel_call(
        kernel,
        "rows_times",
        1 + 3e-9 * 4 * slots * tokens * depth * width,
        (width // block,),
        specs + [weight, weight] + [make(block) for make in extra_specs],
        [out] * count,
        [shape] * count,
    )(*arrays, *weights, *extras)


def weight_grad(pieces, grads, image, ring, first=0, total=None, earlier=()):
    size = ring.size
    far = ring.devices([size // 2])
    specs, arrays, (slots, tokens, depth) = piece_specs(pieces)
    width = grads.shape[3]
    block = column_block(math.gcd(first, width))
    text = tokens - image
    spots = [(k, c) for k in range(4) for c in range(slots)]

    def kernel(far, a, b, c, d, grad, *refs):
        rows = (a, b, c, d)
        image_out, text_out, far_image, far_text, sums, image_turned, text_turned = refs[-7:]

        @pl.when(pl.program_id(0) == 0)
        def _():
            for i, (k, s) in enumerate(spots):
                image_turned[:, pl.ds(i * image, image)] = jnp.transpose(rows[k][s, :image])
            text_turned[...] = jnp.transpose(
                jnp.concatenate([rows[k][s, image:] for k, s in spots], 0)
            )

        image_grads = jnp.concatenate([grad[k, s, :image] for k, s in spots], 0)
        text_grads = jnp.concatenate([grad[k, s, image:] for k, s in spots], 0)
        image_out[...] = (
            mul(image_turned[...], image_grads, DOT_NN).astype(BF16).reshape(image_out.shape)
        )
        text_out[...] = (
            mul(text_turned[...], text_grads, DOT_NN).astype(BF16).reshape(text_out.shape)
        )
        far_image[0] = image_out[far[0]]
        far_text[0] = text_out[far[0]]
        sums[0:1] = jnp.sum(image_grads.astype(F32), 0, keepdims=True)
        sums[1:2] = jnp.sum(text_grads.astype(F32), 0, keepdims=True)

    outs, shapes = [], []
    for count in (size, size, 1, 1):
        outs.append(
            pl.BlockSpec(
                (count, depth // size, block), lambda j, *_: (0, 0, first // block + j)
            )
        )
        shapes.append(jax.ShapeDtypeStruct((count, depth // size, total or width), BF16))
    return kernel_call(
        kernel,
        "weight_grad",
        1 + 3.4e-9 * 4 * slots * tokens * depth * width,
        (width // block,),
        specs
        + [pl.BlockSpec((4, slots, tokens, block), lambda j, *_: (0, 0, 0, j))]
        + [pl.BlockSpec(memory_space=pl.ANY)] * len(earlier),
        outs + [pl.BlockSpec((2, block), lambda j, *_: (0, j))],
        shapes + [jax.ShapeDtypeStruct((2, width), F32)],
        scalars=1,
        scratch=[
            pltpu.VMEM((depth, len(spots) * image), BF16),
            pltpu.VMEM((depth, len(spots) * text), BF16),
        ],
        input_output_aliases={6 + i: i for i in range(len(earlier))},
    )(far, *arrays, grads, *earlier)


def mul(a, b, dims):
    return lax.dot_general(a, b, dims, preferred_element_type=F32)


DOT_NN = (((1,), (0,)), ((), ()))
DOT_NT = (((1,), (1,)), ((), ()))
DOT_TN = (((0,), (0,)), ((), ()))


def lane_masks(dtype):
    lane = lax.broadcasted_iota(jnp.int32, (1, PAIR), 1)
    low = (lane < HEAD_DIM).astype(F32)
    return [low.astype(dtype), (1.0 - low).astype(dtype)]


def stream_rows(ref, image, stream):
    cut = slice(0, image) if stream == 0 else slice(image, ref.shape[2])
    return jnp.concatenate([ref[k, 0, cut] for k in range(4)], 0)


def query_blocks(image, text):
    return [(0, (0, 1), 0), (0, (2, 3), 2 * image), (1, (0, 1, 2, 3), 4 * image)]


def attend(qkv, image, slot, earlier):
    _, slots, tokens, width = qkv.shape
    text, pairs = tokens - image, width // (3 * PAIR)

    def kernel(q, k, v, *refs):
        out, logs_out = refs[-2:]
        keys = [stream_rows(k, image, s) for s in range(2)]
        values = [stream_rows(v, image, s) for s in range(2)]
        masks = lane_masks(F32)
        low = [m.astype(BF16) for m in masks]
        for stream, members, place in query_blocks(image, text):
            cut = slice(0, image) if stream == 0 else slice(image, tokens)
            size = image if stream == 0 else text
            query = jnp.concatenate([q[m, 0, cut] for m in members], 0)
            query = query * jnp.asarray(FACTOR, BF16)
            total = logs = None
            for head in range(2):
                scores = [mul(query * low[head], key, DOT_NT) for key in keys]
                top = jnp.maximum(
                    jnp.max(scores[0], -1, keepdims=True), jnp.max(scores[1], -1, keepdims=True)
                )
                probs = [jnp.exp(s - top) for s in scores]
                denom = jnp.sum(probs[0], -1, keepdims=True) + jnp.sum(
                    probs[1], -1, keepdims=True
                )
                mixed = mul(probs[0].astype(BF16), values[0], DOT_NN) + mul(
                    probs[1].astype(BF16), values[1], DOT_NN
                )
                mixed = mixed * (masks[head] / denom)
                log = (top + jnp.log(denom)) * masks[head]
                total = mixed if total is None else total + mixed
                logs = log if logs is None else logs + log
            for i, m in enumerate(members):
                out[m, 0, cut] = total[i * size : (i + 1) * size].astype(BF16)
            turned = jnp.transpose(logs)
            span = pl.ds(place, size * len(members))
            logs_out[0, 0, 0:1, span] = turned[0:1]
            logs_out[0, 0, 1:2, span] = turned[HEAD_DIM : HEAD_DIM + 1]

    def spec(which):
        return pl.BlockSpec((4, 1, tokens, PAIR), lambda p: (0, slot, 0, which * pairs + p))

    total = 4 * tokens
    return kernel_call(
        kernel,
        "attend",
        15,
        (pairs,),
        [spec(0), spec(1), spec(2)] + [pl.BlockSpec(memory_space=pl.ANY)] * len(earlier),
        [spec(0), pl.BlockSpec((1, 1, 2, total), lambda p: (slot, p, 0, 0))],
        [
            jax.ShapeDtypeStruct((4, slots, tokens, pairs * PAIR), BF16),
            jax.ShapeDtypeStruct((slots, pairs, 2, total), F32),
        ],
        input_output_aliases={3: 0, 4: 1} if earlier else {},
    )(qkv, qkv, qkv, *earlier)


def attend_back(qkv, mixed, grads, logs, image, slot, earlier):
    _, slots, tokens, width = qkv.shape
    text, pairs = tokens - image, width // (3 * PAIR)

    def kernel(q, k, v, mixed, grads, logs, *refs):
        out, key_image, key_text, value_image, value_text = refs[-5:]
        key_sums, value_sums = (key_image, key_text), (value_image, value_text)
        keys = [stream_rows(k, image, s) for s in range(2)]
        values = [stream_rows(v, image, s) for s in range(2)]
        low = lane_masks(BF16)
        pair = pl.program_id(0)

        def lanes(which):
            return pl.ds(pl.multiple_of((which * pairs + pair) * PAIR, PAIR), PAIR)

        first = True
        for stream, members, place in query_blocks(image, text):
            cut = slice(0, image) if stream == 0 else slice(image, tokens)
            size = image if stream == 0 else text
            query = jnp.concatenate([q[m, 0, cut] for m in members], 0)
            query = query * jnp.asarray(FACTOR, BF16)
            grad = jnp.concatenate([grads[m, 0, cut] for m in members], 0)
            output = jnp.concatenate([mixed[m, 0, cut] for m in members], 0)
            inner = jnp.transpose(grad.astype(F32) * output.astype(F32))
            query_grad = None
            for head in range(2):
                head_q, head_g = query * low[head], grad * low[head]
                half = slice(head * HEAD_DIM, (head + 1) * HEAD_DIM)
                delta = jnp.sum(inner[half], 0, keepdims=True)
                log = logs[0, 0, head : head + 1, pl.ds(place, size * len(members))]
                for part in range(2):
                    probs = jnp.exp(mul(keys[part], head_q, DOT_NT) - log)
                    prob_grad = mul(values[part], head_g, DOT_NT)
                    score_grad = (probs * (prob_grad - delta)).astype(BF16)
                    value_part = mul(probs.astype(BF16), head_g, DOT_NN)
                    key_part = mul(score_grad, head_q, DOT_NN)
                    query_part = mul(score_grad, keys[part] * low[head], DOT_TN)
                    query_grad = query_part if query_grad is None else query_grad + query_part
                    if first:
                        value_sums[part][...] = value_part
                        key_sums[part][...] = key_part
                    else:
                        value_sums[part][...] += value_part
                        key_sums[part][...] += key_part
                first = False
            query_grad = query_grad * FACTOR
            for i, m in enumerate(members):
                out[m, 0, cut, lanes(0)] = query_grad[i * size : (i + 1) * size].astype(BF16)
        for which, sums in ((1, key_sums), (2, value_sums)):
            for m in range(4):
                out[m, 0, :image, lanes(which)] = sums[0][
                    m * image : (m + 1) * image
                ].astype(BF16)
                out[m, 0, image:, lanes(which)] = sums[1][m * text : (m + 1) * text].astype(BF16)

    def spec(which):
        return pl.BlockSpec((4, 1, tokens, PAIR), lambda p: (0, slot, 0, which * pairs + p))

    before = [] if earlier is None else [earlier]
    return kernel_call(
        kernel,
        "attend_back",
        29,
        (pairs,),
        [
            spec(0),
            spec(1),
            spec(2),
            spec(0),
            spec(0),
            pl.BlockSpec((1, 1, 2, 4 * tokens), lambda p: (slot, p, 0, 0)),
        ]
        + [pl.BlockSpec(memory_space=pl.ANY)] * len(before),
        pl.BlockSpec((4, 1, tokens, width), lambda p: (0, slot, 0, 0)),
        jax.ShapeDtypeStruct(qkv.shape, BF16),
        scratch=[pltpu.VMEM((4 * image, PAIR), F32), pltpu.VMEM((4 * text, PAIR), F32)] * 2,
        input_output_aliases={6: 0} if before else {},
    )(qkv, qkv, qkv, mixed, grads, logs, *before)


def normalize(values):
    average = jnp.mean(values, -1, keepdims=True)
    centred = values - average
    spread = jnp.mean(centred * centred, -1, keepdims=True)
    inverse = lax.rsqrt(spread + EPSILON)
    return centred * inverse, inverse


def norm_back(grad, normed, inverse, scale):
    scaled = grad * (1.0 + scale)
    return inverse * (
        scaled
        - jnp.mean(scaled, -1, keepdims=True)
        - normed * jnp.mean(scaled * normed, -1, keepdims=True)
    )


def add_up(values):
    return jnp.sum(values, 0, keepdims=True)


def per_slot(function, name, seqs, ins, outs):
    slots = ins[0].shape[0]

    def spec(shape, whole):
        rest = (0,) * (len(shape) - 1)
        if whole:
            return pl.BlockSpec(shape, lambda c, seqs: (0,) + rest)
        return pl.BlockSpec((1,) + tuple(shape[1:]), lambda c, seqs: (c,) + rest)

    def kernel(seqs, *refs):
        function((pl.program_id(0) < seqs[0]).astype(F32), *refs)

    return kernel_call(
        kernel,
        name,
        6,
        (slots,),
        [spec(value.shape, value.ndim == 2) for value in ins],
        [spec(shape, False) for shape, _ in outs],
        [jax.ShapeDtypeStruct(shape, dtype) for shape, dtype in outs],
        scalars=1,
    )(seqs, *ins)


def enter(live, image, text, image_cot, text_cot, vecs, first, mlp_round, sums):
    cut = image.shape[1]
    for s, (tokens, cot, rows) in enumerate(
        ((image, image_cot, slice(0, cut)), (text, text_cot, slice(cut, None)))
    ):
        normed, _ = normalize(tokens[0].astype(F32))
        first[0, rows] = (normed * (1.0 + vecs[0, s, 1:2]) + vecs[0, s, 0:1]).astype(BF16)
        rounded = (cot[0].astype(F32) * live * vecs[0, s, 5:6]).astype(BF16)
        mlp_round[0, rows] = rounded
        sums[0, s : s + 1] = add_up(rounded.astype(F32))


def middle(live, image, text, own, beside, across, vecs, bias, after, branch, second):
    cut = image.shape[1]
    for s, (tokens, rows) in enumerate(((image, slice(0, cut)), (text, slice(cut, None)))):
        value = own[0, rows].astype(F32) + beside[0, rows].astype(F32)
        value = value + across[0, rows].astype(F32) + bias[s : s + 1]
        result = tokens[0].astype(F32) + vecs[0, s, 2:3] * value
        normed, _ = normalize(result)
        branch[0, rows] = value
        after[0, rows] = result
        second[0, rows] = (normed * (1.0 + vecs[0, s, 4:5]) + vecs[0, s, 3:4]).astype(BF16)


def middle_back(
    live, image_cot, text_cot, own, beside, across, vecs, after, branch, residual, rounded, sums
):
    cut = image_cot.shape[1]
    for s, (cot, rows) in enumerate(((image_cot, slice(0, cut)), (text_cot, slice(cut, None)))):
        grad = own[0, rows].astype(F32) + beside[0, rows].astype(F32)
        grad = grad + across[0, rows].astype(F32)
        normed, inverse = normalize(after[0, rows])
        value = cot[0].astype(F32) * live + norm_back(grad, normed, inverse, vecs[0, s, 4:5])
        residual[0, rows] = value
        low = (value * vecs[0, s, 2:3]).astype(BF16)
        rounded[0, rows] = low
        sums[0, s, 0:1] = add_up(value * branch[0, rows])
        sums[0, s, 1:2] = add_up(grad)
        sums[0, s, 2:3] = add_up(grad * normed)
        sums[0, s, 3:4] = add_up(low.astype(F32))


def leave(
    live, image_cot, text_cot, own, beside, across, vecs, after, bias, image_out, text_out, sums
):
    cut = image_cot.shape[1]
    for s, (cot, rows, out) in enumerate(
        ((image_cot, slice(0, cut), image_out), (text_cot, slice(cut, None), text_out))
    ):
        value = own[0, rows].astype(F32) + beside[0, rows].astype(F32)
        value = value + across[0, rows].astype(F32) + bias[s : s + 1]
        out[0] = ((after[0, rows] + vecs[0, s, 5:6] * value) * live).astype(BF16)
        sums[0, s : s + 1] = add_up(cot[0].astype(F32) * live * value)


def enter_back(
    live, image, text, own, beside, across, vecs, residual, image_grad, text_grad, sums
):
    cut = image.shape[1]
    for s, (tokens, rows, out) in enumerate(
        ((image, slice(0, cut), image_grad), (text, slice(cut, None), text_grad))
    ):
        grad = own[0, rows].astype(F32) + beside[0, rows].astype(F32)
        grad = grad + across[0, rows].astype(F32)
        normed, inverse = normalize(tokens[0].astype(F32))
        out[0] = residual[0, rows] + norm_back(grad, normed, inverse, vecs[0, s, 1:2])
        sums[0, s, 0:1] = add_up(grad)
        sums[0, s, 1:2] = add_up(grad * normed)


def bias_spec(block):
    return pl.BlockSpec((2, block), lambda j: (0, j))


def add_bias(stream, spot, cut, sums, bias):
    return [sums + bias[stream : stream + 1]]


def gelu_both(stream, spot, cut, sums, bias):
    value = sums + bias[stream : stream + 1]
    factor = math.sqrt(2.0 / math.pi)
    square = value * value
    bend = jnp.tanh(factor * (value + 0.044715 * value * square))
    half = 0.5 * (1.0 + bend)
    slope = half + 0.5 * value * (1.0 - bend * bend) * factor * (1.0 + 0.134145 * square)
    return [value * half, slope]


def times_slope(stream, spot, cut, sums, slope):
    return [sums * slope[spot[0], spot[1], cut].astype(F32)]


def dot(spec, a, b):
    return jnp.einsum(spec, a, b, preferred_element_type=F32)


def on_device(
    groups,
    image_tokens,
    text_tokens,
    conditioning,
    group_seqs,
    ada_weight,
    ada_bias,
    qkv_weight,
    qv_bias,
    proj_weight,
    proj_bias,
    fc1_weight,
    fc1_bias,
    fc2_weight,
    fc2_bias,
    image_cot,
    text_cot,
):
    column = lax.axis_index("tensor")
    group = lax.axis_index("dp")
    ring = Ring(groups)
    order = Order(group_seqs)
    slots, image, width = image_tokens.shape
    text = text_tokens.shape[1]
    tokens = image + text
    rows = qkv_weight.shape[2]
    col_width = qkv_weight.shape[-1]
    hidden = fc1_weight.shape[-1]
    both = range(2)

    proj_turned = jnp.swapaxes(proj_weight, 1, 2)[:, None]
    fc1_shard = fc1_weight[:, None]
    fc2_turned = jnp.swapaxes(fc2_weight, 1, 2)[:, None]

    ada_part = lax.dynamic_slice_in_dim(ada_bias.astype(F32), column * col_width, col_width, 2)
    qv_part = lax.dynamic_slice_in_dim(qv_bias.astype(F32), column * col_width, col_width, 2)
    fc1_part = lax.dynamic_slice_in_dim(fc1_bias.astype(F32), column * hidden, hidden, 1)
    offsets = jnp.stack([qv_part[:, 0], jnp.zeros_like(qv_part[:, 0]), qv_part[:, 1]], 1)
    offsets = offsets.reshape(2, 3 * col_width)
    proj_add = proj_bias.astype(F32)
    fc2_add = fc2_bias.astype(F32)

    cond_act, silu_back = jax.vjp(jax.nn.silu, conditioning.astype(F32))
    cond_low = cond_act.astype(BF16).reshape(slots, groups, rows)
    cond_sends = jnp.stack(
        [
            lax.dynamic_index_in_dim(cond_low, group ^ mask, 1, keepdims=False)
            for mask in range(groups)
        ]
    )
    cond_rows = order(exchange(cond_sends, "dp", groups)).reshape(groups * slots, rows)
    modul_parts = order(dot("cd,sjdn->csjn", cond_rows, ada_weight))
    modul_parts = modul_parts.reshape((groups, slots) + modul_parts.shape[1:])
    modul_local = order(collect(modul_parts, "dp", groups) + ada_part[None])
    qkv_ring = Gather(ring, order(jnp.concatenate([qkv_weight, proj_turned], 1)))
    qkv_part = (0, 3 * col_width)
    proj_part = (3 * col_width, col_width)
    vecs = order(lax.all_gather(modul_local, "tensor", axis=3, tiled=True))

    first, mlp_round, fc2_bias_local = order.run(
        lambda *a: per_slot(
            enter,
            "enter",
            group_seqs,
            a,
            [
                ((slots, tokens, width), BF16),
                ((slots, tokens, width), BF16),
                ((slots, 2, width), F32),
            ],
        ),
        image_tokens,
        text_tokens,
        image_cot,
        text_cot,
        vecs,
    )
    qkv_ring.arrive(order)
    first_move = Spread(order(first))
    qkv_ring.arrive(order)
    qkv_ring.arrive(order)
    first_move.arrive(order)
    first_full = first_move.finish(order)
    qkv_ring.place(order)
    qkv_ring.arrive(order)
    fc1_ring = Gather(ring, order(fc1_shard))
    mlp_move = Spread(order(mlp_round))
    qkv_full = qkv_ring.finish(order)

    qkv = order.run(
        lambda *a: rows_times(
            a[:4], a[4:], image, False, 1, add_bias, (offsets,), (bias_spec,), qkv_part
        ),
        *first_full,
        *qkv_full,
    )
    fc1_ring.arrive(order)
    mixed = ()
    for slot in range(slots):
        mixed = order.run(
            lambda *a, slot=slot: attend(a[0], image, slot, a[1:]), *((qkv,) + tuple(mixed))
        )
    mixed, logs = mixed
    fc1_ring.arrive(order)
    mlp_move.arrive(order)
    branch_parts = order.run(
        lambda *a: rows_times(a[0], a[1:], image, True, "split", columns=proj_part),
        mixed,
        *qkv_full,
    )
    branch_move = Collect(*order(*branch_parts))
    mlp_full = mlp_move.finish(order)
    branch_move.arrive(order)
    fc1_ring.arrive(order)
    fc1_ring.arrive(order)
    fc2_ring = Gather(ring, order(fc2_turned))
    branch_terms = branch_move.finish(order)
    after, branch, second = order.run(
        lambda *a: per_slot(
            middle,
            "middle",
            group_seqs,
            a,
            [
                ((slots, tokens, width), F32),
                ((slots, tokens, width), F32),
                ((slots, tokens, width), BF16),
            ],
        ),
        image_tokens,
        text_tokens,
        *branch_terms,
        vecs,
        proj_add,
    )
    second_move = Spread(second)
    fc1_full = fc1_ring.finish(order)
    fc2_ring.arrive(order)
    fc2_ring.place(order)
    fc2_ring.arrive(order)
    second_move.arrive(order)
    second_full = second_move.finish(order)
    activated, slope = order.run(
        lambda *a: rows_times(
            a[:4], a[4:], image, False, 2, gelu_both, (fc1_part,), (bias_spec,)
        ),
        *second_full,
        *fc1_full,
    )
    fc2_ring.arrive(order)
    *fc2_grad, _ = order.run(
        lambda *a: weight_grad(a[:4], a[4], image, ring), *mlp_full, activated
    )
    fc2_ring.arrive(order)
    fc2_sums = Scatter(ring, *order(*fc2_grad))
    fc2_full = fc2_ring.finish(order)
    pre_round = order.run(
        lambda *a: rows_times(
            a[:4],
            a[4:],
            image,
            False,
            1,
            times_slope,
            (slope,),
            (
                lambda block: pl.BlockSpec(
                    (4, slots, tokens, block), lambda j: (0, 0, 0, j)
                ),
            ),
        ),
        *mlp_full,
        *fc2_full,
    )
    fc2_sums.arrive(order)
    second_parts = order.run(
        lambda *a: rows_times(a[0], a[1:], image, True, "split"), pre_round, *fc1_full
    )
    second_back = Collect(*second_parts)
    second_back.arrive(order)
    *fc1_grad, fc1_bias_local = order.run(
        lambda *a: weight_grad(a[:4], a[4], image, ring), *second_full, pre_round
    )
    fc1_sums = Scatter(ring, *order(*fc1_grad))
    mlp_parts = order.run(
        lambda *a: rows_times(a[0], a[1:], image, True, "split"), activated, *fc2_full
    )
    fc2_sums.arrive(order)
    second_terms = second_back.finish(order)
    residual, branch_round, middle_vecs = order.run(
        lambda *a: per_slot(
            middle_back,
            "middle_back",
            group_seqs,
            a,
            [
                ((slots, tokens, width), F32),
                ((slots, tokens, width), BF16),
                ((slots, 2, 4, width), F32),
            ],
        ),
        image_cot,
        text_cot,
        *second_terms,
        vecs,
        after,
        branch,
    )
    branch_back = Spread(branch_round)
    fc2_sums.arrive(order)
    fc1_sums.arrive(order)
    branch_back.arrive(order)
    branch_full = branch_back.finish(order)
    mixed_grad = order.run(
        lambda *a: rows_times(a[:4], a[4:], image, False, 1, columns=proj_part),
        *branch_full,
        *qkv_full,
    )
    mlp_back = Collect(*order(*mlp_parts))
    mlp_back.arrive(order)
    *proj_grad, _ = order.run(
        lambda *a: weight_grad(a[:4], a[4], image, ring, 3 * col_width, 4 * col_width),
        *branch_full,
        mixed,
    )
    qkv_grads = None
    for slot in range(slots):
        given = (qkv, mixed, mixed_grad, logs) + (() if slot == 0 else (qkv_grads,))
        qkv_grads = order.run(
            lambda *a, slot=slot: attend_back(
                *a[:4], image, slot, a[4] if len(a) > 4 else None
            ),
            *given,
        )
        if slot == 0:
            fc2_sums.arrive(order)
            fc1_sums.arrive(order)
    mlp_terms = mlp_back.finish(order)
    fc1_sums.arrive(order)
    *qkv_grad, qv_sums = order.run(
        lambda *a: weight_grad(
            a[:4], a[4], image, ring, 0, 4 * col_width, a[5:]
        ),
        *first_full,
        qkv_grads,
        *proj_grad,
    )
    fc1_sums.arrive(order)
    qkv_sums = Scatter(ring, *order(*qkv_grad), "parts")
    first_parts = order.run(
        lambda *a: rows_times(a[0], a[1:], image, True, "split", columns=qkv_part),
        qkv_grads,
        *qkv_full,
    )
    qkv_sums.arrive(order)
    first_back = Collect(*order(*first_parts))
    first_back.arrive(order)
    qv_bias_local = qv_sums.reshape(2, 3, col_width)[:, 0::2]
    proj_bias_local = jnp.sum(middle_vecs[:, :, 3], 0)
    fc2_bias_local = jnp.sum(fc2_bias_local, 0)
    split_sums = jnp.concatenate([qv_bias_local.reshape(-1), fc1_bias_local.reshape(-1)])
    token_sums = jnp.concatenate([proj_bias_local.reshape(-1), fc2_bias_local.reshape(-1)])
    bias_local = jnp.concatenate([split_sums, token_sums])
    image_out, text_out, gate_two = order.run(
        lambda *a: per_slot(
            leave,
            "leave",
            group_seqs,
            a,
            [
                (image_tokens.shape, BF16),
                (text_tokens.shape, BF16),
                ((slots, 2, width), F32),
            ],
        ),
        image_cot,
        text_cot,
        *mlp_terms,
        vecs,
        after,
        fc2_add,
    )
    fc2_sum = order(fc2_sums.finish(order))
    fc1_sum = order(fc1_sums.finish(order))
    qkv_sums.arrive(order)
    first_terms = first_back.finish(order)
    image_grad, text_grad, enter_vecs = order.run(
        lambda *a: per_slot(
            enter_back,
            "enter_back",
            group_seqs,
            a,
            [
                (image_tokens.shape, F32),
                (text_tokens.shape, F32),
                ((slots, 2, 2, width), F32),
            ],
        ),
        image_tokens,
        text_tokens,
        *first_terms,
        vecs,
        residual,
    )
    modul_grad = jnp.concatenate(
        [
            enter_vecs,
            middle_vecs[:, :, 0:3],
            gate_two[:, :, None],
        ],
        2,
    ).reshape(slots, 2, 6, 4, col_width)
    modul_blocks = jnp.stack(
        [
            lax.dynamic_index_in_dim(modul_grad, column ^ mask, 3, keepdims=False)
            for mask in range(4)
        ]
    )
    modul_round = order(collect(modul_blocks, "tensor", 4).astype(BF16))
    qkv_sums.arrive(order)
    shared = jnp.concatenate([modul_round.astype(F32).reshape(-1), bias_local])
    shared = order(spread(order(shared), "dp", groups))
    modul_all = shared[:, : modul_round.size].astype(BF16)
    modul_all = modul_all.reshape((groups * slots,) + modul_round.shape[1:])
    bias_local = jnp.sum(shared[:, modul_round.size :], 0)
    cond_part = dot("csjn,sjdn->cd", modul_all, ada_weight)
    ada_bias_part = jnp.sum(modul_all.astype(F32), 0)
    last = jnp.concatenate([cond_part.reshape(-1), ada_bias_part.reshape(-1), bias_local])
    last = order(spread(order(last), "tensor", 4))
    qkv_sums.arrive(order)
    last = order(last)
    cond_part = jnp.sum(last[:, : cond_part.size], 0).reshape(groups, slots, rows)
    cond_terms = order(exchange(cond_part, "dp", groups))
    cond_term = jnp.stack(
        [
            lax.dynamic_index_in_dim(cond_terms, group ^ place, 0, keepdims=False)
            for place in range(groups)
        ],
        1,
    ).reshape(slots, width)
    cond_grad = lax.dynamic_slice_in_dim(
        silu_back(cond_term)[0], column * col_width, col_width, 1
    )
    last = jnp.stack(
        [
            lax.dynamic_index_in_dim(last[:, cond_part.size :], column ^ place, 0, keepdims=False)
            for place in range(4)
        ]
    )
    ada_bias_grad = by_column(last[:, : ada_bias_part.size], ada_bias_part.shape)
    bias_all = last[:, ada_bias_part.size :]
    cut_a = qv_bias_local.size
    cut_b = cut_a + fc1_bias_local.size
    cut_c = cut_b + proj_bias_local.size
    cut_d = cut_c + fc2_bias_local.size

    qv_bias_grad = by_column(bias_all[:, :cut_a], qv_bias_local.shape)
    fc1_bias_grad = by_column(bias_all[:, cut_a:cut_b], fc1_bias_local.shape)
    proj_bias_grad = jnp.sum(bias_all[:, cut_b:cut_c], 0).reshape(proj_bias_local.shape)
    fc2_bias_grad = jnp.sum(bias_all[:, cut_c:cut_d], 0).reshape(fc2_bias_local.shape)
    ada_grad = dot("cd,csjn->sjdn", cond_rows, modul_all)
    qkv_sum, proj_sum = qkv_sums.finish(order)
    cond_grad = order(cond_grad)
    live = jnp.arange(slots, dtype=jnp.int32) < order.token[0]
    cond_grad = jnp.where(live[:, None], cond_grad, 0.0)
    return (
        image_out,
        text_out,
        image_grad,
        text_grad,
        cond_grad,
        ada_grad,
        ada_bias_grad,
        qkv_sum,
        qv_bias_grad,
        jnp.swapaxes(proj_sum, 1, 2),
        proj_bias_grad,
        fc1_sum,
        fc1_bias_grad,
        jnp.swapaxes(fc2_sum, 1, 2),
        fc2_bias_grad,
    )


def solution(mesh):
    groups = mesh.shape["dp"]
    in_specs = (
        P("dp", "tensor", None),
        P("dp", "tensor", None),
        P("dp", None),
        P("dp"),
        P(None, None, "dp", "tensor"),
        P(),
        P(None, None, "dp", "tensor"),
        P(),
        P(None, "tensor", "dp"),
        P(),
        P(None, "dp", "tensor"),
        P(),
        P(None, "tensor", "dp"),
        P(),
        P("dp", "tensor", None),
        P("dp", "tensor", None),
    )
    out_specs = (
        P("dp", "tensor", None),
        P("dp", "tensor", None),
        P("dp", "tensor", None),
        P("dp", "tensor", None),
        P("dp", "tensor"),
        P(None, None, "dp", "tensor"),
        P(),
        P(None, None, "dp", "tensor"),
        P(),
        P(None, "tensor", "dp"),
        P(),
        P(None, "dp", "tensor"),
        P(),
        P(None, "tensor", "dp"),
        P(),
    )

    def step(*args):
        return on_device(groups, *args)

    return jax.shard_map(
        step, mesh=mesh, in_specs=in_specs, out_specs=out_specs, check_vma=False
    )
```

```python
import math

import jax
import jax.numpy as jnp
from jax import lax
from jax.experimental import pallas as pl
from jax.experimental.pallas import tpu as pltpu
from jax.sharding import PartitionSpec as P

HEAD_DIM = 64
PAIR = 2 * HEAD_DIM
FACTOR = 1.0 / math.sqrt(HEAD_DIM)
VMEM = 60 << 20
FLOPS_PER_US = 460000000
EPSILON = 1e-06
F32 = jnp.float32
BF16 = jnp.bfloat16


def hop(value, axis, mask, size):
    return lax.ppermute(value, axis, [(i, i ^ mask) for i in range(size)])


def halves(size):
    low = 1
    while low * low < size:
        low *= 2
    return low, size // low


def spread(value, axis, size):
    low, high = halves(size)
    held = jnp.stack(
        [value] + [hop(value, axis, low * step, size) for step in range(1, high)]
    )
    full = [held] + [hop(held, axis, mask, size) for mask in range(1, low)]
    return jnp.stack(full, 1).reshape((size,) + value.shape)


def exchange(blocks, axis, size):
    low, high = halves(size)
    blocks = blocks.reshape((high, low) + blocks.shape[1:])
    held = jnp.stack(
        [blocks[0]] + [hop(blocks[step], axis, low * step, size) for step in range(1, high)]
    )
    full = [held[:, 0]] + [hop(held[:, mask], axis, mask, size) for mask in range(1, low)]
    return jnp.stack(full, 1).reshape((size,) + blocks.shape[2:])


def collect(blocks, axis, size):
    low, high = halves(size)
    blocks = blocks.reshape((high, low) + blocks.shape[1:])
    held = blocks[0] + sum(
        hop(blocks[step], axis, low * step, size) for step in range(1, high)
    )
    return held[0] + sum(hop(held[mask], axis, mask, size) for mask in range(1, low))


def by_column(block, shape):
    return jnp.moveaxis(block.reshape((4,) + shape), 0, -2).reshape(
        shape[:-1] + (4 * shape[-1],)
    )


class Order:
    def __init__(self, seed):
        self.token = seed

    def __call__(self, *values):
        self.token, *values = lax.optimization_barrier((self.token, *values))
        return values[0] if len(values) == 1 else values

    def run(self, function, *values):
        results = function(*self(*values)) if len(values) > 1 else function(self(*values))
        return self(*results) if isinstance(results, (tuple, list)) else self(results)


class Ring:
    def __init__(self, size):
        self.size = size
        self.order = list(range(0, size, 2)) + list(range(size - 1, 0, -2))
        self.ahead = [(self.order[i], self.order[(i + 1) % size]) for i in range(size)]
        self.back = [(b, a) for a, b in self.ahead]
        place = [0] * size
        for position, device in enumerate(self.order):
            place[device] = position
        self.mine = jnp.asarray(place, jnp.int32)[lax.axis_index("dp")]
        self.table = jnp.asarray(self.order, jnp.int32)

    def devices(self, distances):
        return self.table[(self.mine + jnp.asarray(distances, jnp.int32)) % self.size]

    def forward(self, value):
        return lax.ppermute(value, "dp", self.ahead)

    def backward(self, value):
        return lax.ppermute(value, "dp", self.back)


class Gather:
    def __init__(self, ring, shard):
        self.ring, self.step = ring, 0
        self.pieces, self.distances, self.streams = [shard], [0], [0]
        self.placed, self.full = 0, ()
        self.send(shard, shard)

    def send(self, ahead, back):
        self.step += 1
        if self.step == self.ring.size // 2:
            ahead, back = ahead[:1], back[1:]
        self.moving = (self.ring.forward(ahead), self.ring.backward(back))

    def arrive(self, order):
        ahead, back = order(*self.moving)
        last = self.step == self.ring.size // 2
        self.pieces += [ahead, back]
        self.distances += [-self.step, self.step]
        self.streams += [0, 1 if last else 0]
        if not last:
            self.send(ahead, back)
        return last

    def finish(self, order):
        while len(self.pieces) < self.ring.size + 1:
            self.arrive(order)
        self.place(order)
        return [f.reshape(-1, f.shape[2]) for f in self.full]

    def place(self, order):
        new = slice(self.placed, None)
        places = self.ring.devices(self.distances[new])
        self.full = order(
            *assemble(self.pieces[new], self.streams[new], places, self.ring.size, self.full)
        )
        self.placed = len(self.pieces)


class Scatter:
    def __init__(self, ring, image, text, far_image, far_text, form="plain"):
        self.ring, self.image, self.text, self.form = ring, image, text, form
        self.left = ring.size // 2
        self.moving = (ring.forward(far_image), ring.backward(far_text))

    def arrive(self, order):
        self.take(order)
        self.add(order)

    def take(self, order):
        self.taken = order(*self.moving)
        self.left -= 1

    def add(self, order):
        ahead, back = order(*self.taken)
        places = self.ring.devices([self.left, -self.left])
        if self.left == 0:
            self.total = ring_total(self.image, self.text, ahead, back, places, self.form)
            return
        ahead, back = order(*ring_add(self.image, self.text, ahead, back, places))
        self.moving = (self.ring.forward(ahead), self.ring.backward(back))

    def finish(self, order):
        while self.left:
            self.arrive(order)
        return self.total


def kernel_call(kernel, name, cost_us, grid, in_specs, out_specs, out_shape, scalars=0, **more):
    return pl.pallas_call(
        kernel,
        grid_spec=pltpu.PrefetchScalarGridSpec(
            num_scalar_prefetch=scalars,
            grid=grid,
            in_specs=in_specs,
            out_specs=out_specs,
            scratch_shapes=more.pop("scratch", ()),
        ),
        out_shape=out_shape,
        compiler_params=pltpu.CompilerParams(vmem_limit_bytes=VMEM),
        cost_estimate=pl.CostEstimate(
            flops=int(cost_us * FLOPS_PER_US), bytes_accessed=1, transcendentals=0
        ),
        name=name,
        **more,
    )


def assemble(pieces, streams, places, size, earlier):
    count = len(pieces)
    parts, rows, width = pieces[0].shape[1:]
    moves = [
        (i, streams[i] + s, s, part)
        for i in range(count)
        for s in range(pieces[i].shape[0])
        for part in range(parts)
    ]

    def kernel(place, *refs):
        shards, refs = refs[:count], refs[count + len(earlier) :]
        full, held, sems_in, sems_out = refs[:2], refs[2:-2], refs[-2], refs[-1]
        ins = [pltpu.make_async_copy(shards[i], held[i], sems_in.at[i]) for i in range(count)]
        for copy in ins:
            copy.start()
        outs, last = [], -1
        for m, (i, stream, s, part) in enumerate(moves):
            if i != last:
                ins[i].wait()
                last = i
            spot = full[stream].at[place[i], :, pl.ds(part * width, width)]
            outs.append(pltpu.make_async_copy(held[i].at[s, part], spot, sems_out.at[m]))
            outs[-1].start()
        for copy in outs:
            copy.wait()

    whole = pl.BlockSpec(memory_space=pltpu.HBM)
    out = jax.ShapeDtypeStruct((size, rows, parts * width), BF16)
    return kernel_call(
        kernel,
        "assemble",
        1 + 3e-7 * sum(math.prod(p.shape) for p in pieces),
        (1,),
        [whole] * (count + len(earlier)),
        [whole] * 2,
        [out] * 2,
        scalars=1,
        scratch=[pltpu.VMEM(p.shape, p.dtype) for p in pieces]
        + [pltpu.SemaphoreType.DMA((count,)), pltpu.SemaphoreType.DMA((len(moves),))],
        input_output_aliases={count + 1: 0, count + 2: 1} if earlier else {},
    )(places, *pieces, *earlier)


def ring_specs(image, ahead, back, block):
    width = image.shape[2]

    def local(which):
        return pl.BlockSpec((1, block, width), lambda i, place: (place[which], i, 0))

    def moved(value):
        return pl.BlockSpec((value.shape[0], block, width), lambda i, place: (0, i, 0))

    return [local(0), local(0), local(1), local(1), moved(ahead), moved(back)]


def ring_add(image, text, ahead, back, places):
    size, rows, width = image.shape
    block = rows // 4 if rows % 64 == 0 else rows
    whole = ahead.shape[0] == 2

    def kernel(place, image_a, text_a, image_b, text_b, ahead, back, send_a, send_b):
        send_a[0] = (image_a[0].astype(F32) + ahead[0].astype(F32)).astype(BF16)
        send_b[1] = (text_b[0].astype(F32) + back[back.shape[0] - 1].astype(F32)).astype(BF16)
        if whole:
            send_a[1] = (text_a[0].astype(F32) + ahead[1].astype(F32)).astype(BF16)
            send_b[0] = (image_b[0].astype(F32) + back[0].astype(F32)).astype(BF16)
        else:
            send_a[1] = text_a[0]
            send_b[0] = image_b[0]

    out = pl.BlockSpec((2, block, width), lambda i, place: (0, i, 0))
    return kernel_call(
        kernel,
        "ring_add",
        1 + 7e-6 * image.shape[1] * image.shape[2] * 2,
        (rows // block,),
        ring_specs(image, ahead, back, block),
        [out] * 2,
        [jax.ShapeDtypeStruct((2, rows, width), BF16)] * 2,
        scalars=1,
    )(places, image, text, image, text, ahead, back)


def ring_total(image, text, ahead, back, places, form):
    size, rows, width = image.shape
    block = rows // 4 if rows % 64 == 0 else rows
    part = width // 4

    def kernel(place, image_a, text_a, image_b, text_b, ahead, back, total, *more):
        for s, mine in enumerate((image_a, text_a)):
            value = mine[0].astype(F32) + ahead[s].astype(F32) + back[s].astype(F32)
            if form == "parts":
                for j in range(3):
                    total[s, j] = value[:, j * part : (j + 1) * part]
                more[0][s] = value[:, 3 * part :]
            else:
                total[s] = value

    shapes = {
        "plain": [(2, rows, width)],
        "parts": [(2, 3, rows, part), (2, rows, part)],
    }[form]
    outs = [
        pl.BlockSpec(
            shape[:-2] + (block, shape[-1]),
            lambda i, place, lead=len(shape) - 2: (0,) * lead + (i, 0),
        )
        for shape in shapes
    ]
    total = kernel_call(
        kernel,
        "ring_total",
        1 + 7e-6 * image.shape[1] * image.shape[2] * 2,
        (rows // block,),
        ring_specs(image, ahead, back, block),
        outs,
        [jax.ShapeDtypeStruct(shape, F32) for shape in shapes],
        scalars=1,
    )(places, image, text, image, text, ahead, back)
    return total if form == "parts" else total[0]


class Spread:
    def __init__(self, part):
        self.part = part
        self.across = hop(part, "tensor", 2, 4)
        self.beside = hop(part, "tensor", 1, 4)

    def arrive(self, order):
        self.across, self.beside = order(self.across, self.beside)
        self.corner = hop(self.across, "tensor", 1, 4)

    def finish(self, order):
        return [self.part, self.beside, self.across, order(self.corner)]


class Collect:
    def __init__(self, own, beside, across, corner):
        self.own, self.kept = own, across
        self.corner = hop(corner, "tensor", 1, 4)
        self.beside = hop(beside, "tensor", 1, 4)

    def arrive(self, order):
        corner = order(self.corner)
        send = (self.kept.astype(F32) + corner.astype(F32)).astype(BF16)
        self.across = hop(order(send), "tensor", 2, 4)
        self.beside = order(self.beside)

    def finish(self, order):
        return [self.own, self.beside, order(self.across)]


def piece_specs(pieces, block=None):
    if isinstance(pieces, (list, tuple)):
        shape = pieces[0].shape
        spec = pl.BlockSpec(shape, lambda j, *_: (0, 0, 0), pipeline_mode=pl.Buffered(1))
        return [spec] * 4, list(pieces), shape
    shape = pieces.shape[1:]
    specs = [
        pl.BlockSpec(
            (None,) + shape, lambda j, *_, k=k: (k, 0, 0, 0), pipeline_mode=pl.Buffered(1)
        )
        for k in range(4)
    ]
    return specs, [pieces] * 4, shape


def column_block(width):
    for block in (512, 384, 256, 128):
        if width % block == 0:
            return block
    return width


def rows_times(
    pieces, weights, image, turned, outputs, finish=None, extras=(), extra_specs=(), columns=None
):
    specs, arrays, (slots, tokens, depth) = piece_specs(pieces)
    start, count = columns or (0, weights[0].shape[1])
    width = weights[0].shape[0] if turned else count
    block = column_block(math.gcd(start, width))
    text = tokens - image
    spots = [(k, c) for k in range(4) for c in range(slots)]
    dims = DOT_NT if turned else DOT_NN
    split = outputs == "split"
    count = 4 if split else outputs

    def kernel(*refs):
        rows, (image_w, text_w) = refs[:4], refs[4:6]
        more, outs = refs[6 : 6 + len(extras)], refs[6 + len(extras) :]

        def store(stream, spot, sums):
            k, c = spot
            cut = slice(0, image) if stream == 0 else slice(image, tokens)
            values = [sums] if finish is None else finish(stream, spot, cut, sums, *more)
            for which, value in enumerate(values):
                if split:
                    outs[k][c, cut] = value.astype(BF16)
                else:
                    outs[which][k, c, cut] = value.astype(BF16)

        for spot in spots:
            store(0, spot, mul(rows[spot[0]][spot[1], :image], image_w[...], dims))
        joined = jnp.concatenate([rows[k][c, image:] for k, c in spots], 0)
        sums = mul(joined, text_w[...], dims)
        for i, spot in enumerate(spots):
            store(1, spot, sums[i * text : (i + 1) * text])

    if turned:
        weight = pl.BlockSpec((block, depth), lambda j: (j, start // depth))
    else:
        weight = pl.BlockSpec((depth, block), lambda j: (0, start // block + j))
    if split:
        out = pl.BlockSpec((slots, tokens, block), lambda j: (0, 0, j))
        shape = jax.ShapeDtypeStruct((slots, tokens, width), BF16)
    else:
        out = pl.BlockSpec((4, slots, tokens, block), lambda j: (0, 0, 0, j))
        shape = jax.ShapeDtypeStruct((4, slots, tokens, width), BF16)
    return kernel_call(
        kernel,
        "rows_times",
        1 + 3e-9 * 4 * slots * tokens * depth * width,
        (width // block,),
        specs + [weight, weight] + [make(block) for make in extra_specs],
        [out] * count,
        [shape] * count,
    )(*arrays, *weights, *extras)


def weight_grad(pieces, grads, image, ring, first=0, total=None, earlier=()):
    size = ring.size
    far = ring.devices([size // 2])
    specs, arrays, (slots, tokens, depth) = piece_specs(pieces)
    width = grads.shape[3]
    block = column_block(math.gcd(first, width))
    text = tokens - image
    spots = [(k, c) for k in range(4) for c in range(slots)]

    def kernel(far, a, b, c, d, grad, *refs):
        rows = (a, b, c, d)
        image_out, text_out, far_image, far_text, sums, image_turned, text_turned = refs[-7:]

        @pl.when(pl.program_id(0) == 0)
        def _():
            for i, (k, s) in enumerate(spots):
                image_turned[:, pl.ds(i * image, image)] = jnp.transpose(rows[k][s, :image])
            text_turned[...] = jnp.transpose(
                jnp.concatenate([rows[k][s, image:] for k, s in spots], 0)
            )

        image_grads = jnp.concatenate([grad[k, s, :image] for k, s in spots], 0)
        text_grads = jnp.concatenate([grad[k, s, image:] for k, s in spots], 0)
        image_out[...] = (
            mul(image_turned[...], image_grads, DOT_NN).astype(BF16).reshape(image_out.shape)
        )
        text_out[...] = (
            mul(text_turned[...], text_grads, DOT_NN).astype(BF16).reshape(text_out.shape)
        )
        far_image[0] = image_out[far[0]]
        far_text[0] = text_out[far[0]]
        sums[0:1] = jnp.sum(image_grads.astype(F32), 0, keepdims=True)
        sums[1:2] = jnp.sum(text_grads.astype(F32), 0, keepdims=True)

    outs, shapes = [], []
    for count in (size, size, 1, 1):
        outs.append(
            pl.BlockSpec(
                (count, depth // size, block), lambda j, *_: (0, 0, first // block + j)
            )
        )
        shapes.append(jax.ShapeDtypeStruct((count, depth // size, total or width), BF16))
    return kernel_call(
        kernel,
        "weight_grad",
        1 + 3.4e-9 * 4 * slots * tokens * depth * width,
        (width // block,),
        specs
        + [pl.BlockSpec((4, slots, tokens, block), lambda j, *_: (0, 0, 0, j))]
        + [pl.BlockSpec(memory_space=pl.ANY)] * len(earlier),
        outs + [pl.BlockSpec((2, block), lambda j, *_: (0, j))],
        shapes + [jax.ShapeDtypeStruct((2, width), F32)],
        scalars=1,
        scratch=[
            pltpu.VMEM((depth, len(spots) * image), BF16),
            pltpu.VMEM((depth, len(spots) * text), BF16),
        ],
        input_output_aliases={6 + i: i for i in range(len(earlier))},
    )(far, *arrays, grads, *earlier)


def mul(a, b, dims):
    return lax.dot_general(a, b, dims, preferred_element_type=F32)


DOT_NN = (((1,), (0,)), ((), ()))
DOT_NT = (((1,), (1,)), ((), ()))
DOT_TN = (((0,), (0,)), ((), ()))


def lane_masks(dtype):
    lane = lax.broadcasted_iota(jnp.int32, (1, PAIR), 1)
    low = (lane < HEAD_DIM).astype(F32)
    return [low.astype(dtype), (1.0 - low).astype(dtype)]


def stream_rows(ref, image, stream):
    cut = slice(0, image) if stream == 0 else slice(image, ref.shape[2])
    return jnp.concatenate([ref[k, 0, cut] for k in range(4)], 0)


def query_blocks(image, text):
    return [(0, (0, 1), 0), (0, (2, 3), 2 * image), (1, (0, 1, 2, 3), 4 * image)]


def attend(qkv, image, slot, earlier):
    _, slots, tokens, width = qkv.shape
    text, pairs = tokens - image, width // (3 * PAIR)

    def kernel(q, k, v, *refs):
        out, logs_out = refs[-2:]
        keys = [stream_rows(k, image, s) for s in range(2)]
        values = [stream_rows(v, image, s) for s in range(2)]
        masks = lane_masks(F32)
        low = [m.astype(BF16) for m in masks]
        for stream, members, place in query_blocks(image, text):
            cut = slice(0, image) if stream == 0 else slice(image, tokens)
            size = image if stream == 0 else text
            query = jnp.concatenate([q[m, 0, cut] for m in members], 0)
            query = query * jnp.asarray(FACTOR, BF16)
            total = logs = None
            for head in range(2):
                scores = [mul(query * low[head], key, DOT_NT) for key in keys]
                top = jnp.maximum(
                    jnp.max(scores[0], -1, keepdims=True), jnp.max(scores[1], -1, keepdims=True)
                )
                probs = [jnp.exp(s - top) for s in scores]
                denom = jnp.sum(probs[0], -1, keepdims=True) + jnp.sum(
                    probs[1], -1, keepdims=True
                )
                mixed = mul(probs[0].astype(BF16), values[0], DOT_NN) + mul(
                    probs[1].astype(BF16), values[1], DOT_NN
                )
                mixed = mixed * (masks[head] / denom)
                log = (top + jnp.log(denom)) * masks[head]
                total = mixed if total is None else total + mixed
                logs = log if logs is None else logs + log
            for i, m in enumerate(members):
                out[m, 0, cut] = total[i * size : (i + 1) * size].astype(BF16)
            turned = jnp.transpose(logs)
            span = pl.ds(place, size * len(members))
            logs_out[0, 0, 0:1, span] = turned[0:1]
            logs_out[0, 0, 1:2, span] = turned[HEAD_DIM : HEAD_DIM + 1]

    def spec(which):
        return pl.BlockSpec((4, 1, tokens, PAIR), lambda p: (0, slot, 0, which * pairs + p))

    total = 4 * tokens
    return kernel_call(
        kernel,
        "attend",
        15,
        (pairs,),
        [spec(0), spec(1), spec(2)] + [pl.BlockSpec(memory_space=pl.ANY)] * len(earlier),
        [spec(0), pl.BlockSpec((1, 1, 2, total), lambda p: (slot, p, 0, 0))],
        [
            jax.ShapeDtypeStruct((4, slots, tokens, pairs * PAIR), BF16),
            jax.ShapeDtypeStruct((slots, pairs, 2, total), F32),
        ],
        input_output_aliases={3: 0, 4: 1} if earlier else {},
    )(qkv, qkv, qkv, *earlier)


def attend_back(qkv, mixed, grads, logs, image, slot, earlier):
    _, slots, tokens, width = qkv.shape
    text, pairs = tokens - image, width // (3 * PAIR)

    def kernel(q, k, v, mixed, grads, logs, *refs):
        out, key_image, key_text, value_image, value_text = refs[-5:]
        key_sums, value_sums = (key_image, key_text), (value_image, value_text)
        keys = [stream_rows(k, image, s) for s in range(2)]
        values = [stream_rows(v, image, s) for s in range(2)]
        low = lane_masks(BF16)
        pair = pl.program_id(0)

        def lanes(which):
            return pl.ds(pl.multiple_of((which * pairs + pair) * PAIR, PAIR), PAIR)

        first = True
        for stream, members, place in query_blocks(image, text):
            cut = slice(0, image) if stream == 0 else slice(image, tokens)
            size = image if stream == 0 else text
            query = jnp.concatenate([q[m, 0, cut] for m in members], 0)
            query = query * jnp.asarray(FACTOR, BF16)
            grad = jnp.concatenate([grads[m, 0, cut] for m in members], 0)
            output = jnp.concatenate([mixed[m, 0, cut] for m in members], 0)
            inner = jnp.transpose(grad.astype(F32) * output.astype(F32))
            query_grad = None
            for head in range(2):
                head_q, head_g = query * low[head], grad * low[head]
                half = slice(head * HEAD_DIM, (head + 1) * HEAD_DIM)
                delta = jnp.sum(inner[half], 0, keepdims=True)
                log = logs[0, 0, head : head + 1, pl.ds(place, size * len(members))]
                for part in range(2):
                    probs = jnp.exp(mul(keys[part], head_q, DOT_NT) - log)
                    prob_grad = mul(values[part], head_g, DOT_NT)
                    score_grad = (probs * (prob_grad - delta)).astype(BF16)
                    value_part = mul(probs.astype(BF16), head_g, DOT_NN)
                    key_part = mul(score_grad, head_q, DOT_NN)
                    query_part = mul(score_grad, keys[part] * low[head], DOT_TN)
                    query_grad = query_part if query_grad is None else query_grad + query_part
                    if first:
                        value_sums[part][...] = value_part
                        key_sums[part][...] = key_part
                    else:
                        value_sums[part][...] += value_part
                        key_sums[part][...] += key_part
                first = False
            query_grad = query_grad * FACTOR
            for i, m in enumerate(members):
                out[m, 0, cut, lanes(0)] = query_grad[i * size : (i + 1) * size].astype(BF16)
        for which, sums in ((1, key_sums), (2, value_sums)):
            for m in range(4):
                out[m, 0, :image, lanes(which)] = sums[0][
                    m * image : (m + 1) * image
                ].astype(BF16)
                out[m, 0, image:, lanes(which)] = sums[1][m * text : (m + 1) * text].astype(BF16)

    def spec(which):
        return pl.BlockSpec((4, 1, tokens, PAIR), lambda p: (0, slot, 0, which * pairs + p))

    before = [] if earlier is None else [earlier]
    return kernel_call(
        kernel,
        "attend_back",
        29,
        (pairs,),
        [
            spec(0),
            spec(1),
            spec(2),
            spec(0),
            spec(0),
            pl.BlockSpec((1, 1, 2, 4 * tokens), lambda p: (slot, p, 0, 0)),
        ]
        + [pl.BlockSpec(memory_space=pl.ANY)] * len(before),
        pl.BlockSpec((4, 1, tokens, width), lambda p: (0, slot, 0, 0)),
        jax.ShapeDtypeStruct(qkv.shape, BF16),
        scratch=[pltpu.VMEM((4 * image, PAIR), F32), pltpu.VMEM((4 * text, PAIR), F32)] * 2,
        input_output_aliases={6: 0} if before else {},
    )(qkv, qkv, qkv, mixed, grads, logs, *before)


def normalize(values):
    average = jnp.mean(values, -1, keepdims=True)
    centred = values - average
    spread = jnp.mean(centred * centred, -1, keepdims=True)
    inverse = lax.rsqrt(spread + EPSILON)
    return centred * inverse, inverse


def norm_back(grad, normed, inverse, scale):
    scaled = grad * (1.0 + scale)
    return inverse * (
        scaled
        - jnp.mean(scaled, -1, keepdims=True)
        - normed * jnp.mean(scaled * normed, -1, keepdims=True)
    )


def add_up(values):
    return jnp.sum(values, 0, keepdims=True)


def per_slot(function, name, seqs, ins, outs):
    slots = ins[0].shape[0]

    def spec(shape, whole):
        rest = (0,) * (len(shape) - 1)
        if whole:
            return pl.BlockSpec(shape, lambda c, seqs: (0,) + rest)
        return pl.BlockSpec((1,) + tuple(shape[1:]), lambda c, seqs: (c,) + rest)

    def kernel(seqs, *refs):
        function((pl.program_id(0) < seqs[0]).astype(F32), *refs)

    return kernel_call(
        kernel,
        name,
        6,
        (slots,),
        [spec(value.shape, value.ndim == 2) for value in ins],
        [spec(shape, False) for shape, _ in outs],
        [jax.ShapeDtypeStruct(shape, dtype) for shape, dtype in outs],
        scalars=1,
    )(seqs, *ins)


def enter(live, image, text, image_cot, text_cot, vecs, first, mlp_round, sums):
    cut = image.shape[1]
    for s, (tokens, cot, rows) in enumerate(
        ((image, image_cot, slice(0, cut)), (text, text_cot, slice(cut, None)))
    ):
        normed, _ = normalize(tokens[0].astype(F32))
        first[0, rows] = (normed * (1.0 + vecs[0, s, 1:2]) + vecs[0, s, 0:1]).astype(BF16)
        rounded = (cot[0].astype(F32) * live * vecs[0, s, 5:6]).astype(BF16)
        mlp_round[0, rows] = rounded
        sums[0, s : s + 1] = add_up(rounded.astype(F32))


def middle(live, image, text, own, beside, across, vecs, bias, after, branch, second):
    cut = image.shape[1]
    for s, (tokens, rows) in enumerate(((image, slice(0, cut)), (text, slice(cut, None)))):
        value = own[0, rows].astype(F32) + beside[0, rows].astype(F32)
        value = value + across[0, rows].astype(F32) + bias[s : s + 1]
        result = tokens[0].astype(F32) + vecs[0, s, 2:3] * value
        normed, _ = normalize(result)
        branch[0, rows] = value
        after[0, rows] = result
        second[0, rows] = (normed * (1.0 + vecs[0, s, 4:5]) + vecs[0, s, 3:4]).astype(BF16)


def middle_back(
    live, image_cot, text_cot, own, beside, across, vecs, after, branch, residual, rounded, sums
):
    cut = image_cot.shape[1]
    for s, (cot, rows) in enumerate(((image_cot, slice(0, cut)), (text_cot, slice(cut, None)))):
        grad = own[0, rows].astype(F32) + beside[0, rows].astype(F32)
        grad = grad + across[0, rows].astype(F32)
        normed, inverse = normalize(after[0, rows])
        value = cot[0].astype(F32) * live + norm_back(grad, normed, inverse, vecs[0, s, 4:5])
        residual[0, rows] = value
        low = (value * vecs[0, s, 2:3]).astype(BF16)
        rounded[0, rows] = low
        sums[0, s, 0:1] = add_up(value * branch[0, rows])
        sums[0, s, 1:2] = add_up(grad)
        sums[0, s, 2:3] = add_up(grad * normed)
        sums[0, s, 3:4] = add_up(low.astype(F32))


def leave(
    live, image_cot, text_cot, own, beside, across, vecs, after, bias, image_out, text_out, sums
):
    cut = image_cot.shape[1]
    for s, (cot, rows, out) in enumerate(
        ((image_cot, slice(0, cut), image_out), (text_cot, slice(cut, None), text_out))
    ):
        value = own[0, rows].astype(F32) + beside[0, rows].astype(F32)
        value = value + across[0, rows].astype(F32) + bias[s : s + 1]
        out[0] = ((after[0, rows] + vecs[0, s, 5:6] * value) * live).astype(BF16)
        sums[0, s : s + 1] = add_up(cot[0].astype(F32) * live * value)


def enter_back(
    live, image, text, own, beside, across, vecs, residual, image_grad, text_grad, sums
):
    cut = image.shape[1]
    for s, (tokens, rows, out) in enumerate(
        ((image, slice(0, cut), image_grad), (text, slice(cut, None), text_grad))
    ):
        grad = own[0, rows].astype(F32) + beside[0, rows].astype(F32)
        grad = grad + across[0, rows].astype(F32)
        normed, inverse = normalize(tokens[0].astype(F32))
        out[0] = residual[0, rows] + norm_back(grad, normed, inverse, vecs[0, s, 1:2])
        sums[0, s, 0:1] = add_up(grad)
        sums[0, s, 1:2] = add_up(grad * normed)


def bias_spec(block):
    return pl.BlockSpec((2, block), lambda j: (0, j))


def add_bias(stream, spot, cut, sums, bias):
    return [sums + bias[stream : stream + 1]]


def gelu_both(stream, spot, cut, sums, bias):
    value = sums + bias[stream : stream + 1]
    factor = math.sqrt(2.0 / math.pi)
    square = value * value
    bend = jnp.tanh(factor * (value + 0.044715 * value * square))
    half = 0.5 * (1.0 + bend)
    slope = half + 0.5 * value * (1.0 - bend * bend) * factor * (1.0 + 0.134145 * square)
    return [value * half, slope]


def times_slope(stream, spot, cut, sums, slope):
    return [sums * slope[spot[0], spot[1], cut].astype(F32)]


def dot(spec, a, b):
    return jnp.einsum(spec, a, b, preferred_element_type=F32)


def on_device(
    groups,
    image_tokens,
    text_tokens,
    conditioning,
    group_seqs,
    ada_weight,
    ada_bias,
    qkv_weight,
    qv_bias,
    proj_weight,
    proj_bias,
    fc1_weight,
    fc1_bias,
    fc2_weight,
    fc2_bias,
    image_cot,
    text_cot,
):
    column = lax.axis_index("tensor")
    group = lax.axis_index("dp")
    ring = Ring(groups)
    order = Order(group_seqs)
    slots, image, width = image_tokens.shape
    text = text_tokens.shape[1]
    tokens = image + text
    rows = qkv_weight.shape[2]
    col_width = qkv_weight.shape[-1]
    hidden = fc1_weight.shape[-1]
    both = range(2)

    proj_turned = jnp.swapaxes(proj_weight, 1, 2)[:, None]
    fc1_shard = fc1_weight[:, None]
    fc2_turned = jnp.swapaxes(fc2_weight, 1, 2)[:, None]

    ada_part = lax.dynamic_slice_in_dim(ada_bias.astype(F32), column * col_width, col_width, 2)
    qv_part = lax.dynamic_slice_in_dim(qv_bias.astype(F32), column * col_width, col_width, 2)
    fc1_part = lax.dynamic_slice_in_dim(fc1_bias.astype(F32), column * hidden, hidden, 1)
    offsets = jnp.stack([qv_part[:, 0], jnp.zeros_like(qv_part[:, 0]), qv_part[:, 1]], 1)
    offsets = offsets.reshape(2, 3 * col_width)
    proj_add = proj_bias.astype(F32)
    fc2_add = fc2_bias.astype(F32)

    cond_act, silu_back = jax.vjp(jax.nn.silu, conditioning.astype(F32))
    cond_low = cond_act.astype(BF16).reshape(slots, groups, rows)
    cond_sends = jnp.stack(
        [
            lax.dynamic_index_in_dim(cond_low, group ^ mask, 1, keepdims=False)
            for mask in range(groups)
        ]
    )
    cond_rows = order(exchange(cond_sends, "dp", groups)).reshape(groups * slots, rows)
    modul_parts = order(dot("cd,sjdn->csjn", cond_rows, ada_weight))
    modul_parts = modul_parts.reshape((groups, slots) + modul_parts.shape[1:])
    modul_local = order(collect(modul_parts, "dp", groups) + ada_part[None])
    qkv_ring = Gather(ring, order(jnp.concatenate([qkv_weight, proj_turned], 1)))
    qkv_part = (0, 3 * col_width)
    proj_part = (3 * col_width, col_width)
    vecs = order(lax.all_gather(modul_local, "tensor", axis=3, tiled=True))

    first, mlp_round, fc2_bias_local = order.run(
        lambda *a: per_slot(
            enter,
            "enter",
            group_seqs,
            a,
            [
                ((slots, tokens, width), BF16),
                ((slots, tokens, width), BF16),
                ((slots, 2, width), F32),
            ],
        ),
        image_tokens,
        text_tokens,
        image_cot,
        text_cot,
        vecs,
    )
    qkv_ring.arrive(order)
    first_move = Spread(order(first))
    qkv_ring.arrive(order)
    qkv_ring.arrive(order)
    first_move.arrive(order)
    first_full = first_move.finish(order)
    qkv_ring.place(order)
    qkv_ring.arrive(order)
    fc1_ring = Gather(ring, order(fc1_shard))
    mlp_move = Spread(order(mlp_round))
    qkv_full = qkv_ring.finish(order)

    qkv = order.run(
        lambda *a: rows_times(
            a[:4], a[4:], image, False, 1, add_bias, (offsets,), (bias_spec,), qkv_part
        ),
        *first_full,
        *qkv_full,
    )
    fc1_ring.arrive(order)
    mixed = ()
    for slot in range(slots):
        mixed = order.run(
            lambda *a, slot=slot: attend(a[0], image, slot, a[1:]), *((qkv,) + tuple(mixed))
        )
    mixed, logs = mixed
    fc1_ring.arrive(order)
    mlp_move.arrive(order)
    branch_parts = order.run(
        lambda *a: rows_times(a[0], a[1:], image, True, "split", columns=proj_part),
        mixed,
        *qkv_full,
    )
    branch_move = Collect(*order(*branch_parts))
    mlp_full = mlp_move.finish(order)
    branch_move.arrive(order)
    fc1_ring.arrive(order)
    fc1_ring.arrive(order)
    fc2_ring = Gather(ring, order(fc2_turned))
    branch_terms = branch_move.finish(order)
    after, branch, second = order.run(
        lambda *a: per_slot(
            middle,
            "middle",
            group_seqs,
            a,
            [
                ((slots, tokens, width), F32),
                ((slots, tokens, width), F32),
                ((slots, tokens, width), BF16),
            ],
        ),
        image_tokens,
        text_tokens,
        *branch_terms,
        vecs,
        proj_add,
    )
    second_move = Spread(second)
    fc1_full = fc1_ring.finish(order)
    fc2_ring.arrive(order)
    fc2_ring.place(order)
    fc2_ring.arrive(order)
    second_move.arrive(order)
    second_full = second_move.finish(order)
    activated, slope = order.run(
        lambda *a: rows_times(
            a[:4], a[4:], image, False, 2, gelu_both, (fc1_part,), (bias_spec,)
        ),
        *second_full,
        *fc1_full,
    )
    fc2_ring.arrive(order)
    *fc2_grad, _ = order.run(
        lambda *a: weight_grad(a[:4], a[4], image, ring), *mlp_full, activated
    )
    fc2_ring.arrive(order)
    fc2_sums = Scatter(ring, *order(*fc2_grad))
    fc2_full = fc2_ring.finish(order)
    pre_round = order.run(
        lambda *a: rows_times(
            a[:4],
            a[4:],
            image,
            False,
            1,
            times_slope,
            (slope,),
            (
                lambda block: pl.BlockSpec(
                    (4, slots, tokens, block), lambda j: (0, 0, 0, j)
                ),
            ),
        ),
        *mlp_full,
        *fc2_full,
    )
    fc2_sums.take(order)
    second_parts = order.run(
        lambda *a: rows_times(a[0], a[1:], image, True, "split"), pre_round, *fc1_full
    )
    second_back = Collect(*second_parts)
    fc2_sums.add(order)
    second_back.arrive(order)
    *fc1_grad, fc1_bias_local = order.run(
        lambda *a: weight_grad(a[:4], a[4], image, ring), *second_full, pre_round
    )
    fc1_sums = Scatter(ring, *order(*fc1_grad))
    mlp_parts = order.run(
        lambda *a: rows_times(a[0], a[1:], image, True, "split"), activated, *fc2_full
    )
    fc2_sums.take(order)
    second_terms = second_back.finish(order)
    residual, branch_round, middle_vecs = order.run(
        lambda *a: per_slot(
            middle_back,
            "middle_back",
            group_seqs,
            a,
            [
                ((slots, tokens, width), F32),
                ((slots, tokens, width), BF16),
                ((slots, 2, 4, width), F32),
            ],
        ),
        image_cot,
        text_cot,
        *second_terms,
        vecs,
        after,
        branch,
    )
    branch_back = Spread(branch_round)
    fc2_sums.add(order)
    fc2_sums.arrive(order)
    fc1_sums.arrive(order)
    branch_back.arrive(order)
    branch_full = branch_back.finish(order)
    mixed_grad = order.run(
        lambda *a: rows_times(a[:4], a[4:], image, False, 1, columns=proj_part),
        *branch_full,
        *qkv_full,
    )
    mlp_back = Collect(*order(*mlp_parts))
    mlp_back.arrive(order)
    *proj_grad, _ = order.run(
        lambda *a: weight_grad(a[:4], a[4], image, ring, 3 * col_width, 4 * col_width),
        *branch_full,
        mixed,
    )
    qkv_grads = None
    for slot in range(slots):
        given = (qkv, mixed, mixed_grad, logs) + (() if slot == 0 else (qkv_grads,))
        qkv_grads = order.run(
            lambda *a, slot=slot: attend_back(
                *a[:4], image, slot, a[4] if len(a) > 4 else None
            ),
            *given,
        )
        if slot == 0:
            fc2_sums.arrive(order)
            fc1_sums.arrive(order)
    mlp_terms = mlp_back.finish(order)
    fc1_sums.arrive(order)
    *qkv_grad, qv_sums = order.run(
        lambda *a: weight_grad(
            a[:4], a[4], image, ring, 0, 4 * col_width, a[5:]
        ),
        *first_full,
        qkv_grads,
        *proj_grad,
    )
    fc1_sums.arrive(order)
    qkv_sums = Scatter(ring, *order(*qkv_grad), "parts")
    first_parts = order.run(
        lambda *a: rows_times(a[0], a[1:], image, True, "split", columns=qkv_part),
        qkv_grads,
        *qkv_full,
    )
    qkv_sums.take(order)
    first_back = Collect(*order(*first_parts))
    qkv_sums.add(order)
    first_back.arrive(order)
    qv_bias_local = qv_sums.reshape(2, 3, col_width)[:, 0::2]
    proj_bias_local = jnp.sum(middle_vecs[:, :, 3], 0)
    fc2_bias_local = jnp.sum(fc2_bias_local, 0)
    split_sums = jnp.concatenate([qv_bias_local.reshape(-1), fc1_bias_local.reshape(-1)])
    token_sums = jnp.concatenate([proj_bias_local.reshape(-1), fc2_bias_local.reshape(-1)])
    bias_local = jnp.concatenate([split_sums, token_sums])
    image_out, text_out, gate_two = order.run(
        lambda *a: per_slot(
            leave,
            "leave",
            group_seqs,
            a,
            [
                (image_tokens.shape, BF16),
                (text_tokens.shape, BF16),
                ((slots, 2, width), F32),
            ],
        ),
        image_cot,
        text_cot,
        *mlp_terms,
        vecs,
        after,
        fc2_add,
    )
    fc2_sum = order(fc2_sums.finish(order))
    fc1_sum = order(fc1_sums.finish(order))
    qkv_sums.arrive(order)
    first_terms = first_back.finish(order)
    image_grad, text_grad, enter_vecs = order.run(
        lambda *a: per_slot(
            enter_back,
            "enter_back",
            group_seqs,
            a,
            [
                (image_tokens.shape, F32),
                (text_tokens.shape, F32),
                ((slots, 2, 2, width), F32),
            ],
        ),
        image_tokens,
        text_tokens,
        *first_terms,
        vecs,
        residual,
    )
    modul_grad = jnp.concatenate(
        [
            enter_vecs,
            middle_vecs[:, :, 0:3],
            gate_two[:, :, None],
        ],
        2,
    ).reshape(slots, 2, 6, 4, col_width)
    modul_blocks = jnp.stack(
        [
            lax.dynamic_index_in_dim(modul_grad, column ^ mask, 3, keepdims=False)
            for mask in range(4)
        ]
    )
    modul_round = order(collect(modul_blocks, "tensor", 4).astype(BF16))
    qkv_sums.take(order)
    shared = jnp.concatenate([modul_round.astype(F32).reshape(-1), bias_local])
    shared = order(shared)
    qkv_sums.add(order)
    shared = order(spread(shared, "dp", groups))
    modul_all = shared[:, : modul_round.size].astype(BF16)
    modul_all = modul_all.reshape((groups * slots,) + modul_round.shape[1:])
    bias_local = jnp.sum(shared[:, modul_round.size :], 0)
    cond_part = dot("csjn,sjdn->cd", modul_all, ada_weight)
    ada_bias_part = jnp.sum(modul_all.astype(F32), 0)
    last = jnp.concatenate([cond_part.reshape(-1), ada_bias_part.reshape(-1), bias_local])
    last = order(spread(order(last), "tensor", 4))
    qkv_sums.arrive(order)
    last = order(last)
    cond_part = jnp.sum(last[:, : cond_part.size], 0).reshape(groups, slots, rows)
    cond_terms = order(exchange(cond_part, "dp", groups))
    cond_term = jnp.stack(
        [
            lax.dynamic_index_in_dim(cond_terms, group ^ place, 0, keepdims=False)
            for place in range(groups)
        ],
        1,
    ).reshape(slots, width)
    cond_grad = lax.dynamic_slice_in_dim(
        silu_back(cond_term)[0], column * col_width, col_width, 1
    )
    last = jnp.stack(
        [
            lax.dynamic_index_in_dim(last[:, cond_part.size :], column ^ place, 0, keepdims=False)
            for place in range(4)
        ]
    )
    ada_bias_grad = by_column(last[:, : ada_bias_part.size], ada_bias_part.shape)
    bias_all = last[:, ada_bias_part.size :]
    cut_a = qv_bias_local.size
    cut_b = cut_a + fc1_bias_local.size
    cut_c = cut_b + proj_bias_local.size
    cut_d = cut_c + fc2_bias_local.size

    qv_bias_grad = by_column(bias_all[:, :cut_a], qv_bias_local.shape)
    fc1_bias_grad = by_column(bias_all[:, cut_a:cut_b], fc1_bias_local.shape)
    proj_bias_grad = jnp.sum(bias_all[:, cut_b:cut_c], 0).reshape(proj_bias_local.shape)
    fc2_bias_grad = jnp.sum(bias_all[:, cut_c:cut_d], 0).reshape(fc2_bias_local.shape)
    ada_grad = dot("cd,csjn->sjdn", cond_rows, modul_all)
    qkv_sum, proj_sum = qkv_sums.finish(order)
    cond_grad = order(cond_grad)
    live = jnp.arange(slots, dtype=jnp.int32) < order.token[0]
    cond_grad = jnp.where(live[:, None], cond_grad, 0.0)
    return (
        image_out,
        text_out,
        image_grad,
        text_grad,
        cond_grad,
        ada_grad,
        ada_bias_grad,
        qkv_sum,
        qv_bias_grad,
        jnp.swapaxes(proj_sum, 1, 2),
        proj_bias_grad,
        fc1_sum,
        fc1_bias_grad,
        jnp.swapaxes(fc2_sum, 1, 2),
        fc2_bias_grad,
    )


def solution(mesh):
    groups = mesh.shape["dp"]
    in_specs = (
        P("dp", "tensor", None),
        P("dp", "tensor", None),
        P("dp", None),
        P("dp"),
        P(None, None, "dp", "tensor"),
        P(),
        P(None, None, "dp", "tensor"),
        P(),
        P(None, "tensor", "dp"),
        P(),
        P(None, "dp", "tensor"),
        P(),
        P(None, "tensor", "dp"),
        P(),
        P("dp", "tensor", None),
        P("dp", "tensor", None),
    )
    out_specs = (
        P("dp", "tensor", None),
        P("dp", "tensor", None),
        P("dp", "tensor", None),
        P("dp", "tensor", None),
        P("dp", "tensor"),
        P(None, None, "dp", "tensor"),
        P(),
        P(None, None, "dp", "tensor"),
        P(),
        P(None, "tensor", "dp"),
        P(),
        P(None, "dp", "tensor"),
        P(),
        P(None, "tensor", "dp"),
        P(),
    )

    def step(*args):
        return on_device(groups, *args)

    return jax.shard_map(
        step, mesh=mesh, in_specs=in_specs, out_specs=out_specs, check_vma=False
    )
```

```python
import math

import jax
import jax.numpy as jnp
from jax import lax
from jax.experimental import pallas as pl
from jax.experimental.pallas import tpu as pltpu
from jax.sharding import PartitionSpec as P

HEAD_DIM = 64
PAIR = 2 * HEAD_DIM
FACTOR = 1.0 / math.sqrt(HEAD_DIM)
VMEM = 60 << 20
FLOPS_PER_US = 460000000
EPSILON = 1e-06
F32 = jnp.float32
BF16 = jnp.bfloat16


def hop(value, axis, mask, size):
    return lax.ppermute(value, axis, [(i, i ^ mask) for i in range(size)])


def halves(size):
    low = 1
    while low * low < size:
        low *= 2
    return low, size // low


def spread(value, axis, size):
    low, high = halves(size)
    held = jnp.stack(
        [value] + [hop(value, axis, low * step, size) for step in range(1, high)]
    )
    full = [held] + [hop(held, axis, mask, size) for mask in range(1, low)]
    return jnp.stack(full, 1).reshape((size,) + value.shape)


def exchange(blocks, axis, size):
    low, high = halves(size)
    blocks = blocks.reshape((high, low) + blocks.shape[1:])
    held = jnp.stack(
        [blocks[0]] + [hop(blocks[step], axis, low * step, size) for step in range(1, high)]
    )
    full = [held[:, 0]] + [hop(held[:, mask], axis, mask, size) for mask in range(1, low)]
    return jnp.stack(full, 1).reshape((size,) + blocks.shape[2:])


def collect(blocks, axis, size):
    low, high = halves(size)
    blocks = blocks.reshape((high, low) + blocks.shape[1:])
    held = blocks[0] + sum(
        hop(blocks[step], axis, low * step, size) for step in range(1, high)
    )
    return held[0] + sum(hop(held[mask], axis, mask, size) for mask in range(1, low))


def by_column(block, shape):
    return jnp.moveaxis(block.reshape((4,) + shape), 0, -2).reshape(
        shape[:-1] + (4 * shape[-1],)
    )


class Order:
    def __init__(self, seed):
        self.token = seed

    def __call__(self, *values):
        self.token, *values = lax.optimization_barrier((self.token, *values))
        return values[0] if len(values) == 1 else values

    def run(self, function, *values):
        results = function(*self(*values)) if len(values) > 1 else function(self(*values))
        return self(*results) if isinstance(results, (tuple, list)) else self(results)


class Ring:
    def __init__(self, size):
        self.size = size
        self.order = list(range(0, size, 2)) + list(range(size - 1, 0, -2))
        self.ahead = [(self.order[i], self.order[(i + 1) % size]) for i in range(size)]
        self.back = [(b, a) for a, b in self.ahead]
        place = [0] * size
        for position, device in enumerate(self.order):
            place[device] = position
        self.mine = jnp.asarray(place, jnp.int32)[lax.axis_index("dp")]
        self.table = jnp.asarray(self.order, jnp.int32)

    def devices(self, distances):
        return self.table[(self.mine + jnp.asarray(distances, jnp.int32)) % self.size]

    def forward(self, value):
        return lax.ppermute(value, "dp", self.ahead)

    def backward(self, value):
        return lax.ppermute(value, "dp", self.back)


class Gather:
    def __init__(self, ring, shard):
        self.ring, self.step = ring, 0
        self.pieces, self.distances, self.streams = [shard], [0], [0]
        self.placed, self.full = 0, ()
        self.send(shard, shard)

    def send(self, ahead, back):
        self.step += 1
        if self.step == self.ring.size // 2:
            ahead, back = ahead[:1], back[1:]
        self.moving = (self.ring.forward(ahead), self.ring.backward(back))

    def arrive(self, order):
        ahead, back = order(*self.moving)
        last = self.step == self.ring.size // 2
        self.pieces += [ahead, back]
        self.distances += [-self.step, self.step]
        self.streams += [0, 1 if last else 0]
        if not last:
            self.send(ahead, back)
        return last

    def finish(self, order):
        while len(self.pieces) < self.ring.size + 1:
            self.arrive(order)
        self.place(order)
        return [f.reshape(-1, f.shape[2]) for f in self.full]

    def place(self, order):
        new = slice(self.placed, None)
        places = self.ring.devices(self.distances[new])
        self.full = order(
            *assemble(self.pieces[new], self.streams[new], places, self.ring.size, self.full)
        )
        self.placed = len(self.pieces)


class Scatter:
    def __init__(self, ring, image, text, far_image, far_text, form="plain"):
        self.ring, self.image, self.text, self.form = ring, image, text, form
        self.left = ring.size // 2
        self.moving = (ring.forward(far_image), ring.backward(far_text))

    def arrive(self, order):
        self.take(order)
        self.add(order)

    def take(self, order):
        self.taken = order(*self.moving)
        self.left -= 1

    def add(self, order):
        ahead, back = order(*self.taken)
        places = self.ring.devices([self.left, -self.left])
        if self.left == 0:
            self.total = ring_total(self.image, self.text, ahead, back, places, self.form)
            return
        ahead, back = order(*ring_add(self.image, self.text, ahead, back, places))
        self.moving = (self.ring.forward(ahead), self.ring.backward(back))

    def finish(self, order):
        while self.left:
            self.arrive(order)
        return self.total


def kernel_call(kernel, name, cost_us, grid, in_specs, out_specs, out_shape, scalars=0, **more):
    return pl.pallas_call(
        kernel,
        grid_spec=pltpu.PrefetchScalarGridSpec(
            num_scalar_prefetch=scalars,
            grid=grid,
            in_specs=in_specs,
            out_specs=out_specs,
            scratch_shapes=more.pop("scratch", ()),
        ),
        out_shape=out_shape,
        compiler_params=pltpu.CompilerParams(vmem_limit_bytes=VMEM),
        cost_estimate=pl.CostEstimate(
            flops=int(cost_us * FLOPS_PER_US), bytes_accessed=1, transcendentals=0
        ),
        name=name,
        **more,
    )


def assemble(pieces, streams, places, size, earlier):
    count = len(pieces)
    parts, rows, width = pieces[0].shape[1:]
    moves = [
        (i, streams[i] + s, s, part)
        for i in range(count)
        for s in range(pieces[i].shape[0])
        for part in range(parts)
    ]

    def kernel(place, *refs):
        shards, refs = refs[:count], refs[count + len(earlier) :]
        full, held, sems_in, sems_out = refs[:2], refs[2:-2], refs[-2], refs[-1]
        ins = [pltpu.make_async_copy(shards[i], held[i], sems_in.at[i]) for i in range(count)]
        for copy in ins:
            copy.start()
        outs, last = [], -1
        for m, (i, stream, s, part) in enumerate(moves):
            if i != last:
                ins[i].wait()
                last = i
            spot = full[stream].at[place[i], :, pl.ds(part * width, width)]
            outs.append(pltpu.make_async_copy(held[i].at[s, part], spot, sems_out.at[m]))
            outs[-1].start()
        for copy in outs:
            copy.wait()

    whole = pl.BlockSpec(memory_space=pltpu.HBM)
    out = jax.ShapeDtypeStruct((size, rows, parts * width), BF16)
    return kernel_call(
        kernel,
        "assemble",
        1 + 3e-7 * sum(math.prod(p.shape) for p in pieces),
        (1,),
        [whole] * (count + len(earlier)),
        [whole] * 2,
        [out] * 2,
        scalars=1,
        scratch=[pltpu.VMEM(p.shape, p.dtype) for p in pieces]
        + [pltpu.SemaphoreType.DMA((count,)), pltpu.SemaphoreType.DMA((len(moves),))],
        input_output_aliases={count + 1: 0, count + 2: 1} if earlier else {},
    )(places, *pieces, *earlier)


def ring_specs(image, ahead, back, block):
    width = image.shape[2]

    def local(which):
        return pl.BlockSpec((1, block, width), lambda i, place: (place[which], i, 0))

    def moved(value):
        return pl.BlockSpec((value.shape[0], block, width), lambda i, place: (0, i, 0))

    return [local(0), local(0), local(1), local(1), moved(ahead), moved(back)]


def ring_add(image, text, ahead, back, places):
    size, rows, width = image.shape
    block = rows // 4 if rows % 64 == 0 else rows
    whole = ahead.shape[0] == 2

    def kernel(place, image_a, text_a, image_b, text_b, ahead, back, send_a, send_b):
        send_a[0] = (image_a[0].astype(F32) + ahead[0].astype(F32)).astype(BF16)
        send_b[1] = (text_b[0].astype(F32) + back[back.shape[0] - 1].astype(F32)).astype(BF16)
        if whole:
            send_a[1] = (text_a[0].astype(F32) + ahead[1].astype(F32)).astype(BF16)
            send_b[0] = (image_b[0].astype(F32) + back[0].astype(F32)).astype(BF16)
        else:
            send_a[1] = text_a[0]
            send_b[0] = image_b[0]

    out = pl.BlockSpec((2, block, width), lambda i, place: (0, i, 0))
    return kernel_call(
        kernel,
        "ring_add",
        1 + 7e-6 * image.shape[1] * image.shape[2] * 2,
        (rows // block,),
        ring_specs(image, ahead, back, block),
        [out] * 2,
        [jax.ShapeDtypeStruct((2, rows, width), BF16)] * 2,
        scalars=1,
    )(places, image, text, image, text, ahead, back)


def ring_total(image, text, ahead, back, places, form):
    size, rows, width = image.shape
    block = rows // 4 if rows % 64 == 0 else rows
    part = width // 4

    def kernel(place, image_a, text_a, image_b, text_b, ahead, back, total, *more):
        for s, mine in enumerate((image_a, text_a)):
            value = mine[0].astype(F32) + ahead[s].astype(F32) + back[s].astype(F32)
            if form == "parts":
                for j in range(3):
                    total[s, j] = value[:, j * part : (j + 1) * part]
                more[0][s] = value[:, 3 * part :]
            else:
                total[s] = value

    shapes = {
        "plain": [(2, rows, width)],
        "parts": [(2, 3, rows, part), (2, rows, part)],
    }[form]
    outs = [
        pl.BlockSpec(
            shape[:-2] + (block, shape[-1]),
            lambda i, place, lead=len(shape) - 2: (0,) * lead + (i, 0),
        )
        for shape in shapes
    ]
    total = kernel_call(
        kernel,
        "ring_total",
        1 + 7e-6 * image.shape[1] * image.shape[2] * 2,
        (rows // block,),
        ring_specs(image, ahead, back, block),
        outs,
        [jax.ShapeDtypeStruct(shape, F32) for shape in shapes],
        scalars=1,
    )(places, image, text, image, text, ahead, back)
    return total if form == "parts" else total[0]


class Spread:
    def __init__(self, part):
        self.part = part
        self.across = hop(part, "tensor", 2, 4)
        self.beside = hop(part, "tensor", 1, 4)

    def arrive(self, order):
        self.across, self.beside = order(self.across, self.beside)
        self.corner = hop(self.across, "tensor", 1, 4)

    def finish(self, order):
        return [self.part, self.beside, self.across, order(self.corner)]


class Collect:
    def __init__(self, own, beside, across, corner):
        self.own, self.kept = own, across
        self.corner = hop(corner, "tensor", 1, 4)
        self.beside = hop(beside, "tensor", 1, 4)

    def arrive(self, order):
        corner = order(self.corner)
        send = (self.kept.astype(F32) + corner.astype(F32)).astype(BF16)
        self.across = hop(order(send), "tensor", 2, 4)
        self.beside = order(self.beside)

    def finish(self, order):
        return [self.own, self.beside, order(self.across)]


def piece_specs(pieces, block=None):
    if isinstance(pieces, (list, tuple)):
        shape = pieces[0].shape
        spec = pl.BlockSpec(shape, lambda j, *_: (0, 0, 0), pipeline_mode=pl.Buffered(1))
        return [spec] * 4, list(pieces), shape
    shape = pieces.shape[1:]
    specs = [
        pl.BlockSpec(
            (None,) + shape, lambda j, *_, k=k: (k, 0, 0, 0), pipeline_mode=pl.Buffered(1)
        )
        for k in range(4)
    ]
    return specs, [pieces] * 4, shape


def column_block(width):
    for block in (512, 384, 256, 128):
        if width % block == 0:
            return block
    return width


def rows_times(
    pieces, weights, image, turned, outputs, finish=None, extras=(), extra_specs=(), columns=None
):
    specs, arrays, (slots, tokens, depth) = piece_specs(pieces)
    start, count = columns or (0, weights[0].shape[1])
    width = weights[0].shape[0] if turned else count
    block = column_block(math.gcd(start, width))
    text = tokens - image
    spots = [(k, c) for k in range(4) for c in range(slots)]
    dims = DOT_NT if turned else DOT_NN
    split = outputs == "split"
    count = 4 if split else outputs

    def kernel(*refs):
        rows, (image_w, text_w) = refs[:4], refs[4:6]
        more, outs = refs[6 : 6 + len(extras)], refs[6 + len(extras) :]

        def store(stream, spot, sums):
            k, c = spot
            cut = slice(0, image) if stream == 0 else slice(image, tokens)
            values = [sums] if finish is None else finish(stream, spot, cut, sums, *more)
            for which, value in enumerate(values):
                if split:
                    outs[k][c, cut] = value.astype(BF16)
                else:
                    outs[which][k, c, cut] = value.astype(BF16)

        for spot in spots:
            store(0, spot, mul(rows[spot[0]][spot[1], :image], image_w[...], dims))
        joined = jnp.concatenate([rows[k][c, image:] for k, c in spots], 0)
        sums = mul(joined, text_w[...], dims)
        for i, spot in enumerate(spots):
            store(1, spot, sums[i * text : (i + 1) * text])

    if turned:
        weight = pl.BlockSpec((block, depth), lambda j: (j, start // depth))
    else:
        weight = pl.BlockSpec((depth, block), lambda j: (0, start // block + j))
    if split:
        out = pl.BlockSpec((slots, tokens, block), lambda j: (0, 0, j))
        shape = jax.ShapeDtypeStruct((slots, tokens, width), BF16)
    else:
        out = pl.BlockSpec((4, slots, tokens, block), lambda j: (0, 0, 0, j))
        shape = jax.ShapeDtypeStruct((4, slots, tokens, width), BF16)
    return kernel_call(
        kernel,
        "rows_times",
        1 + 3e-9 * 4 * slots * tokens * depth * width,
        (width // block,),
        specs + [weight, weight] + [make(block) for make in extra_specs],
        [out] * count,
        [shape] * count,
    )(*arrays, *weights, *extras)


def weight_grad(pieces, grads, image, ring, first=0, total=None, earlier=()):
    size = ring.size
    far = ring.devices([size // 2])
    specs, arrays, (slots, tokens, depth) = piece_specs(pieces)
    width = grads.shape[3]
    block = column_block(math.gcd(first, width))
    text = tokens - image
    spots = [(k, c) for k in range(4) for c in range(slots)]

    def kernel(far, a, b, c, d, grad, *refs):
        rows = (a, b, c, d)
        image_out, text_out, far_image, far_text, sums, image_turned, text_turned = refs[-7:]

        @pl.when(pl.program_id(0) == 0)
        def _():
            for i, (k, s) in enumerate(spots):
                image_turned[:, pl.ds(i * image, image)] = jnp.transpose(rows[k][s, :image])
            text_turned[...] = jnp.transpose(
                jnp.concatenate([rows[k][s, image:] for k, s in spots], 0)
            )

        image_grads = jnp.concatenate([grad[k, s, :image] for k, s in spots], 0)
        text_grads = jnp.concatenate([grad[k, s, image:] for k, s in spots], 0)
        image_out[...] = (
            mul(image_turned[...], image_grads, DOT_NN).astype(BF16).reshape(image_out.shape)
        )
        text_out[...] = (
            mul(text_turned[...], text_grads, DOT_NN).astype(BF16).reshape(text_out.shape)
        )
        far_image[0] = image_out[far[0]]
        far_text[0] = text_out[far[0]]
        sums[0:1] = jnp.sum(image_grads.astype(F32), 0, keepdims=True)
        sums[1:2] = jnp.sum(text_grads.astype(F32), 0, keepdims=True)

    outs, shapes = [], []
    for count in (size, size, 1, 1):
        outs.append(
            pl.BlockSpec(
                (count, depth // size, block), lambda j, *_: (0, 0, first // block + j)
            )
        )
        shapes.append(jax.ShapeDtypeStruct((count, depth // size, total or width), BF16))
    return kernel_call(
        kernel,
        "weight_grad",
        1 + 3.4e-9 * 4 * slots * tokens * depth * width,
        (width // block,),
        specs
        + [pl.BlockSpec((4, slots, tokens, block), lambda j, *_: (0, 0, 0, j))]
        + [pl.BlockSpec(memory_space=pl.ANY)] * len(earlier),
        outs + [pl.BlockSpec((2, block), lambda j, *_: (0, j))],
        shapes + [jax.ShapeDtypeStruct((2, width), F32)],
        scalars=1,
        scratch=[
            pltpu.VMEM((depth, len(spots) * image), BF16),
            pltpu.VMEM((depth, len(spots) * text), BF16),
        ],
        input_output_aliases={6 + i: i for i in range(len(earlier))},
    )(far, *arrays, grads, *earlier)


def mul(a, b, dims):
    return lax.dot_general(a, b, dims, preferred_element_type=F32)


DOT_NN = (((1,), (0,)), ((), ()))
DOT_NT = (((1,), (1,)), ((), ()))
DOT_TN = (((0,), (0,)), ((), ()))


def lane_masks(dtype):
    lane = lax.broadcasted_iota(jnp.int32, (1, PAIR), 1)
    low = (lane < HEAD_DIM).astype(F32)
    return [low.astype(dtype), (1.0 - low).astype(dtype)]


def stream_rows(ref, image, stream):
    cut = slice(0, image) if stream == 0 else slice(image, ref.shape[2])
    return jnp.concatenate([ref[k, 0, cut] for k in range(4)], 0)


def query_blocks(image, text):
    return [(0, (0, 1), 0), (0, (2, 3), 2 * image), (1, (0, 1, 2, 3), 4 * image)]


def attend(qkv, image, slot, earlier):
    _, slots, tokens, width = qkv.shape
    text, pairs = tokens - image, width // (3 * PAIR)

    def kernel(q, k, v, *refs):
        out, logs_out = refs[-2:]
        keys = [stream_rows(k, image, s) for s in range(2)]
        values = [stream_rows(v, image, s) for s in range(2)]
        masks = lane_masks(F32)
        low = [m.astype(BF16) for m in masks]
        for stream, members, place in query_blocks(image, text):
            cut = slice(0, image) if stream == 0 else slice(image, tokens)
            size = image if stream == 0 else text
            query = jnp.concatenate([q[m, 0, cut] for m in members], 0)
            query = query * jnp.asarray(FACTOR, BF16)
            total = logs = None
            for head in range(2):
                scores = [mul(query * low[head], key, DOT_NT) for key in keys]
                top = jnp.maximum(
                    jnp.max(scores[0], -1, keepdims=True), jnp.max(scores[1], -1, keepdims=True)
                )
                probs = [jnp.exp(s - top) for s in scores]
                denom = jnp.sum(probs[0], -1, keepdims=True) + jnp.sum(
                    probs[1], -1, keepdims=True
                )
                mixed = mul(probs[0].astype(BF16), values[0], DOT_NN) + mul(
                    probs[1].astype(BF16), values[1], DOT_NN
                )
                mixed = mixed * (masks[head] / denom)
                log = (top + jnp.log(denom)) * masks[head]
                total = mixed if total is None else total + mixed
                logs = log if logs is None else logs + log
            for i, m in enumerate(members):
                out[m, 0, cut] = total[i * size : (i + 1) * size].astype(BF16)
            turned = jnp.transpose(logs)
            span = pl.ds(place, size * len(members))
            logs_out[0, 0, 0:1, span] = turned[0:1]
            logs_out[0, 0, 1:2, span] = turned[HEAD_DIM : HEAD_DIM + 1]

    def spec(which):
        return pl.BlockSpec((4, 1, tokens, PAIR), lambda p: (0, slot, 0, which * pairs + p))

    total = 4 * tokens
    return kernel_call(
        kernel,
        "attend",
        15,
        (pairs,),
        [spec(0), spec(1), spec(2)] + [pl.BlockSpec(memory_space=pl.ANY)] * len(earlier),
        [spec(0), pl.BlockSpec((1, 1, 2, total), lambda p: (slot, p, 0, 0))],
        [
            jax.ShapeDtypeStruct((4, slots, tokens, pairs * PAIR), BF16),
            jax.ShapeDtypeStruct((slots, pairs, 2, total), F32),
        ],
        input_output_aliases={3: 0, 4: 1} if earlier else {},
    )(qkv, qkv, qkv, *earlier)


def attend_back(qkv, mixed, grads, logs, image, slot, earlier):
    _, slots, tokens, width = qkv.shape
    text, pairs = tokens - image, width // (3 * PAIR)

    def kernel(q, k, v, mixed, grads, logs, *refs):
        out, key_image, key_text, value_image, value_text = refs[-5:]
        key_sums, value_sums = (key_image, key_text), (value_image, value_text)
        keys = [stream_rows(k, image, s) for s in range(2)]
        values = [stream_rows(v, image, s) for s in range(2)]
        low = lane_masks(BF16)
        pair = pl.program_id(0)

        def lanes(which):
            return pl.ds(pl.multiple_of((which * pairs + pair) * PAIR, PAIR), PAIR)

        first = True
        for stream, members, place in query_blocks(image, text):
            cut = slice(0, image) if stream == 0 else slice(image, tokens)
            size = image if stream == 0 else text
            query = jnp.concatenate([q[m, 0, cut] for m in members], 0)
            query = query * jnp.asarray(FACTOR, BF16)
            grad = jnp.concatenate([grads[m, 0, cut] for m in members], 0)
            output = jnp.concatenate([mixed[m, 0, cut] for m in members], 0)
            inner = jnp.transpose(grad.astype(F32) * output.astype(F32))
            query_grad = None
            for head in range(2):
                head_q, head_g = query * low[head], grad * low[head]
                half = slice(head * HEAD_DIM, (head + 1) * HEAD_DIM)
                delta = jnp.sum(inner[half], 0, keepdims=True)
                log = logs[0, 0, head : head + 1, pl.ds(place, size * len(members))]
                for part in range(2):
                    probs = jnp.exp(mul(keys[part], head_q, DOT_NT) - log)
                    prob_grad = mul(values[part], head_g, DOT_NT)
                    score_grad = (probs * (prob_grad - delta)).astype(BF16)
                    value_part = mul(probs.astype(BF16), head_g, DOT_NN)
                    key_part = mul(score_grad, head_q, DOT_NN)
                    query_part = mul(score_grad, keys[part] * low[head], DOT_TN)
                    query_grad = query_part if query_grad is None else query_grad + query_part
                    if first:
                        value_sums[part][...] = value_part
                        key_sums[part][...] = key_part
                    else:
                        value_sums[part][...] += value_part
                        key_sums[part][...] += key_part
                first = False
            query_grad = query_grad * FACTOR
            for i, m in enumerate(members):
                out[m, 0, cut, lanes(0)] = query_grad[i * size : (i + 1) * size].astype(BF16)
        for which, sums in ((1, key_sums), (2, value_sums)):
            for m in range(4):
                out[m, 0, :image, lanes(which)] = sums[0][
                    m * image : (m + 1) * image
                ].astype(BF16)
                out[m, 0, image:, lanes(which)] = sums[1][m * text : (m + 1) * text].astype(BF16)

    def spec(which):
        return pl.BlockSpec((4, 1, tokens, PAIR), lambda p: (0, slot, 0, which * pairs + p))

    before = [] if earlier is None else [earlier]
    return kernel_call(
        kernel,
        "attend_back",
        29,
        (pairs,),
        [
            spec(0),
            spec(1),
            spec(2),
            spec(0),
            spec(0),
            pl.BlockSpec((1, 1, 2, 4 * tokens), lambda p: (slot, p, 0, 0)),
        ]
        + [pl.BlockSpec(memory_space=pl.ANY)] * len(before),
        pl.BlockSpec((4, 1, tokens, width), lambda p: (0, slot, 0, 0)),
        jax.ShapeDtypeStruct(qkv.shape, BF16),
        scratch=[pltpu.VMEM((4 * image, PAIR), F32), pltpu.VMEM((4 * text, PAIR), F32)] * 2,
        input_output_aliases={6: 0} if before else {},
    )(qkv, qkv, qkv, mixed, grads, logs, *before)


def normalize(values):
    average = jnp.mean(values, -1, keepdims=True)
    centred = values - average
    spread = jnp.mean(centred * centred, -1, keepdims=True)
    inverse = lax.rsqrt(spread + EPSILON)
    return centred * inverse, inverse


def norm_back(grad, normed, inverse, scale):
    scaled = grad * (1.0 + scale)
    return inverse * (
        scaled
        - jnp.mean(scaled, -1, keepdims=True)
        - normed * jnp.mean(scaled * normed, -1, keepdims=True)
    )


def add_up(values):
    return jnp.sum(values, 0, keepdims=True)


def per_slot(function, name, seqs, ins, outs):
    slots = ins[0].shape[0]

    def spec(shape, whole):
        rest = (0,) * (len(shape) - 1)
        if whole:
            return pl.BlockSpec(shape, lambda c, seqs: (0,) + rest)
        return pl.BlockSpec((1,) + tuple(shape[1:]), lambda c, seqs: (c,) + rest)

    def kernel(seqs, *refs):
        function((pl.program_id(0) < seqs[0]).astype(F32), *refs)

    return kernel_call(
        kernel,
        name,
        6,
        (slots,),
        [spec(value.shape, value.ndim == 2) for value in ins],
        [spec(shape, False) for shape, _ in outs],
        [jax.ShapeDtypeStruct(shape, dtype) for shape, dtype in outs],
        scalars=1,
    )(seqs, *ins)


def enter(live, image, text, image_cot, text_cot, vecs, first, mlp_round, sums):
    cut = image.shape[1]
    for s, (tokens, cot, rows) in enumerate(
        ((image, image_cot, slice(0, cut)), (text, text_cot, slice(cut, None)))
    ):
        normed, _ = normalize(tokens[0].astype(F32))
        first[0, rows] = (normed * (1.0 + vecs[0, s, 1:2]) + vecs[0, s, 0:1]).astype(BF16)
        rounded = (cot[0].astype(F32) * live * vecs[0, s, 5:6]).astype(BF16)
        mlp_round[0, rows] = rounded
        sums[0, s : s + 1] = add_up(rounded.astype(F32))


def middle(live, image, text, own, beside, across, vecs, bias, after, branch, second):
    cut = image.shape[1]
    for s, (tokens, rows) in enumerate(((image, slice(0, cut)), (text, slice(cut, None)))):
        value = own[0, rows].astype(F32) + beside[0, rows].astype(F32)
        value = value + across[0, rows].astype(F32) + bias[s : s + 1]
        result = tokens[0].astype(F32) + vecs[0, s, 2:3] * value
        normed, _ = normalize(result)
        branch[0, rows] = value
        after[0, rows] = result
        second[0, rows] = (normed * (1.0 + vecs[0, s, 4:5]) + vecs[0, s, 3:4]).astype(BF16)


def middle_back(
    live, image_cot, text_cot, own, beside, across, vecs, after, branch, residual, rounded, sums
):
    cut = image_cot.shape[1]
    for s, (cot, rows) in enumerate(((image_cot, slice(0, cut)), (text_cot, slice(cut, None)))):
        grad = own[0, rows].astype(F32) + beside[0, rows].astype(F32)
        grad = grad + across[0, rows].astype(F32)
        normed, inverse = normalize(after[0, rows])
        value = cot[0].astype(F32) * live + norm_back(grad, normed, inverse, vecs[0, s, 4:5])
        residual[0, rows] = value
        low = (value * vecs[0, s, 2:3]).astype(BF16)
        rounded[0, rows] = low
        sums[0, s, 0:1] = add_up(value * branch[0, rows])
        sums[0, s, 1:2] = add_up(grad)
        sums[0, s, 2:3] = add_up(grad * normed)
        sums[0, s, 3:4] = add_up(low.astype(F32))


def leave(
    live, image_cot, text_cot, own, beside, across, vecs, after, bias, image_out, text_out, sums
):
    cut = image_cot.shape[1]
    for s, (cot, rows, out) in enumerate(
        ((image_cot, slice(0, cut), image_out), (text_cot, slice(cut, None), text_out))
    ):
        value = own[0, rows].astype(F32) + beside[0, rows].astype(F32)
        value = value + across[0, rows].astype(F32) + bias[s : s + 1]
        out[0] = ((after[0, rows] + vecs[0, s, 5:6] * value) * live).astype(BF16)
        sums[0, s : s + 1] = add_up(cot[0].astype(F32) * live * value)


def enter_back(
    live, image, text, own, beside, across, vecs, residual, image_grad, text_grad, sums
):
    cut = image.shape[1]
    for s, (tokens, rows, out) in enumerate(
        ((image, slice(0, cut), image_grad), (text, slice(cut, None), text_grad))
    ):
        grad = own[0, rows].astype(F32) + beside[0, rows].astype(F32)
        grad = grad + across[0, rows].astype(F32)
        normed, inverse = normalize(tokens[0].astype(F32))
        out[0] = residual[0, rows] + norm_back(grad, normed, inverse, vecs[0, s, 1:2])
        sums[0, s, 0:1] = add_up(grad)
        sums[0, s, 1:2] = add_up(grad * normed)


def bias_spec(block):
    return pl.BlockSpec((2, block), lambda j: (0, j))


def add_bias(stream, spot, cut, sums, bias):
    return [sums + bias[stream : stream + 1]]


def gelu_both(stream, spot, cut, sums, bias):
    value = sums + bias[stream : stream + 1]
    factor = math.sqrt(2.0 / math.pi)
    square = value * value
    bend = jnp.tanh(factor * (value + 0.044715 * value * square))
    half = 0.5 * (1.0 + bend)
    slope = half + 0.5 * value * (1.0 - bend * bend) * factor * (1.0 + 0.134145 * square)
    return [value * half, slope]


def times_slope(stream, spot, cut, sums, slope):
    return [sums * slope[spot[0], spot[1], cut].astype(F32)]


def dot(spec, a, b):
    return jnp.einsum(spec, a, b, preferred_element_type=F32)


def on_device(
    groups,
    image_tokens,
    text_tokens,
    conditioning,
    group_seqs,
    ada_weight,
    ada_bias,
    qkv_weight,
    qv_bias,
    proj_weight,
    proj_bias,
    fc1_weight,
    fc1_bias,
    fc2_weight,
    fc2_bias,
    image_cot,
    text_cot,
):
    column = lax.axis_index("tensor")
    group = lax.axis_index("dp")
    ring = Ring(groups)
    order = Order(group_seqs)
    slots, image, width = image_tokens.shape
    text = text_tokens.shape[1]
    tokens = image + text
    rows = qkv_weight.shape[2]
    col_width = qkv_weight.shape[-1]
    hidden = fc1_weight.shape[-1]
    both = range(2)

    proj_turned = jnp.swapaxes(proj_weight, 1, 2)[:, None]
    fc1_shard = fc1_weight[:, None]
    fc2_turned = jnp.swapaxes(fc2_weight, 1, 2)[:, None]

    ada_part = lax.dynamic_slice_in_dim(ada_bias.astype(F32), column * col_width, col_width, 2)
    qv_part = lax.dynamic_slice_in_dim(qv_bias.astype(F32), column * col_width, col_width, 2)
    fc1_part = lax.dynamic_slice_in_dim(fc1_bias.astype(F32), column * hidden, hidden, 1)
    offsets = jnp.stack([qv_part[:, 0], jnp.zeros_like(qv_part[:, 0]), qv_part[:, 1]], 1)
    offsets = offsets.reshape(2, 3 * col_width)
    proj_add = proj_bias.astype(F32)
    fc2_add = fc2_bias.astype(F32)

    cond_act, silu_back = jax.vjp(jax.nn.silu, conditioning.astype(F32))
    cond_low = cond_act.astype(BF16).reshape(slots, groups, rows)
    cond_sends = jnp.stack(
        [
            lax.dynamic_index_in_dim(cond_low, group ^ mask, 1, keepdims=False)
            for mask in range(groups)
        ]
    )
    cond_rows = order(exchange(cond_sends, "dp", groups)).reshape(groups * slots, rows)
    modul_parts = order(dot("cd,sjdn->csjn", cond_rows, ada_weight))
    modul_parts = modul_parts.reshape((groups, slots) + modul_parts.shape[1:])
    modul_local = order(collect(modul_parts, "dp", groups) + ada_part[None])
    qkv_ring = Gather(ring, order(jnp.concatenate([qkv_weight, proj_turned], 1)))
    qkv_part = (0, 3 * col_width)
    proj_part = (3 * col_width, col_width)
    vecs = order(lax.all_gather(modul_local, "tensor", axis=3, tiled=True))

    first, mlp_round, fc2_bias_local = order.run(
        lambda *a: per_slot(
            enter,
            "enter",
            group_seqs,
            a,
            [
                ((slots, tokens, width), BF16),
                ((slots, tokens, width), BF16),
                ((slots, 2, width), F32),
            ],
        ),
        image_tokens,
        text_tokens,
        image_cot,
        text_cot,
        vecs,
    )
    qkv_ring.arrive(order)
    first_move = Spread(order(first))
    qkv_ring.arrive(order)
    qkv_ring.arrive(order)
    first_move.arrive(order)
    first_full = first_move.finish(order)
    qkv_ring.place(order)
    qkv_ring.arrive(order)
    fc1_ring = Gather(ring, order(fc1_shard))
    mlp_move = Spread(order(mlp_round))
    qkv_full = qkv_ring.finish(order)

    qkv = order.run(
        lambda *a: rows_times(
            a[:4], a[4:], image, False, 1, add_bias, (offsets,), (bias_spec,), qkv_part
        ),
        *first_full,
        *qkv_full,
    )
    fc1_ring.arrive(order)
    mixed = ()
    for slot in range(slots):
        mixed = order.run(
            lambda *a, slot=slot: attend(a[0], image, slot, a[1:]), *((qkv,) + tuple(mixed))
        )
    mixed, logs = mixed
    fc1_ring.arrive(order)
    mlp_move.arrive(order)
    branch_parts = order.run(
        lambda *a: rows_times(a[0], a[1:], image, True, "split", columns=proj_part),
        mixed,
        *qkv_full,
    )
    branch_move = Collect(*order(*branch_parts))
    mlp_full = mlp_move.finish(order)
    branch_move.arrive(order)
    fc1_ring.arrive(order)
    fc1_ring.arrive(order)
    fc2_ring = Gather(ring, order(fc2_turned))
    branch_terms = branch_move.finish(order)
    after, branch, second = order.run(
        lambda *a: per_slot(
            middle,
            "middle",
            group_seqs,
            a,
            [
                ((slots, tokens, width), F32),
                ((slots, tokens, width), F32),
                ((slots, tokens, width), BF16),
            ],
        ),
        image_tokens,
        text_tokens,
        *branch_terms,
        vecs,
        proj_add,
    )
    second_move = Spread(second)
    fc1_full = fc1_ring.finish(order)
    fc2_ring.arrive(order)
    fc2_ring.place(order)
    fc2_ring.arrive(order)
    second_move.arrive(order)
    second_full = second_move.finish(order)
    activated, slope = order.run(
        lambda *a: rows_times(
            a[:4], a[4:], image, False, 2, gelu_both, (fc1_part,), (bias_spec,)
        ),
        *second_full,
        *fc1_full,
    )
    fc2_ring.arrive(order)
    *fc2_grad, _ = order.run(
        lambda *a: weight_grad(a[:4], a[4], image, ring), *mlp_full, activated
    )
    fc2_ring.arrive(order)
    fc2_sums = Scatter(ring, *order(*fc2_grad))
    fc2_full = fc2_ring.finish(order)
    pre_round = order.run(
        lambda *a: rows_times(
            a[:4],
            a[4:],
            image,
            False,
            1,
            times_slope,
            (slope,),
            (
                lambda block: pl.BlockSpec(
                    (4, slots, tokens, block), lambda j: (0, 0, 0, j)
                ),
            ),
        ),
        *mlp_full,
        *fc2_full,
    )
    fc2_sums.take(order)
    second_parts = order.run(
        lambda *a: rows_times(a[0], a[1:], image, True, "split"), pre_round, *fc1_full
    )
    second_back = Collect(*second_parts)
    fc2_sums.add(order)
    second_back.arrive(order)
    *fc1_grad, fc1_bias_local = order.run(
        lambda *a: weight_grad(a[:4], a[4], image, ring), *second_full, pre_round
    )
    fc1_sums = Scatter(ring, *order(*fc1_grad))
    mlp_parts = order.run(
        lambda *a: rows_times(a[0], a[1:], image, True, "split"), activated, *fc2_full
    )
    fc2_sums.take(order)
    second_terms = second_back.finish(order)
    residual, branch_round, middle_vecs = order.run(
        lambda *a: per_slot(
            middle_back,
            "middle_back",
            group_seqs,
            a,
            [
                ((slots, tokens, width), F32),
                ((slots, tokens, width), BF16),
                ((slots, 2, 4, width), F32),
            ],
        ),
        image_cot,
        text_cot,
        *second_terms,
        vecs,
        after,
        branch,
    )
    branch_back = Spread(branch_round)
    fc2_sums.add(order)
    fc2_sums.arrive(order)
    fc1_sums.arrive(order)
    branch_back.arrive(order)
    branch_full = branch_back.finish(order)
    mixed_grad = order.run(
        lambda *a: rows_times(a[:4], a[4:], image, False, 1, columns=proj_part),
        *branch_full,
        *qkv_full,
    )
    mlp_back = Collect(*order(*mlp_parts))
    mlp_back.arrive(order)
    *proj_grad, _ = order.run(
        lambda *a: weight_grad(a[:4], a[4], image, ring, 3 * col_width, 4 * col_width),
        *branch_full,
        mixed,
    )
    qkv_grads = None
    for slot in range(slots):
        given = (qkv, mixed, mixed_grad, logs) + (() if slot == 0 else (qkv_grads,))
        qkv_grads = order.run(
            lambda *a, slot=slot: attend_back(
                *a[:4], image, slot, a[4] if len(a) > 4 else None
            ),
            *given,
        )
        if slot == 0:
            fc2_sums.arrive(order)
            fc1_sums.arrive(order)
    mlp_terms = mlp_back.finish(order)
    fc1_sums.arrive(order)
    *qkv_grad, qv_sums = order.run(
        lambda *a: weight_grad(
            a[:4], a[4], image, ring, 0, 4 * col_width, a[5:]
        ),
        *first_full,
        qkv_grads,
        *proj_grad,
    )
    fc1_sums.arrive(order)
    qkv_sums = Scatter(ring, *order(*qkv_grad), "parts")
    first_parts = order.run(
        lambda *a: rows_times(a[0], a[1:], image, True, "split", columns=qkv_part),
        qkv_grads,
        *qkv_full,
    )
    qkv_sums.take(order)
    first_back = Collect(*order(*first_parts))
    qkv_sums.add(order)
    first_back.arrive(order)
    qv_bias_local = qv_sums.reshape(2, 3, col_width)[:, 0::2]
    proj_bias_local = jnp.sum(middle_vecs[:, :, 3], 0)
    fc2_bias_local = jnp.sum(fc2_bias_local, 0)
    split_sums = jnp.concatenate([qv_bias_local.reshape(-1), fc1_bias_local.reshape(-1)])
    token_sums = jnp.concatenate([proj_bias_local.reshape(-1), fc2_bias_local.reshape(-1)])
    bias_local = jnp.concatenate([split_sums, token_sums])
    image_out, text_out, gate_two = order.run(
        lambda *a: per_slot(
            leave,
            "leave",
            group_seqs,
            a,
            [
                (image_tokens.shape, BF16),
                (text_tokens.shape, BF16),
                ((slots, 2, width), F32),
            ],
        ),
        image_cot,
        text_cot,
        *mlp_terms,
        vecs,
        after,
        fc2_add,
    )
    fc2_sum = order(fc2_sums.finish(order))
    fc1_sum = order(fc1_sums.finish(order))
    qkv_sums.arrive(order)
    first_terms = first_back.finish(order)
    image_grad, text_grad, enter_vecs = order.run(
        lambda *a: per_slot(
            enter_back,
            "enter_back",
            group_seqs,
            a,
            [
                (image_tokens.shape, F32),
                (text_tokens.shape, F32),
                ((slots, 2, 2, width), F32),
            ],
        ),
        image_tokens,
        text_tokens,
        *first_terms,
        vecs,
        residual,
    )
    modul_grad = jnp.concatenate(
        [
            enter_vecs,
            middle_vecs[:, :, 0:3],
            gate_two[:, :, None],
        ],
        2,
    ).reshape(slots, 2, 6, 4, col_width)
    modul_blocks = jnp.stack(
        [
            lax.dynamic_index_in_dim(modul_grad, column ^ mask, 3, keepdims=False)
            for mask in range(4)
        ]
    )
    modul_round = order(collect(modul_blocks, "tensor", 4).astype(BF16))
    qkv_sums.take(order)
    shared = jnp.concatenate([modul_round.astype(F32).reshape(-1), bias_local])
    shared = order(shared)
    qkv_sums.add(order)
    shared = order(spread(shared, "dp", groups))
    modul_all = shared[:, : modul_round.size].astype(BF16)
    modul_all = modul_all.reshape((groups * slots,) + modul_round.shape[1:])
    bias_local = jnp.sum(shared[:, modul_round.size :], 0)
    cond_part = dot("csjn,sjdn->cd", modul_all, ada_weight)
    ada_bias_part = jnp.sum(modul_all.astype(F32), 0)
    last = jnp.concatenate([cond_part.reshape(-1), ada_bias_part.reshape(-1), bias_local])
    last = order(last)
    qkv_sums.take(order)
    last = order(spread(order(last), "tensor", 4))
    qkv_sums.add(order)
    cond_part = jnp.sum(last[:, : cond_part.size], 0).reshape(groups, slots, rows)
    cond_terms = order(exchange(cond_part, "dp", groups))
    cond_term = jnp.stack(
        [
            lax.dynamic_index_in_dim(cond_terms, group ^ place, 0, keepdims=False)
            for place in range(groups)
        ],
        1,
    ).reshape(slots, width)
    cond_grad = lax.dynamic_slice_in_dim(
        silu_back(cond_term)[0], column * col_width, col_width, 1
    )
    last = jnp.stack(
        [
            lax.dynamic_index_in_dim(last[:, cond_part.size :], column ^ place, 0, keepdims=False)
            for place in range(4)
        ]
    )
    ada_bias_grad = by_column(last[:, : ada_bias_part.size], ada_bias_part.shape)
    bias_all = last[:, ada_bias_part.size :]
    cut_a = qv_bias_local.size
    cut_b = cut_a + fc1_bias_local.size
    cut_c = cut_b + proj_bias_local.size
    cut_d = cut_c + fc2_bias_local.size

    qv_bias_grad = by_column(bias_all[:, :cut_a], qv_bias_local.shape)
    fc1_bias_grad = by_column(bias_all[:, cut_a:cut_b], fc1_bias_local.shape)
    proj_bias_grad = jnp.sum(bias_all[:, cut_b:cut_c], 0).reshape(proj_bias_local.shape)
    fc2_bias_grad = jnp.sum(bias_all[:, cut_c:cut_d], 0).reshape(fc2_bias_local.shape)
    ada_grad = dot("cd,csjn->sjdn", cond_rows, modul_all)
    qkv_sum, proj_sum = qkv_sums.finish(order)
    cond_grad = order(cond_grad)
    live = jnp.arange(slots, dtype=jnp.int32) < order.token[0]
    cond_grad = jnp.where(live[:, None], cond_grad, 0.0)
    return (
        image_out,
        text_out,
        image_grad,
        text_grad,
        cond_grad,
        ada_grad,
        ada_bias_grad,
        qkv_sum,
        qv_bias_grad,
        jnp.swapaxes(proj_sum, 1, 2),
        proj_bias_grad,
        fc1_sum,
        fc1_bias_grad,
        jnp.swapaxes(fc2_sum, 1, 2),
        fc2_bias_grad,
    )


def solution(mesh):
    groups = mesh.shape["dp"]
    in_specs = (
        P("dp", "tensor", None),
        P("dp", "tensor", None),
        P("dp", None),
        P("dp"),
        P(None, None, "dp", "tensor"),
        P(),
        P(None, None, "dp", "tensor"),
        P(),
        P(None, "tensor", "dp"),
        P(),
        P(None, "dp", "tensor"),
        P(),
        P(None, "tensor", "dp"),
        P(),
        P("dp", "tensor", None),
        P("dp", "tensor", None),
    )
    out_specs = (
        P("dp", "tensor", None),
        P("dp", "tensor", None),
        P("dp", "tensor", None),
        P("dp", "tensor", None),
        P("dp", "tensor"),
        P(None, None, "dp", "tensor"),
        P(),
        P(None, None, "dp", "tensor"),
        P(),
        P(None, "tensor", "dp"),
        P(),
        P(None, "dp", "tensor"),
        P(),
        P(None, "tensor", "dp"),
        P(),
    )

    def step(*args):
        return on_device(groups, *args)

    return jax.shard_map(
        step, mesh=mesh, in_specs=in_specs, out_specs=out_specs, check_vma=False
    )
```

```python
import math

import jax
import jax.numpy as jnp
from jax import lax
from jax.experimental import pallas as pl
from jax.experimental.pallas import tpu as pltpu
from jax.sharding import PartitionSpec as P

HEAD_DIM = 64
PAIR = 2 * HEAD_DIM
FACTOR = 1.0 / math.sqrt(HEAD_DIM)
VMEM = 60 << 20
FLOPS_PER_US = 345000000
EPSILON = 1e-06
F32 = jnp.float32
BF16 = jnp.bfloat16


def hop(value, axis, mask, size):
    return lax.ppermute(value, axis, [(i, i ^ mask) for i in range(size)])


def halves(size):
    low = 1
    while low * low < size:
        low *= 2
    return low, size // low


def spread(value, axis, size):
    low, high = halves(size)
    held = jnp.stack(
        [value] + [hop(value, axis, low * step, size) for step in range(1, high)]
    )
    full = [held] + [hop(held, axis, mask, size) for mask in range(1, low)]
    return jnp.stack(full, 1).reshape((size,) + value.shape)


def exchange(blocks, axis, size):
    low, high = halves(size)
    blocks = blocks.reshape((high, low) + blocks.shape[1:])
    held = jnp.stack(
        [blocks[0]] + [hop(blocks[step], axis, low * step, size) for step in range(1, high)]
    )
    full = [held[:, 0]] + [hop(held[:, mask], axis, mask, size) for mask in range(1, low)]
    return jnp.stack(full, 1).reshape((size,) + blocks.shape[2:])


def collect(blocks, axis, size):
    low, high = halves(size)
    blocks = blocks.reshape((high, low) + blocks.shape[1:])
    held = blocks[0] + sum(
        hop(blocks[step], axis, low * step, size) for step in range(1, high)
    )
    return held[0] + sum(hop(held[mask], axis, mask, size) for mask in range(1, low))


def by_column(block, shape):
    return jnp.moveaxis(block.reshape((4,) + shape), 0, -2).reshape(
        shape[:-1] + (4 * shape[-1],)
    )


class Order:
    def __init__(self, seed):
        self.token = seed

    def __call__(self, *values):
        self.token, *values = lax.optimization_barrier((self.token, *values))
        return values[0] if len(values) == 1 else values

    def run(self, function, *values):
        results = function(*self(*values)) if len(values) > 1 else function(self(*values))
        return self(*results) if isinstance(results, (tuple, list)) else self(results)


class Ring:
    def __init__(self, size):
        self.size = size
        self.order = list(range(0, size, 2)) + list(range(size - 1, 0, -2))
        self.ahead = [(self.order[i], self.order[(i + 1) % size]) for i in range(size)]
        self.back = [(b, a) for a, b in self.ahead]
        place = [0] * size
        for position, device in enumerate(self.order):
            place[device] = position
        self.mine = jnp.asarray(place, jnp.int32)[lax.axis_index("dp")]
        self.table = jnp.asarray(self.order, jnp.int32)

    def devices(self, distances):
        return self.table[(self.mine + jnp.asarray(distances, jnp.int32)) % self.size]

    def forward(self, value):
        return lax.ppermute(value, "dp", self.ahead)

    def backward(self, value):
        return lax.ppermute(value, "dp", self.back)


class Gather:
    def __init__(self, ring, shard):
        self.ring, self.step = ring, 0
        self.pieces, self.distances, self.streams = [shard], [0], [0]
        self.placed, self.full = 0, ()
        self.send(shard, shard)

    def send(self, ahead, back):
        self.step += 1
        if self.step == self.ring.size // 2:
            ahead, back = ahead[:1], back[1:]
        self.moving = (self.ring.forward(ahead), self.ring.backward(back))

    def arrive(self, order):
        ahead, back = order(*self.moving)
        last = self.step == self.ring.size // 2
        self.pieces += [ahead, back]
        self.distances += [-self.step, self.step]
        self.streams += [0, 1 if last else 0]
        if not last:
            self.send(ahead, back)
        return last

    def finish(self, order):
        while len(self.pieces) < self.ring.size + 1:
            self.arrive(order)
        self.place(order)
        return [f.reshape(-1, f.shape[2]) for f in self.full]

    def place(self, order):
        new = slice(self.placed, None)
        places = self.ring.devices(self.distances[new])
        self.full = order(
            *assemble(self.pieces[new], self.streams[new], places, self.ring.size, self.full)
        )
        self.placed = len(self.pieces)


class Scatter:
    def __init__(self, ring, image, text, far_image, far_text, form="plain"):
        self.ring, self.image, self.text, self.form = ring, image, text, form
        self.left = ring.size // 2
        self.moving = (ring.forward(far_image), ring.backward(far_text))

    def arrive(self, order):
        self.take(order)
        self.add(order)

    def take(self, order):
        self.taken = order(*self.moving)
        self.left -= 1

    def add(self, order):
        ahead, back = order(*self.taken)
        places = self.ring.devices([self.left, -self.left])
        if self.left == 0:
            self.total = ring_total(self.image, self.text, ahead, back, places, self.form)
            return
        ahead, back = order(*ring_add(self.image, self.text, ahead, back, places))
        self.moving = (self.ring.forward(ahead), self.ring.backward(back))

    def finish(self, order):
        while self.left:
            self.arrive(order)
        return self.total


def kernel_call(kernel, name, cost_us, grid, in_specs, out_specs, out_shape, scalars=0, **more):
    return pl.pallas_call(
        kernel,
        grid_spec=pltpu.PrefetchScalarGridSpec(
            num_scalar_prefetch=scalars,
            grid=grid,
            in_specs=in_specs,
            out_specs=out_specs,
            scratch_shapes=more.pop("scratch", ()),
        ),
        out_shape=out_shape,
        compiler_params=pltpu.CompilerParams(vmem_limit_bytes=VMEM),
        cost_estimate=pl.CostEstimate(
            flops=int(cost_us * FLOPS_PER_US), bytes_accessed=1, transcendentals=0
        ),
        name=name,
        **more,
    )


def assemble(pieces, streams, places, size, earlier):
    count = len(pieces)
    parts, rows, width = pieces[0].shape[1:]
    moves = [
        (i, streams[i] + s, s, part)
        for i in range(count)
        for s in range(pieces[i].shape[0])
        for part in range(parts)
    ]

    def kernel(place, *refs):
        shards, refs = refs[:count], refs[count + len(earlier) :]
        full, held, sems_in, sems_out = refs[:2], refs[2:-2], refs[-2], refs[-1]
        ins = [pltpu.make_async_copy(shards[i], held[i], sems_in.at[i]) for i in range(count)]
        for copy in ins:
            copy.start()
        outs, last = [], -1
        for m, (i, stream, s, part) in enumerate(moves):
            if i != last:
                ins[i].wait()
                last = i
            spot = full[stream].at[place[i], :, pl.ds(part * width, width)]
            outs.append(pltpu.make_async_copy(held[i].at[s, part], spot, sems_out.at[m]))
            outs[-1].start()
        for copy in outs:
            copy.wait()

    whole = pl.BlockSpec(memory_space=pltpu.HBM)
    out = jax.ShapeDtypeStruct((size, rows, parts * width), BF16)
    return kernel_call(
        kernel,
        "assemble",
        1 + 3e-7 * sum(math.prod(p.shape) for p in pieces),
        (1,),
        [whole] * (count + len(earlier)),
        [whole] * 2,
        [out] * 2,
        scalars=1,
        scratch=[pltpu.VMEM(p.shape, p.dtype) for p in pieces]
        + [pltpu.SemaphoreType.DMA((count,)), pltpu.SemaphoreType.DMA((len(moves),))],
        input_output_aliases={count + 1: 0, count + 2: 1} if earlier else {},
    )(places, *pieces, *earlier)


def ring_specs(image, ahead, back, block):
    width = image.shape[2]

    def local(which):
        return pl.BlockSpec((1, block, width), lambda i, place: (place[which], i, 0))

    def moved(value):
        return pl.BlockSpec((value.shape[0], block, width), lambda i, place: (0, i, 0))

    return [local(0), local(0), local(1), local(1), moved(ahead), moved(back)]


def ring_add(image, text, ahead, back, places):
    size, rows, width = image.shape
    block = rows // 4 if rows % 64 == 0 else rows
    whole = ahead.shape[0] == 2

    def kernel(place, image_a, text_a, image_b, text_b, ahead, back, send_a, send_b):
        send_a[0] = (image_a[0].astype(F32) + ahead[0].astype(F32)).astype(BF16)
        send_b[1] = (text_b[0].astype(F32) + back[back.shape[0] - 1].astype(F32)).astype(BF16)
        if whole:
            send_a[1] = (text_a[0].astype(F32) + ahead[1].astype(F32)).astype(BF16)
            send_b[0] = (image_b[0].astype(F32) + back[0].astype(F32)).astype(BF16)
        else:
            send_a[1] = text_a[0]
            send_b[0] = image_b[0]

    out = pl.BlockSpec((2, block, width), lambda i, place: (0, i, 0))
    return kernel_call(
        kernel,
        "ring_add",
        1 + 7e-6 * image.shape[1] * image.shape[2] * 2,
        (rows // block,),
        ring_specs(image, ahead, back, block),
        [out] * 2,
        [jax.ShapeDtypeStruct((2, rows, width), BF16)] * 2,
        scalars=1,
    )(places, image, text, image, text, ahead, back)


def ring_total(image, text, ahead, back, places, form):
    size, rows, width = image.shape
    block = rows // 4 if rows % 64 == 0 else rows
    part = width // 4

    def kernel(place, image_a, text_a, image_b, text_b, ahead, back, total, *more):
        for s, mine in enumerate((image_a, text_a)):
            value = mine[0].astype(F32) + ahead[s].astype(F32) + back[s].astype(F32)
            if form == "parts":
                for j in range(3):
                    total[s, j] = value[:, j * part : (j + 1) * part]
                more[0][s] = value[:, 3 * part :]
            else:
                total[s] = value

    shapes = {
        "plain": [(2, rows, width)],
        "parts": [(2, 3, rows, part), (2, rows, part)],
    }[form]
    outs = [
        pl.BlockSpec(
            shape[:-2] + (block, shape[-1]),
            lambda i, place, lead=len(shape) - 2: (0,) * lead + (i, 0),
        )
        for shape in shapes
    ]
    total = kernel_call(
        kernel,
        "ring_total",
        1 + 7e-6 * image.shape[1] * image.shape[2] * 2,
        (rows // block,),
        ring_specs(image, ahead, back, block),
        outs,
        [jax.ShapeDtypeStruct(shape, F32) for shape in shapes],
        scalars=1,
    )(places, image, text, image, text, ahead, back)
    return total if form == "parts" else total[0]


class Spread:
    def __init__(self, part):
        self.part = part
        self.across = hop(part, "tensor", 2, 4)
        self.beside = hop(part, "tensor", 1, 4)

    def arrive(self, order):
        self.across, self.beside = order(self.across, self.beside)
        self.corner = hop(self.across, "tensor", 1, 4)

    def finish(self, order):
        return [self.part, self.beside, self.across, order(self.corner)]


class Collect:
    def __init__(self, own, beside, across, corner):
        self.own, self.kept = own, across
        self.corner = hop(corner, "tensor", 1, 4)
        self.beside = hop(beside, "tensor", 1, 4)

    def arrive(self, order):
        corner = order(self.corner)
        send = (self.kept.astype(F32) + corner.astype(F32)).astype(BF16)
        self.across = hop(order(send), "tensor", 2, 4)
        self.beside = order(self.beside)

    def finish(self, order):
        return [self.own, self.beside, order(self.across)]


def piece_specs(pieces, block=None):
    if isinstance(pieces, (list, tuple)):
        shape = pieces[0].shape
        spec = pl.BlockSpec(shape, lambda j, *_: (0, 0, 0), pipeline_mode=pl.Buffered(1))
        return [spec] * 4, list(pieces), shape
    shape = pieces.shape[1:]
    specs = [
        pl.BlockSpec(
            (None,) + shape, lambda j, *_, k=k: (k, 0, 0, 0), pipeline_mode=pl.Buffered(1)
        )
        for k in range(4)
    ]
    return specs, [pieces] * 4, shape


def column_block(width):
    for block in (512, 384, 256, 128):
        if width % block == 0:
            return block
    return width


def rows_times(
    pieces, weights, image, turned, outputs, finish=None, extras=(), extra_specs=(), columns=None
):
    specs, arrays, (slots, tokens, depth) = piece_specs(pieces)
    start, count = columns or (0, weights[0].shape[1])
    width = weights[0].shape[0] if turned else count
    block = column_block(math.gcd(start, width))
    text = tokens - image
    spots = [(k, c) for k in range(4) for c in range(slots)]
    dims = DOT_NT if turned else DOT_NN
    split = outputs == "split"
    count = 4 if split else outputs

    def kernel(*refs):
        rows, (image_w, text_w) = refs[:4], refs[4:6]
        more, outs = refs[6 : 6 + len(extras)], refs[6 + len(extras) :]

        def store(stream, spot, sums):
            k, c = spot
            cut = slice(0, image) if stream == 0 else slice(image, tokens)
            values = [sums] if finish is None else finish(stream, spot, cut, sums, *more)
            for which, value in enumerate(values):
                if split:
                    outs[k][c, cut] = value.astype(BF16)
                else:
                    outs[which][k, c, cut] = value.astype(BF16)

        for spot in spots:
            store(0, spot, mul(rows[spot[0]][spot[1], :image], image_w[...], dims))
        joined = jnp.concatenate([rows[k][c, image:] for k, c in spots], 0)
        sums = mul(joined, text_w[...], dims)
        for i, spot in enumerate(spots):
            store(1, spot, sums[i * text : (i + 1) * text])

    if turned:
        weight = pl.BlockSpec((block, depth), lambda j: (j, start // depth))
    else:
        weight = pl.BlockSpec((depth, block), lambda j: (0, start // block + j))
    if split:
        out = pl.BlockSpec((slots, tokens, block), lambda j: (0, 0, j))
        shape = jax.ShapeDtypeStruct((slots, tokens, width), BF16)
    else:
        out = pl.BlockSpec((4, slots, tokens, block), lambda j: (0, 0, 0, j))
        shape = jax.ShapeDtypeStruct((4, slots, tokens, width), BF16)
    return kernel_call(
        kernel,
        "rows_times",
        1 + 3e-9 * 4 * slots * tokens * depth * width,
        (width // block,),
        specs + [weight, weight] + [make(block) for make in extra_specs],
        [out] * count,
        [shape] * count,
    )(*arrays, *weights, *extras)


def weight_grad(pieces, grads, image, ring, first=0, total=None, earlier=()):
    size = ring.size
    far = ring.devices([size // 2])
    specs, arrays, (slots, tokens, depth) = piece_specs(pieces)
    width = grads.shape[3]
    block = column_block(math.gcd(first, width))
    text = tokens - image
    spots = [(k, c) for k in range(4) for c in range(slots)]

    def kernel(far, a, b, c, d, grad, *refs):
        rows = (a, b, c, d)
        image_out, text_out, far_image, far_text, sums, image_turned, text_turned = refs[-7:]

        @pl.when(pl.program_id(0) == 0)
        def _():
            for i, (k, s) in enumerate(spots):
                image_turned[:, pl.ds(i * image, image)] = jnp.transpose(rows[k][s, :image])
            text_turned[...] = jnp.transpose(
                jnp.concatenate([rows[k][s, image:] for k, s in spots], 0)
            )

        image_grads = jnp.concatenate([grad[k, s, :image] for k, s in spots], 0)
        text_grads = jnp.concatenate([grad[k, s, image:] for k, s in spots], 0)
        image_out[...] = (
            mul(image_turned[...], image_grads, DOT_NN).astype(BF16).reshape(image_out.shape)
        )
        text_out[...] = (
            mul(text_turned[...], text_grads, DOT_NN).astype(BF16).reshape(text_out.shape)
        )
        far_image[0] = image_out[far[0]]
        far_text[0] = text_out[far[0]]
        sums[0:1] = jnp.sum(image_grads.astype(F32), 0, keepdims=True)
        sums[1:2] = jnp.sum(text_grads.astype(F32), 0, keepdims=True)

    outs, shapes = [], []
    for count in (size, size, 1, 1):
        outs.append(
            pl.BlockSpec(
                (count, depth // size, block), lambda j, *_: (0, 0, first // block + j)
            )
        )
        shapes.append(jax.ShapeDtypeStruct((count, depth // size, total or width), BF16))
    return kernel_call(
        kernel,
        "weight_grad",
        1 + 3.4e-9 * 4 * slots * tokens * depth * width,
        (width // block,),
        specs
        + [pl.BlockSpec((4, slots, tokens, block), lambda j, *_: (0, 0, 0, j))]
        + [pl.BlockSpec(memory_space=pl.ANY)] * len(earlier),
        outs + [pl.BlockSpec((2, block), lambda j, *_: (0, j))],
        shapes + [jax.ShapeDtypeStruct((2, width), F32)],
        scalars=1,
        scratch=[
            pltpu.VMEM((depth, len(spots) * image), BF16),
            pltpu.VMEM((depth, len(spots) * text), BF16),
        ],
        input_output_aliases={6 + i: i for i in range(len(earlier))},
    )(far, *arrays, grads, *earlier)


def mul(a, b, dims):
    return lax.dot_general(a, b, dims, preferred_element_type=F32)


DOT_NN = (((1,), (0,)), ((), ()))
DOT_NT = (((1,), (1,)), ((), ()))
DOT_TN = (((0,), (0,)), ((), ()))


def lane_masks(dtype):
    lane = lax.broadcasted_iota(jnp.int32, (1, PAIR), 1)
    low = (lane < HEAD_DIM).astype(F32)
    return [low.astype(dtype), (1.0 - low).astype(dtype)]


def stream_rows(ref, image, stream):
    cut = slice(0, image) if stream == 0 else slice(image, ref.shape[2])
    return jnp.concatenate([ref[k, 0, cut] for k in range(4)], 0)


def query_blocks(image, text):
    return [(0, (0, 1), 0), (0, (2, 3), 2 * image), (1, (0, 1, 2, 3), 4 * image)]


def attend(qkv, image, slot, earlier):
    _, slots, tokens, width = qkv.shape
    text, pairs = tokens - image, width // (3 * PAIR)

    def kernel(q, k, v, *refs):
        out, logs_out = refs[-2:]
        keys = [stream_rows(k, image, s) for s in range(2)]
        values = [stream_rows(v, image, s) for s in range(2)]
        masks = lane_masks(F32)
        low = [m.astype(BF16) for m in masks]
        for stream, members, place in query_blocks(image, text):
            cut = slice(0, image) if stream == 0 else slice(image, tokens)
            size = image if stream == 0 else text
            query = jnp.concatenate([q[m, 0, cut] for m in members], 0)
            query = query * jnp.asarray(FACTOR, BF16)
            total = logs = None
            for head in range(2):
                scores = [mul(query * low[head], key, DOT_NT) for key in keys]
                top = jnp.maximum(
                    jnp.max(scores[0], -1, keepdims=True), jnp.max(scores[1], -1, keepdims=True)
                )
                probs = [jnp.exp(s - top) for s in scores]
                denom = jnp.sum(probs[0], -1, keepdims=True) + jnp.sum(
                    probs[1], -1, keepdims=True
                )
                mixed = mul(probs[0].astype(BF16), values[0], DOT_NN) + mul(
                    probs[1].astype(BF16), values[1], DOT_NN
                )
                mixed = mixed * (masks[head] / denom)
                log = (top + jnp.log(denom)) * masks[head]
                total = mixed if total is None else total + mixed
                logs = log if logs is None else logs + log
            for i, m in enumerate(members):
                out[m, 0, cut] = total[i * size : (i + 1) * size].astype(BF16)
            turned = jnp.transpose(logs)
            span = pl.ds(place, size * len(members))
            logs_out[0, 0, 0:1, span] = turned[0:1]
            logs_out[0, 0, 1:2, span] = turned[HEAD_DIM : HEAD_DIM + 1]

    def spec(which):
        return pl.BlockSpec((4, 1, tokens, PAIR), lambda p: (0, slot, 0, which * pairs + p))

    total = 4 * tokens
    return kernel_call(
        kernel,
        "attend",
        15,
        (pairs,),
        [spec(0), spec(1), spec(2)] + [pl.BlockSpec(memory_space=pl.ANY)] * len(earlier),
        [spec(0), pl.BlockSpec((1, 1, 2, total), lambda p: (slot, p, 0, 0))],
        [
            jax.ShapeDtypeStruct((4, slots, tokens, pairs * PAIR), BF16),
            jax.ShapeDtypeStruct((slots, pairs, 2, total), F32),
        ],
        input_output_aliases={3: 0, 4: 1} if earlier else {},
    )(qkv, qkv, qkv, *earlier)


def attend_back(qkv, mixed, grads, logs, image, slot, earlier):
    _, slots, tokens, width = qkv.shape
    text, pairs = tokens - image, width // (3 * PAIR)

    def kernel(q, k, v, mixed, grads, logs, *refs):
        out, key_image, key_text, value_image, value_text = refs[-5:]
        key_sums, value_sums = (key_image, key_text), (value_image, value_text)
        keys = [stream_rows(k, image, s) for s in range(2)]
        values = [stream_rows(v, image, s) for s in range(2)]
        low = lane_masks(BF16)
        pair = pl.program_id(0)

        def lanes(which):
            return pl.ds(pl.multiple_of((which * pairs + pair) * PAIR, PAIR), PAIR)

        first = True
        for stream, members, place in query_blocks(image, text):
            cut = slice(0, image) if stream == 0 else slice(image, tokens)
            size = image if stream == 0 else text
            query = jnp.concatenate([q[m, 0, cut] for m in members], 0)
            query = query * jnp.asarray(FACTOR, BF16)
            grad = jnp.concatenate([grads[m, 0, cut] for m in members], 0)
            output = jnp.concatenate([mixed[m, 0, cut] for m in members], 0)
            inner = jnp.transpose(grad.astype(F32) * output.astype(F32))
            query_grad = None
            for head in range(2):
                head_q, head_g = query * low[head], grad * low[head]
                half = slice(head * HEAD_DIM, (head + 1) * HEAD_DIM)
                delta = jnp.sum(inner[half], 0, keepdims=True)
                log = logs[0, 0, head : head + 1, pl.ds(place, size * len(members))]
                for part in range(2):
                    probs = jnp.exp(mul(keys[part], head_q, DOT_NT) - log)
                    prob_grad = mul(values[part], head_g, DOT_NT)
                    score_grad = (probs * (prob_grad - delta)).astype(BF16)
                    value_part = mul(probs.astype(BF16), head_g, DOT_NN)
                    key_part = mul(score_grad, head_q, DOT_NN)
                    query_part = mul(score_grad, keys[part] * low[head], DOT_TN)
                    query_grad = query_part if query_grad is None else query_grad + query_part
                    if first:
                        value_sums[part][...] = value_part
                        key_sums[part][...] = key_part
                    else:
                        value_sums[part][...] += value_part
                        key_sums[part][...] += key_part
                first = False
            query_grad = query_grad * FACTOR
            for i, m in enumerate(members):
                out[m, 0, cut, lanes(0)] = query_grad[i * size : (i + 1) * size].astype(BF16)
        for which, sums in ((1, key_sums), (2, value_sums)):
            for m in range(4):
                out[m, 0, :image, lanes(which)] = sums[0][
                    m * image : (m + 1) * image
                ].astype(BF16)
                out[m, 0, image:, lanes(which)] = sums[1][m * text : (m + 1) * text].astype(BF16)

    def spec(which):
        return pl.BlockSpec((4, 1, tokens, PAIR), lambda p: (0, slot, 0, which * pairs + p))

    before = [] if earlier is None else [earlier]
    return kernel_call(
        kernel,
        "attend_back",
        29,
        (pairs,),
        [
            spec(0),
            spec(1),
            spec(2),
            spec(0),
            spec(0),
            pl.BlockSpec((1, 1, 2, 4 * tokens), lambda p: (slot, p, 0, 0)),
        ]
        + [pl.BlockSpec(memory_space=pl.ANY)] * len(before),
        pl.BlockSpec((4, 1, tokens, width), lambda p: (0, slot, 0, 0)),
        jax.ShapeDtypeStruct(qkv.shape, BF16),
        scratch=[pltpu.VMEM((4 * image, PAIR), F32), pltpu.VMEM((4 * text, PAIR), F32)] * 2,
        input_output_aliases={6: 0} if before else {},
    )(qkv, qkv, qkv, mixed, grads, logs, *before)


def normalize(values):
    average = jnp.mean(values, -1, keepdims=True)
    centred = values - average
    spread = jnp.mean(centred * centred, -1, keepdims=True)
    inverse = lax.rsqrt(spread + EPSILON)
    return centred * inverse, inverse


def norm_back(grad, normed, inverse, scale):
    scaled = grad * (1.0 + scale)
    return inverse * (
        scaled
        - jnp.mean(scaled, -1, keepdims=True)
        - normed * jnp.mean(scaled * normed, -1, keepdims=True)
    )


def add_up(values):
    return jnp.sum(values, 0, keepdims=True)


def per_slot(function, name, seqs, ins, outs):
    slots = ins[0].shape[0]

    def spec(shape, whole):
        rest = (0,) * (len(shape) - 1)
        if whole:
            return pl.BlockSpec(shape, lambda c, seqs: (0,) + rest)
        return pl.BlockSpec((1,) + tuple(shape[1:]), lambda c, seqs: (c,) + rest)

    def kernel(seqs, *refs):
        function((pl.program_id(0) < seqs[0]).astype(F32), *refs)

    return kernel_call(
        kernel,
        name,
        6,
        (slots,),
        [spec(value.shape, value.ndim == 2) for value in ins],
        [spec(shape, False) for shape, _ in outs],
        [jax.ShapeDtypeStruct(shape, dtype) for shape, dtype in outs],
        scalars=1,
    )(seqs, *ins)


def enter(live, image, text, image_cot, text_cot, vecs, first, mlp_round, sums):
    cut = image.shape[1]
    for s, (tokens, cot, rows) in enumerate(
        ((image, image_cot, slice(0, cut)), (text, text_cot, slice(cut, None)))
    ):
        normed, _ = normalize(tokens[0].astype(F32))
        first[0, rows] = (normed * (1.0 + vecs[0, s, 1:2]) + vecs[0, s, 0:1]).astype(BF16)
        rounded = (cot[0].astype(F32) * live * vecs[0, s, 5:6]).astype(BF16)
        mlp_round[0, rows] = rounded
        sums[0, s : s + 1] = add_up(rounded.astype(F32))


def middle(live, image, text, own, beside, across, vecs, bias, after, branch, second):
    cut = image.shape[1]
    for s, (tokens, rows) in enumerate(((image, slice(0, cut)), (text, slice(cut, None)))):
        value = own[0, rows].astype(F32) + beside[0, rows].astype(F32)
        value = value + across[0, rows].astype(F32) + bias[s : s + 1]
        result = tokens[0].astype(F32) + vecs[0, s, 2:3] * value
        normed, _ = normalize(result)
        branch[0, rows] = value
        after[0, rows] = result
        second[0, rows] = (normed * (1.0 + vecs[0, s, 4:5]) + vecs[0, s, 3:4]).astype(BF16)


def middle_back(
    live, image_cot, text_cot, own, beside, across, vecs, after, branch, residual, rounded, sums
):
    cut = image_cot.shape[1]
    for s, (cot, rows) in enumerate(((image_cot, slice(0, cut)), (text_cot, slice(cut, None)))):
        grad = own[0, rows].astype(F32) + beside[0, rows].astype(F32)
        grad = grad + across[0, rows].astype(F32)
        normed, inverse = normalize(after[0, rows])
        value = cot[0].astype(F32) * live + norm_back(grad, normed, inverse, vecs[0, s, 4:5])
        residual[0, rows] = value
        low = (value * vecs[0, s, 2:3]).astype(BF16)
        rounded[0, rows] = low
        sums[0, s, 0:1] = add_up(value * branch[0, rows])
        sums[0, s, 1:2] = add_up(grad)
        sums[0, s, 2:3] = add_up(grad * normed)
        sums[0, s, 3:4] = add_up(low.astype(F32))


def leave(
    live, image_cot, text_cot, own, beside, across, vecs, after, bias, image_out, text_out, sums
):
    cut = image_cot.shape[1]
    for s, (cot, rows, out) in enumerate(
        ((image_cot, slice(0, cut), image_out), (text_cot, slice(cut, None), text_out))
    ):
        value = own[0, rows].astype(F32) + beside[0, rows].astype(F32)
        value = value + across[0, rows].astype(F32) + bias[s : s + 1]
        out[0] = ((after[0, rows] + vecs[0, s, 5:6] * value) * live).astype(BF16)
        sums[0, s : s + 1] = add_up(cot[0].astype(F32) * live * value)


def enter_back(
    live, image, text, own, beside, across, vecs, residual, image_grad, text_grad, sums
):
    cut = image.shape[1]
    for s, (tokens, rows, out) in enumerate(
        ((image, slice(0, cut), image_grad), (text, slice(cut, None), text_grad))
    ):
        grad = own[0, rows].astype(F32) + beside[0, rows].astype(F32)
        grad = grad + across[0, rows].astype(F32)
        normed, inverse = normalize(tokens[0].astype(F32))
        out[0] = residual[0, rows] + norm_back(grad, normed, inverse, vecs[0, s, 1:2])
        sums[0, s, 0:1] = add_up(grad)
        sums[0, s, 1:2] = add_up(grad * normed)


def bias_spec(block):
    return pl.BlockSpec((2, block), lambda j: (0, j))


def add_bias(stream, spot, cut, sums, bias):
    return [sums + bias[stream : stream + 1]]


def gelu_both(stream, spot, cut, sums, bias):
    value = sums + bias[stream : stream + 1]
    factor = math.sqrt(2.0 / math.pi)
    square = value * value
    bend = jnp.tanh(factor * (value + 0.044715 * value * square))
    half = 0.5 * (1.0 + bend)
    slope = half + 0.5 * value * (1.0 - bend * bend) * factor * (1.0 + 0.134145 * square)
    return [value * half, slope]


def times_slope(stream, spot, cut, sums, slope):
    return [sums * slope[spot[0], spot[1], cut].astype(F32)]


def dot(spec, a, b):
    return jnp.einsum(spec, a, b, preferred_element_type=F32)


def on_device(
    groups,
    image_tokens,
    text_tokens,
    conditioning,
    group_seqs,
    ada_weight,
    ada_bias,
    qkv_weight,
    qv_bias,
    proj_weight,
    proj_bias,
    fc1_weight,
    fc1_bias,
    fc2_weight,
    fc2_bias,
    image_cot,
    text_cot,
):
    column = lax.axis_index("tensor")
    group = lax.axis_index("dp")
    ring = Ring(groups)
    order = Order(group_seqs)
    slots, image, width = image_tokens.shape
    text = text_tokens.shape[1]
    tokens = image + text
    rows = qkv_weight.shape[2]
    col_width = qkv_weight.shape[-1]
    hidden = fc1_weight.shape[-1]
    both = range(2)

    proj_turned = jnp.swapaxes(proj_weight, 1, 2)[:, None]
    fc1_shard = fc1_weight[:, None]
    fc2_turned = jnp.swapaxes(fc2_weight, 1, 2)[:, None]

    ada_part = lax.dynamic_slice_in_dim(ada_bias.astype(F32), column * col_width, col_width, 2)
    qv_part = lax.dynamic_slice_in_dim(qv_bias.astype(F32), column * col_width, col_width, 2)
    fc1_part = lax.dynamic_slice_in_dim(fc1_bias.astype(F32), column * hidden, hidden, 1)
    offsets = jnp.stack([qv_part[:, 0], jnp.zeros_like(qv_part[:, 0]), qv_part[:, 1]], 1)
    offsets = offsets.reshape(2, 3 * col_width)
    proj_add = proj_bias.astype(F32)
    fc2_add = fc2_bias.astype(F32)

    cond_act, silu_back = jax.vjp(jax.nn.silu, conditioning.astype(F32))
    cond_low = cond_act.astype(BF16).reshape(slots, groups, rows)
    cond_sends = jnp.stack(
        [
            lax.dynamic_index_in_dim(cond_low, group ^ mask, 1, keepdims=False)
            for mask in range(groups)
        ]
    )
    cond_rows = order(exchange(cond_sends, "dp", groups)).reshape(groups * slots, rows)
    modul_parts = order(dot("cd,sjdn->csjn", cond_rows, ada_weight))
    modul_parts = modul_parts.reshape((groups, slots) + modul_parts.shape[1:])
    modul_local = order(collect(modul_parts, "dp", groups) + ada_part[None])
    qkv_ring = Gather(ring, order(jnp.concatenate([qkv_weight, proj_turned], 1)))
    qkv_part = (0, 3 * col_width)
    proj_part = (3 * col_width, col_width)
    vecs = order(lax.all_gather(modul_local, "tensor", axis=3, tiled=True))

    first, mlp_round, fc2_bias_local = order.run(
        lambda *a: per_slot(
            enter,
            "enter",
            group_seqs,
            a,
            [
                ((slots, tokens, width), BF16),
                ((slots, tokens, width), BF16),
                ((slots, 2, width), F32),
            ],
        ),
        image_tokens,
        text_tokens,
        image_cot,
        text_cot,
        vecs,
    )
    qkv_ring.arrive(order)
    first_move = Spread(order(first))
    qkv_ring.arrive(order)
    qkv_ring.arrive(order)
    first_move.arrive(order)
    first_full = first_move.finish(order)
    qkv_ring.place(order)
    qkv_ring.arrive(order)
    fc1_ring = Gather(ring, order(fc1_shard))
    mlp_move = Spread(order(mlp_round))
    qkv_full = qkv_ring.finish(order)

    qkv = order.run(
        lambda *a: rows_times(
            a[:4], a[4:], image, False, 1, add_bias, (offsets,), (bias_spec,), qkv_part
        ),
        *first_full,
        *qkv_full,
    )
    fc1_ring.arrive(order)
    mixed = ()
    for slot in range(slots):
        mixed = order.run(
            lambda *a, slot=slot: attend(a[0], image, slot, a[1:]), *((qkv,) + tuple(mixed))
        )
    mixed, logs = mixed
    fc1_ring.arrive(order)
    mlp_move.arrive(order)
    branch_parts = order.run(
        lambda *a: rows_times(a[0], a[1:], image, True, "split", columns=proj_part),
        mixed,
        *qkv_full,
    )
    branch_move = Collect(*order(*branch_parts))
    mlp_full = mlp_move.finish(order)
    branch_move.arrive(order)
    fc1_ring.arrive(order)
    fc1_ring.arrive(order)
    fc2_ring = Gather(ring, order(fc2_turned))
    branch_terms = branch_move.finish(order)
    after, branch, second = order.run(
        lambda *a: per_slot(
            middle,
            "middle",
            group_seqs,
            a,
            [
                ((slots, tokens, width), F32),
                ((slots, tokens, width), F32),
                ((slots, tokens, width), BF16),
            ],
        ),
        image_tokens,
        text_tokens,
        *branch_terms,
        vecs,
        proj_add,
    )
    second_move = Spread(second)
    fc1_full = fc1_ring.finish(order)
    fc2_ring.arrive(order)
    fc2_ring.place(order)
    fc2_ring.arrive(order)
    second_move.arrive(order)
    second_full = second_move.finish(order)
    activated, slope = order.run(
        lambda *a: rows_times(
            a[:4], a[4:], image, False, 2, gelu_both, (fc1_part,), (bias_spec,)
        ),
        *second_full,
        *fc1_full,
    )
    fc2_ring.arrive(order)
    *fc2_grad, _ = order.run(
        lambda *a: weight_grad(a[:4], a[4], image, ring), *mlp_full, activated
    )
    fc2_ring.arrive(order)
    fc2_sums = Scatter(ring, *order(*fc2_grad))
    fc2_full = fc2_ring.finish(order)
    pre_round = order.run(
        lambda *a: rows_times(
            a[:4],
            a[4:],
            image,
            False,
            1,
            times_slope,
            (slope,),
            (
                lambda block: pl.BlockSpec(
                    (4, slots, tokens, block), lambda j: (0, 0, 0, j)
                ),
            ),
        ),
        *mlp_full,
        *fc2_full,
    )
    fc2_sums.take(order)
    second_parts = order.run(
        lambda *a: rows_times(a[0], a[1:], image, True, "split"), pre_round, *fc1_full
    )
    second_back = Collect(*second_parts)
    fc2_sums.add(order)
    second_back.arrive(order)
    *fc1_grad, fc1_bias_local = order.run(
        lambda *a: weight_grad(a[:4], a[4], image, ring), *second_full, pre_round
    )
    fc1_sums = Scatter(ring, *order(*fc1_grad))
    mlp_parts = order.run(
        lambda *a: rows_times(a[0], a[1:], image, True, "split"), activated, *fc2_full
    )
    fc2_sums.take(order)
    second_terms = second_back.finish(order)
    residual, branch_round, middle_vecs = order.run(
        lambda *a: per_slot(
            middle_back,
            "middle_back",
            group_seqs,
            a,
            [
                ((slots, tokens, width), F32),
                ((slots, tokens, width), BF16),
                ((slots, 2, 4, width), F32),
            ],
        ),
        image_cot,
        text_cot,
        *second_terms,
        vecs,
        after,
        branch,
    )
    branch_back = Spread(branch_round)
    fc2_sums.add(order)
    fc2_sums.arrive(order)
    fc1_sums.arrive(order)
    branch_back.arrive(order)
    branch_full = branch_back.finish(order)
    mixed_grad = order.run(
        lambda *a: rows_times(a[:4], a[4:], image, False, 1, columns=proj_part),
        *branch_full,
        *qkv_full,
    )
    mlp_back = Collect(*order(*mlp_parts))
    mlp_back.arrive(order)
    *proj_grad, _ = order.run(
        lambda *a: weight_grad(a[:4], a[4], image, ring, 3 * col_width, 4 * col_width),
        *branch_full,
        mixed,
    )
    qkv_grads = None
    for slot in range(slots):
        given = (qkv, mixed, mixed_grad, logs) + (() if slot == 0 else (qkv_grads,))
        qkv_grads = order.run(
            lambda *a, slot=slot: attend_back(
                *a[:4], image, slot, a[4] if len(a) > 4 else None
            ),
            *given,
        )
        if slot == 0:
            fc2_sums.arrive(order)
            fc1_sums.arrive(order)
    mlp_terms = mlp_back.finish(order)
    fc1_sums.arrive(order)
    *qkv_grad, qv_sums = order.run(
        lambda *a: weight_grad(
            a[:4], a[4], image, ring, 0, 4 * col_width, a[5:]
        ),
        *first_full,
        qkv_grads,
        *proj_grad,
    )
    fc1_sums.arrive(order)
    qkv_sums = Scatter(ring, *order(*qkv_grad), "parts")
    first_parts = order.run(
        lambda *a: rows_times(a[0], a[1:], image, True, "split", columns=qkv_part),
        qkv_grads,
        *qkv_full,
    )
    qkv_sums.take(order)
    first_back = Collect(*order(*first_parts))
    qkv_sums.add(order)
    first_back.arrive(order)
    qv_bias_local = qv_sums.reshape(2, 3, col_width)[:, 0::2]
    proj_bias_local = jnp.sum(middle_vecs[:, :, 3], 0)
    fc2_bias_local = jnp.sum(fc2_bias_local, 0)
    split_sums = jnp.concatenate([qv_bias_local.reshape(-1), fc1_bias_local.reshape(-1)])
    token_sums = jnp.concatenate([proj_bias_local.reshape(-1), fc2_bias_local.reshape(-1)])
    bias_local = jnp.concatenate([split_sums, token_sums])
    image_out, text_out, gate_two = order.run(
        lambda *a: per_slot(
            leave,
            "leave",
            group_seqs,
            a,
            [
                (image_tokens.shape, BF16),
                (text_tokens.shape, BF16),
                ((slots, 2, width), F32),
            ],
        ),
        image_cot,
        text_cot,
        *mlp_terms,
        vecs,
        after,
        fc2_add,
    )
    fc2_sum = order(fc2_sums.finish(order))
    fc1_sum = order(fc1_sums.finish(order))
    qkv_sums.arrive(order)
    first_terms = first_back.finish(order)
    image_grad, text_grad, enter_vecs = order.run(
        lambda *a: per_slot(
            enter_back,
            "enter_back",
            group_seqs,
            a,
            [
                (image_tokens.shape, F32),
                (text_tokens.shape, F32),
                ((slots, 2, 2, width), F32),
            ],
        ),
        image_tokens,
        text_tokens,
        *first_terms,
        vecs,
        residual,
    )
    modul_grad = jnp.concatenate(
        [
            enter_vecs,
            middle_vecs[:, :, 0:3],
            gate_two[:, :, None],
        ],
        2,
    ).reshape(slots, 2, 6, 4, col_width)
    modul_blocks = jnp.stack(
        [
            lax.dynamic_index_in_dim(modul_grad, column ^ mask, 3, keepdims=False)
            for mask in range(4)
        ]
    )
    modul_round = order(collect(modul_blocks, "tensor", 4).astype(BF16))
    qkv_sums.take(order)
    shared = jnp.concatenate([modul_round.astype(F32).reshape(-1), bias_local])
    shared = order(shared)
    qkv_sums.add(order)
    shared = order(spread(shared, "dp", groups))
    modul_all = shared[:, : modul_round.size].astype(BF16)
    modul_all = modul_all.reshape((groups * slots,) + modul_round.shape[1:])
    bias_local = jnp.sum(shared[:, modul_round.size :], 0)
    cond_part = dot("csjn,sjdn->cd", modul_all, ada_weight)
    ada_bias_part = jnp.sum(modul_all.astype(F32), 0)
    last = jnp.concatenate([cond_part.reshape(-1), ada_bias_part.reshape(-1), bias_local])
    last = order(spread(order(last), "tensor", 4))
    qkv_sums.arrive(order)
    last = order(last)
    cond_part = jnp.sum(last[:, : cond_part.size], 0).reshape(groups, slots, rows)
    cond_terms = order(exchange(cond_part, "dp", groups))
    cond_term = jnp.stack(
        [
            lax.dynamic_index_in_dim(cond_terms, group ^ place, 0, keepdims=False)
            for place in range(groups)
        ],
        1,
    ).reshape(slots, width)
    cond_grad = lax.dynamic_slice_in_dim(
        silu_back(cond_term)[0], column * col_width, col_width, 1
    )
    last = jnp.stack(
        [
            lax.dynamic_index_in_dim(last[:, cond_part.size :], column ^ place, 0, keepdims=False)
            for place in range(4)
        ]
    )
    ada_bias_grad = by_column(last[:, : ada_bias_part.size], ada_bias_part.shape)
    bias_all = last[:, ada_bias_part.size :]
    cut_a = qv_bias_local.size
    cut_b = cut_a + fc1_bias_local.size
    cut_c = cut_b + proj_bias_local.size
    cut_d = cut_c + fc2_bias_local.size

    qv_bias_grad = by_column(bias_all[:, :cut_a], qv_bias_local.shape)
    fc1_bias_grad = by_column(bias_all[:, cut_a:cut_b], fc1_bias_local.shape)
    proj_bias_grad = jnp.sum(bias_all[:, cut_b:cut_c], 0).reshape(proj_bias_local.shape)
    fc2_bias_grad = jnp.sum(bias_all[:, cut_c:cut_d], 0).reshape(fc2_bias_local.shape)
    ada_grad = dot("cd,csjn->sjdn", cond_rows, modul_all)
    qkv_sum, proj_sum = qkv_sums.finish(order)
    cond_grad = order(cond_grad)
    live = jnp.arange(slots, dtype=jnp.int32) < order.token[0]
    cond_grad = jnp.where(live[:, None], cond_grad, 0.0)
    return (
        image_out,
        text_out,
        image_grad,
        text_grad,
        cond_grad,
        ada_grad,
        ada_bias_grad,
        qkv_sum,
        qv_bias_grad,
        jnp.swapaxes(proj_sum, 1, 2),
        proj_bias_grad,
        fc1_sum,
        fc1_bias_grad,
        jnp.swapaxes(fc2_sum, 1, 2),
        fc2_bias_grad,
    )


def solution(mesh):
    groups = mesh.shape["dp"]
    in_specs = (
        P("dp", "tensor", None),
        P("dp", "tensor", None),
        P("dp", None),
        P("dp"),
        P(None, None, "dp", "tensor"),
        P(),
        P(None, None, "dp", "tensor"),
        P(),
        P(None, "tensor", "dp"),
        P(),
        P(None, "dp", "tensor"),
        P(),
        P(None, "tensor", "dp"),
        P(),
        P("dp", "tensor", None),
        P("dp", "tensor", None),
    )
    out_specs = (
        P("dp", "tensor", None),
        P("dp", "tensor", None),
        P("dp", "tensor", None),
        P("dp", "tensor", None),
        P("dp", "tensor"),
        P(None, None, "dp", "tensor"),
        P(),
        P(None, None, "dp", "tensor"),
        P(),
        P(None, "tensor", "dp"),
        P(),
        P(None, "dp", "tensor"),
        P(),
        P(None, "tensor", "dp"),
        P(),
    )

    def step(*args):
        return on_device(groups, *args)

    return jax.shard_map(
        step, mesh=mesh, in_specs=in_specs, out_specs=out_specs, check_vma=False
    )
```

```python
import math

import jax
import jax.numpy as jnp
from jax import lax
from jax.experimental import pallas as pl
from jax.experimental.pallas import tpu as pltpu
from jax.sharding import PartitionSpec as P

HEAD_DIM = 64
PAIR = 2 * HEAD_DIM
FACTOR = 1.0 / math.sqrt(HEAD_DIM)
VMEM = 60 << 20
FLOPS_PER_US = 253000000
EPSILON = 1e-06
F32 = jnp.float32
BF16 = jnp.bfloat16


def hop(value, axis, mask, size):
    return lax.ppermute(value, axis, [(i, i ^ mask) for i in range(size)])


def halves(size):
    low = 1
    while low * low < size:
        low *= 2
    return low, size // low


def spread(value, axis, size):
    low, high = halves(size)
    held = jnp.stack(
        [value] + [hop(value, axis, low * step, size) for step in range(1, high)]
    )
    full = [held] + [hop(held, axis, mask, size) for mask in range(1, low)]
    return jnp.stack(full, 1).reshape((size,) + value.shape)


def exchange(blocks, axis, size):
    low, high = halves(size)
    blocks = blocks.reshape((high, low) + blocks.shape[1:])
    held = jnp.stack(
        [blocks[0]] + [hop(blocks[step], axis, low * step, size) for step in range(1, high)]
    )
    full = [held[:, 0]] + [hop(held[:, mask], axis, mask, size) for mask in range(1, low)]
    return jnp.stack(full, 1).reshape((size,) + blocks.shape[2:])


def collect(blocks, axis, size):
    low, high = halves(size)
    blocks = blocks.reshape((high, low) + blocks.shape[1:])
    held = blocks[0] + sum(
        hop(blocks[step], axis, low * step, size) for step in range(1, high)
    )
    return held[0] + sum(hop(held[mask], axis, mask, size) for mask in range(1, low))


def by_column(block, shape):
    return jnp.moveaxis(block.reshape((4,) + shape), 0, -2).reshape(
        shape[:-1] + (4 * shape[-1],)
    )


class Order:
    def __init__(self, seed):
        self.token = seed

    def __call__(self, *values):
        self.token, *values = lax.optimization_barrier((self.token, *values))
        return values[0] if len(values) == 1 else values

    def run(self, function, *values):
        results = function(*self(*values)) if len(values) > 1 else function(self(*values))
        return self(*results) if isinstance(results, (tuple, list)) else self(results)


class Ring:
    def __init__(self, size):
        self.size = size
        self.order = list(range(0, size, 2)) + list(range(size - 1, 0, -2))
        self.ahead = [(self.order[i], self.order[(i + 1) % size]) for i in range(size)]
        self.back = [(b, a) for a, b in self.ahead]
        place = [0] * size
        for position, device in enumerate(self.order):
            place[device] = position
        self.mine = jnp.asarray(place, jnp.int32)[lax.axis_index("dp")]
        self.table = jnp.asarray(self.order, jnp.int32)

    def devices(self, distances):
        return self.table[(self.mine + jnp.asarray(distances, jnp.int32)) % self.size]

    def forward(self, value):
        return lax.ppermute(value, "dp", self.ahead)

    def backward(self, value):
        return lax.ppermute(value, "dp", self.back)


class Gather:
    def __init__(self, ring, shard):
        self.ring, self.step = ring, 0
        self.pieces, self.distances, self.streams = [shard], [0], [0]
        self.placed, self.full = 0, ()
        self.send(shard, shard)

    def send(self, ahead, back):
        self.step += 1
        if self.step == self.ring.size // 2:
            ahead, back = ahead[:1], back[1:]
        self.moving = (self.ring.forward(ahead), self.ring.backward(back))

    def arrive(self, order):
        ahead, back = order(*self.moving)
        last = self.step == self.ring.size // 2
        self.pieces += [ahead, back]
        self.distances += [-self.step, self.step]
        self.streams += [0, 1 if last else 0]
        if not last:
            self.send(ahead, back)
        return last

    def finish(self, order):
        while len(self.pieces) < self.ring.size + 1:
            self.arrive(order)
        self.place(order)
        return [f.reshape(-1, f.shape[2]) for f in self.full]

    def place(self, order):
        new = slice(self.placed, None)
        places = self.ring.devices(self.distances[new])
        self.full = order(
            *assemble(self.pieces[new], self.streams[new], places, self.ring.size, self.full)
        )
        self.placed = len(self.pieces)


class Scatter:
    def __init__(self, ring, image, text, far_image, far_text, form="plain"):
        self.ring, self.image, self.text, self.form = ring, image, text, form
        self.left = ring.size // 2
        self.moving = (ring.forward(far_image), ring.backward(far_text))

    def arrive(self, order):
        self.take(order)
        self.add(order)

    def take(self, order):
        self.taken = order(*self.moving)
        self.left -= 1

    def add(self, order):
        ahead, back = order(*self.taken)
        places = self.ring.devices([self.left, -self.left])
        if self.left == 0:
            self.total = ring_total(self.image, self.text, ahead, back, places, self.form)
            return
        ahead, back = order(*ring_add(self.image, self.text, ahead, back, places))
        self.moving = (self.ring.forward(ahead), self.ring.backward(back))

    def finish(self, order):
        while self.left:
            self.arrive(order)
        return self.total


def kernel_call(kernel, name, cost_us, grid, in_specs, out_specs, out_shape, scalars=0, **more):
    return pl.pallas_call(
        kernel,
        grid_spec=pltpu.PrefetchScalarGridSpec(
            num_scalar_prefetch=scalars,
            grid=grid,
            in_specs=in_specs,
            out_specs=out_specs,
            scratch_shapes=more.pop("scratch", ()),
        ),
        out_shape=out_shape,
        compiler_params=pltpu.CompilerParams(vmem_limit_bytes=VMEM),
        cost_estimate=pl.CostEstimate(
            flops=int(cost_us * FLOPS_PER_US), bytes_accessed=1, transcendentals=0
        ),
        name=name,
        **more,
    )


def assemble(pieces, streams, places, size, earlier):
    count = len(pieces)
    parts, rows, width = pieces[0].shape[1:]
    moves = [
        (i, streams[i] + s, s, part)
        for i in range(count)
        for s in range(pieces[i].shape[0])
        for part in range(parts)
    ]

    def kernel(place, *refs):
        shards, refs = refs[:count], refs[count + len(earlier) :]
        full, held, sems_in, sems_out = refs[:2], refs[2:-2], refs[-2], refs[-1]
        ins = [pltpu.make_async_copy(shards[i], held[i], sems_in.at[i]) for i in range(count)]
        for copy in ins:
            copy.start()
        outs, last = [], -1
        for m, (i, stream, s, part) in enumerate(moves):
            if i != last:
                ins[i].wait()
                last = i
            spot = full[stream].at[place[i], :, pl.ds(part * width, width)]
            outs.append(pltpu.make_async_copy(held[i].at[s, part], spot, sems_out.at[m]))
            outs[-1].start()
        for copy in outs:
            copy.wait()

    whole = pl.BlockSpec(memory_space=pltpu.HBM)
    out = jax.ShapeDtypeStruct((size, rows, parts * width), BF16)
    return kernel_call(
        kernel,
        "assemble",
        1 + 3e-7 * sum(math.prod(p.shape) for p in pieces),
        (1,),
        [whole] * (count + len(earlier)),
        [whole] * 2,
        [out] * 2,
        scalars=1,
        scratch=[pltpu.VMEM(p.shape, p.dtype) for p in pieces]
        + [pltpu.SemaphoreType.DMA((count,)), pltpu.SemaphoreType.DMA((len(moves),))],
        input_output_aliases={count + 1: 0, count + 2: 1} if earlier else {},
    )(places, *pieces, *earlier)


def ring_specs(image, ahead, back, block):
    width = image.shape[2]

    def local(which):
        return pl.BlockSpec((1, block, width), lambda i, place: (place[which], i, 0))

    def moved(value):
        return pl.BlockSpec((value.shape[0], block, width), lambda i, place: (0, i, 0))

    return [local(0), local(0), local(1), local(1), moved(ahead), moved(back)]


def ring_add(image, text, ahead, back, places):
    size, rows, width = image.shape
    block = rows // 4 if rows % 64 == 0 else rows
    whole = ahead.shape[0] == 2

    def kernel(place, image_a, text_a, image_b, text_b, ahead, back, send_a, send_b):
        send_a[0] = (image_a[0].astype(F32) + ahead[0].astype(F32)).astype(BF16)
        send_b[1] = (text_b[0].astype(F32) + back[back.shape[0] - 1].astype(F32)).astype(BF16)
        if whole:
            send_a[1] = (text_a[0].astype(F32) + ahead[1].astype(F32)).astype(BF16)
            send_b[0] = (image_b[0].astype(F32) + back[0].astype(F32)).astype(BF16)
        else:
            send_a[1] = text_a[0]
            send_b[0] = image_b[0]

    out = pl.BlockSpec((2, block, width), lambda i, place: (0, i, 0))
    return kernel_call(
        kernel,
        "ring_add",
        1 + 7e-6 * image.shape[1] * image.shape[2] * 2,
        (rows // block,),
        ring_specs(image, ahead, back, block),
        [out] * 2,
        [jax.ShapeDtypeStruct((2, rows, width), BF16)] * 2,
        scalars=1,
    )(places, image, text, image, text, ahead, back)


def ring_total(image, text, ahead, back, places, form):
    size, rows, width = image.shape
    block = rows // 4 if rows % 64 == 0 else rows
    part = width // 4

    def kernel(place, image_a, text_a, image_b, text_b, ahead, back, total, *more):
        for s, mine in enumerate((image_a, text_a)):
            value = mine[0].astype(F32) + ahead[s].astype(F32) + back[s].astype(F32)
            if form == "parts":
                for j in range(3):
                    total[s, j] = value[:, j * part : (j + 1) * part]
                more[0][s] = value[:, 3 * part :]
            else:
                total[s] = value

    shapes = {
        "plain": [(2, rows, width)],
        "parts": [(2, 3, rows, part), (2, rows, part)],
    }[form]
    outs = [
        pl.BlockSpec(
            shape[:-2] + (block, shape[-1]),
            lambda i, place, lead=len(shape) - 2: (0,) * lead + (i, 0),
        )
        for shape in shapes
    ]
    total = kernel_call(
        kernel,
        "ring_total",
        1 + 7e-6 * image.shape[1] * image.shape[2] * 2,
        (rows // block,),
        ring_specs(image, ahead, back, block),
        outs,
        [jax.ShapeDtypeStruct(shape, F32) for shape in shapes],
        scalars=1,
    )(places, image, text, image, text, ahead, back)
    return total if form == "parts" else total[0]


class Spread:
    def __init__(self, part):
        self.part = part
        self.across = hop(part, "tensor", 2, 4)
        self.beside = hop(part, "tensor", 1, 4)

    def arrive(self, order):
        self.across, self.beside = order(self.across, self.beside)
        self.corner = hop(self.across, "tensor", 1, 4)

    def finish(self, order):
        return [self.part, self.beside, self.across, order(self.corner)]


class Collect:
    def __init__(self, own, beside, across, corner):
        self.own, self.kept = own, across
        self.corner = hop(corner, "tensor", 1, 4)
        self.beside = hop(beside, "tensor", 1, 4)

    def arrive(self, order):
        corner = order(self.corner)
        send = (self.kept.astype(F32) + corner.astype(F32)).astype(BF16)
        self.across = hop(order(send), "tensor", 2, 4)
        self.beside = order(self.beside)

    def finish(self, order):
        return [self.own, self.beside, order(self.across)]


def piece_specs(pieces, block=None):
    if isinstance(pieces, (list, tuple)):
        shape = pieces[0].shape
        spec = pl.BlockSpec(shape, lambda j, *_: (0, 0, 0), pipeline_mode=pl.Buffered(1))
        return [spec] * 4, list(pieces), shape
    shape = pieces.shape[1:]
    specs = [
        pl.BlockSpec(
            (None,) + shape, lambda j, *_, k=k: (k, 0, 0, 0), pipeline_mode=pl.Buffered(1)
        )
        for k in range(4)
    ]
    return specs, [pieces] * 4, shape


def column_block(width):
    for block in (512, 384, 256, 128):
        if width % block == 0:
            return block
    return width


def rows_times(
    pieces, weights, image, turned, outputs, finish=None, extras=(), extra_specs=(), columns=None
):
    specs, arrays, (slots, tokens, depth) = piece_specs(pieces)
    start, count = columns or (0, weights[0].shape[1])
    width = weights[0].shape[0] if turned else count
    block = column_block(math.gcd(start, width))
    text = tokens - image
    spots = [(k, c) for k in range(4) for c in range(slots)]
    dims = DOT_NT if turned else DOT_NN
    split = outputs == "split"
    count = 4 if split else outputs

    def kernel(*refs):
        rows, (image_w, text_w) = refs[:4], refs[4:6]
        more, outs = refs[6 : 6 + len(extras)], refs[6 + len(extras) :]

        def store(stream, spot, sums):
            k, c = spot
            cut = slice(0, image) if stream == 0 else slice(image, tokens)
            values = [sums] if finish is None else finish(stream, spot, cut, sums, *more)
            for which, value in enumerate(values):
                if split:
                    outs[k][c, cut] = value.astype(BF16)
                else:
                    outs[which][k, c, cut] = value.astype(BF16)

        for spot in spots:
            store(0, spot, mul(rows[spot[0]][spot[1], :image], image_w[...], dims))
        joined = jnp.concatenate([rows[k][c, image:] for k, c in spots], 0)
        sums = mul(joined, text_w[...], dims)
        for i, spot in enumerate(spots):
            store(1, spot, sums[i * text : (i + 1) * text])

    if turned:
        weight = pl.BlockSpec((block, depth), lambda j: (j, start // depth))
    else:
        weight = pl.BlockSpec((depth, block), lambda j: (0, start // block + j))
    if split:
        out = pl.BlockSpec((slots, tokens, block), lambda j: (0, 0, j))
        shape = jax.ShapeDtypeStruct((slots, tokens, width), BF16)
    else:
        out = pl.BlockSpec((4, slots, tokens, block), lambda j: (0, 0, 0, j))
        shape = jax.ShapeDtypeStruct((4, slots, tokens, width), BF16)
    return kernel_call(
        kernel,
        "rows_times",
        1 + 3e-9 * 4 * slots * tokens * depth * width,
        (width // block,),
        specs + [weight, weight] + [make(block) for make in extra_specs],
        [out] * count,
        [shape] * count,
    )(*arrays, *weights, *extras)


def weight_grad(pieces, grads, image, ring, first=0, total=None, earlier=()):
    size = ring.size
    far = ring.devices([size // 2])
    specs, arrays, (slots, tokens, depth) = piece_specs(pieces)
    width = grads.shape[3]
    block = column_block(math.gcd(first, width))
    text = tokens - image
    spots = [(k, c) for k in range(4) for c in range(slots)]

    def kernel(far, a, b, c, d, grad, *refs):
        rows = (a, b, c, d)
        image_out, text_out, far_image, far_text, sums, image_turned, text_turned = refs[-7:]

        @pl.when(pl.program_id(0) == 0)
        def _():
            for i, (k, s) in enumerate(spots):
                image_turned[:, pl.ds(i * image, image)] = jnp.transpose(rows[k][s, :image])
            text_turned[...] = jnp.transpose(
                jnp.concatenate([rows[k][s, image:] for k, s in spots], 0)
            )

        image_grads = jnp.concatenate([grad[k, s, :image] for k, s in spots], 0)
        text_grads = jnp.concatenate([grad[k, s, image:] for k, s in spots], 0)
        image_out[...] = (
            mul(image_turned[...], image_grads, DOT_NN).astype(BF16).reshape(image_out.shape)
        )
        text_out[...] = (
            mul(text_turned[...], text_grads, DOT_NN).astype(BF16).reshape(text_out.shape)
        )
        far_image[0] = image_out[far[0]]
        far_text[0] = text_out[far[0]]
        sums[0:1] = jnp.sum(image_grads.astype(F32), 0, keepdims=True)
        sums[1:2] = jnp.sum(text_grads.astype(F32), 0, keepdims=True)

    outs, shapes = [], []
    for count in (size, size, 1, 1):
        outs.append(
            pl.BlockSpec(
                (count, depth // size, block), lambda j, *_: (0, 0, first // block + j)
            )
        )
        shapes.append(jax.ShapeDtypeStruct((count, depth // size, total or width), BF16))
    return kernel_call(
        kernel,
        "weight_grad",
        1 + 3.4e-9 * 4 * slots * tokens * depth * width,
        (width // block,),
        specs
        + [pl.BlockSpec((4, slots, tokens, block), lambda j, *_: (0, 0, 0, j))]
        + [pl.BlockSpec(memory_space=pl.ANY)] * len(earlier),
        outs + [pl.BlockSpec((2, block), lambda j, *_: (0, j))],
        shapes + [jax.ShapeDtypeStruct((2, width), F32)],
        scalars=1,
        scratch=[
            pltpu.VMEM((depth, len(spots) * image), BF16),
            pltpu.VMEM((depth, len(spots) * text), BF16),
        ],
        input_output_aliases={6 + i: i for i in range(len(earlier))},
    )(far, *arrays, grads, *earlier)


def mul(a, b, dims):
    return lax.dot_general(a, b, dims, preferred_element_type=F32)


DOT_NN = (((1,), (0,)), ((), ()))
DOT_NT = (((1,), (1,)), ((), ()))
DOT_TN = (((0,), (0,)), ((), ()))


def lane_masks(dtype):
    lane = lax.broadcasted_iota(jnp.int32, (1, PAIR), 1)
    low = (lane < HEAD_DIM).astype(F32)
    return [low.astype(dtype), (1.0 - low).astype(dtype)]


def stream_rows(ref, image, stream):
    cut = slice(0, image) if stream == 0 else slice(image, ref.shape[2])
    return jnp.concatenate([ref[k, 0, cut] for k in range(4)], 0)


def query_blocks(image, text):
    return [(0, (0, 1), 0), (0, (2, 3), 2 * image), (1, (0, 1, 2, 3), 4 * image)]


def attend(qkv, image, slot, earlier):
    _, slots, tokens, width = qkv.shape
    text, pairs = tokens - image, width // (3 * PAIR)

    def kernel(q, k, v, *refs):
        out, logs_out = refs[-2:]
        keys = [stream_rows(k, image, s) for s in range(2)]
        values = [stream_rows(v, image, s) for s in range(2)]
        masks = lane_masks(F32)
        low = [m.astype(BF16) for m in masks]
        for stream, members, place in query_blocks(image, text):
            cut = slice(0, image) if stream == 0 else slice(image, tokens)
            size = image if stream == 0 else text
            query = jnp.concatenate([q[m, 0, cut] for m in members], 0)
            query = query * jnp.asarray(FACTOR, BF16)
            total = logs = None
            for head in range(2):
                scores = [mul(query * low[head], key, DOT_NT) for key in keys]
                top = jnp.maximum(
                    jnp.max(scores[0], -1, keepdims=True), jnp.max(scores[1], -1, keepdims=True)
                )
                probs = [jnp.exp(s - top) for s in scores]
                denom = jnp.sum(probs[0], -1, keepdims=True) + jnp.sum(
                    probs[1], -1, keepdims=True
                )
                mixed = mul(probs[0].astype(BF16), values[0], DOT_NN) + mul(
                    probs[1].astype(BF16), values[1], DOT_NN
                )
                mixed = mixed * (masks[head] / denom)
                log = (top + jnp.log(denom)) * masks[head]
                total = mixed if total is None else total + mixed
                logs = log if logs is None else logs + log
            for i, m in enumerate(members):
                out[m, 0, cut] = total[i * size : (i + 1) * size].astype(BF16)
            turned = jnp.transpose(logs)
            span = pl.ds(place, size * len(members))
            logs_out[0, 0, 0:1, span] = turned[0:1]
            logs_out[0, 0, 1:2, span] = turned[HEAD_DIM : HEAD_DIM + 1]

    def spec(which):
        return pl.BlockSpec((4, 1, tokens, PAIR), lambda p: (0, slot, 0, which * pairs + p))

    total = 4 * tokens
    return kernel_call(
        kernel,
        "attend",
        15,
        (pairs,),
        [spec(0), spec(1), spec(2)] + [pl.BlockSpec(memory_space=pl.ANY)] * len(earlier),
        [spec(0), pl.BlockSpec((1, 1, 2, total), lambda p: (slot, p, 0, 0))],
        [
            jax.ShapeDtypeStruct((4, slots, tokens, pairs * PAIR), BF16),
            jax.ShapeDtypeStruct((slots, pairs, 2, total), F32),
        ],
        input_output_aliases={3: 0, 4: 1} if earlier else {},
    )(qkv, qkv, qkv, *earlier)


def attend_back(qkv, mixed, grads, logs, image, slot, earlier):
    _, slots, tokens, width = qkv.shape
    text, pairs = tokens - image, width // (3 * PAIR)

    def kernel(q, k, v, mixed, grads, logs, *refs):
        out, key_image, key_text, value_image, value_text = refs[-5:]
        key_sums, value_sums = (key_image, key_text), (value_image, value_text)
        keys = [stream_rows(k, image, s) for s in range(2)]
        values = [stream_rows(v, image, s) for s in range(2)]
        low = lane_masks(BF16)
        pair = pl.program_id(0)

        def lanes(which):
            return pl.ds(pl.multiple_of((which * pairs + pair) * PAIR, PAIR), PAIR)

        first = True
        for stream, members, place in query_blocks(image, text):
            cut = slice(0, image) if stream == 0 else slice(image, tokens)
            size = image if stream == 0 else text
            query = jnp.concatenate([q[m, 0, cut] for m in members], 0)
            query = query * jnp.asarray(FACTOR, BF16)
            grad = jnp.concatenate([grads[m, 0, cut] for m in members], 0)
            output = jnp.concatenate([mixed[m, 0, cut] for m in members], 0)
            inner = jnp.transpose(grad.astype(F32) * output.astype(F32))
            query_grad = None
            for head in range(2):
                head_q, head_g = query * low[head], grad * low[head]
                half = slice(head * HEAD_DIM, (head + 1) * HEAD_DIM)
                delta = jnp.sum(inner[half], 0, keepdims=True)
                log = logs[0, 0, head : head + 1, pl.ds(place, size * len(members))]
                for part in range(2):
                    probs = jnp.exp(mul(keys[part], head_q, DOT_NT) - log)
                    prob_grad = mul(values[part], head_g, DOT_NT)
                    score_grad = (probs * (prob_grad - delta)).astype(BF16)
                    value_part = mul(probs.astype(BF16), head_g, DOT_NN)
                    key_part = mul(score_grad, head_q, DOT_NN)
                    query_part = mul(score_grad, keys[part] * low[head], DOT_TN)
                    query_grad = query_part if query_grad is None else query_grad + query_part
                    if first:
                        value_sums[part][...] = value_part
                        key_sums[part][...] = key_part
                    else:
                        value_sums[part][...] += value_part
                        key_sums[part][...] += key_part
                first = False
            query_grad = query_grad * FACTOR
            for i, m in enumerate(members):
                out[m, 0, cut, lanes(0)] = query_grad[i * size : (i + 1) * size].astype(BF16)
        for which, sums in ((1, key_sums), (2, value_sums)):
            for m in range(4):
                out[m, 0, :image, lanes(which)] = sums[0][
                    m * image : (m + 1) * image
                ].astype(BF16)
                out[m, 0, image:, lanes(which)] = sums[1][m * text : (m + 1) * text].astype(BF16)

    def spec(which):
        return pl.BlockSpec((4, 1, tokens, PAIR), lambda p: (0, slot, 0, which * pairs + p))

    before = [] if earlier is None else [earlier]
    return kernel_call(
        kernel,
        "attend_back",
        29,
        (pairs,),
        [
            spec(0),
            spec(1),
            spec(2),
            spec(0),
            spec(0),
            pl.BlockSpec((1, 1, 2, 4 * tokens), lambda p: (slot, p, 0, 0)),
        ]
        + [pl.BlockSpec(memory_space=pl.ANY)] * len(before),
        pl.BlockSpec((4, 1, tokens, width), lambda p: (0, slot, 0, 0)),
        jax.ShapeDtypeStruct(qkv.shape, BF16),
        scratch=[pltpu.VMEM((4 * image, PAIR), F32), pltpu.VMEM((4 * text, PAIR), F32)] * 2,
        input_output_aliases={6: 0} if before else {},
    )(qkv, qkv, qkv, mixed, grads, logs, *before)


def normalize(values):
    average = jnp.mean(values, -1, keepdims=True)
    centred = values - average
    spread = jnp.mean(centred * centred, -1, keepdims=True)
    inverse = lax.rsqrt(spread + EPSILON)
    return centred * inverse, inverse


def norm_back(grad, normed, inverse, scale):
    scaled = grad * (1.0 + scale)
    return inverse * (
        scaled
        - jnp.mean(scaled, -1, keepdims=True)
        - normed * jnp.mean(scaled * normed, -1, keepdims=True)
    )


def add_up(values):
    return jnp.sum(values, 0, keepdims=True)


def per_slot(function, name, seqs, ins, outs):
    slots = ins[0].shape[0]

    def spec(shape, whole):
        rest = (0,) * (len(shape) - 1)
        if whole:
            return pl.BlockSpec(shape, lambda c, seqs: (0,) + rest)
        return pl.BlockSpec((1,) + tuple(shape[1:]), lambda c, seqs: (c,) + rest)

    def kernel(seqs, *refs):
        function((pl.program_id(0) < seqs[0]).astype(F32), *refs)

    return kernel_call(
        kernel,
        name,
        6,
        (slots,),
        [spec(value.shape, value.ndim == 2) for value in ins],
        [spec(shape, False) for shape, _ in outs],
        [jax.ShapeDtypeStruct(shape, dtype) for shape, dtype in outs],
        scalars=1,
    )(seqs, *ins)


def enter(live, image, text, image_cot, text_cot, vecs, first, mlp_round, sums):
    cut = image.shape[1]
    for s, (tokens, cot, rows) in enumerate(
        ((image, image_cot, slice(0, cut)), (text, text_cot, slice(cut, None)))
    ):
        normed, _ = normalize(tokens[0].astype(F32))
        first[0, rows] = (normed * (1.0 + vecs[0, s, 1:2]) + vecs[0, s, 0:1]).astype(BF16)
        rounded = (cot[0].astype(F32) * live * vecs[0, s, 5:6]).astype(BF16)
        mlp_round[0, rows] = rounded
        sums[0, s : s + 1] = add_up(rounded.astype(F32))


def middle(live, image, text, own, beside, across, vecs, bias, after, branch, second):
    cut = image.shape[1]
    for s, (tokens, rows) in enumerate(((image, slice(0, cut)), (text, slice(cut, None)))):
        value = own[0, rows].astype(F32) + beside[0, rows].astype(F32)
        value = value + across[0, rows].astype(F32) + bias[s : s + 1]
        result = tokens[0].astype(F32) + vecs[0, s, 2:3] * value
        normed, _ = normalize(result)
        branch[0, rows] = value
        after[0, rows] = result
        second[0, rows] = (normed * (1.0 + vecs[0, s, 4:5]) + vecs[0, s, 3:4]).astype(BF16)


def middle_back(
    live, image_cot, text_cot, own, beside, across, vecs, after, branch, residual, rounded, sums
):
    cut = image_cot.shape[1]
    for s, (cot, rows) in enumerate(((image_cot, slice(0, cut)), (text_cot, slice(cut, None)))):
        grad = own[0, rows].astype(F32) + beside[0, rows].astype(F32)
        grad = grad + across[0, rows].astype(F32)
        normed, inverse = normalize(after[0, rows])
        value = cot[0].astype(F32) * live + norm_back(grad, normed, inverse, vecs[0, s, 4:5])
        residual[0, rows] = value
        low = (value * vecs[0, s, 2:3]).astype(BF16)
        rounded[0, rows] = low
        sums[0, s, 0:1] = add_up(value * branch[0, rows])
        sums[0, s, 1:2] = add_up(grad)
        sums[0, s, 2:3] = add_up(grad * normed)
        sums[0, s, 3:4] = add_up(low.astype(F32))


def leave(
    live, image_cot, text_cot, own, beside, across, vecs, after, bias, image_out, text_out, sums
):
    cut = image_cot.shape[1]
    for s, (cot, rows, out) in enumerate(
        ((image_cot, slice(0, cut), image_out), (text_cot, slice(cut, None), text_out))
    ):
        value = own[0, rows].astype(F32) + beside[0, rows].astype(F32)
        value = value + across[0, rows].astype(F32) + bias[s : s + 1]
        out[0] = ((after[0, rows] + vecs[0, s, 5:6] * value) * live).astype(BF16)
        sums[0, s : s + 1] = add_up(cot[0].astype(F32) * live * value)


def enter_back(
    live, image, text, own, beside, across, vecs, residual, image_grad, text_grad, sums
):
    cut = image.shape[1]
    for s, (tokens, rows, out) in enumerate(
        ((image, slice(0, cut), image_grad), (text, slice(cut, None), text_grad))
    ):
        grad = own[0, rows].astype(F32) + beside[0, rows].astype(F32)
        grad = grad + across[0, rows].astype(F32)
        normed, inverse = normalize(tokens[0].astype(F32))
        out[0] = residual[0, rows] + norm_back(grad, normed, inverse, vecs[0, s, 1:2])
        sums[0, s, 0:1] = add_up(grad)
        sums[0, s, 1:2] = add_up(grad * normed)


def bias_spec(block):
    return pl.BlockSpec((2, block), lambda j: (0, j))


def add_bias(stream, spot, cut, sums, bias):
    return [sums + bias[stream : stream + 1]]


def gelu_both(stream, spot, cut, sums, bias):
    value = sums + bias[stream : stream + 1]
    factor = math.sqrt(2.0 / math.pi)
    square = value * value
    bend = jnp.tanh(factor * (value + 0.044715 * value * square))
    half = 0.5 * (1.0 + bend)
    slope = half + 0.5 * value * (1.0 - bend * bend) * factor * (1.0 + 0.134145 * square)
    return [value * half, slope]


def times_slope(stream, spot, cut, sums, slope):
    return [sums * slope[spot[0], spot[1], cut].astype(F32)]


def dot(spec, a, b):
    return jnp.einsum(spec, a, b, preferred_element_type=F32)


def on_device(
    groups,
    image_tokens,
    text_tokens,
    conditioning,
    group_seqs,
    ada_weight,
    ada_bias,
    qkv_weight,
    qv_bias,
    proj_weight,
    proj_bias,
    fc1_weight,
    fc1_bias,
    fc2_weight,
    fc2_bias,
    image_cot,
    text_cot,
):
    column = lax.axis_index("tensor")
    group = lax.axis_index("dp")
    ring = Ring(groups)
    order = Order(group_seqs)
    slots, image, width = image_tokens.shape
    text = text_tokens.shape[1]
    tokens = image + text
    rows = qkv_weight.shape[2]
    col_width = qkv_weight.shape[-1]
    hidden = fc1_weight.shape[-1]
    both = range(2)

    proj_turned = jnp.swapaxes(proj_weight, 1, 2)[:, None]
    fc1_shard = fc1_weight[:, None]
    fc2_turned = jnp.swapaxes(fc2_weight, 1, 2)[:, None]

    ada_part = lax.dynamic_slice_in_dim(ada_bias.astype(F32), column * col_width, col_width, 2)
    qv_part = lax.dynamic_slice_in_dim(qv_bias.astype(F32), column * col_width, col_width, 2)
    fc1_part = lax.dynamic_slice_in_dim(fc1_bias.astype(F32), column * hidden, hidden, 1)
    offsets = jnp.stack([qv_part[:, 0], jnp.zeros_like(qv_part[:, 0]), qv_part[:, 1]], 1)
    offsets = offsets.reshape(2, 3 * col_width)
    proj_add = proj_bias.astype(F32)
    fc2_add = fc2_bias.astype(F32)

    cond_act, silu_back = jax.vjp(jax.nn.silu, conditioning.astype(F32))
    cond_low = cond_act.astype(BF16).reshape(slots, groups, rows)
    cond_sends = jnp.stack(
        [
            lax.dynamic_index_in_dim(cond_low, group ^ mask, 1, keepdims=False)
            for mask in range(groups)
        ]
    )
    cond_rows = order(exchange(cond_sends, "dp", groups)).reshape(groups * slots, rows)
    modul_parts = order(dot("cd,sjdn->csjn", cond_rows, ada_weight))
    modul_parts = modul_parts.reshape((groups, slots) + modul_parts.shape[1:])
    modul_local = order(collect(modul_parts, "dp", groups) + ada_part[None])
    qkv_ring = Gather(ring, order(jnp.concatenate([qkv_weight, proj_turned], 1)))
    qkv_part = (0, 3 * col_width)
    proj_part = (3 * col_width, col_width)
    vecs = order(lax.all_gather(modul_local, "tensor", axis=3, tiled=True))

    first, mlp_round, fc2_bias_local = order.run(
        lambda *a: per_slot(
            enter,
            "enter",
            group_seqs,
            a,
            [
                ((slots, tokens, width), BF16),
                ((slots, tokens, width), BF16),
                ((slots, 2, width), F32),
            ],
        ),
        image_tokens,
        text_tokens,
        image_cot,
        text_cot,
        vecs,
    )
    qkv_ring.arrive(order)
    first_move = Spread(order(first))
    qkv_ring.arrive(order)
    qkv_ring.arrive(order)
    first_move.arrive(order)
    first_full = first_move.finish(order)
    qkv_ring.place(order)
    qkv_ring.arrive(order)
    fc1_ring = Gather(ring, order(fc1_shard))
    mlp_move = Spread(order(mlp_round))
    qkv_full = qkv_ring.finish(order)

    qkv = order.run(
        lambda *a: rows_times(
            a[:4], a[4:], image, False, 1, add_bias, (offsets,), (bias_spec,), qkv_part
        ),
        *first_full,
        *qkv_full,
    )
    fc1_ring.arrive(order)
    mixed = ()
    for slot in range(slots):
        mixed = order.run(
            lambda *a, slot=slot: attend(a[0], image, slot, a[1:]), *((qkv,) + tuple(mixed))
        )
    mixed, logs = mixed
    fc1_ring.arrive(order)
    mlp_move.arrive(order)
    branch_parts = order.run(
        lambda *a: rows_times(a[0], a[1:], image, True, "split", columns=proj_part),
        mixed,
        *qkv_full,
    )
    branch_move = Collect(*order(*branch_parts))
    mlp_full = mlp_move.finish(order)
    branch_move.arrive(order)
    fc1_ring.arrive(order)
    fc1_ring.arrive(order)
    fc2_ring = Gather(ring, order(fc2_turned))
    branch_terms = branch_move.finish(order)
    after, branch, second = order.run(
        lambda *a: per_slot(
            middle,
            "middle",
            group_seqs,
            a,
            [
                ((slots, tokens, width), F32),
                ((slots, tokens, width), F32),
                ((slots, tokens, width), BF16),
            ],
        ),
        image_tokens,
        text_tokens,
        *branch_terms,
        vecs,
        proj_add,
    )
    second_move = Spread(second)
    fc1_full = fc1_ring.finish(order)
    fc2_ring.arrive(order)
    fc2_ring.place(order)
    fc2_ring.arrive(order)
    second_move.arrive(order)
    second_full = second_move.finish(order)
    activated, slope = order.run(
        lambda *a: rows_times(
            a[:4], a[4:], image, False, 2, gelu_both, (fc1_part,), (bias_spec,)
        ),
        *second_full,
        *fc1_full,
    )
    fc2_ring.arrive(order)
    *fc2_grad, _ = order.run(
        lambda *a: weight_grad(a[:4], a[4], image, ring), *mlp_full, activated
    )
    fc2_ring.arrive(order)
    fc2_sums = Scatter(ring, *order(*fc2_grad))
    fc2_full = fc2_ring.finish(order)
    pre_round = order.run(
        lambda *a: rows_times(
            a[:4],
            a[4:],
            image,
            False,
            1,
            times_slope,
            (slope,),
            (
                lambda block: pl.BlockSpec(
                    (4, slots, tokens, block), lambda j: (0, 0, 0, j)
                ),
            ),
        ),
        *mlp_full,
        *fc2_full,
    )
    fc2_sums.take(order)
    second_parts = order.run(
        lambda *a: rows_times(a[0], a[1:], image, True, "split"), pre_round, *fc1_full
    )
    second_back = Collect(*second_parts)
    fc2_sums.add(order)
    second_back.arrive(order)
    *fc1_grad, fc1_bias_local = order.run(
        lambda *a: weight_grad(a[:4], a[4], image, ring), *second_full, pre_round
    )
    fc1_sums = Scatter(ring, *order(*fc1_grad))
    mlp_parts = order.run(
        lambda *a: rows_times(a[0], a[1:], image, True, "split"), activated, *fc2_full
    )
    fc2_sums.take(order)
    second_terms = second_back.finish(order)
    residual, branch_round, middle_vecs = order.run(
        lambda *a: per_slot(
            middle_back,
            "middle_back",
            group_seqs,
            a,
            [
                ((slots, tokens, width), F32),
                ((slots, tokens, width), BF16),
                ((slots, 2, 4, width), F32),
            ],
        ),
        image_cot,
        text_cot,
        *second_terms,
        vecs,
        after,
        branch,
    )
    branch_back = Spread(branch_round)
    fc2_sums.add(order)
    fc2_sums.arrive(order)
    fc1_sums.arrive(order)
    branch_back.arrive(order)
    branch_full = branch_back.finish(order)
    mixed_grad = order.run(
        lambda *a: rows_times(a[:4], a[4:], image, False, 1, columns=proj_part),
        *branch_full,
        *qkv_full,
    )
    mlp_back = Collect(*order(*mlp_parts))
    mlp_back.arrive(order)
    *proj_grad, _ = order.run(
        lambda *a: weight_grad(a[:4], a[4], image, ring, 3 * col_width, 4 * col_width),
        *branch_full,
        mixed,
    )
    qkv_grads = None
    for slot in range(slots):
        given = (qkv, mixed, mixed_grad, logs) + (() if slot == 0 else (qkv_grads,))
        qkv_grads = order.run(
            lambda *a, slot=slot: attend_back(
                *a[:4], image, slot, a[4] if len(a) > 4 else None
            ),
            *given,
        )
        if slot == 0:
            fc2_sums.arrive(order)
            fc1_sums.arrive(order)
    mlp_terms = mlp_back.finish(order)
    fc1_sums.arrive(order)
    *qkv_grad, qv_sums = order.run(
        lambda *a: weight_grad(
            a[:4], a[4], image, ring, 0, 4 * col_width, a[5:]
        ),
        *first_full,
        qkv_grads,
        *proj_grad,
    )
    fc1_sums.arrive(order)
    qkv_sums = Scatter(ring, *order(*qkv_grad), "parts")
    first_parts = order.run(
        lambda *a: rows_times(a[0], a[1:], image, True, "split", columns=qkv_part),
        qkv_grads,
        *qkv_full,
    )
    qkv_sums.take(order)
    first_back = Collect(*order(*first_parts))
    qkv_sums.add(order)
    first_back.arrive(order)
    qv_bias_local = qv_sums.reshape(2, 3, col_width)[:, 0::2]
    proj_bias_local = jnp.sum(middle_vecs[:, :, 3], 0)
    fc2_bias_local = jnp.sum(fc2_bias_local, 0)
    split_sums = jnp.concatenate([qv_bias_local.reshape(-1), fc1_bias_local.reshape(-1)])
    token_sums = jnp.concatenate([proj_bias_local.reshape(-1), fc2_bias_local.reshape(-1)])
    bias_local = jnp.concatenate([split_sums, token_sums])
    image_out, text_out, gate_two = order.run(
        lambda *a: per_slot(
            leave,
            "leave",
            group_seqs,
            a,
            [
                (image_tokens.shape, BF16),
                (text_tokens.shape, BF16),
                ((slots, 2, width), F32),
            ],
        ),
        image_cot,
        text_cot,
        *mlp_terms,
        vecs,
        after,
        fc2_add,
    )
    fc2_sum = order(fc2_sums.finish(order))
    fc1_sum = order(fc1_sums.finish(order))
    qkv_sums.arrive(order)
    first_terms = first_back.finish(order)
    image_grad, text_grad, enter_vecs = order.run(
        lambda *a: per_slot(
            enter_back,
            "enter_back",
            group_seqs,
            a,
            [
                (image_tokens.shape, F32),
                (text_tokens.shape, F32),
                ((slots, 2, 2, width), F32),
            ],
        ),
        image_tokens,
        text_tokens,
        *first_terms,
        vecs,
        residual,
    )
    modul_grad = jnp.concatenate(
        [
            enter_vecs,
            middle_vecs[:, :, 0:3],
            gate_two[:, :, None],
        ],
        2,
    ).reshape(slots, 2, 6, 4, col_width)
    modul_blocks = jnp.stack(
        [
            lax.dynamic_index_in_dim(modul_grad, column ^ mask, 3, keepdims=False)
            for mask in range(4)
        ]
    )
    modul_round = order(collect(modul_blocks, "tensor", 4).astype(BF16))
    qkv_sums.take(order)
    shared = jnp.concatenate([modul_round.astype(F32).reshape(-1), bias_local])
    shared = order(shared)
    qkv_sums.add(order)
    shared = order(spread(shared, "dp", groups))
    modul_all = shared[:, : modul_round.size].astype(BF16)
    modul_all = modul_all.reshape((groups * slots,) + modul_round.shape[1:])
    bias_local = jnp.sum(shared[:, modul_round.size :], 0)
    cond_part = dot("csjn,sjdn->cd", modul_all, ada_weight)
    ada_bias_part = jnp.sum(modul_all.astype(F32), 0)
    last = jnp.concatenate([cond_part.reshape(-1), ada_bias_part.reshape(-1), bias_local])
    last = order(spread(order(last), "tensor", 4))
    qkv_sums.arrive(order)
    last = order(last)
    cond_part = jnp.sum(last[:, : cond_part.size], 0).reshape(groups, slots, rows)
    cond_terms = order(exchange(cond_part, "dp", groups))
    cond_term = jnp.stack(
        [
            lax.dynamic_index_in_dim(cond_terms, group ^ place, 0, keepdims=False)
            for place in range(groups)
        ],
        1,
    ).reshape(slots, width)
    cond_grad = lax.dynamic_slice_in_dim(
        silu_back(cond_term)[0], column * col_width, col_width, 1
    )
    last = jnp.stack(
        [
            lax.dynamic_index_in_dim(last[:, cond_part.size :], column ^ place, 0, keepdims=False)
            for place in range(4)
        ]
    )
    ada_bias_grad = by_column(last[:, : ada_bias_part.size], ada_bias_part.shape)
    bias_all = last[:, ada_bias_part.size :]
    cut_a = qv_bias_local.size
    cut_b = cut_a + fc1_bias_local.size
    cut_c = cut_b + proj_bias_local.size
    cut_d = cut_c + fc2_bias_local.size

    qv_bias_grad = by_column(bias_all[:, :cut_a], qv_bias_local.shape)
    fc1_bias_grad = by_column(bias_all[:, cut_a:cut_b], fc1_bias_local.shape)
    proj_bias_grad = jnp.sum(bias_all[:, cut_b:cut_c], 0).reshape(proj_bias_local.shape)
    fc2_bias_grad = jnp.sum(bias_all[:, cut_c:cut_d], 0).reshape(fc2_bias_local.shape)
    ada_grad = dot("cd,csjn->sjdn", cond_rows, modul_all)
    qkv_sum, proj_sum = qkv_sums.finish(order)
    cond_grad = order(cond_grad)
    live = jnp.arange(slots, dtype=jnp.int32) < order.token[0]
    cond_grad = jnp.where(live[:, None], cond_grad, 0.0)
    return (
        image_out,
        text_out,
        image_grad,
        text_grad,
        cond_grad,
        ada_grad,
        ada_bias_grad,
        qkv_sum,
        qv_bias_grad,
        jnp.swapaxes(proj_sum, 1, 2),
        proj_bias_grad,
        fc1_sum,
        fc1_bias_grad,
        jnp.swapaxes(fc2_sum, 1, 2),
        fc2_bias_grad,
    )


def solution(mesh):
    groups = mesh.shape["dp"]
    in_specs = (
        P("dp", "tensor", None),
        P("dp", "tensor", None),
        P("dp", None),
        P("dp"),
        P(None, None, "dp", "tensor"),
        P(),
        P(None, None, "dp", "tensor"),
        P(),
        P(None, "tensor", "dp"),
        P(),
        P(None, "dp", "tensor"),
        P(),
        P(None, "tensor", "dp"),
        P(),
        P("dp", "tensor", None),
        P("dp", "tensor", None),
    )
    out_specs = (
        P("dp", "tensor", None),
        P("dp", "tensor", None),
        P("dp", "tensor", None),
        P("dp", "tensor", None),
        P("dp", "tensor"),
        P(None, None, "dp", "tensor"),
        P(),
        P(None, None, "dp", "tensor"),
        P(),
        P(None, "tensor", "dp"),
        P(),
        P(None, "dp", "tensor"),
        P(),
        P(None, "tensor", "dp"),
        P(),
    )

    def step(*args):
        return on_device(groups, *args)

    return jax.shard_map(
        step, mesh=mesh, in_specs=in_specs, out_specs=out_specs, check_vma=False
    )
```
